32 devices in a mesh: seq: 8 (over y, x, core), head: 4 (over z).
Axes of the slice: x: 2, y: 2, z: 4, core: 2. Of those that a mesh axis runs over, the one named last changes fastest.
Arguments:
- tokens: bfloat16 [16, 1024, 768], P(None, 'seq'), may hold values from -6 to 6
- starts: int32 [16, 8], replicated, may hold values from 0 to 128, as said below
- in_weight: bfloat16 [768, 24, 130], P('seq', 'head'), may hold values from -0.21875 to 0.21875
- state_weight: bfloat16 [768, 256], P('seq'), may hold values from -0.21875 to 0.21875
- state_conv: bfloat16 [256, 5], P('seq'), may hold values from -3 to 3
- out_weight: bfloat16 [768, 24, 64], P('seq', 'head'), may hold values from -0.15625 to 0.15625
- value_conv: bfloat16 [64, 24, 5], P('seq', 'head'), may hold values from -3 to 3
- norm_gain: bfloat16 [768], P('seq'), may hold values from 0.25 to 1.75
- gate_gain: bfloat16 [64, 24], P('seq', 'head'), may hold values from 0.25 to 1.75
- step_bias: float32 [2, 24], P(None, 'head'), may hold values from -1 to 0.5
- decay_log: float32 [24], P('head'), may hold values from -10 to -2.5
- skip: float32 [24], P('head'), may hold values from 0.5 to 8
- out_cotangent: float32 [16, 1024, 768], P(None, 'seq'), may hold values from -6 to 6
Outputs:
- output: float32 [16, 1024, 768], P(None, 'seq')
- input_gradient: float32 [16, 1024, 768], P(None, 'seq')
- in_weight_gradient: float32 [768, 24, 130], P('seq', 'head')
- state_weight_gradient: float32 [768, 256], P(('seq', 'head'))
- state_conv_gradient: float32 [256, 5], P(('seq', 'head'))
- out_weight_gradient: float32 [768, 24, 64], P('seq', 'head')
- value_conv_gradient: float32 [64, 24, 5], P('seq', 'head')
- norm_gain_gradient: float32 [768], P('seq')
- gate_gain_gradient: float32 [64, 24], P('seq', 'head')
- step_bias_gradient: float32 [2, 24], P(None, 'head')
- decay_log_gradient: float32 [24], P('head')
- skip_gradient: float32 [24], P('head')
The draws below stay inside these ranges and needn't reach their ends.
Inputs may be any that keep to these rules, and one draw needn't show every extreme that they name: Entry [s, b] is the offset, within block b of 128 tokens of sequence s, of the token where a document begins, or 128 if none begins there; block 0 of every sequence holds 0; further document starts, at most one a block, lie only in blocks from 2 to 5; in one sequence, drawn from the seed, no other block begins a document.
All inputs are finite; a program needn't handle non-finite values.
Results may differ from the reference program's by a relative error of at most 0.019.
The reference program's roundings to bfloat16 on the way count: a program that leaves them out, or rounds other values in their place, can miss the bound.
Values may be sent and summed in bfloat16 or wider, within the bound.
No kernel may reach another device: no remote copies, remote signals or barrier semaphores. Data moves between devices by JAX's collectives and lax.ppermute only.
A program may use at most 320 MiB of HBM per device.

```python
import math
import jax
import jax.numpy as jnp
from jax import lax

D = 768
HEADS = 24
HEADDIM = 64
STATE = 64
CONV = 4
BLOCK = 128
SEQS = 16
INNER = 1536
PROJ = 130
BLOCKS = 8
SEQ_LEN = 1024


def draw_starts(key, part):
    first_key = jax.random.fold_in(key, 11)
    second_key = jax.random.fold_in(key, 12)
    third_key = jax.random.fold_in(key, 13)
    present = jax.random.randint(first_key, (SEQS, BLOCKS), 0, 2) == 0
    offsets = jax.random.randint(second_key, (SEQS, BLOCKS), 0, BLOCK)
    single = jax.random.randint(third_key, (), 0, SEQS)
    rows = jnp.arange(SEQS)[:, None]
    columns = jnp.arange(BLOCKS)[None, :]
    middle = (columns >= BLOCKS // 4) & (columns < 3 * BLOCKS // 4)
    result = jnp.where(middle & present, offsets, BLOCK)
    result = jnp.where(rows == single, BLOCK, result)
    result = jnp.where(columns == 0, 0, result)
    return result.astype(jnp.int32)


def draw_decay_log(key, part):
    low_end = jnp.log(jnp.float32(0.5) / SEQ_LEN)
    high_end = jnp.log(jnp.float32(0.05))
    fraction = jax.random.uniform(jax.random.fold_in(key, 7), (HEADS,), jnp.float32)
    return (low_end + fraction * (high_end - low_end)).astype(jnp.float32)


def block_levels(own_key, extent, pieces, low, largest):
    level, own = 1.0, jax.random.fold_in(own_key, 6)
    for dim, blocks in pieces:
        steps = jnp.exp(jax.random.uniform(jax.random.fold_in(own, dim), (blocks,), jnp.float32, low / len(pieces), largest / len(pieces)))
        level = level * jnp.repeat(steps, extent[dim] // blocks).reshape([-1 if axis == dim else 1 for axis in range(len(extent))])
    return level


def scatter_about(stream_key, extent, deviation, most, pieces=(), held_as=jnp.bfloat16):
    level = block_levels(stream_key, extent, pieces, -0.22, 0.18) if pieces else 1.0
    values = jax.random.normal(stream_key, extent, jnp.float32) * deviation * level
    return jnp.minimum(jnp.maximum(values, -most), most).astype(held_as)


def setup_inputs(seed: int = 0) -> dict:
    arg_keys = jax.random.split(jax.random.key(seed), 14)
    tokens = scatter_about(arg_keys[0], (SEQS, SEQ_LEN, D), 1.0, 6.0, ((1, 8),))
    starts = draw_starts(jax.random.fold_in(arg_keys[13], 71), 0)
    in_weight = scatter_about(arg_keys[2], (D, HEADS, PROJ), D ** -0.5, 0.21875, ((0, 8), (1, 4)))
    state_weight = scatter_about(arg_keys[3], (D, 4 * STATE), D ** -0.5, 0.21875, ((0, 8),))
    state_conv = scatter_about(arg_keys[4], (4 * STATE, CONV + 1), CONV ** -0.5, 3.0, ((0, 8),))
    out_weight = scatter_about(arg_keys[5], (D, HEADS, HEADDIM), INNER ** -0.5, 0.15625, ((0, 8), (1, 4)))
    value_conv = scatter_about(arg_keys[6], (HEADDIM, HEADS, CONV + 1), CONV ** -0.5, 3.0, ((0, 8), (1, 4)))
    norm_gain = jnp.clip(1.0 + 0.15 * jax.random.normal(arg_keys[7], (D,), jnp.float32), 0.25, 1.75).astype(jnp.bfloat16)
    gate_gain = jnp.clip(1.0 + 0.15 * jax.random.normal(arg_keys[8], (HEADDIM, HEADS), jnp.float32), 0.25, 1.75).astype(jnp.bfloat16)
    step_bias = jnp.clip(-1.0 + 1.5 * jax.random.uniform(arg_keys[9], (2, HEADS), jnp.float32) ** block_levels(arg_keys[9], (2, HEADS), ((1, 4),), -0.2, 0.2), -1.0, 0.5)
    decay_log = draw_decay_log(jax.random.fold_in(arg_keys[13], 71), 0)
    skip = jnp.clip(jnp.exp(math.log(8.0) - 2.7725887 * jax.random.uniform(arg_keys[11], (HEADS,), jnp.float32) ** block_levels(arg_keys[11], (HEADS,), ((0, 4),), -0.2, 0.2)), 0.5, 8.0)
    out_cotangent = scatter_about(arg_keys[12], (SEQS, SEQ_LEN, D), 1.0, 6.0, ((1, 8),), jnp.float32)
    return {"tokens": tokens, "starts": starts, "in_weight": in_weight, "state_weight": state_weight, "state_conv": state_conv, "out_weight": out_weight, "value_conv": value_conv, "norm_gain": norm_gain, "gate_gain": gate_gain, "step_bias": step_bias, "decay_log": decay_log, "skip": skip, "out_cotangent": out_cotangent}


@jax.custom_vjp
def low(v):
    return lax.optimization_barrier(v.astype(jnp.bfloat16)).astype(jnp.float32)

@jax.custom_vjp
def low_back(v):
    return v

def low_keep(v):
    return (low(v), None)

def low_pass(kept, grad):
    return (grad,)

def back_keep(v):
    return (v, None)

def back_low(kept, grad):
    return (low(grad),)
low.defvjp(low_keep, low_pass)
low_back.defvjp(back_keep, back_low)
precise = lax.Precision.HIGHEST

def document_numbers(positions, starts_row):
    begins = jnp.arange(starts_row.shape[0], dtype=jnp.int32) * BLOCK + starts_row
    valid = starts_row < BLOCK
    hits = (begins[None, :] <= positions[:, None]) & valid[None, :]
    return lax.optimization_barrier(jnp.sum(hits.astype(jnp.int32), axis=1))

def convolve(inputs, taps, lag_masks):
    length = inputs.shape[0]
    reach = taps.shape[1] - 1
    padded = jnp.pad(inputs, ((reach - 1, 0), (0, 0)))
    total = jnp.broadcast_to(taps[:, reach], inputs.shape)
    for lag in range(reach):
        total = total + taps[:, lag] * padded[reach - 1 - lag:reach - 1 - lag + length] * lag_masks[:, lag:lag + 1]
    return total

def chain_block(state, inputs):
    readout, intake, values, log_decay, step_size, segment = inputs
    decay_sum = jnp.cumsum(log_decay, axis=0)
    order = jnp.arange(readout.shape[0])
    mask = ((order[:, None] > order[None, :]) & (segment[:, None] == segment[None, :]))[:, :, None]
    scores = low_back(jnp.dot(readout, intake.T, precision=precise))
    gap = jnp.where(mask, decay_sum[:, None, :] - decay_sum[None, :, :], 0.0)
    mixing = low(jnp.where(mask, jnp.exp(gap), 0.0) * step_size[None, :, :] * scores[:, :, None])
    inner = jnp.einsum('tjh,jhp->thp', mixing, values, precision=precise)
    carried = low_back(jnp.einsum('tn,hnp->thp', readout, low(state), precision=precise))
    head_scale = jnp.exp(decay_sum) * (segment == 0)[:, None]
    tail = jnp.exp(decay_sum[-1][None, :] - decay_sum) * step_size * (segment == segment[-1])[:, None]
    scaled_intake = low(tail[:, :, None] * intake[:, None, :])
    local_state = low_back(jnp.einsum('jhn,jhp->hnp', scaled_intake, values, precision=precise))
    block_decay = jnp.exp(decay_sum[-1]) * (segment[-1] == 0)
    return (block_decay[:, None, None] * state + local_state, inner + head_scale[:, :, None] * carried)

def chain(readout, intake, values, log_decay, step_size, flags):
    blocks = readout.shape[0] // BLOCK

    def split(array):
        return array.reshape((blocks, BLOCK) + array.shape[1:])
    segment = jnp.cumsum(split(flags), axis=1).astype(jnp.int32)
    initial = jnp.zeros((values.shape[1], STATE, HEADDIM), jnp.float32)
    final, outputs = lax.scan(jax.checkpoint(chain_block), initial, (split(readout), split(intake), split(values), split(log_decay), split(step_size), segment))
    return outputs.reshape(values.shape)

def layer(tokens, in_weight, state_weight, state_conv, out_weight, value_conv, norm_gain, gate_gain, step_bias, decay_log, skip, starts_row):
    length = tokens.shape[0]
    heads = in_weight.shape[1]
    reach = state_conv.shape[1] - 1
    numbers = document_numbers(jnp.arange(-(reach - 1), length + 1, dtype=jnp.int32), starts_row)
    here = numbers[reach - 1:reach - 1 + length]
    lag_masks = jnp.stack([here == numbers[reach - 1 - lag:reach - 1 - lag + length] for lag in range(reach)], axis=1).astype(jnp.float32)
    first = (here != numbers[reach - 2:reach - 2 + length]).astype(jnp.int32)
    ending = jnp.arange(length) == length - 1
    last = ((numbers[reach:reach + length] != here) | ending).astype(jnp.int32)
    normed = low(tokens * lax.rsqrt(lax.optimization_barrier(jnp.mean(tokens * tokens, axis=1, keepdims=True)) + 1e-05) * norm_gain)
    projected = low_back(jnp.einsum('td,dhk->thk', normed, in_weight, precision=precise))
    state_proj = low_back(jnp.dot(normed, state_weight, precision=precise))
    gate = projected[:, :, :HEADDIM]
    value_in = low(projected[:, :, HEADDIM:2 * HEADDIM].reshape(length, heads * HEADDIM))
    step_raw = projected[:, :, 2 * HEADDIM:]
    state_in = low(state_proj)
    value_taps = jnp.transpose(value_conv, (1, 0, 2)).reshape(heads * HEADDIM, reach + 1)
    values = low(jax.nn.silu(convolve(value_in, value_taps, lag_masks))).reshape(length, heads, HEADDIM)
    states = low(jax.nn.silu(convolve(state_in, state_conv, lag_masks)))
    intake_forward = states[:, :STATE]
    readout_forward = states[:, STATE:2 * STATE]
    intake_reverse = states[:, 2 * STATE:3 * STATE]
    readout_reverse = states[:, 3 * STATE:]
    step = jax.nn.softplus(step_raw + jnp.transpose(step_bias)[None])
    rate = jnp.exp(decay_log)
    log_decay = -step * rate[None, :, None]
    forward_out = chain(readout_forward, intake_forward, values, log_decay[:, :, 0], step[:, :, 0], first)
    reverse_out = jnp.flip(chain(jnp.flip(readout_reverse, 0), jnp.flip(intake_reverse, 0), jnp.flip(values, 0), jnp.flip(log_decay[:, :, 1], 0), jnp.flip(step[:, :, 1], 0), jnp.flip(last, 0)), 0)
    core = low_back(forward_out + reverse_out + skip[None, :, None] * values)
    gated = core * jax.nn.silu(gate)
    gate_scale = lax.rsqrt(lax.optimization_barrier(jnp.mean(gated * gated, axis=(1, 2))) + 1e-05)
    unscaled = low(gated * jnp.transpose(gate_gain)[None])
    pre_out = low_back(jnp.einsum('thp,dhp->td', unscaled, out_weight, precision=precise))
    return tokens + gate_scale[:, None] * pre_out

def reference(tokens, starts, in_weight, state_weight, state_conv, out_weight, value_conv, norm_gain, gate_gain, step_bias, decay_log, skip, out_cotangent):
    weights = (in_weight.astype(jnp.float32), state_weight.astype(jnp.float32), state_conv.astype(jnp.float32), out_weight.astype(jnp.float32), value_conv.astype(jnp.float32), norm_gain.astype(jnp.float32), gate_gain.astype(jnp.float32), step_bias.astype(jnp.float32), decay_log.astype(jnp.float32), skip.astype(jnp.float32))

    def one_sequence(totals, item):
        sequence, cotangent, starts_row = item

        def forward_pass(sequence_in, *params):
            return layer(sequence_in, *params, starts_row)
        result, pullback = jax.vjp(forward_pass, sequence.astype(jnp.float32), *weights)
        grads = pullback(cotangent)
        summed = tuple((total + extra for total, extra in zip(totals, grads[1:])))
        return (summed, (result, grads[0]))
    zeros = tuple((jnp.zeros_like(weight) for weight in weights))
    totals, (outputs, input_grads) = lax.scan(one_sequence, zeros, (tokens, out_cotangent, starts))
    return (outputs, input_grads, totals[0], totals[1], totals[2], totals[3], totals[4], totals[5], totals[6], totals[7], totals[8], totals[9])
```

```python
import jax
import jax.numpy as jnp
from jax import lax
from jax.sharding import Mesh, PartitionSpec as P

HEADS = 24
HEADDIM = 64
STATE = 64
CHIP_SEQUENCES = 16


def from_behind(value, axis, by):
    devices = lax.axis_size(axis)
    pairs = [(i, i + by) for i in range(devices) if 0 <= i + by < devices]
    return lax.ppermute(value, axis, pairs)


def entering(value, axis, join, neutral, backward):
    count, mine = (lax.axis_size(axis), lax.axis_index(axis))
    pieces = jax.tree.map(lambda part: lax.all_gather(part, axis), value)
    if backward:
        pieces = jax.tree.map(lambda part: part[::-1], pieces)
        mine = count - 1 - mine
    running = jax.tree.map(
        lambda part, zero: jnp.full_like(part, 0) + jnp.asarray(zero, part.dtype), value, neutral
    )

    def step(position, running):
        longer = join(running, jax.tree.map(lambda part: part[position], pieces))
        return jax.tree.map(lambda new, old: jnp.where(position < mine, new, old), longer, running)

    return lax.fori_loop(0, count - 1, step, running)


def affine(earlier, later):
    return (earlier[0] * later[0], later[0][..., None, None] * earlier[1] + later[1])


def document_numbers(starts, first_position, count, block_size):
    blocks = starts.shape[1]
    begins = jnp.arange(blocks, dtype=jnp.int32)[None, :] * block_size + starts
    valid = starts < block_size
    places = first_position + jnp.arange(count, dtype=jnp.int32)
    hits = (begins[:, None, :] <= places[None, :, None]) & valid[:, None, :]
    return jnp.sum(hits.astype(jnp.int32), axis=2)


def running_sum(value):
    length, shift = value.shape[-1], 1
    while shift < length:
        pad = [(0, 0)] * (value.ndim - 1) + [(shift, 0)]
        value = value + jnp.pad(value[..., : length - shift], pad)
        shift *= 2
    return value


def chain_forward(readout, intake, values, log_decay, step_size, flags):
    block_size = readout.shape[1]
    segment = running_sum(flags)
    decay_sum = running_sum(log_decay)
    scores = jnp.einsum("mtn,mjn->mtj", readout, intake, preferred_element_type=jnp.float32)
    order = jnp.arange(block_size)
    mask = ((order[:, None] > order[None, :])[None] & (segment[:, :, None] == segment[:, None, :]))[
        :, None
    ]
    gap = jnp.where(mask, decay_sum[:, :, :, None] - decay_sum[:, :, None, :], 0.0)
    decay_table = jnp.where(mask, jnp.exp(gap), 0.0)
    mixing = (scores[:, None] * decay_table * step_size[:, :, None, :]).astype(jnp.bfloat16)
    inner = jnp.einsum("mhtj,mjhp->mthp", mixing, values, preferred_element_type=jnp.float32)
    tail_factor = (
        jnp.exp(decay_sum[:, :, -1:] - decay_sum) * (segment == segment[:, -1:])[:, None, :]
    )
    scaled_intake = (
        (tail_factor * step_size)[..., None] * intake[:, None].astype(jnp.float32)
    ).astype(jnp.bfloat16)
    local_state = jnp.einsum(
        "mhjn,mjhp->mhnp", scaled_intake, values, preferred_element_type=jnp.float32
    )
    block_decay = jnp.exp(decay_sum[:, :, -1]) * (segment[:, -1] == 0)[:, None]
    head_scale = jnp.exp(decay_sum) * (segment == 0)[:, None, :]
    saved = (scores, decay_table, mixing, tail_factor, scaled_intake, head_scale)
    return (inner, local_state, block_decay, saved)


def chain_finish(inner, readout, state_in, head_scale):
    state_low = state_in.astype(jnp.bfloat16)
    carried = jnp.einsum("mtn,mhnp->mthp", readout, state_low, preferred_element_type=jnp.float32)
    return (inner + jnp.swapaxes(head_scale, 1, 2)[..., None] * carried, carried, state_low)


def chain_back_state(grad_out, readout, carried, state_low, head_scale):
    grad_wide = grad_out.astype(jnp.float32)
    carried_grad = (jnp.swapaxes(head_scale, 1, 2)[..., None] * grad_wide).astype(jnp.bfloat16)
    state_in_grad = jnp.einsum(
        "mtn,mthp->mhnp", readout, carried_grad, preferred_element_type=jnp.float32
    )
    readout_grad = jnp.einsum(
        "mthp,mhnp->mtn", carried_grad, state_low, preferred_element_type=jnp.float32
    )
    sum_grad = jnp.swapaxes(jnp.sum(grad_wide * carried, axis=3), 1, 2) * head_scale
    return (state_in_grad, readout_grad, sum_grad)


def chain_back_rest(
    grad_out,
    readout,
    intake,
    values,
    step_size,
    state_in,
    later,
    block_decay,
    saved,
    readout_grad,
    sum_grad,
):
    scores, decay_table, mixing, tail_factor, scaled_intake, head_scale = saved
    later_low = later.astype(jnp.bfloat16)
    scaled_grad = jnp.einsum(
        "mjhp,mhnp->mhjn", values, later_low, preferred_element_type=jnp.float32
    )
    values_grad = jnp.einsum(
        "mhjn,mhnp->mjhp", scaled_intake, later_low, preferred_element_type=jnp.float32
    )
    tail_grad = jnp.einsum("mhjn,mjn->mhj", scaled_grad, intake.astype(jnp.float32))
    intake_grad = jnp.einsum("mhjn,mhj->mjn", scaled_grad, tail_factor * step_size)
    step_grad = tail_grad * tail_factor
    tail_term = tail_grad * tail_factor * step_size
    decay_grad = jnp.sum(later * state_in, axis=(2, 3)) * block_decay
    sum_grad = (sum_grad - tail_term).at[:, :, -1].add(jnp.sum(tail_term, axis=2) + decay_grad)
    mixing_grad = jnp.einsum(
        "mthp,mjhp->mhtj", grad_out, values, preferred_element_type=jnp.float32
    )
    values_grad = values_grad + jnp.einsum(
        "mhtj,mthp->mjhp", mixing, grad_out, preferred_element_type=jnp.float32
    )
    through = mixing_grad * decay_table
    scores_grad = jnp.sum(through * step_size[:, :, None, :], axis=1).astype(jnp.bfloat16)
    readout_grad = readout_grad + jnp.einsum(
        "mtj,mjn->mtn", scores_grad, intake, preferred_element_type=jnp.float32
    )
    intake_grad = intake_grad + jnp.einsum(
        "mtj,mtn->mjn", scores_grad, readout, preferred_element_type=jnp.float32
    )
    kernel = through * scores[:, None]
    step_grad = step_grad + jnp.sum(kernel, axis=2)
    weighted = kernel * step_size[:, :, None, :]
    sum_grad = sum_grad + jnp.sum(weighted, axis=3) - jnp.sum(weighted, axis=2)
    log_grad = jnp.flip(running_sum(jnp.flip(sum_grad, 2)), 2)
    return (values_grad, readout_grad, intake_grad, step_grad, log_grad)


def split_plan(
    tokens,
    starts,
    in_weight,
    state_weight,
    state_conv,
    out_weight,
    value_conv,
    norm_gain,
    gate_gain,
    step_bias,
    decay_log,
    skip,
    out_cotangent,
):
    sequences, block_size, width = tokens.shape
    place = lax.axis_index("seq")
    devices_seq = lax.axis_size("seq")
    in_weights, state_weights, state_taps, out_weights, value_taps, norm_whole, gate_whole = (
        lax.all_gather(in_weight, "seq", axis=0, tiled=True),
        lax.all_gather(state_weight, "seq", axis=0, tiled=True),
        lax.all_gather(state_conv, "seq", axis=0, tiled=True),
        lax.all_gather(out_weight, "seq", axis=0, tiled=True),
        lax.all_gather(value_conv, "seq", axis=0, tiled=True),
        lax.all_gather(norm_gain, "seq", axis=0, tiled=True),
        lax.all_gather(gate_gain, "seq", axis=0, tiled=True),
    )
    heads_here = in_weight.shape[1]
    value_width = heads_here * HEADDIM
    reach = state_conv.shape[1] - 1
    edge = reach - 1
    numbers = document_numbers(starts, place * block_size - edge, block_size + 2 * edge, block_size)
    lag_masks = jnp.stack(
        [
            numbers[:, edge:] == numbers[:, edge - lag : block_size + 2 * edge - lag]
            for lag in range(reach)
        ],
        axis=2,
    ).astype(jnp.float32)
    first = (
        numbers[:, edge : edge + block_size] != numbers[:, edge - 1 : edge + block_size - 1]
    ).astype(jnp.int32)
    positions = place * block_size + jnp.arange(block_size, dtype=jnp.int32)
    ending = (positions == devices_seq * block_size - 1)[None, :]
    last = (
        (numbers[:, edge + 1 : edge + block_size + 1] != numbers[:, edge : edge + block_size])
        | ending
    ).astype(jnp.int32)
    tokens_wide = tokens.astype(jnp.float32)
    in_scale = lax.rsqrt(jnp.mean(tokens_wide * tokens_wide, axis=2, keepdims=True) + 1e-05)
    unit = tokens_wide * in_scale
    norm_wide = norm_whole.astype(jnp.float32)
    normed = (unit * norm_wide).astype(jnp.bfloat16)
    projected = jnp.einsum("mtd,dhk->mthk", normed, in_weights, preferred_element_type=jnp.float32)
    state_proj = jnp.einsum(
        "mtd,dn->mtn", normed, state_weights, preferred_element_type=jnp.float32
    )
    gate = projected[..., :HEADDIM]
    step_raw = projected[..., 2 * HEADDIM :]
    conv_input = jnp.concatenate(
        [
            projected[..., HEADDIM : 2 * HEADDIM].reshape(sequences, block_size, value_width),
            state_proj,
        ],
        axis=2,
    ).astype(jnp.bfloat16)
    channels = conv_input.shape[2]
    halo_rows = from_behind(conv_input[:, block_size - edge :], "seq", 1)
    extended = jnp.concatenate([halo_rows, conv_input], axis=1)
    taps = jnp.concatenate(
        [jnp.transpose(value_taps, (1, 0, 2)).reshape(value_width, reach + 1), state_taps], axis=0
    ).astype(jnp.float32)
    pre_active = jnp.broadcast_to(taps[:, reach], (sequences, block_size, channels))
    for lag in range(reach):
        pre_active = (
            pre_active
            + taps[:, lag]
            * extended[:, edge - lag : edge - lag + block_size]
            * lag_masks[:, :block_size, lag, None]
        )
    active_sigma = jax.nn.sigmoid(pre_active)
    activated = (pre_active * active_sigma).astype(jnp.bfloat16)
    values = activated[..., :value_width].reshape(sequences, block_size, heads_here, HEADDIM)
    intake_forward = activated[..., value_width : value_width + STATE]
    readout_forward = activated[..., value_width + STATE : value_width + 2 * STATE]
    intake_reverse = jnp.flip(activated[..., value_width + 2 * STATE : value_width + 3 * STATE], 1)
    readout_reverse = jnp.flip(activated[..., value_width + 3 * STATE :], 1)
    values_reversed = jnp.flip(values, 1)
    rate = jnp.exp(decay_log)
    bias_here = jnp.transpose(step_bias)[None, None]
    step_all = jax.nn.softplus(step_raw + bias_here)
    step_forward = jnp.transpose(step_all[..., 0], (0, 2, 1))
    step_reverse = jnp.flip(jnp.transpose(step_all[..., 1], (0, 2, 1)), 2)
    log_forward = -step_forward * rate[None, :, None]
    log_reverse = -step_reverse * rate[None, :, None]
    inner_forward, local_forward, decay_forward, saved_forward = chain_forward(
        readout_forward, intake_forward, values, log_forward, step_forward, first
    )
    inner_reverse, local_reverse, decay_reverse, saved_reverse = chain_forward(
        readout_reverse,
        intake_reverse,
        values_reversed,
        log_reverse,
        step_reverse,
        jnp.flip(last, 1),
    )
    identity = (jnp.ones_like(decay_forward), jnp.zeros_like(local_forward))
    state_forward = entering((decay_forward, local_forward), "seq", affine, identity, False)[1]
    state_reverse = entering((decay_reverse, local_reverse), "seq", affine, identity, True)[1]
    out_forward, carried_forward, state_low_forward = chain_finish(
        inner_forward, readout_forward, state_forward, saved_forward[5]
    )
    out_reverse, carried_reverse, state_low_reverse = chain_finish(
        inner_reverse, readout_reverse, state_reverse, saved_reverse[5]
    )
    core = (
        out_forward
        + jnp.flip(out_reverse, 1)
        + skip[None, None, :, None] * values.astype(jnp.float32)
    )
    gate_sigma = jax.nn.sigmoid(gate)
    gated = core * gate * gate_sigma
    gate_gains = jnp.transpose(gate_whole).astype(jnp.float32)
    unscaled = (gated * gate_gains).astype(jnp.bfloat16)
    squares = jnp.sum(gated * gated, axis=(2, 3))
    partial_value = jnp.einsum(
        "mthp,dhp->mtd", unscaled, out_weights, preferred_element_type=jnp.float32
    )
    pre_out, square_sum = lax.psum((partial_value, squares), "head")
    inner_width = HEADS * HEADDIM
    gate_scale = lax.rsqrt(square_sum / inner_width + 1e-05)
    output = tokens_wide + gate_scale[..., None] * pre_out
    total_grad = (gate_scale[..., None] * out_cotangent).astype(jnp.bfloat16)
    unscaled_grad = jnp.einsum(
        "mtd,dhp->mthp", total_grad, out_weights, preferred_element_type=jnp.float32
    )
    out_weight_grad = jnp.einsum(
        "mtd,mthp->dhp", total_grad, unscaled, preferred_element_type=jnp.float32
    )
    scale_grad = jnp.sum(out_cotangent * pre_out, axis=2)
    square_grad = -0.5 * scale_grad * gate_scale**3 / inner_width
    gated_grad = unscaled_grad * gate_gains + 2.0 * gated * square_grad[..., None, None]
    gate_gain_grad = jnp.transpose(jnp.sum(unscaled_grad * gated, axis=(0, 1)))
    core_grad = (gated_grad * gate * gate_sigma).astype(jnp.bfloat16)
    gate_grad = gated_grad * core * gate_sigma * (1.0 + gate * (1.0 - gate_sigma))
    skip_grad = jnp.sum(core_grad.astype(jnp.float32) * values.astype(jnp.float32), axis=(0, 1, 3))
    core_reversed = jnp.flip(core_grad, 1)
    state_grad_forward, readout_grad_forward, sum_grad_forward = chain_back_state(
        core_grad, readout_forward, carried_forward, state_low_forward, saved_forward[5]
    )
    state_grad_reverse, readout_grad_reverse, sum_grad_reverse = chain_back_state(
        core_reversed, readout_reverse, carried_reverse, state_low_reverse, saved_reverse[5]
    )
    later_forward = entering((decay_forward, state_grad_forward), "seq", affine, identity, True)[1]
    later_reverse = entering((decay_reverse, state_grad_reverse), "seq", affine, identity, False)[1]
    (
        values_grad_forward,
        readout_grad_forward,
        intake_grad_forward,
        step_grad_forward,
        log_grad_forward,
    ) = chain_back_rest(
        core_grad,
        readout_forward,
        intake_forward,
        values,
        step_forward,
        state_forward,
        later_forward,
        decay_forward,
        saved_forward,
        readout_grad_forward,
        sum_grad_forward,
    )
    (
        values_grad_reverse,
        readout_grad_reverse,
        intake_grad_reverse,
        step_grad_reverse,
        log_grad_reverse,
    ) = chain_back_rest(
        core_reversed,
        readout_reverse,
        intake_reverse,
        values_reversed,
        step_reverse,
        state_reverse,
        later_reverse,
        decay_reverse,
        saved_reverse,
        readout_grad_reverse,
        sum_grad_reverse,
    )
    values_grad = (
        values_grad_forward
        + jnp.flip(values_grad_reverse, 1)
        + skip[None, None, :, None] * core_grad.astype(jnp.float32)
    )
    step_total_forward = step_grad_forward - rate[None, :, None] * log_grad_forward
    step_total_reverse = jnp.flip(step_grad_reverse - rate[None, :, None] * log_grad_reverse, 2)
    decay_log_grad = jnp.sum(log_grad_forward * log_forward, axis=(0, 2)) + jnp.sum(
        log_grad_reverse * log_reverse, axis=(0, 2)
    )
    step_total = jnp.stack(
        [
            jnp.transpose(step_total_forward, (0, 2, 1)),
            jnp.transpose(step_total_reverse, (0, 2, 1)),
        ],
        axis=3,
    )
    raw_grad = step_total * jax.nn.sigmoid(step_raw + bias_here)
    step_bias_grad = jnp.transpose(jnp.sum(raw_grad, axis=(0, 1)))
    state_grads = jnp.concatenate(
        [
            intake_grad_forward,
            readout_grad_forward,
            jnp.flip(intake_grad_reverse, 1),
            jnp.flip(readout_grad_reverse, 1),
        ],
        axis=2,
    )
    active_grad = jnp.concatenate(
        [values_grad.reshape(sequences, block_size, value_width), state_grads], axis=2
    )
    pre_grad = active_grad * active_sigma * (1.0 + pre_active * (1.0 - active_sigma))
    following = from_behind(pre_grad[:, :edge], "seq", -1)
    grad_extended = jnp.concatenate([pre_grad, following], axis=1)
    conv_input_grad = jnp.zeros((sequences, block_size, channels), jnp.float32)
    tap_grads = []
    for lag in range(reach):
        conv_input_grad = (
            conv_input_grad
            + taps[:, lag]
            * grad_extended[:, lag : lag + block_size]
            * lag_masks[:, lag : lag + block_size, lag, None]
        )
        tap_grads.append(
            jnp.sum(
                pre_grad
                * extended[:, edge - lag : edge - lag + block_size]
                * lag_masks[:, :block_size, lag, None],
                axis=(0, 1),
            )
        )
    tap_grads.append(jnp.sum(pre_grad, axis=(0, 1)))
    taps_grad = jnp.stack(tap_grads, axis=1)
    value_conv_grad = jnp.transpose(
        taps_grad[:value_width].reshape(heads_here, HEADDIM, reach + 1), (1, 0, 2)
    )
    state_conv_grad = taps_grad[value_width:]
    proj_grad = jnp.concatenate(
        [
            gate_grad,
            conv_input_grad[..., :value_width].reshape(sequences, block_size, heads_here, HEADDIM),
            raw_grad,
        ],
        axis=3,
    ).astype(jnp.bfloat16)
    state_proj_grad = conv_input_grad[..., value_width:].astype(jnp.bfloat16)
    normed_part = jnp.einsum(
        "mthk,dhk->mtd", proj_grad, in_weights, preferred_element_type=jnp.float32
    )
    normed_part = normed_part + jnp.einsum(
        "mtn,dn->mtd", state_proj_grad, state_weights, preferred_element_type=jnp.float32
    )
    normed_grad = lax.psum(normed_part, "head")
    in_weight_grad = jnp.einsum(
        "mtd,mthk->dhk", normed, proj_grad, preferred_element_type=jnp.float32
    )
    state_weight_grad = jnp.einsum(
        "mtd,mtn->dn", normed, state_proj_grad, preferred_element_type=jnp.float32
    )
    norm_gain_grad = jnp.sum(normed_grad * unit, axis=(0, 1))
    unit_grad = normed_grad * norm_wide
    input_gradient = out_cotangent + in_scale * (
        unit_grad - unit * jnp.mean(unit_grad * unit, axis=2, keepdims=True)
    )
    in_weight_out, out_weight_out, value_conv_out, norm_gain_out, gate_gain_out = (
        lax.psum_scatter(in_weight_grad, "seq", scatter_dimension=0, tiled=True),
        lax.psum_scatter(out_weight_grad, "seq", scatter_dimension=0, tiled=True),
        lax.psum_scatter(value_conv_grad, "seq", scatter_dimension=0, tiled=True),
        lax.psum_scatter(norm_gain_grad, "seq", scatter_dimension=0, tiled=True),
        lax.psum_scatter(gate_gain_grad, "seq", scatter_dimension=0, tiled=True),
    )
    state_weight_out, state_conv_out = (
        lax.psum_scatter(state_weight_grad, ("seq", "head"), scatter_dimension=0, tiled=True),
        lax.psum_scatter(state_conv_grad, ("seq", "head"), scatter_dimension=0, tiled=True),
    )
    step_bias_out, decay_log_out, skip_out = lax.psum(
        (step_bias_grad, decay_log_grad, skip_grad), "seq"
    )
    return (
        output,
        input_gradient,
        in_weight_out,
        state_weight_out,
        state_conv_out,
        out_weight_out,
        value_conv_out,
        norm_gain_out,
        gate_gain_out,
        step_bias_out,
        decay_log_out,
        skip_out,
    )


def line_gather(value, axis):
    count, mine = lax.axis_size(axis), lax.axis_index(axis)
    right = [(i, i + 1) for i in range(count - 1)]
    left = [(i + 1, i) for i in range(count - 1)]
    rights, lefts = [value], [value]
    for _ in range(count - 1):
        rights.append(lax.ppermute(rights[-1], axis, right))
        lefts.append(lax.ppermute(lefts[-1], axis, left))
    return [value] + [
        jnp.where(mine >= k, rights[k], lefts[count - k]) for k in range(1, count)
    ]


def spread(value, axis):
    count = lax.axis_size(axis)
    return lax.all_to_all(jnp.broadcast_to(value[None], (count,) + value.shape), axis, 0, 0)


def swap_core(value):
    return lax.ppermute(value, "core", [(0, 1), (1, 0)])


def both_cores(value):
    other = swap_core(value)
    first = lax.axis_index("core") == 0
    return jnp.stack([jnp.where(first, value, other), jnp.where(first, other, value)])


def triangle(size, lower):
    order = jnp.arange(size)
    keep = order[:, None] >= order[None, :] if lower else order[:, None] <= order[None, :]
    return keep.astype(jnp.float32)


def block_sum(value, lower):
    return jnp.einsum(
        "mhu,tu->mht", value, triangle(value.shape[2], lower), precision=lax.Precision.HIGHEST
    )


def local_forward(readout, intake, values, log_decay, step_size, segment, reverse):
    block_size = readout.shape[1]
    end = 0 if reverse else block_size - 1
    decay_sum = block_sum(log_decay, not reverse)
    scores = jnp.einsum("mtn,mjn->mtj", readout, intake, preferred_element_type=jnp.float32)
    order = jnp.arange(block_size)
    before = order[:, None] < order[None, :] if reverse else order[:, None] > order[None, :]
    mask = (before[None] & (segment[:, :, None] == segment[:, None, :]))[:, None]
    gap = jnp.where(mask, decay_sum[:, :, :, None] - decay_sum[:, :, None, :], 0.0)
    decay_table = jnp.where(mask, jnp.exp(gap), 0.0)
    mixing = (scores[:, None] * decay_table * step_size[:, :, None, :]).astype(jnp.bfloat16)
    inner = jnp.einsum("mhtj,mjhp->mthp", mixing, values, preferred_element_type=jnp.float32)
    tail_factor = (
        jnp.exp(decay_sum[:, :, end : end + 1] - decay_sum)
        * (segment == segment[:, end : end + 1])[:, None, :]
    )
    scaled_intake = (
        (tail_factor * step_size)[..., None] * intake[:, None].astype(jnp.float32)
    ).astype(jnp.bfloat16)
    local_state = jnp.einsum(
        "mhjn,mjhp->mhnp", scaled_intake, values, preferred_element_type=jnp.float32
    )
    block_decay = jnp.exp(decay_sum[:, :, end]) * (segment[:, end] == 0)[:, None]
    head_scale = jnp.exp(decay_sum) * (segment == 0)[:, None, :]
    saved = (scores, decay_table, mixing, tail_factor, scaled_intake, head_scale)
    return (inner, local_state, block_decay, saved)


def carry_states(decay, states, forward):
    blocks = states.shape[0]
    running, result = jnp.zeros_like(states[0]), [None] * blocks
    for block in range(blocks) if forward else range(blocks - 1, -1, -1):
        result[block] = running
        running = decay[block][:, None, None] * running + states[block]
    return jnp.stack(result)


def local_back_rest(
    grad_out, readout, intake, values, step_size, state_in, later, block_decay, saved,
    readout_grad, sum_grad, reverse,
):
    scores, decay_table, mixing, tail_factor, scaled_intake, head_scale = saved
    end = 0 if reverse else readout.shape[1] - 1
    later_low = later.astype(jnp.bfloat16)
    scaled_grad = jnp.einsum(
        "mjhp,mhnp->mhjn", values, later_low, preferred_element_type=jnp.float32
    )
    values_grad = jnp.einsum(
        "mhjn,mhnp->mjhp", scaled_intake, later_low, preferred_element_type=jnp.float32
    )
    tail_grad = jnp.sum(scaled_grad * intake[:, None].astype(jnp.float32), axis=3)
    intake_grad = jnp.sum(scaled_grad * (tail_factor * step_size)[..., None], axis=1)
    step_grad = tail_grad * tail_factor
    tail_term = tail_grad * tail_factor * step_size
    decay_grad = jnp.sum(later * state_in, axis=(2, 3)) * block_decay
    sum_grad = (sum_grad - tail_term).at[:, :, end].add(jnp.sum(tail_term, axis=2) + decay_grad)
    mixing_grad = jnp.einsum(
        "mthp,mjhp->mhtj", grad_out, values, preferred_element_type=jnp.float32
    )
    values_grad = values_grad + jnp.einsum(
        "mhtj,mthp->mjhp", mixing, grad_out, preferred_element_type=jnp.float32
    )
    through = mixing_grad * decay_table
    scores_grad = jnp.sum(through * step_size[:, :, None, :], axis=1).astype(jnp.bfloat16)
    readout_grad = readout_grad + jnp.einsum(
        "mtj,mjn->mtn", scores_grad, intake, preferred_element_type=jnp.float32
    )
    intake_grad = intake_grad + jnp.einsum(
        "mtj,mtn->mjn", scores_grad, readout, preferred_element_type=jnp.float32
    )
    kernel = through * scores[:, None]
    step_grad = step_grad + jnp.sum(kernel, axis=2)
    weighted = kernel * step_size[:, :, None, :]
    sum_grad = sum_grad + jnp.sum(weighted, axis=3) - jnp.sum(weighted, axis=2)
    log_grad = block_sum(sum_grad, reverse)
    return (values_grad, readout_grad, intake_grad, step_grad, log_grad)


def chip_plan(
    tokens,
    starts,
    in_weight,
    state_weight,
    state_conv,
    out_weight,
    value_conv,
    norm_gain,
    gate_gain,
    step_bias,
    decay_log,
    skip,
    out_cotangent,
):
    low, wide = jnp.bfloat16, jnp.float32
    sequences, block_size, width = tokens.shape
    chips, planes = lax.axis_size("chip"), lax.axis_size("head")
    chip, core, plane = lax.axis_index("chip"), lax.axis_index("core"), lax.axis_index("head")
    blocks = starts.shape[1]
    length = blocks * block_size
    rows, group = in_weight.shape[:2]
    groups = planes // 2
    heads_here = group * groups
    inner_here = heads_here * HEADDIM
    reach = state_conv.shape[1] - 1
    edge = reach - 1

    def own_plane(value):
        return lax.dynamic_slice_in_dim(value, plane * chips, chips, 0)

    def to_sequence(mine):
        return jnp.swapaxes(both_cores(mine), 0, 1).reshape((length,) + mine.shape[2:])

    tokens_mine = lax.all_to_all(own_plane(tokens), "chip", 0, 0)
    tokens_whole = to_sequence(tokens_mine)
    cotangent_mine = lax.all_to_all(own_plane(out_cotangent).astype(low), "chip", 0, 0)
    cotangent = to_sequence(cotangent_mine)

    small = jnp.concatenate(
        [value_conv.transpose(1, 0, 2).reshape(-1), gate_gain.transpose(1, 0).reshape(-1)]
    )
    small_cols = -(-small.size // rows)
    small = jnp.pad(small, (0, small_cols * rows - small.size)).reshape(rows, small_cols)
    flat_in = in_weight.reshape(rows, -1)
    slab = jnp.concatenate([flat_in, out_weight.reshape(rows, -1), small], axis=1)
    by_plane = spread(slab, "head")
    mine = lax.dynamic_slice_in_dim(by_plane, core * groups, groups, 0)
    theirs = swap_core(lax.dynamic_slice_in_dim(by_plane, (1 - core) * groups, groups, 0))
    first = core == 0
    pair = jnp.stack([jnp.where(first, mine, theirs), jnp.where(first, theirs, mine)])
    slabs = spread(pair, "chip").reshape(2 * chips, groups, rows, -1)
    in_cols, out_cols = flat_in.shape[1], group * HEADDIM
    in_heads = slabs[..., :in_cols].reshape(2 * chips, groups, rows, group, -1)
    in_heads = in_heads.transpose(0, 2, 1, 3, 4).reshape(width, heads_here, -1)
    out_heads = slabs[..., in_cols : in_cols + out_cols].reshape(2 * chips, groups, rows, group, -1)
    out_heads = out_heads.transpose(0, 2, 1, 3, 4).reshape(width, heads_here, HEADDIM)
    small_all = slabs[..., in_cols + out_cols :].reshape(2 * chips, groups, -1)
    taps_size = value_conv.size
    part = value_conv.shape[0]
    value_taps = small_all[..., :taps_size].reshape(2 * chips, groups, group, part, reach + 1)
    value_taps = value_taps.transpose(1, 2, 0, 3, 4).reshape(inner_here, reach + 1)
    gate_gains = small_all[..., taps_size : taps_size + gate_gain.size]
    gate_gains = gate_gains.reshape(2 * chips, groups, group, part)
    gate_gains = gate_gains.transpose(1, 2, 0, 3).reshape(heads_here, HEADDIM).astype(wide)
    conv_flat = state_conv.reshape(-1)
    conv_cols = -(-conv_flat.size // rows)
    conv_flat = jnp.pad(conv_flat, (0, conv_cols * rows - conv_flat.size)).reshape(rows, conv_cols)
    state_slab = jnp.concatenate([state_weight, norm_gain[:, None], conv_flat], axis=1)
    state_slabs = spread(both_cores(state_slab), "chip").reshape(2 * chips, rows, -1)
    channels_state = state_weight.shape[1]
    state_weights = state_slabs[..., :channels_state].reshape(width, channels_state)
    norm_wide = state_slabs[..., channels_state].reshape(width).astype(wide)
    state_taps = state_slabs[..., channels_state + 1 :].reshape(2 * chips, -1)
    state_taps = state_taps[:, : state_conv.size].reshape(channels_state, reach + 1)

    def own_heads(value, axis):
        every = spread(value, "head")
        picked = lax.dynamic_slice_in_dim(every, core * groups, groups, 0)
        return jnp.concatenate([picked[i] for i in range(groups)], axis=axis)

    scalars = own_heads(jnp.concatenate([step_bias, decay_log[None], skip[None]], axis=0), 1)
    bias_here, rate, skip_here = jnp.transpose(scalars[:2]), jnp.exp(scalars[2]), scalars[3]

    starts_row = lax.dynamic_slice_in_dim(starts, plane * chips + chip, 1, 0)
    numbers = document_numbers(starts_row, -edge, length + 2 * edge, block_size)[0]
    lag_masks = jnp.stack(
        [numbers[edge:] == numbers[edge - lag : length + 2 * edge - lag] for lag in range(reach)],
        axis=1,
    ).astype(wide)
    here = numbers[edge : edge + length]
    first_flag = (here != numbers[edge - 1 : edge + length - 1]).astype(jnp.int32)
    ending = jnp.arange(length) == length - 1
    last_flag = ((numbers[edge + 1 : edge + length + 1] != here) | ending).astype(jnp.int32)
    segment_forward = running_sum(first_flag.reshape(blocks, block_size))
    segment_reverse = jnp.flip(running_sum(jnp.flip(last_flag.reshape(blocks, block_size), 1)), 1)

    tokens_wide = tokens_whole.astype(wide)
    in_scale = lax.rsqrt(jnp.mean(tokens_wide * tokens_wide, axis=1, keepdims=True) + 1e-05)
    unit = tokens_wide * in_scale
    normed = (unit * norm_wide).astype(low)
    projected = jnp.einsum("td,dhk->thk", normed, in_heads, preferred_element_type=wide)
    state_proj = jnp.einsum("td,dn->tn", normed, state_weights, preferred_element_type=wide)
    gate = projected[..., :HEADDIM]
    step_raw = projected[..., 2 * HEADDIM :]
    conv_input = jnp.concatenate(
        [projected[..., HEADDIM : 2 * HEADDIM].reshape(length, inner_here), state_proj], axis=1
    ).astype(low)
    channels = conv_input.shape[1]
    extended = jnp.pad(conv_input, ((edge, 0), (0, 0)))
    taps = jnp.concatenate([value_taps, state_taps], axis=0).astype(wide)
    pre_active = jnp.broadcast_to(taps[:, reach], (length, channels))
    for lag in range(reach):
        pre_active = (
            pre_active
            + taps[:, lag]
            * extended[edge - lag : edge - lag + length]
            * lag_masks[:length, lag, None]
        )
    active_sigma = jax.nn.sigmoid(pre_active)
    activated = (pre_active * active_sigma).astype(low)
    values = activated[:, :inner_here].reshape(blocks, block_size, heads_here, HEADDIM)
    state_act = activated[:, inner_here:].reshape(blocks, block_size, 4, STATE)
    intake_f, readout_f, intake_r, readout_r = (state_act[:, :, i] for i in range(4))
    step_all = jax.nn.softplus(step_raw + bias_here).reshape(blocks, block_size, heads_here, 2)
    step_f = jnp.transpose(step_all[..., 0], (0, 2, 1))
    step_r = jnp.transpose(step_all[..., 1], (0, 2, 1))
    log_f = -step_f * rate[None, :, None]
    log_r = -step_r * rate[None, :, None]

    inner_f, local_f, decay_f, saved_f = local_forward(
        readout_f, intake_f, values, log_f, step_f, segment_forward, False
    )
    inner_r, local_r, decay_r, saved_r = local_forward(
        readout_r, intake_r, values, log_r, step_r, segment_reverse, True
    )
    state_f = carry_states(decay_f, local_f, True)
    state_r = carry_states(decay_r, local_r, False)
    out_f, carried_f, low_f = chain_finish(inner_f, readout_f, state_f, saved_f[5])
    out_r, carried_r, low_r = chain_finish(inner_r, readout_r, state_r, saved_r[5])
    core_out = out_f + out_r + skip_here[:, None] * values.astype(wide)
    gate = gate.reshape(blocks, block_size, heads_here, HEADDIM)
    gate_sigma = jax.nn.sigmoid(gate)
    gated = core_out * gate * gate_sigma
    unscaled = (gated * gate_gains).astype(low)
    squares = jnp.sum(gated * gated, axis=(2, 3)).reshape(length)
    flat_unscaled = unscaled.reshape(length, inner_here)
    flat_out = out_heads.reshape(width, inner_here)

    raw_unscaled_grad = jnp.einsum("td,dk->tk", cotangent, flat_out, preferred_element_type=wide)
    projections = jnp.sum(raw_unscaled_grad * flat_unscaled.astype(wide), axis=1)
    own_sums = jnp.stack([squares, projections])
    sums = own_sums + swap_core(own_sums)
    inner_width = HEADS * HEADDIM
    gate_scale = lax.rsqrt(sums[0] / inner_width + 1e-05)
    scale_grad = sums[1]

    partial_out = jnp.einsum("tk,dk->td", flat_unscaled, flat_out, preferred_element_type=wide)

    def reduce_cores(value):
        pieces = value.reshape(chips, 2, block_size, width)
        keep = lax.dynamic_index_in_dim(pieces, core, 1, keepdims=False)
        send = lax.dynamic_index_in_dim(pieces, 1 - core, 1, keepdims=False).astype(low)
        return keep + swap_core(send).astype(wide)

    def own_parity(value):
        pieces = value.reshape((chips, 2, block_size) + value.shape[1:])
        return lax.dynamic_index_in_dim(pieces, core, 1, keepdims=False)

    def deliver(delta, base):
        pieces = line_gather(lax.all_to_all(delta.astype(low), "chip", 0, 0), "head")
        result = jnp.zeros(base.shape, wide).reshape((planes, chips) + base.shape[1:])
        base = base.reshape(result.shape)
        for k, piece in enumerate(pieces):
            at = (plane - k) % planes
            summed = lax.dynamic_index_in_dim(base, at, 0, keepdims=True).astype(wide) + piece[
                None
            ].astype(wide)
            result = lax.dynamic_update_slice_in_dim(result, summed, at, 0)
        return result.reshape(sequences, block_size, width)

    out_delta = own_parity(gate_scale)[..., None] * reduce_cores(partial_out)
    output = deliver(out_delta, tokens)

    total_grad = (gate_scale[:, None] * cotangent.astype(wide)).astype(low)
    out_weight_grad = jnp.einsum("td,tk->dk", total_grad, flat_unscaled, preferred_element_type=wide)
    unscaled_grad = (gate_scale[:, None] * raw_unscaled_grad).reshape(gated.shape)
    square_grad = (scale_grad * gate_scale**3 / inner_width).reshape(blocks, block_size, 1, 1)
    gated_grad = unscaled_grad * gate_gains - gated * square_grad
    gate_gain_grad = jnp.sum(unscaled_grad * gated, axis=(0, 1))
    core_grad = (gated_grad * gate * gate_sigma).astype(low)
    gate_grad = gated_grad * core_out * gate_sigma * (1.0 + gate * (1.0 - gate_sigma))
    skip_grad = jnp.sum(core_grad.astype(wide) * values.astype(wide), axis=(0, 1, 3))

    back_f, readout_grad_f, sum_grad_f = chain_back_state(
        core_grad, readout_f, carried_f, low_f, saved_f[5]
    )
    back_r, readout_grad_r, sum_grad_r = chain_back_state(
        core_grad, readout_r, carried_r, low_r, saved_r[5]
    )
    later_f = carry_states(decay_f, back_f, False)
    later_r = carry_states(decay_r, back_r, True)
    values_grad_f, readout_grad_f, intake_grad_f, step_grad_f, log_grad_f = local_back_rest(
        core_grad, readout_f, intake_f, values, step_f, state_f, later_f, decay_f, saved_f,
        readout_grad_f, sum_grad_f, False,
    )
    values_grad_r, readout_grad_r, intake_grad_r, step_grad_r, log_grad_r = local_back_rest(
        core_grad, readout_r, intake_r, values, step_r, state_r, later_r, decay_r, saved_r,
        readout_grad_r, sum_grad_r, True,
    )
    values_grad = values_grad_f + values_grad_r + skip_here[:, None] * core_grad.astype(wide)
    total_f = step_grad_f - rate[None, :, None] * log_grad_f
    total_r = step_grad_r - rate[None, :, None] * log_grad_r
    decay_log_grad = jnp.sum(log_grad_f * log_f + log_grad_r * log_r, axis=(0, 2))
    step_total = jnp.stack(
        [jnp.transpose(total_f, (0, 2, 1)), jnp.transpose(total_r, (0, 2, 1))], axis=3
    ).reshape(length, heads_here, 2)
    raw_grad = step_total * jax.nn.sigmoid(step_raw + bias_here)
    step_bias_grad = jnp.transpose(jnp.sum(raw_grad, axis=0))

    active_grad = jnp.concatenate(
        [
            values_grad.reshape(length, inner_here),
            *(
                part.reshape(length, STATE)
                for part in (intake_grad_f, readout_grad_f, intake_grad_r, readout_grad_r)
            ),
        ],
        axis=1,
    )
    pre_grad = active_grad * active_sigma * (1.0 + pre_active * (1.0 - active_sigma))
    grad_extended = jnp.pad(pre_grad, ((0, edge), (0, 0)))
    conv_input_grad = jnp.zeros((length, channels), wide)
    tap_grads = []
    for lag in range(reach):
        conv_input_grad = (
            conv_input_grad
            + taps[:, lag]
            * grad_extended[lag : lag + length]
            * lag_masks[lag : lag + length, lag, None]
        )
        tap_grads.append(
            jnp.sum(
                pre_grad
                * extended[edge - lag : edge - lag + length]
                * lag_masks[:length, lag, None],
                axis=0,
            )
        )
    tap_grads.append(jnp.sum(pre_grad, axis=0))
    taps_grad = jnp.stack(tap_grads, axis=1)

    proj_grad = jnp.concatenate(
        [
            gate_grad.reshape(length, heads_here, HEADDIM),
            conv_input_grad[:, :inner_here].reshape(length, heads_here, HEADDIM),
            raw_grad,
        ],
        axis=2,
    ).astype(low)
    state_proj_grad = conv_input_grad[:, inner_here:].astype(low)
    normed_part = jnp.einsum("thk,dhk->td", proj_grad, in_heads, preferred_element_type=wide)
    normed_part = normed_part + jnp.einsum(
        "tn,dn->td", state_proj_grad, state_weights, preferred_element_type=wide
    )
    normed_grad = reduce_cores(normed_part)
    unit_mine = own_parity(unit)
    unit_grad = normed_grad * norm_wide
    delta = own_parity(in_scale) * (
        unit_grad - unit_mine * jnp.mean(unit_grad * unit_mine, axis=2, keepdims=True)
    )
    input_gradient = deliver(delta, out_cotangent)
    norm_gain_grad = jnp.sum(normed_grad * unit_mine, axis=(0, 1))

    in_weight_grad = jnp.einsum("td,thk->dhk", normed, proj_grad, preferred_element_type=wide)
    state_weight_grad = jnp.einsum("td,tn->dn", normed, state_proj_grad, preferred_element_type=wide)
    value_conv_grad = taps_grad[:inner_here].reshape(groups, group, 2 * chips, part, reach + 1)
    value_conv_grad = value_conv_grad.transpose(2, 0, 1, 3, 4).reshape(2 * chips, groups, -1)
    gain_grad = gate_gain_grad.reshape(groups, group, 2 * chips, part)
    gain_grad = gain_grad.transpose(2, 0, 1, 3).reshape(2 * chips, groups, -1)
    small_grad = jnp.concatenate([value_conv_grad, gain_grad], axis=2)
    small_grad = jnp.pad(
        small_grad, ((0, 0), (0, 0), (0, small_cols * rows - small_grad.shape[2]))
    ).reshape(2 * chips, groups, rows, small_cols)

    def by_owner(value):
        value = value.reshape(2 * chips, rows, groups, -1)
        return value.transpose(0, 2, 1, 3)

    slab_grad = jnp.concatenate(
        [by_owner(in_weight_grad), by_owner(out_weight_grad), small_grad], axis=3
    ).reshape(chips, 2, groups, rows, -1)
    state_grad = jnp.concatenate(
        [
            state_weight_grad.reshape(2 * chips, -1),
            taps_grad[inner_here:].reshape(2 * chips, -1),
        ],
        axis=1,
    ).reshape(chips, 2, -1)

    def over_chips(value):
        moved = lax.all_to_all(value.astype(low), "chip", 0, 0)
        return jnp.sum(moved.astype(wide), axis=0)

    slab_pair = over_chips(slab_grad).astype(low)
    keep = lax.dynamic_index_in_dim(slab_pair, core, 0, keepdims=False)
    got = swap_core(lax.dynamic_index_in_dim(slab_pair, 1 - core, 0, keepdims=False))
    by_group = jnp.concatenate(
        [jnp.where(first, keep, got), jnp.where(first, got, keep)], axis=0
    )
    slab_sum = jnp.sum(lax.all_to_all(by_group, "head", 0, 0).astype(wide), axis=0)
    in_weight_out = slab_sum[:, :in_cols].reshape(rows, group, -1)
    out_weight_out = slab_sum[:, in_cols : in_cols + out_cols].reshape(rows, group, HEADDIM)
    small_out = slab_sum[:, in_cols + out_cols :].reshape(-1)
    value_conv_out = small_out[:taps_size].reshape(group, part, reach + 1).transpose(1, 0, 2)
    gate_gain_out = small_out[taps_size : taps_size + gate_gain.size].reshape(group, part)
    gate_gain_out = gate_gain_out.transpose(1, 0)
    state_pair = over_chips(state_grad)
    state_mine = lax.dynamic_index_in_dim(state_pair, core, 0, keepdims=False)
    state_send = lax.dynamic_index_in_dim(state_pair, 1 - core, 0, keepdims=False)
    state_mine = state_mine + swap_core(state_send)
    weight_size = state_weight.size
    state_mine = jnp.concatenate(
        [
            state_mine[:weight_size].reshape(planes, -1),
            state_mine[weight_size:].reshape(planes, -1),
        ],
        axis=1,
    )
    state_out = jnp.sum(lax.all_to_all(state_mine.astype(low), "head", 0, 0).astype(wide), axis=0)
    state_weight_out = state_out[: weight_size // planes].reshape(-1, channels_state)
    state_conv_out = state_out[weight_size // planes :].reshape(-1, reach + 1)

    scalar_grad = jnp.concatenate([step_bias_grad, decay_log_grad[None], skip_grad[None]], axis=0)
    scalar_all = jnp.zeros((4, planes * group), wide)
    scalar_all = lax.dynamic_update_slice_in_dim(scalar_all, scalar_grad, core * heads_here, 1)
    everything = lax.psum(
        jnp.concatenate([norm_gain_grad, scalar_all.reshape(-1)]), ("chip", "core", "head")
    )
    norm_gain_out = lax.dynamic_slice_in_dim(everything, (2 * chip + core) * rows, rows, 0)
    scalar_out = everything[width:].reshape(4, planes * group)
    scalar_out = lax.dynamic_slice_in_dim(scalar_out, plane * group, group, 1)
    return (
        output,
        input_gradient,
        in_weight_out,
        state_weight_out,
        state_conv_out,
        out_weight_out,
        value_conv_out,
        norm_gain_out,
        gate_gain_out,
        scalar_out[:2],
        scalar_out[2],
        scalar_out[3],
    )


def solution(mesh):
    devices_seq, planes = mesh.devices.shape
    seq, plan = "seq", split_plan
    if devices_seq % 2 == 0 and planes % 2 == 0 and devices_seq // 2 * planes == CHIP_SEQUENCES:
        shape = (devices_seq // 2, 2, planes)
        mesh = Mesh(mesh.devices.reshape(shape), ("chip", "core", "head"))
        seq, plan = ("chip", "core"), chip_plan
    both = seq + ("head",) if isinstance(seq, tuple) else (seq, "head")
    return jax.shard_map(
        plan,
        mesh=mesh,
        in_specs=(
            P(None, seq, None),
            P(),
            P(seq, "head", None),
            P(seq, None),
            P(seq, None),
            P(seq, "head", None),
            P(seq, "head", None),
            P(seq),
            P(seq, "head"),
            P(None, "head"),
            P("head"),
            P("head"),
            P(None, seq, None),
        ),
        out_specs=(
            P(None, seq, None),
            P(None, seq, None),
            P(seq, "head", None),
            P(both, None),
            P(both, None),
            P(seq, "head", None),
            P(seq, "head", None),
            P(seq),
            P(seq, "head"),
            P(None, "head"),
            P("head"),
            P("head"),
        ),
        check_vma=False,
    )
```

```python
import jax
import jax.numpy as jnp
from jax import lax
from jax.experimental import pallas as pl
from jax.experimental.pallas import tpu as pltpu
from jax.sharding import Mesh, PartitionSpec as P

HEADS = 24
HEADDIM = 64
STATE = 64
CHIP_SEQUENCES = 16


def from_behind(value, axis, by):
    devices = lax.axis_size(axis)
    pairs = [(i, i + by) for i in range(devices) if 0 <= i + by < devices]
    return lax.ppermute(value, axis, pairs)


def entering(value, axis, join, neutral, backward):
    count, mine = (lax.axis_size(axis), lax.axis_index(axis))
    pieces = jax.tree.map(lambda part: lax.all_gather(part, axis), value)
    if backward:
        pieces = jax.tree.map(lambda part: part[::-1], pieces)
        mine = count - 1 - mine
    running = jax.tree.map(
        lambda part, zero: jnp.full_like(part, 0) + jnp.asarray(zero, part.dtype), value, neutral
    )

    def step(position, running):
        longer = join(running, jax.tree.map(lambda part: part[position], pieces))
        return jax.tree.map(lambda new, old: jnp.where(position < mine, new, old), longer, running)

    return lax.fori_loop(0, count - 1, step, running)


def affine(earlier, later):
    return (earlier[0] * later[0], later[0][..., None, None] * earlier[1] + later[1])


def document_numbers(starts, first_position, count, block_size):
    blocks = starts.shape[1]
    begins = jnp.arange(blocks, dtype=jnp.int32)[None, :] * block_size + starts
    valid = starts < block_size
    places = first_position + jnp.arange(count, dtype=jnp.int32)
    hits = (begins[:, None, :] <= places[None, :, None]) & valid[:, None, :]
    return jnp.sum(hits.astype(jnp.int32), axis=2)


def running_sum(value):
    length, shift = value.shape[-1], 1
    while shift < length:
        pad = [(0, 0)] * (value.ndim - 1) + [(shift, 0)]
        value = value + jnp.pad(value[..., : length - shift], pad)
        shift *= 2
    return value


def chain_forward(readout, intake, values, log_decay, step_size, flags):
    block_size = readout.shape[1]
    segment = running_sum(flags)
    decay_sum = running_sum(log_decay)
    scores = jnp.einsum("mtn,mjn->mtj", readout, intake, preferred_element_type=jnp.float32)
    order = jnp.arange(block_size)
    mask = ((order[:, None] > order[None, :])[None] & (segment[:, :, None] == segment[:, None, :]))[
        :, None
    ]
    gap = jnp.where(mask, decay_sum[:, :, :, None] - decay_sum[:, :, None, :], 0.0)
    decay_table = jnp.where(mask, jnp.exp(gap), 0.0)
    mixing = (scores[:, None] * decay_table * step_size[:, :, None, :]).astype(jnp.bfloat16)
    inner = jnp.einsum("mhtj,mjhp->mthp", mixing, values, preferred_element_type=jnp.float32)
    tail_factor = (
        jnp.exp(decay_sum[:, :, -1:] - decay_sum) * (segment == segment[:, -1:])[:, None, :]
    )
    scaled_intake = (
        (tail_factor * step_size)[..., None] * intake[:, None].astype(jnp.float32)
    ).astype(jnp.bfloat16)
    local_state = jnp.einsum(
        "mhjn,mjhp->mhnp", scaled_intake, values, preferred_element_type=jnp.float32
    )
    block_decay = jnp.exp(decay_sum[:, :, -1]) * (segment[:, -1] == 0)[:, None]
    head_scale = jnp.exp(decay_sum) * (segment == 0)[:, None, :]
    saved = (scores, decay_table, mixing, tail_factor, scaled_intake, head_scale)
    return (inner, local_state, block_decay, saved)


def chain_finish(inner, readout, state_in, head_scale):
    state_low = state_in.astype(jnp.bfloat16)
    carried = jnp.einsum("mtn,mhnp->mthp", readout, state_low, preferred_element_type=jnp.float32)
    return (inner + jnp.swapaxes(head_scale, 1, 2)[..., None] * carried, carried, state_low)


def chain_back_state(grad_out, readout, carried, state_low, head_scale):
    grad_wide = grad_out.astype(jnp.float32)
    carried_grad = (jnp.swapaxes(head_scale, 1, 2)[..., None] * grad_wide).astype(jnp.bfloat16)
    state_in_grad = jnp.einsum(
        "mtn,mthp->mhnp", readout, carried_grad, preferred_element_type=jnp.float32
    )
    readout_grad = jnp.einsum(
        "mthp,mhnp->mtn", carried_grad, state_low, preferred_element_type=jnp.float32
    )
    sum_grad = jnp.swapaxes(jnp.sum(grad_wide * carried, axis=3), 1, 2) * head_scale
    return (state_in_grad, readout_grad, sum_grad)


def chain_back_rest(
    grad_out,
    readout,
    intake,
    values,
    step_size,
    state_in,
    later,
    block_decay,
    saved,
    readout_grad,
    sum_grad,
):
    scores, decay_table, mixing, tail_factor, scaled_intake, head_scale = saved
    later_low = later.astype(jnp.bfloat16)
    scaled_grad = jnp.einsum(
        "mjhp,mhnp->mhjn", values, later_low, preferred_element_type=jnp.float32
    )
    values_grad = jnp.einsum(
        "mhjn,mhnp->mjhp", scaled_intake, later_low, preferred_element_type=jnp.float32
    )
    tail_grad = jnp.einsum("mhjn,mjn->mhj", scaled_grad, intake.astype(jnp.float32))
    intake_grad = jnp.einsum("mhjn,mhj->mjn", scaled_grad, tail_factor * step_size)
    step_grad = tail_grad * tail_factor
    tail_term = tail_grad * tail_factor * step_size
    decay_grad = jnp.sum(later * state_in, axis=(2, 3)) * block_decay
    sum_grad = (sum_grad - tail_term).at[:, :, -1].add(jnp.sum(tail_term, axis=2) + decay_grad)
    mixing_grad = jnp.einsum(
        "mthp,mjhp->mhtj", grad_out, values, preferred_element_type=jnp.float32
    )
    values_grad = values_grad + jnp.einsum(
        "mhtj,mthp->mjhp", mixing, grad_out, preferred_element_type=jnp.float32
    )
    through = mixing_grad * decay_table
    scores_grad = jnp.sum(through * step_size[:, :, None, :], axis=1).astype(jnp.bfloat16)
    readout_grad = readout_grad + jnp.einsum(
        "mtj,mjn->mtn", scores_grad, intake, preferred_element_type=jnp.float32
    )
    intake_grad = intake_grad + jnp.einsum(
        "mtj,mtn->mjn", scores_grad, readout, preferred_element_type=jnp.float32
    )
    kernel = through * scores[:, None]
    step_grad = step_grad + jnp.sum(kernel, axis=2)
    weighted = kernel * step_size[:, :, None, :]
    sum_grad = sum_grad + jnp.sum(weighted, axis=3) - jnp.sum(weighted, axis=2)
    log_grad = jnp.flip(running_sum(jnp.flip(sum_grad, 2)), 2)
    return (values_grad, readout_grad, intake_grad, step_grad, log_grad)


def split_plan(
    tokens,
    starts,
    in_weight,
    state_weight,
    state_conv,
    out_weight,
    value_conv,
    norm_gain,
    gate_gain,
    step_bias,
    decay_log,
    skip,
    out_cotangent,
):
    sequences, block_size, width = tokens.shape
    place = lax.axis_index("seq")
    devices_seq = lax.axis_size("seq")
    in_weights, state_weights, state_taps, out_weights, value_taps, norm_whole, gate_whole = (
        lax.all_gather(in_weight, "seq", axis=0, tiled=True),
        lax.all_gather(state_weight, "seq", axis=0, tiled=True),
        lax.all_gather(state_conv, "seq", axis=0, tiled=True),
        lax.all_gather(out_weight, "seq", axis=0, tiled=True),
        lax.all_gather(value_conv, "seq", axis=0, tiled=True),
        lax.all_gather(norm_gain, "seq", axis=0, tiled=True),
        lax.all_gather(gate_gain, "seq", axis=0, tiled=True),
    )
    heads_here = in_weight.shape[1]
    value_width = heads_here * HEADDIM
    reach = state_conv.shape[1] - 1
    edge = reach - 1
    numbers = document_numbers(starts, place * block_size - edge, block_size + 2 * edge, block_size)
    lag_masks = jnp.stack(
        [
            numbers[:, edge:] == numbers[:, edge - lag : block_size + 2 * edge - lag]
            for lag in range(reach)
        ],
        axis=2,
    ).astype(jnp.float32)
    first = (
        numbers[:, edge : edge + block_size] != numbers[:, edge - 1 : edge + block_size - 1]
    ).astype(jnp.int32)
    positions = place * block_size + jnp.arange(block_size, dtype=jnp.int32)
    ending = (positions == devices_seq * block_size - 1)[None, :]
    last = (
        (numbers[:, edge + 1 : edge + block_size + 1] != numbers[:, edge : edge + block_size])
        | ending
    ).astype(jnp.int32)
    tokens_wide = tokens.astype(jnp.float32)
    in_scale = lax.rsqrt(jnp.mean(tokens_wide * tokens_wide, axis=2, keepdims=True) + 1e-05)
    unit = tokens_wide * in_scale
    norm_wide = norm_whole.astype(jnp.float32)
    normed = (unit * norm_wide).astype(jnp.bfloat16)
    projected = jnp.einsum("mtd,dhk->mthk", normed, in_weights, preferred_element_type=jnp.float32)
    state_proj = jnp.einsum(
        "mtd,dn->mtn", normed, state_weights, preferred_element_type=jnp.float32
    )
    gate = projected[..., :HEADDIM]
    step_raw = projected[..., 2 * HEADDIM :]
    conv_input = jnp.concatenate(
        [
            projected[..., HEADDIM : 2 * HEADDIM].reshape(sequences, block_size, value_width),
            state_proj,
        ],
        axis=2,
    ).astype(jnp.bfloat16)
    channels = conv_input.shape[2]
    halo_rows = from_behind(conv_input[:, block_size - edge :], "seq", 1)
    extended = jnp.concatenate([halo_rows, conv_input], axis=1)
    taps = jnp.concatenate(
        [jnp.transpose(value_taps, (1, 0, 2)).reshape(value_width, reach + 1), state_taps], axis=0
    ).astype(jnp.float32)
    pre_active = jnp.broadcast_to(taps[:, reach], (sequences, block_size, channels))
    for lag in range(reach):
        pre_active = (
            pre_active
            + taps[:, lag]
            * extended[:, edge - lag : edge - lag + block_size]
            * lag_masks[:, :block_size, lag, None]
        )
    active_sigma = jax.nn.sigmoid(pre_active)
    activated = (pre_active * active_sigma).astype(jnp.bfloat16)
    values = activated[..., :value_width].reshape(sequences, block_size, heads_here, HEADDIM)
    intake_forward = activated[..., value_width : value_width + STATE]
    readout_forward = activated[..., value_width + STATE : value_width + 2 * STATE]
    intake_reverse = jnp.flip(activated[..., value_width + 2 * STATE : value_width + 3 * STATE], 1)
    readout_reverse = jnp.flip(activated[..., value_width + 3 * STATE :], 1)
    values_reversed = jnp.flip(values, 1)
    rate = jnp.exp(decay_log)
    bias_here = jnp.transpose(step_bias)[None, None]
    step_all = jax.nn.softplus(step_raw + bias_here)
    step_forward = jnp.transpose(step_all[..., 0], (0, 2, 1))
    step_reverse = jnp.flip(jnp.transpose(step_all[..., 1], (0, 2, 1)), 2)
    log_forward = -step_forward * rate[None, :, None]
    log_reverse = -step_reverse * rate[None, :, None]
    inner_forward, local_forward, decay_forward, saved_forward = chain_forward(
        readout_forward, intake_forward, values, log_forward, step_forward, first
    )
    inner_reverse, local_reverse, decay_reverse, saved_reverse = chain_forward(
        readout_reverse,
        intake_reverse,
        values_reversed,
        log_reverse,
        step_reverse,
        jnp.flip(last, 1),
    )
    identity = (jnp.ones_like(decay_forward), jnp.zeros_like(local_forward))
    state_forward = entering((decay_forward, local_forward), "seq", affine, identity, False)[1]
    state_reverse = entering((decay_reverse, local_reverse), "seq", affine, identity, True)[1]
    out_forward, carried_forward, state_low_forward = chain_finish(
        inner_forward, readout_forward, state_forward, saved_forward[5]
    )
    out_reverse, carried_reverse, state_low_reverse = chain_finish(
        inner_reverse, readout_reverse, state_reverse, saved_reverse[5]
    )
    core = (
        out_forward
        + jnp.flip(out_reverse, 1)
        + skip[None, None, :, None] * values.astype(jnp.float32)
    )
    gate_sigma = jax.nn.sigmoid(gate)
    gated = core * gate * gate_sigma
    gate_gains = jnp.transpose(gate_whole).astype(jnp.float32)
    unscaled = (gated * gate_gains).astype(jnp.bfloat16)
    squares = jnp.sum(gated * gated, axis=(2, 3))
    partial_value = jnp.einsum(
        "mthp,dhp->mtd", unscaled, out_weights, preferred_element_type=jnp.float32
    )
    pre_out, square_sum = lax.psum((partial_value, squares), "head")
    inner_width = HEADS * HEADDIM
    gate_scale = lax.rsqrt(square_sum / inner_width + 1e-05)
    output = tokens_wide + gate_scale[..., None] * pre_out
    total_grad = (gate_scale[..., None] * out_cotangent).astype(jnp.bfloat16)
    unscaled_grad = jnp.einsum(
        "mtd,dhp->mthp", total_grad, out_weights, preferred_element_type=jnp.float32
    )
    out_weight_grad = jnp.einsum(
        "mtd,mthp->dhp", total_grad, unscaled, preferred_element_type=jnp.float32
    )
    scale_grad = jnp.sum(out_cotangent * pre_out, axis=2)
    square_grad = -0.5 * scale_grad * gate_scale**3 / inner_width
    gated_grad = unscaled_grad * gate_gains + 2.0 * gated * square_grad[..., None, None]
    gate_gain_grad = jnp.transpose(jnp.sum(unscaled_grad * gated, axis=(0, 1)))
    core_grad = (gated_grad * gate * gate_sigma).astype(jnp.bfloat16)
    gate_grad = gated_grad * core * gate_sigma * (1.0 + gate * (1.0 - gate_sigma))
    skip_grad = jnp.sum(core_grad.astype(jnp.float32) * values.astype(jnp.float32), axis=(0, 1, 3))
    core_reversed = jnp.flip(core_grad, 1)
    state_grad_forward, readout_grad_forward, sum_grad_forward = chain_back_state(
        core_grad, readout_forward, carried_forward, state_low_forward, saved_forward[5]
    )
    state_grad_reverse, readout_grad_reverse, sum_grad_reverse = chain_back_state(
        core_reversed, readout_reverse, carried_reverse, state_low_reverse, saved_reverse[5]
    )
    later_forward = entering((decay_forward, state_grad_forward), "seq", affine, identity, True)[1]
    later_reverse = entering((decay_reverse, state_grad_reverse), "seq", affine, identity, False)[1]
    (
        values_grad_forward,
        readout_grad_forward,
        intake_grad_forward,
        step_grad_forward,
        log_grad_forward,
    ) = chain_back_rest(
        core_grad,
        readout_forward,
        intake_forward,
        values,
        step_forward,
        state_forward,
        later_forward,
        decay_forward,
        saved_forward,
        readout_grad_forward,
        sum_grad_forward,
    )
    (
        values_grad_reverse,
        readout_grad_reverse,
        intake_grad_reverse,
        step_grad_reverse,
        log_grad_reverse,
    ) = chain_back_rest(
        core_reversed,
        readout_reverse,
        intake_reverse,
        values_reversed,
        step_reverse,
        state_reverse,
        later_reverse,
        decay_reverse,
        saved_reverse,
        readout_grad_reverse,
        sum_grad_reverse,
    )
    values_grad = (
        values_grad_forward
        + jnp.flip(values_grad_reverse, 1)
        + skip[None, None, :, None] * core_grad.astype(jnp.float32)
    )
    step_total_forward = step_grad_forward - rate[None, :, None] * log_grad_forward
    step_total_reverse = jnp.flip(step_grad_reverse - rate[None, :, None] * log_grad_reverse, 2)
    decay_log_grad = jnp.sum(log_grad_forward * log_forward, axis=(0, 2)) + jnp.sum(
        log_grad_reverse * log_reverse, axis=(0, 2)
    )
    step_total = jnp.stack(
        [
            jnp.transpose(step_total_forward, (0, 2, 1)),
            jnp.transpose(step_total_reverse, (0, 2, 1)),
        ],
        axis=3,
    )
    raw_grad = step_total * jax.nn.sigmoid(step_raw + bias_here)
    step_bias_grad = jnp.transpose(jnp.sum(raw_grad, axis=(0, 1)))
    state_grads = jnp.concatenate(
        [
            intake_grad_forward,
            readout_grad_forward,
            jnp.flip(intake_grad_reverse, 1),
            jnp.flip(readout_grad_reverse, 1),
        ],
        axis=2,
    )
    active_grad = jnp.concatenate(
        [values_grad.reshape(sequences, block_size, value_width), state_grads], axis=2
    )
    pre_grad = active_grad * active_sigma * (1.0 + pre_active * (1.0 - active_sigma))
    following = from_behind(pre_grad[:, :edge], "seq", -1)
    grad_extended = jnp.concatenate([pre_grad, following], axis=1)
    conv_input_grad = jnp.zeros((sequences, block_size, channels), jnp.float32)
    tap_grads = []
    for lag in range(reach):
        conv_input_grad = (
            conv_input_grad
            + taps[:, lag]
            * grad_extended[:, lag : lag + block_size]
            * lag_masks[:, lag : lag + block_size, lag, None]
        )
        tap_grads.append(
            jnp.sum(
                pre_grad
                * extended[:, edge - lag : edge - lag + block_size]
                * lag_masks[:, :block_size, lag, None],
                axis=(0, 1),
            )
        )
    tap_grads.append(jnp.sum(pre_grad, axis=(0, 1)))
    taps_grad = jnp.stack(tap_grads, axis=1)
    value_conv_grad = jnp.transpose(
        taps_grad[:value_width].reshape(heads_here, HEADDIM, reach + 1), (1, 0, 2)
    )
    state_conv_grad = taps_grad[value_width:]
    proj_grad = jnp.concatenate(
        [
            gate_grad,
            conv_input_grad[..., :value_width].reshape(sequences, block_size, heads_here, HEADDIM),
            raw_grad,
        ],
        axis=3,
    ).astype(jnp.bfloat16)
    state_proj_grad = conv_input_grad[..., value_width:].astype(jnp.bfloat16)
    normed_part = jnp.einsum(
        "mthk,dhk->mtd", proj_grad, in_weights, preferred_element_type=jnp.float32
    )
    normed_part = normed_part + jnp.einsum(
        "mtn,dn->mtd", state_proj_grad, state_weights, preferred_element_type=jnp.float32
    )
    normed_grad = lax.psum(normed_part, "head")
    in_weight_grad = jnp.einsum(
        "mtd,mthk->dhk", normed, proj_grad, preferred_element_type=jnp.float32
    )
    state_weight_grad = jnp.einsum(
        "mtd,mtn->dn", normed, state_proj_grad, preferred_element_type=jnp.float32
    )
    norm_gain_grad = jnp.sum(normed_grad * unit, axis=(0, 1))
    unit_grad = normed_grad * norm_wide
    input_gradient = out_cotangent + in_scale * (
        unit_grad - unit * jnp.mean(unit_grad * unit, axis=2, keepdims=True)
    )
    in_weight_out, out_weight_out, value_conv_out, norm_gain_out, gate_gain_out = (
        lax.psum_scatter(in_weight_grad, "seq", scatter_dimension=0, tiled=True),
        lax.psum_scatter(out_weight_grad, "seq", scatter_dimension=0, tiled=True),
        lax.psum_scatter(value_conv_grad, "seq", scatter_dimension=0, tiled=True),
        lax.psum_scatter(norm_gain_grad, "seq", scatter_dimension=0, tiled=True),
        lax.psum_scatter(gate_gain_grad, "seq", scatter_dimension=0, tiled=True),
    )
    state_weight_out, state_conv_out = (
        lax.psum_scatter(state_weight_grad, ("seq", "head"), scatter_dimension=0, tiled=True),
        lax.psum_scatter(state_conv_grad, ("seq", "head"), scatter_dimension=0, tiled=True),
    )
    step_bias_out, decay_log_out, skip_out = lax.psum(
        (step_bias_grad, decay_log_grad, skip_grad), "seq"
    )
    return (
        output,
        input_gradient,
        in_weight_out,
        state_weight_out,
        state_conv_out,
        out_weight_out,
        value_conv_out,
        norm_gain_out,
        gate_gain_out,
        step_bias_out,
        decay_log_out,
        skip_out,
    )


def line_gather(value, axis):
    count, mine = lax.axis_size(axis), lax.axis_index(axis)
    right = [(i, i + 1) for i in range(count - 1)]
    left = [(i + 1, i) for i in range(count - 1)]
    rights, lefts = [value], [value]
    for _ in range(count - 1):
        rights.append(lax.ppermute(rights[-1], axis, right))
        lefts.append(lax.ppermute(lefts[-1], axis, left))
    return [value] + [
        jnp.where(mine >= k, rights[k], lefts[count - k]) for k in range(1, count)
    ]


def spread(value, axis):
    count = lax.axis_size(axis)
    return lax.all_to_all(jnp.broadcast_to(value[None], (count,) + value.shape), axis, 0, 0)


def swap_core(value):
    return lax.ppermute(value, "core", [(0, 1), (1, 0)])


def both_cores(value):
    other = swap_core(value)
    first = lax.axis_index("core") == 0
    return jnp.stack([jnp.where(first, value, other), jnp.where(first, other, value)])


LANES = 128
WIDE, LOW = jnp.float32, jnp.bfloat16
FAR = -1e30


def dot(left, right):
    return jnp.dot(left, right, preferred_element_type=WIDE)


def dot_nt(left, right):
    return lax.dot_general(left, right, (((1,), (1,)), ((), ())), preferred_element_type=WIDE)


def exact_dot(left, right):
    return jnp.dot(left, right, precision=lax.Precision.HIGHEST, preferred_element_type=WIDE)


def halves(value):
    high = value.astype(LOW)
    return jnp.concatenate([high, (value - high.astype(WIDE)).astype(LOW)], axis=1)


def iota(shape, axis):
    return lax.broadcasted_iota(jnp.int32, shape, axis)


def head_columns(heads):
    row = jnp.arange(2 * LANES)[:, None] % LANES
    head = jnp.arange(heads * HEADDIM)[None, :] // HEADDIM
    spread_both = [(row == 2 * head + d).astype(LOW) for d in range(2)]
    gather_both = [jnp.concatenate([s[:LANES].T, s[:LANES].T], axis=0) for s in spread_both]
    return spread_both, gather_both


def steps_of(raw, bias):
    shifted = raw + bias
    small = jnp.exp(-jnp.abs(shifted))
    exponent = jnp.exp(jnp.minimum(shifted, 0.0))
    step = jnp.where(
        shifted < -15.0, exponent, jnp.maximum(shifted, 0.0) + jnp.log1p(small)
    )
    sigma = exponent / (1.0 + small)
    ratio = jnp.where(shifted < -15.0, 1.0, sigma / step)
    return step, sigma, ratio


def odd_lanes(shape):
    return iota(shape, 1) % 2 == 1


def running_sums(value, flip):
    size = value.shape[0]
    row, col = iota((size, size), 0), iota((size, size), 1)
    before = exact_dot((row >= col).astype(WIDE), value)
    after = exact_dot((row <= col).astype(WIDE), value)
    odd = odd_lanes(value.shape)
    return jnp.where(odd, before, after) if flip else jnp.where(odd, after, before)


def start_masks(starts, block, blocks, shape):
    size = shape[0]
    start = starts[block]
    following = starts[jnp.minimum(block + 1, blocks - 1)]
    none = start >= size
    ended = jnp.logical_or(block == blocks - 1, following == 0)
    row, odd = iota(shape, 0), odd_lanes(shape)
    after = row >= start
    tail_forward = jnp.logical_or(after, none)
    tail_reverse = jnp.logical_or(jnp.logical_not(after), jnp.logical_or(none, start == 0))
    head_forward = jnp.logical_not(after)
    head_reverse = jnp.logical_and(jnp.logical_or(after, none), jnp.logical_not(ended))
    tail = jnp.where(odd, tail_reverse.astype(WIDE), tail_forward.astype(WIDE))
    head = jnp.where(odd, head_reverse.astype(WIDE), head_forward.astype(WIDE))
    whole_reverse = jnp.logical_and(jnp.logical_or(none, start == 0), jnp.logical_not(ended))
    whole = jnp.where(
        odd[:8],
        jnp.where(whole_reverse, 1.0, 0.0),
        jnp.where(none, 1.0, 0.0),
    )
    return tail, head, whole


def chain_last(cum):
    return jnp.where(odd_lanes((1, cum.shape[1])), cum[:1], cum[-1:])


def table_bias(starts, block, size):
    row, col = iota((size, size), 0), iota((size, size), 1)
    start = starts[block]
    same = (row >= start) == (col >= start)
    return jnp.where(jnp.logical_and(same, row != col), 0.0, FAR)


def lane_half(size, second):
    return ((iota((size, LANES), 1) >= HEADDIM) == second).astype(WIDE).astype(LOW)


def block_diagonal(pair):
    size = pair.shape[0]
    return jnp.concatenate([pair * lane_half(size, False), pair * lane_half(size, True)], axis=0)


def silu_slope(value, sigma):
    return sigma * (1.0 + value * (1.0 - sigma))


def below(value):
    return jnp.concatenate([jnp.zeros_like(value), value], axis=0)


def above(value):
    return jnp.concatenate([value, jnp.zeros_like(value)], axis=0)


def rows_sum(value):
    total = value[:8]
    for at in range(8, value.shape[0], 8):
        total = total + value[at : at + 8]
    return total


def forward_kernel(
    starts, tokens, weights, norm_row, taps, bias_row, rate_row, spread_f, spread_r,
    normed_o, conv_o, pre_o, act_o, out_f_o, inner_r_o, cum_o, raw_o, state_f_o, local_r_o,
    decay_f_o, decay_r_o,
    tail_s, state_s,
):
    block, blocks = pl.program_id(0), pl.num_programs(0)
    size = tokens.shape[0]
    inner = out_f_o.shape[1]
    channels = inner + 4 * STATE
    reach = 4

    @pl.when(block == 0)
    def _():
        tail_s[...] = jnp.zeros_like(tail_s)
        state_s[...] = jnp.zeros_like(state_s)

    wide = tokens[...].astype(WIDE)
    scale = lax.rsqrt(jnp.mean(wide * wide, axis=1, keepdims=True) + 1e-05)
    normed = (wide * scale * norm_row[...]).astype(LOW)
    normed_o[...] = normed
    projected = dot(normed, weights[...])
    raw = projected[:, channels:]
    raw_o[...] = raw
    start = starts[block]
    previous = starts[jnp.maximum(block - 1, 0)]
    row = iota((size, LANES), 0)
    number = (row >= start).astype(jnp.int32)
    masks = []
    for lag in range(1, reach):
        source = row - lag
        inside = (source >= start).astype(jnp.int32)
        outside = jnp.where(
            jnp.logical_and(previous < size, source + size < previous), -1, 0
        )
        masks.append(
            (number == jnp.where(source >= 0, inside, outside)).astype(WIDE)
        )
    for at in range(0, channels, LANES):
        lanes = slice(at, at + LANES)
        low = projected[:, lanes].astype(LOW)
        conv_o[:, lanes] = low
        here = low.astype(WIDE)
        extended = jnp.concatenate([tail_s[:, lanes], here], axis=0)
        tail_s[:, lanes] = here[size - 8 :]
        pre = taps[4:5, lanes] + taps[0:1, lanes] * here
        for lag in range(1, reach):
            shifted = pltpu.roll(extended, lag, 0)[8:]
            pre = pre + taps[lag : lag + 1, lanes] * shifted * masks[lag - 1]
        pre_o[:, lanes] = pre
        act_o[:, lanes] = (pre * jax.nn.sigmoid(pre)).astype(LOW)

    step, _, _ = steps_of(raw, bias_row[...])
    cum = running_sums(-step * rate_row[...], False)
    cum_o[...] = cum
    late = cum - jnp.log(step)
    late_rows = late.T
    tail_mask, head_mask, whole = start_masks(starts, block, blocks, cum.shape)
    tail = halves(jnp.exp(chain_last(cum) - late) * tail_mask)
    head = halves(jnp.exp(cum) * head_mask)
    decay = halves(jnp.exp(jnp.broadcast_to(chain_last(cum), (8, LANES))) * whole)
    decay_f, decay_r = dot(decay, spread_f[...]), dot(decay, spread_r[...])
    decay_f_o[...] = decay_f
    decay_r_o[...] = decay_r

    values = act_o[:, :inner]
    values_wide = values.astype(WIDE)
    state_act = act_o[:, inner:]
    turned = state_act.astype(WIDE).T.astype(LOW)
    forward_act, reverse_act = state_act[:, : 2 * STATE], state_act[:, 2 * STATE :]
    row, col = iota((size, size), 0), iota((size, size), 1)
    lower = row > col
    lower_low = lower.astype(WIDE).astype(LOW)
    upper_low = (row < col).astype(WIDE).astype(LOW)
    scores = jnp.where(
        lower,
        dot(forward_act, below(turned[:STATE])),
        dot(reverse_act, below(turned[2 * STATE : 3 * STATE])),
    )
    bias = table_bias(starts, block, size)
    for pair in range(inner // LANES):
        lanes = slice(pair * LANES, (pair + 1) * LANES)
        lefts, rights = [], []
        for head_at in (2 * pair, 2 * pair + 1):
            c = 2 * head_at
            gap = jnp.where(
                lower,
                cum[:, c : c + 1] - late_rows[c : c + 1],
                cum[:, c + 1 : c + 2] - late_rows[c + 1 : c + 2],
            )
            mix = (scores * jnp.exp(gap + bias)).astype(LOW)
            lefts.append(mix * lower_low)
            rights.append(mix * upper_low)
        both = jnp.concatenate(
            [jnp.concatenate(lefts, axis=1), jnp.concatenate(rights, axis=1)], axis=0
        )
        result = dot(both, block_diagonal(act_o[:, lanes]))
        out_f_o[:, lanes] = result[:size]
        inner_r_o[:, lanes] = result[size:]

    state = state_s[...]
    state_f_o[...] = state
    carried = dot(forward_act, below(state.astype(LOW)))
    out_f_o[...] += dot(head, spread_f[...]) * carried
    local_f = dot(turned[:STATE], (dot(tail, spread_f[...]) * values_wide).astype(LOW))
    state_s[...] = decay_f[:1] * state + local_f
    local_r_o[...] = dot(
        turned[2 * STATE : 3 * STATE], (dot(tail, spread_r[...]) * values_wide).astype(LOW)
    )


def output_kernel(
    starts, normed, act, out_f, inner_r, cum, local_r, decay_r, cotangent, gate_w, out_w,
    skip_row, gain_row, spread_r,
    out_r_o, state_r_o, gate_o, unscaled_o, unscaled_grad_o, sums_o, pre_out_o,
    state_s,
):
    step, blocks = pl.program_id(0), pl.num_programs(0)
    block = blocks - 1 - step
    inner = out_f.shape[1]

    @pl.when(step == 0)
    def _():
        state_s[...] = jnp.zeros_like(state_s)

    _, head_mask, _ = start_masks(starts, block, blocks, cum.shape)
    head = halves(jnp.exp(cum[...]) * head_mask)
    state = state_s[...]
    state_r_o[...] = state
    reverse_act = act[:, inner + 2 * STATE :]
    carried = dot(reverse_act, below(state.astype(LOW)))
    out_r = inner_r[...] + dot(head, spread_r[...]) * carried
    out_r_o[...] = out_r
    state_s[...] = decay_r[:1] * state + local_r[...]
    core = out_f[...] + out_r + skip_row[...] * act[:, :inner].astype(WIDE)
    gate = dot(normed[...], gate_w[...])
    gate_o[...] = gate
    gated = core * gate * jax.nn.sigmoid(gate)
    unscaled = (gated * gain_row[...]).astype(LOW)
    unscaled_o[...] = unscaled
    unscaled_grad = dot(cotangent[...], out_w[...])
    unscaled_grad_o[...] = unscaled_grad
    squares = jnp.sum(gated * gated, axis=1, keepdims=True)
    products = jnp.sum(unscaled_grad * unscaled.astype(WIDE), axis=1, keepdims=True)
    sums_o[...] = jnp.where(iota(sums_o.shape, 1) == 0, squares, products)
    pre_out_o[...] = dot_nt(unscaled, out_w[...]).astype(LOW)


def gate_back_kernel(
    starts, sums, cotangent, out_f, out_r, act, gate, unscaled_grad, cum, decay_r, skip_row,
    gain_row, spread_f, spread_r, gather_f, gather_r,
    total_o, core_grad_o, gate_grad_o, row_sums_o, back_f_o, later_r_o, gain_grad_o, skip_grad_o,
    later_s,
):
    block, blocks = pl.program_id(0), pl.num_programs(0)
    inner = out_f.shape[1]
    inner_width = HEADS * HEADDIM

    @pl.when(block == 0)
    def _():
        later_s[...] = jnp.zeros_like(later_s)
        gain_grad_o[...] = jnp.zeros_like(gain_grad_o)
        skip_grad_o[...] = jnp.zeros_like(skip_grad_o)

    scale = lax.rsqrt(sums[:, 0:1] / inner_width + 1e-05)
    square_grad = sums[:, 1:2] * scale * scale * scale / inner_width
    total_o[...] = (scale * cotangent[...].astype(WIDE)).astype(LOW)
    values = act[:, :inner].astype(WIDE)
    core = out_f[...] + out_r[...] + skip_row[...] * values
    gate_value = gate[...]
    sigma = jax.nn.sigmoid(gate_value)
    slope = gate_value * sigma
    gated = core * slope
    unscaled = scale * unscaled_grad[...]
    gain_grad_o[...] += rows_sum(unscaled * gated)
    gated_grad = unscaled * gain_row[...] - gated * square_grad
    core_grad = (gated_grad * slope).astype(LOW)
    core_grad_o[...] = core_grad
    gate_grad_o[...] = (gated_grad * core * silu_slope(gate_value, sigma)).astype(LOW)
    grad_wide = core_grad.astype(WIDE)
    skip_grad_o[...] += rows_sum(grad_wide * values)
    row_sums_o[...] = dot(halves(grad_wide * out_f[...]), gather_f[...]) + dot(
        halves(grad_wide * out_r[...]), gather_r[...]
    )
    _, head_mask, _ = start_masks(starts, block, blocks, cum.shape)
    head = halves(jnp.exp(cum[...]) * head_mask)
    turned = act[:, inner:].astype(WIDE).T.astype(LOW)
    back_f_o[...] = dot(
        turned[STATE : 2 * STATE], (dot(head, spread_f[...]) * grad_wide).astype(LOW)
    )
    back_r = dot(turned[3 * STATE :], (dot(head, spread_r[...]) * grad_wide).astype(LOW))
    later = later_s[...]
    later_r_o[...] = later
    later_s[...] = decay_r[:1] * later + back_r


def chain_back_kernel(
    starts, core_grad, gate_grad, act, conv, pre, cum, raw, row_sums, state_f, state_f_next,
    state_r, state_r_last, back_f, later_r, decay_f, gate_w, weights, taps, bias_row, rate_row,
    skip_row, spread_f, spread_r, gather_f, gather_r,
    proj_o, normed_o, taps_grad_o, scalar_o,
    later_s, next_s, values_f_s, values_r_s, active_s,
):
    step_at, blocks = pl.program_id(0), pl.num_programs(0)
    block = blocks - 1 - step_at
    size, inner = core_grad.shape
    channels = inner + 4 * STATE
    reach = 4

    @pl.when(step_at == 0)
    def _():
        later_s[...] = jnp.zeros_like(later_s)
        next_s[...] = jnp.zeros_like(next_s)
        taps_grad_o[...] = jnp.zeros_like(taps_grad_o)
        scalar_o[...] = jnp.zeros_like(scalar_o)

    cum_here = cum[...]
    step, sigma, ratio = steps_of(raw[...], bias_row[...])
    late = cum_here - jnp.log(step)
    cum_rows = cum_here.T
    tail_mask, head_mask, _ = start_masks(starts, block, blocks, cum_here.shape)
    tail = halves(jnp.exp(chain_last(cum_here) - late) * tail_mask)
    head = halves(jnp.exp(cum_here) * head_mask)
    state_act = act[:, inner:]
    turned = state_act.astype(WIDE).T.astype(LOW)
    forward_act, reverse_act = state_act[:, : 2 * STATE], state_act[:, 2 * STATE :]
    row, col = iota((size, size), 0), iota((size, size), 1)
    ahead = col > row
    ahead_low = ahead.astype(WIDE).astype(LOW)
    behind_low = (col < row).astype(WIDE).astype(LOW)
    scores = jnp.where(
        ahead,
        dot(forward_act, above(turned[STATE : 2 * STATE])),
        dot(reverse_act, above(turned[3 * STATE :])),
    )
    bias = table_bias(starts, block, size)
    scores_grad = jnp.zeros((size, size), WIDE)
    for pair in range(inner // LANES):
        lanes = slice(pair * LANES, (pair + 1) * LANES)
        grad_blocks = block_diagonal(core_grad[:, lanes])
        mix_grad = dot_nt(act[:, lanes], grad_blocks)
        lefts, rights = [], []
        for at in range(2):
            c = 2 * (2 * pair + at)
            gap = jnp.where(
                ahead,
                cum_rows[c : c + 1] - late[:, c : c + 1],
                cum_rows[c + 1 : c + 2] - late[:, c + 1 : c + 2],
            )
            table = jnp.exp(gap + bias)
            mix = (scores * table).astype(LOW)
            lefts.append(mix * ahead_low)
            rights.append(mix * behind_low)
            scores_grad = scores_grad + mix_grad[:, at * size : (at + 1) * size] * table
        both = jnp.concatenate(
            [jnp.concatenate(lefts, axis=1), jnp.concatenate(rights, axis=1)], axis=0
        )
        result = dot(both, grad_blocks)
        values_f_s[:, lanes] = result[:size]
        values_r_s[:, lanes] = result[size:]

    grad_wide = core_grad[...].astype(WIDE)
    values = act[:, :inner].astype(WIDE)
    later_f, later_r_here = later_s[...], later_r[...]
    later_f_low, later_r_low = later_f.astype(LOW), later_r_here.astype(LOW)
    tail_f, tail_r = dot(tail, spread_f[...]), dot(tail, spread_r[...])
    values_f = values_f_s[...] + tail_f * dot(forward_act, above(later_f_low))
    values_r = values_r_s[...] + tail_r * dot(reverse_act, above(later_r_low))
    col_sums = dot(halves(values * values_f), gather_f[...]) + dot(
        halves(values * values_r), gather_r[...]
    )
    end_f = rows_sum(later_f * state_f_next[...])
    end_r = rows_sum(later_r_here * state_r_last[...])
    end_f = jnp.sum(dot(halves(end_f), gather_f[...]), axis=0, keepdims=True)
    end_r = jnp.sum(dot(halves(end_r), gather_r[...]), axis=0, keepdims=True)
    row = iota(cum_here.shape, 0)
    cum_grad = row_sums[...] - col_sums
    cum_grad = cum_grad + jnp.where(row == size - 1, end_f, 0.0) + jnp.where(row == 0, end_r, 0.0)
    log_grad = running_sums(cum_grad, True)
    raw_grad = col_sums * ratio - rate_row[...] * log_grad * sigma
    scalar_o[0:8] += rows_sum(raw_grad)
    scalar_o[8:16] += rows_sum(log_grad * (-step * rate_row[...]))

    mid = scores_grad.T
    pieces = []
    for act_pair, spread_head, state, later_low, forward_side in (
        (forward_act, spread_f, state_f, later_f_low, True),
        (reverse_act, spread_r, state_r, later_r_low, False),
    ):
        tail_here = tail_f if forward_side else tail_r
        scaled = (tail_here * values).astype(LOW)
        carried_grad = (dot(head, spread_head[...]) * grad_wide).astype(LOW)
        own = ahead_low if forward_side else behind_low
        mirrored = behind_low if forward_side else ahead_low
        sides = jnp.concatenate(
            [scores_grad.astype(LOW) * own, mid.astype(LOW) * mirrored], axis=1
        )
        swapped = pltpu.roll(act_pair.astype(WIDE), STATE, 1).astype(LOW)
        pieces.append(
            dot_nt(scaled, above(later_low))
            + dot_nt(carried_grad, below(state[...].astype(LOW)))
            + dot(sides, block_diagonal(swapped))
        )
    active_s[:, :inner] = values_f + values_r + skip_row[...] * grad_wide
    active_s[:, inner : inner + LANES] = pieces[0]
    active_s[:, inner + LANES :] = pieces[1]
    decay = decay_f[...]
    later_s[...] = decay[:1] * later_f + back_f[...]

    start = starts[block]
    following = starts[jnp.minimum(block + 1, blocks - 1)]
    row = iota((size, LANES), 0)
    number = (row >= start).astype(jnp.int32)
    masks = []
    for lag in range(1, reach):
        source = row + lag
        inside = (source >= start).astype(jnp.int32)
        outside = jnp.where(start < size, 1, 0) + (source - size >= following).astype(jnp.int32)
        masks.append((number == jnp.where(source < size, inside, outside)).astype(WIDE))
    for at in range(0, channels, LANES):
        lanes = slice(at, at + LANES)
        pre_here = pre[:, lanes]
        grad = active_s[:, lanes] * silu_slope(pre_here, jax.nn.sigmoid(pre_here))
        extended = jnp.concatenate([grad, next_s[:, lanes]], axis=0)
        next_s[:, lanes] = grad[:8]
        source = conv[:, lanes].astype(WIDE)
        result = taps[0:1, lanes] * grad
        taps_grad_o[0:8, lanes] += rows_sum(grad * source)
        taps_grad_o[32:40, lanes] += rows_sum(grad)
        for lag in range(1, reach):
            shifted = pltpu.roll(extended, size + 8 - lag, 0)[:size] * masks[lag - 1]
            result = result + taps[lag : lag + 1, lanes] * shifted
            taps_grad_o[8 * lag : 8 * lag + 8, lanes] += rows_sum(shifted * source)
        proj_o[:, lanes] = result.astype(LOW)
    proj_o[:, channels:] = raw_grad.astype(LOW)
    normed_o[...] = dot_nt(gate_grad[...], gate_w[...]) + dot_nt(proj_o[...], weights[...])


def by_block(kernel, blocks, size, reverse, ins, outs, scratch, name):
    def at(i):
        return blocks - 1 - i if reverse else i

    def spec(shape, kind):
        if kind == "scalar":
            return pl.BlockSpec(memory_space=pltpu.SMEM)
        if kind == "whole":
            return pl.BlockSpec(shape, lambda i: (0,) * len(shape))
        if kind == "rows":
            return pl.BlockSpec((shape[0] // blocks,) + shape[1:], lambda i: (at(i), 0))
        if kind == "next":
            return pl.BlockSpec(
                (shape[0] // blocks,) + shape[1:],
                lambda i: (jnp.minimum(at(i) + 1, blocks - 1), 0),
            )
        if kind == "last":
            return pl.BlockSpec(
                (shape[0] // blocks,) + shape[1:], lambda i: (jnp.maximum(at(i) - 1, 0), 0)
            )
        raise ValueError(kind)

    return pl.pallas_call(
        kernel,
        grid=(blocks,),
        in_specs=[spec(value.shape, kind) for value, kind in ins],
        out_specs=[spec(value.shape, kind) for value, kind in outs],
        out_shape=[value for value, _ in outs],
        scratch_shapes=[pltpu.VMEM(shape, dtype) for shape, dtype in scratch],
        compiler_params=pltpu.CompilerParams(
            dimension_semantics=("arbitrary",), vmem_limit_bytes=56 * 1024 * 1024
        ),
        name=name,
    )(*[value for value, _ in ins])


def chip_plan(
    tokens,
    starts,
    in_weight,
    state_weight,
    state_conv,
    out_weight,
    value_conv,
    norm_gain,
    gate_gain,
    step_bias,
    decay_log,
    skip,
    out_cotangent,
):
    low, wide = jnp.bfloat16, jnp.float32
    sequences, block_size, width = tokens.shape
    chips, planes = lax.axis_size("chip"), lax.axis_size("head")
    chip, core, plane = lax.axis_index("chip"), lax.axis_index("core"), lax.axis_index("head")
    blocks = starts.shape[1]
    length = blocks * block_size
    rows, group = in_weight.shape[:2]
    groups = planes // 2
    heads_here = group * groups
    inner_here = heads_here * HEADDIM
    reach = state_conv.shape[1] - 1
    edge = reach - 1

    def own_plane(value):
        return lax.dynamic_slice_in_dim(value, plane * chips, chips, 0)

    def to_sequence(mine):
        return jnp.swapaxes(both_cores(mine), 0, 1).reshape((length,) + mine.shape[2:])

    tokens_mine = lax.all_to_all(own_plane(tokens), "chip", 0, 0)
    tokens_whole = to_sequence(tokens_mine)
    cotangent_mine = lax.all_to_all(own_plane(out_cotangent).astype(low), "chip", 0, 0)
    cotangent = to_sequence(cotangent_mine)

    small = jnp.concatenate(
        [value_conv.transpose(1, 0, 2).reshape(-1), gate_gain.transpose(1, 0).reshape(-1)]
    )
    small_cols = -(-small.size // rows)
    small = jnp.pad(small, (0, small_cols * rows - small.size)).reshape(rows, small_cols)
    flat_in = in_weight.reshape(rows, -1)
    slab = jnp.concatenate([flat_in, out_weight.reshape(rows, -1), small], axis=1)
    by_plane = spread(slab, "head")
    mine = lax.dynamic_slice_in_dim(by_plane, core * groups, groups, 0)
    theirs = swap_core(lax.dynamic_slice_in_dim(by_plane, (1 - core) * groups, groups, 0))
    first = core == 0
    pair = jnp.stack([jnp.where(first, mine, theirs), jnp.where(first, theirs, mine)])
    slabs = spread(pair, "chip").reshape(2 * chips, groups, rows, -1)
    in_cols, out_cols = flat_in.shape[1], group * HEADDIM
    in_heads = slabs[..., :in_cols].reshape(2 * chips, groups, rows, group, -1)
    in_heads = in_heads.transpose(0, 2, 1, 3, 4).reshape(width, heads_here, -1)
    out_heads = slabs[..., in_cols : in_cols + out_cols].reshape(2 * chips, groups, rows, group, -1)
    out_heads = out_heads.transpose(0, 2, 1, 3, 4).reshape(width, heads_here, HEADDIM)
    small_all = slabs[..., in_cols + out_cols :].reshape(2 * chips, groups, -1)
    taps_size = value_conv.size
    part = value_conv.shape[0]
    value_taps = small_all[..., :taps_size].reshape(2 * chips, groups, group, part, reach + 1)
    value_taps = value_taps.transpose(1, 2, 0, 3, 4).reshape(inner_here, reach + 1)
    gate_gains = small_all[..., taps_size : taps_size + gate_gain.size]
    gate_gains = gate_gains.reshape(2 * chips, groups, group, part)
    gate_gains = gate_gains.transpose(1, 2, 0, 3).reshape(heads_here, HEADDIM).astype(wide)
    conv_flat = state_conv.reshape(-1)
    conv_cols = -(-conv_flat.size // rows)
    conv_flat = jnp.pad(conv_flat, (0, conv_cols * rows - conv_flat.size)).reshape(rows, conv_cols)
    state_slab = jnp.concatenate([state_weight, norm_gain[:, None], conv_flat], axis=1)
    state_slabs = spread(both_cores(state_slab), "chip").reshape(2 * chips, rows, -1)
    channels_state = state_weight.shape[1]
    state_weights = state_slabs[..., :channels_state].reshape(width, channels_state)
    norm_wide = state_slabs[..., channels_state].reshape(width).astype(wide)
    state_taps = state_slabs[..., channels_state + 1 :].reshape(2 * chips, -1)
    state_taps = state_taps[:, : state_conv.size].reshape(channels_state, reach + 1)

    def own_heads(value, axis):
        every = spread(value, "head")
        picked = lax.dynamic_slice_in_dim(every, core * groups, groups, 0)
        return jnp.concatenate([picked[i] for i in range(groups)], axis=axis)

    scalars = own_heads(jnp.concatenate([step_bias, decay_log[None], skip[None]], axis=0), 1)
    bias_here, rate, skip_here = jnp.transpose(scalars[:2]), jnp.exp(scalars[2]), scalars[3]

    starts_row = lax.dynamic_index_in_dim(starts, plane * chips + chip, 0, keepdims=False)
    bias_row = jnp.pad(bias_here.reshape(1, -1), ((0, 0), (0, LANES - 2 * heads_here)))
    rate_row = jnp.pad(jnp.repeat(rate, 2)[None], ((0, 0), (0, LANES - 2 * heads_here)))
    skip_row = jnp.repeat(skip_here, HEADDIM)[None]
    gain_row = gate_gains.reshape(1, inner_here)
    norm_row = norm_wide[None]
    (spread_f, spread_r), (gather_f, gather_r) = head_columns(heads_here)
    taps = jnp.concatenate([value_taps, state_taps], axis=0).astype(wide).T
    taps = jnp.pad(taps, ((0, 8 - taps.shape[0]), (0, 0)))
    channels = inner_here + channels_state
    gate_w = in_heads[..., :HEADDIM].reshape(width, inner_here)
    weights = jnp.concatenate(
        [
            in_heads[..., HEADDIM : 2 * HEADDIM].reshape(width, inner_here),
            state_weights,
            in_heads[..., 2 * HEADDIM :].reshape(width, -1),
            jnp.zeros((width, LANES - 2 * heads_here), low),
        ],
        axis=1,
    )
    out_w = out_heads.reshape(width, inner_here)

    def shape(rows_, cols, dtype):
        return jax.ShapeDtypeStruct((rows_, cols), dtype)

    states = blocks * STATE
    (normed, conv_input, pre_active, act, out_f, inner_r, cum, step_raw, state_f, local_r, decay_f, decay_r) = by_block(
        forward_kernel, blocks, block_size, False,
        [
            (starts_row, "scalar"), (tokens_whole, "rows"), (weights, "whole"), (norm_row, "whole"),
            (taps, "whole"), (bias_row, "whole"), (rate_row, "whole"), (spread_f, "whole"),
            (spread_r, "whole"),
        ],
        [
            (shape(length, width, low), "rows"), (shape(length, channels, low), "rows"),
            (shape(length, channels, wide), "rows"), (shape(length, channels, low), "rows"),
            (shape(length, inner_here, wide), "rows"), (shape(length, inner_here, wide), "rows"),
            (shape(length, LANES, wide), "rows"), (shape(length, LANES, wide), "rows"),
            (shape(states, inner_here, wide), "rows"), (shape(states, inner_here, wide), "rows"),
            (shape(8 * blocks, inner_here, wide), "rows"), (shape(8 * blocks, inner_here, wide), "rows"),
        ],
        [((8, channels), wide), ((STATE, inner_here), wide)],
        "forward",
    )
    out_r, state_r, gate, unscaled, unscaled_grad, own_sums, partial_out = by_block(
        output_kernel, blocks, block_size, True,
        [
            (starts_row, "scalar"), (normed, "rows"), (act, "rows"), (out_f, "rows"), (inner_r, "rows"),
            (cum, "rows"), (local_r, "rows"), (decay_r, "rows"), (cotangent, "rows"), (gate_w, "whole"),
            (out_w, "whole"), (skip_row, "whole"), (gain_row, "whole"), (spread_r, "whole"),
        ],
        [
            (shape(length, inner_here, wide), "rows"), (shape(states, inner_here, wide), "rows"),
            (shape(length, inner_here, wide), "rows"), (shape(length, inner_here, low), "rows"),
            (shape(length, inner_here, wide), "rows"), (shape(length, LANES, wide), "rows"),
            (shape(length, width, low), "rows"),
        ],
        [((STATE, inner_here), wide)],
        "outputs",
    )
    sums = own_sums + swap_core(own_sums)
    inner_width = HEADS * HEADDIM
    gate_scale = lax.rsqrt(sums[:, 0] / inner_width + 1e-05)

    def reduce_cores(value):
        pieces = value.reshape(chips, 2, block_size, width)
        keep = lax.dynamic_index_in_dim(pieces, core, 1, keepdims=False)
        send = lax.dynamic_index_in_dim(pieces, 1 - core, 1, keepdims=False).astype(low)
        return keep.astype(wide) + swap_core(send).astype(wide)

    def own_parity(value):
        pieces = value.reshape((chips, 2, block_size) + value.shape[1:])
        return lax.dynamic_index_in_dim(pieces, core, 1, keepdims=False)

    def deliver(delta, base):
        pieces = line_gather(lax.all_to_all(delta.astype(low), "chip", 0, 0), "head")
        result = jnp.zeros(base.shape, wide).reshape((planes, chips) + base.shape[1:])
        base = base.reshape(result.shape)
        for k, piece in enumerate(pieces):
            at = (plane - k) % planes
            summed = lax.dynamic_index_in_dim(base, at, 0, keepdims=True).astype(wide) + piece[
                None
            ].astype(wide)
            result = lax.dynamic_update_slice_in_dim(result, summed, at, 0)
        return result.reshape(sequences, block_size, width)

    out_delta = own_parity(gate_scale)[..., None] * reduce_cores(partial_out)
    output = deliver(out_delta, tokens)

    (total_grad, core_grad, gate_grad, row_sums, back_f, later_r, gain_grad, skip_grad) = by_block(
        gate_back_kernel, blocks, block_size, False,
        [
            (starts_row, "scalar"), (sums, "rows"), (cotangent, "rows"), (out_f, "rows"), (out_r, "rows"),
            (act, "rows"), (gate, "rows"), (unscaled_grad, "rows"), (cum, "rows"), (decay_r, "rows"),
            (skip_row, "whole"), (gain_row, "whole"), (spread_f, "whole"), (spread_r, "whole"),
            (gather_f, "whole"), (gather_r, "whole"),
        ],
        [
            (shape(length, width, low), "rows"), (shape(length, inner_here, low), "rows"),
            (shape(length, inner_here, low), "rows"), (shape(length, LANES, wide), "rows"),
            (shape(states, inner_here, wide), "rows"), (shape(states, inner_here, wide), "rows"),
            (shape(8, inner_here, wide), "whole"), (shape(8, inner_here, wide), "whole"),
        ],
        [((STATE, inner_here), wide)],
        "gate_back",
    )
    proj_grad_all, normed_part, taps_grad, scalar_part = by_block(
        chain_back_kernel, blocks, block_size, True,
        [
            (starts_row, "scalar"), (core_grad, "rows"), (gate_grad, "rows"), (act, "rows"),
            (conv_input, "rows"), (pre_active, "rows"), (cum, "rows"), (step_raw, "rows"),
            (row_sums, "rows"), (state_f, "rows"), (state_f, "next"), (state_r, "rows"),
            (state_r, "last"), (back_f, "rows"), (later_r, "rows"), (decay_f, "rows"),
            (gate_w, "whole"), (weights, "whole"), (taps, "whole"), (bias_row, "whole"),
            (rate_row, "whole"), (skip_row, "whole"), (spread_f, "whole"), (spread_r, "whole"),
            (gather_f, "whole"), (gather_r, "whole"),
        ],
        [
            (shape(length, channels + LANES, low), "rows"), (shape(length, width, wide), "rows"),
            (shape(40, channels, wide), "whole"), (shape(16, LANES, wide), "whole"),
        ],
        [
            ((STATE, inner_here), wide), ((8, channels), wide), ((block_size, inner_here), wide),
            ((block_size, inner_here), wide), ((block_size, channels), wide),
        ],
        "chain_back",
    )
    taps_grad = jnp.sum(taps_grad.reshape(5, 8, channels), axis=1).T
    scalar_part = jnp.sum(scalar_part.reshape(2, 8, LANES), axis=1)[:, : 2 * heads_here]
    scalar_part = scalar_part.reshape(2, heads_here, 2)
    step_bias_grad = scalar_part[0].T
    decay_log_grad = jnp.sum(scalar_part[1], axis=1)
    skip_grad = jnp.sum(skip_grad.reshape(8, heads_here, HEADDIM), axis=(0, 2))
    gate_gain_grad = jnp.sum(gain_grad, axis=0).reshape(heads_here, HEADDIM)
    out_weight_grad = jnp.einsum("td,tk->dk", total_grad, unscaled, preferred_element_type=wide)
    tokens_wide = tokens_mine.astype(wide)
    in_scale = lax.rsqrt(jnp.mean(tokens_wide * tokens_wide, axis=2, keepdims=True) + 1e-05)
    unit_mine = tokens_wide * in_scale
    normed_grad = reduce_cores(normed_part)
    unit_grad = normed_grad * norm_wide
    delta = in_scale * (
        unit_grad - unit_mine * jnp.mean(unit_grad * unit_mine, axis=2, keepdims=True)
    )
    input_gradient = deliver(delta, out_cotangent)
    norm_gain_grad = jnp.sum(normed_grad * unit_mine, axis=(0, 1))
    gate_w_grad = jnp.einsum("td,tk->dk", normed, gate_grad, preferred_element_type=wide)
    rest_grad = jnp.einsum("td,tk->dk", normed, proj_grad_all, preferred_element_type=wide)
    in_weight_grad = jnp.concatenate(
        [
            gate_w_grad.reshape(width, heads_here, HEADDIM),
            rest_grad[:, :inner_here].reshape(width, heads_here, HEADDIM),
            rest_grad[:, channels : channels + 2 * heads_here].reshape(width, heads_here, 2),
        ],
        axis=2,
    )
    state_weight_grad = rest_grad[:, inner_here:channels]

    value_conv_grad = taps_grad[:inner_here].reshape(groups, group, 2 * chips, part, reach + 1)
    value_conv_grad = value_conv_grad.transpose(2, 0, 1, 3, 4).reshape(2 * chips, groups, -1)
    gain_grad = gate_gain_grad.reshape(groups, group, 2 * chips, part)
    gain_grad = gain_grad.transpose(2, 0, 1, 3).reshape(2 * chips, groups, -1)
    small_grad = jnp.concatenate([value_conv_grad, gain_grad], axis=2)
    small_grad = jnp.pad(
        small_grad, ((0, 0), (0, 0), (0, small_cols * rows - small_grad.shape[2]))
    ).reshape(2 * chips, groups, rows, small_cols)

    def by_owner(value):
        value = value.reshape(2 * chips, rows, groups, -1)
        return value.transpose(0, 2, 1, 3)

    slab_grad = jnp.concatenate(
        [by_owner(in_weight_grad), by_owner(out_weight_grad), small_grad], axis=3
    ).reshape(chips, 2, groups, rows, -1)
    state_grad = jnp.concatenate(
        [
            state_weight_grad.reshape(2 * chips, -1),
            taps_grad[inner_here:].reshape(2 * chips, -1),
        ],
        axis=1,
    ).reshape(chips, 2, -1)

    def over_chips(value):
        moved = lax.all_to_all(value.astype(low), "chip", 0, 0)
        return jnp.sum(moved.astype(wide), axis=0)

    slab_pair = over_chips(slab_grad).astype(low)
    keep = lax.dynamic_index_in_dim(slab_pair, core, 0, keepdims=False)
    got = swap_core(lax.dynamic_index_in_dim(slab_pair, 1 - core, 0, keepdims=False))
    by_group = jnp.concatenate(
        [jnp.where(first, keep, got), jnp.where(first, got, keep)], axis=0
    )
    slab_sum = jnp.sum(lax.all_to_all(by_group, "head", 0, 0).astype(wide), axis=0)
    in_weight_out = slab_sum[:, :in_cols].reshape(rows, group, -1)
    out_weight_out = slab_sum[:, in_cols : in_cols + out_cols].reshape(rows, group, HEADDIM)
    small_out = slab_sum[:, in_cols + out_cols :].reshape(-1)
    value_conv_out = small_out[:taps_size].reshape(group, part, reach + 1).transpose(1, 0, 2)
    gate_gain_out = small_out[taps_size : taps_size + gate_gain.size].reshape(group, part)
    gate_gain_out = gate_gain_out.transpose(1, 0)
    state_pair = over_chips(state_grad)
    state_mine = lax.dynamic_index_in_dim(state_pair, core, 0, keepdims=False)
    state_send = lax.dynamic_index_in_dim(state_pair, 1 - core, 0, keepdims=False)
    state_mine = state_mine + swap_core(state_send)
    weight_size = state_weight.size
    state_mine = jnp.concatenate(
        [
            state_mine[:weight_size].reshape(planes, -1),
            state_mine[weight_size:].reshape(planes, -1),
        ],
        axis=1,
    )
    state_out = jnp.sum(lax.all_to_all(state_mine.astype(low), "head", 0, 0).astype(wide), axis=0)
    state_weight_out = state_out[: weight_size // planes].reshape(-1, channels_state)
    state_conv_out = state_out[weight_size // planes :].reshape(-1, reach + 1)

    scalar_grad = jnp.concatenate([step_bias_grad, decay_log_grad[None], skip_grad[None]], axis=0)
    scalar_all = jnp.zeros((4, planes * group), wide)
    scalar_all = lax.dynamic_update_slice_in_dim(scalar_all, scalar_grad, core * heads_here, 1)
    everything = lax.psum(
        jnp.concatenate([norm_gain_grad, scalar_all.reshape(-1)]), ("chip", "core", "head")
    )
    norm_gain_out = lax.dynamic_slice_in_dim(everything, (2 * chip + core) * rows, rows, 0)
    scalar_out = everything[width:].reshape(4, planes * group)
    scalar_out = lax.dynamic_slice_in_dim(scalar_out, plane * group, group, 1)
    return (
        output,
        input_gradient,
        in_weight_out,
        state_weight_out,
        state_conv_out,
        out_weight_out,
        value_conv_out,
        norm_gain_out,
        gate_gain_out,
        scalar_out[:2],
        scalar_out[2],
        scalar_out[3],
    )


def solution(mesh):
    devices_seq, planes = mesh.devices.shape
    seq, plan = "seq", split_plan
    if devices_seq % 2 == 0 and planes % 2 == 0 and devices_seq // 2 * planes == CHIP_SEQUENCES:
        shape = (devices_seq // 2, 2, planes)
        mesh = Mesh(mesh.devices.reshape(shape), ("chip", "core", "head"))
        seq, plan = ("chip", "core"), chip_plan
    both = seq + ("head",) if isinstance(seq, tuple) else (seq, "head")
    return jax.shard_map(
        plan,
        mesh=mesh,
        in_specs=(
            P(None, seq, None),
            P(),
            P(seq, "head", None),
            P(seq, None),
            P(seq, None),
            P(seq, "head", None),
            P(seq, "head", None),
            P(seq),
            P(seq, "head"),
            P(None, "head"),
            P("head"),
            P("head"),
            P(None, seq, None),
        ),
        out_specs=(
            P(None, seq, None),
            P(None, seq, None),
            P(seq, "head", None),
            P(both, None),
            P(both, None),
            P(seq, "head", None),
            P(seq, "head", None),
            P(seq),
            P(seq, "head"),
            P(None, "head"),
            P("head"),
            P("head"),
        ),
        check_vma=False,
    )
```

```python
import jax
import jax.numpy as jnp
from jax import lax
from jax.experimental import pallas as pl
from jax.experimental.pallas import tpu as pltpu
from jax.sharding import Mesh, PartitionSpec as P

HEADS = 24
HEADDIM = 64
STATE = 64
CHIP_SEQUENCES = 16


def from_behind(value, axis, by):
    devices = lax.axis_size(axis)
    pairs = [(i, i + by) for i in range(devices) if 0 <= i + by < devices]
    return lax.ppermute(value, axis, pairs)


def entering(value, axis, join, neutral, backward):
    count, mine = (lax.axis_size(axis), lax.axis_index(axis))
    pieces = jax.tree.map(lambda part: lax.all_gather(part, axis), value)
    if backward:
        pieces = jax.tree.map(lambda part: part[::-1], pieces)
        mine = count - 1 - mine
    running = jax.tree.map(
        lambda part, zero: jnp.full_like(part, 0) + jnp.asarray(zero, part.dtype), value, neutral
    )

    def step(position, running):
        longer = join(running, jax.tree.map(lambda part: part[position], pieces))
        return jax.tree.map(lambda new, old: jnp.where(position < mine, new, old), longer, running)

    return lax.fori_loop(0, count - 1, step, running)


def affine(earlier, later):
    return (earlier[0] * later[0], later[0][..., None, None] * earlier[1] + later[1])


def document_numbers(starts, first_position, count, block_size):
    blocks = starts.shape[1]
    begins = jnp.arange(blocks, dtype=jnp.int32)[None, :] * block_size + starts
    valid = starts < block_size
    places = first_position + jnp.arange(count, dtype=jnp.int32)
    hits = (begins[:, None, :] <= places[None, :, None]) & valid[:, None, :]
    return jnp.sum(hits.astype(jnp.int32), axis=2)


def running_sum(value):
    length, shift = value.shape[-1], 1
    while shift < length:
        pad = [(0, 0)] * (value.ndim - 1) + [(shift, 0)]
        value = value + jnp.pad(value[..., : length - shift], pad)
        shift *= 2
    return value


def chain_forward(readout, intake, values, log_decay, step_size, flags):
    block_size = readout.shape[1]
    segment = running_sum(flags)
    decay_sum = running_sum(log_decay)
    scores = jnp.einsum("mtn,mjn->mtj", readout, intake, preferred_element_type=jnp.float32)
    order = jnp.arange(block_size)
    mask = ((order[:, None] > order[None, :])[None] & (segment[:, :, None] == segment[:, None, :]))[
        :, None
    ]
    gap = jnp.where(mask, decay_sum[:, :, :, None] - decay_sum[:, :, None, :], 0.0)
    decay_table = jnp.where(mask, jnp.exp(gap), 0.0)
    mixing = (scores[:, None] * decay_table * step_size[:, :, None, :]).astype(jnp.bfloat16)
    inner = jnp.einsum("mhtj,mjhp->mthp", mixing, values, preferred_element_type=jnp.float32)
    tail_factor = (
        jnp.exp(decay_sum[:, :, -1:] - decay_sum) * (segment == segment[:, -1:])[:, None, :]
    )
    scaled_intake = (
        (tail_factor * step_size)[..., None] * intake[:, None].astype(jnp.float32)
    ).astype(jnp.bfloat16)
    local_state = jnp.einsum(
        "mhjn,mjhp->mhnp", scaled_intake, values, preferred_element_type=jnp.float32
    )
    block_decay = jnp.exp(decay_sum[:, :, -1]) * (segment[:, -1] == 0)[:, None]
    head_scale = jnp.exp(decay_sum) * (segment == 0)[:, None, :]
    saved = (scores, decay_table, mixing, tail_factor, scaled_intake, head_scale)
    return (inner, local_state, block_decay, saved)


def chain_finish(inner, readout, state_in, head_scale):
    state_low = state_in.astype(jnp.bfloat16)
    carried = jnp.einsum("mtn,mhnp->mthp", readout, state_low, preferred_element_type=jnp.float32)
    return (inner + jnp.swapaxes(head_scale, 1, 2)[..., None] * carried, carried, state_low)


def chain_back_state(grad_out, readout, carried, state_low, head_scale):
    grad_wide = grad_out.astype(jnp.float32)
    carried_grad = (jnp.swapaxes(head_scale, 1, 2)[..., None] * grad_wide).astype(jnp.bfloat16)
    state_in_grad = jnp.einsum(
        "mtn,mthp->mhnp", readout, carried_grad, preferred_element_type=jnp.float32
    )
    readout_grad = jnp.einsum(
        "mthp,mhnp->mtn", carried_grad, state_low, preferred_element_type=jnp.float32
    )
    sum_grad = jnp.swapaxes(jnp.sum(grad_wide * carried, axis=3), 1, 2) * head_scale
    return (state_in_grad, readout_grad, sum_grad)


def chain_back_rest(
    grad_out,
    readout,
    intake,
    values,
    step_size,
    state_in,
    later,
    block_decay,
    saved,
    readout_grad,
    sum_grad,
):
    scores, decay_table, mixing, tail_factor, scaled_intake, head_scale = saved
    later_low = later.astype(jnp.bfloat16)
    scaled_grad = jnp.einsum(
        "mjhp,mhnp->mhjn", values, later_low, preferred_element_type=jnp.float32
    )
    values_grad = jnp.einsum(
        "mhjn,mhnp->mjhp", scaled_intake, later_low, preferred_element_type=jnp.float32
    )
    tail_grad = jnp.einsum("mhjn,mjn->mhj", scaled_grad, intake.astype(jnp.float32))
    intake_grad = jnp.einsum("mhjn,mhj->mjn", scaled_grad, tail_factor * step_size)
    step_grad = tail_grad * tail_factor
    tail_term = tail_grad * tail_factor * step_size
    decay_grad = jnp.sum(later * state_in, axis=(2, 3)) * block_decay
    sum_grad = (sum_grad - tail_term).at[:, :, -1].add(jnp.sum(tail_term, axis=2) + decay_grad)
    mixing_grad = jnp.einsum(
        "mthp,mjhp->mhtj", grad_out, values, preferred_element_type=jnp.float32
    )
    values_grad = values_grad + jnp.einsum(
        "mhtj,mthp->mjhp", mixing, grad_out, preferred_element_type=jnp.float32
    )
    through = mixing_grad * decay_table
    scores_grad = jnp.sum(through * step_size[:, :, None, :], axis=1).astype(jnp.bfloat16)
    readout_grad = readout_grad + jnp.einsum(
        "mtj,mjn->mtn", scores_grad, intake, preferred_element_type=jnp.float32
    )
    intake_grad = intake_grad + jnp.einsum(
        "mtj,mtn->mjn", scores_grad, readout, preferred_element_type=jnp.float32
    )
    kernel = through * scores[:, None]
    step_grad = step_grad + jnp.sum(kernel, axis=2)
    weighted = kernel * step_size[:, :, None, :]
    sum_grad = sum_grad + jnp.sum(weighted, axis=3) - jnp.sum(weighted, axis=2)
    log_grad = jnp.flip(running_sum(jnp.flip(sum_grad, 2)), 2)
    return (values_grad, readout_grad, intake_grad, step_grad, log_grad)


def split_plan(
    tokens,
    starts,
    in_weight,
    state_weight,
    state_conv,
    out_weight,
    value_conv,
    norm_gain,
    gate_gain,
    step_bias,
    decay_log,
    skip,
    out_cotangent,
):
    sequences, block_size, width = tokens.shape
    place = lax.axis_index("seq")
    devices_seq = lax.axis_size("seq")
    in_weights, state_weights, state_taps, out_weights, value_taps, norm_whole, gate_whole = (
        lax.all_gather(in_weight, "seq", axis=0, tiled=True),
        lax.all_gather(state_weight, "seq", axis=0, tiled=True),
        lax.all_gather(state_conv, "seq", axis=0, tiled=True),
        lax.all_gather(out_weight, "seq", axis=0, tiled=True),
        lax.all_gather(value_conv, "seq", axis=0, tiled=True),
        lax.all_gather(norm_gain, "seq", axis=0, tiled=True),
        lax.all_gather(gate_gain, "seq", axis=0, tiled=True),
    )
    heads_here = in_weight.shape[1]
    value_width = heads_here * HEADDIM
    reach = state_conv.shape[1] - 1
    edge = reach - 1
    numbers = document_numbers(starts, place * block_size - edge, block_size + 2 * edge, block_size)
    lag_masks = jnp.stack(
        [
            numbers[:, edge:] == numbers[:, edge - lag : block_size + 2 * edge - lag]
            for lag in range(reach)
        ],
        axis=2,
    ).astype(jnp.float32)
    first = (
        numbers[:, edge : edge + block_size] != numbers[:, edge - 1 : edge + block_size - 1]
    ).astype(jnp.int32)
    positions = place * block_size + jnp.arange(block_size, dtype=jnp.int32)
    ending = (positions == devices_seq * block_size - 1)[None, :]
    last = (
        (numbers[:, edge + 1 : edge + block_size + 1] != numbers[:, edge : edge + block_size])
        | ending
    ).astype(jnp.int32)
    tokens_wide = tokens.astype(jnp.float32)
    in_scale = lax.rsqrt(jnp.mean(tokens_wide * tokens_wide, axis=2, keepdims=True) + 1e-05)
    unit = tokens_wide * in_scale
    norm_wide = norm_whole.astype(jnp.float32)
    normed = (unit * norm_wide).astype(jnp.bfloat16)
    projected = jnp.einsum("mtd,dhk->mthk", normed, in_weights, preferred_element_type=jnp.float32)
    state_proj = jnp.einsum(
        "mtd,dn->mtn", normed, state_weights, preferred_element_type=jnp.float32
    )
    gate = projected[..., :HEADDIM]
    step_raw = projected[..., 2 * HEADDIM :]
    conv_input = jnp.concatenate(
        [
            projected[..., HEADDIM : 2 * HEADDIM].reshape(sequences, block_size, value_width),
            state_proj,
        ],
        axis=2,
    ).astype(jnp.bfloat16)
    channels = conv_input.shape[2]
    halo_rows = from_behind(conv_input[:, block_size - edge :], "seq", 1)
    extended = jnp.concatenate([halo_rows, conv_input], axis=1)
    taps = jnp.concatenate(
        [jnp.transpose(value_taps, (1, 0, 2)).reshape(value_width, reach + 1), state_taps], axis=0
    ).astype(jnp.float32)
    pre_active = jnp.broadcast_to(taps[:, reach], (sequences, block_size, channels))
    for lag in range(reach):
        pre_active = (
            pre_active
            + taps[:, lag]
            * extended[:, edge - lag : edge - lag + block_size]
            * lag_masks[:, :block_size, lag, None]
        )
    active_sigma = jax.nn.sigmoid(pre_active)
    activated = (pre_active * active_sigma).astype(jnp.bfloat16)
    values = activated[..., :value_width].reshape(sequences, block_size, heads_here, HEADDIM)
    intake_forward = activated[..., value_width : value_width + STATE]
    readout_forward = activated[..., value_width + STATE : value_width + 2 * STATE]
    intake_reverse = jnp.flip(activated[..., value_width + 2 * STATE : value_width + 3 * STATE], 1)
    readout_reverse = jnp.flip(activated[..., value_width + 3 * STATE :], 1)
    values_reversed = jnp.flip(values, 1)
    rate = jnp.exp(decay_log)
    bias_here = jnp.transpose(step_bias)[None, None]
    step_all = jax.nn.softplus(step_raw + bias_here)
    step_forward = jnp.transpose(step_all[..., 0], (0, 2, 1))
    step_reverse = jnp.flip(jnp.transpose(step_all[..., 1], (0, 2, 1)), 2)
    log_forward = -step_forward * rate[None, :, None]
    log_reverse = -step_reverse * rate[None, :, None]
    inner_forward, local_forward, decay_forward, saved_forward = chain_forward(
        readout_forward, intake_forward, values, log_forward, step_forward, first
    )
    inner_reverse, local_reverse, decay_reverse, saved_reverse = chain_forward(
        readout_reverse,
        intake_reverse,
        values_reversed,
        log_reverse,
        step_reverse,
        jnp.flip(last, 1),
    )
    identity = (jnp.ones_like(decay_forward), jnp.zeros_like(local_forward))
    state_forward = entering((decay_forward, local_forward), "seq", affine, identity, False)[1]
    state_reverse = entering((decay_reverse, local_reverse), "seq", affine, identity, True)[1]
    out_forward, carried_forward, state_low_forward = chain_finish(
        inner_forward, readout_forward, state_forward, saved_forward[5]
    )
    out_reverse, carried_reverse, state_low_reverse = chain_finish(
        inner_reverse, readout_reverse, state_reverse, saved_reverse[5]
    )
    core = (
        out_forward
        + jnp.flip(out_reverse, 1)
        + skip[None, None, :, None] * values.astype(jnp.float32)
    )
    gate_sigma = jax.nn.sigmoid(gate)
    gated = core * gate * gate_sigma
    gate_gains = jnp.transpose(gate_whole).astype(jnp.float32)
    unscaled = (gated * gate_gains).astype(jnp.bfloat16)
    squares = jnp.sum(gated * gated, axis=(2, 3))
    partial_value = jnp.einsum(
        "mthp,dhp->mtd", unscaled, out_weights, preferred_element_type=jnp.float32
    )
    pre_out, square_sum = lax.psum((partial_value, squares), "head")
    inner_width = HEADS * HEADDIM
    gate_scale = lax.rsqrt(square_sum / inner_width + 1e-05)
    output = tokens_wide + gate_scale[..., None] * pre_out
    total_grad = (gate_scale[..., None] * out_cotangent).astype(jnp.bfloat16)
    unscaled_grad = jnp.einsum(
        "mtd,dhp->mthp", total_grad, out_weights, preferred_element_type=jnp.float32
    )
    out_weight_grad = jnp.einsum(
        "mtd,mthp->dhp", total_grad, unscaled, preferred_element_type=jnp.float32
    )
    scale_grad = jnp.sum(out_cotangent * pre_out, axis=2)
    square_grad = -0.5 * scale_grad * gate_scale**3 / inner_width
    gated_grad = unscaled_grad * gate_gains + 2.0 * gated * square_grad[..., None, None]
    gate_gain_grad = jnp.transpose(jnp.sum(unscaled_grad * gated, axis=(0, 1)))
    core_grad = (gated_grad * gate * gate_sigma).astype(jnp.bfloat16)
    gate_grad = gated_grad * core * gate_sigma * (1.0 + gate * (1.0 - gate_sigma))
    skip_grad = jnp.sum(core_grad.astype(jnp.float32) * values.astype(jnp.float32), axis=(0, 1, 3))
    core_reversed = jnp.flip(core_grad, 1)
    state_grad_forward, readout_grad_forward, sum_grad_forward = chain_back_state(
        core_grad, readout_forward, carried_forward, state_low_forward, saved_forward[5]
    )
    state_grad_reverse, readout_grad_reverse, sum_grad_reverse = chain_back_state(
        core_reversed, readout_reverse, carried_reverse, state_low_reverse, saved_reverse[5]
    )
    later_forward = entering((decay_forward, state_grad_forward), "seq", affine, identity, True)[1]
    later_reverse = entering((decay_reverse, state_grad_reverse), "seq", affine, identity, False)[1]
    (
        values_grad_forward,
        readout_grad_forward,
        intake_grad_forward,
        step_grad_forward,
        log_grad_forward,
    ) = chain_back_rest(
        core_grad,
        readout_forward,
        intake_forward,
        values,
        step_forward,
        state_forward,
        later_forward,
        decay_forward,
        saved_forward,
        readout_grad_forward,
        sum_grad_forward,
    )
    (
        values_grad_reverse,
        readout_grad_reverse,
        intake_grad_reverse,
        step_grad_reverse,
        log_grad_reverse,
    ) = chain_back_rest(
        core_reversed,
        readout_reverse,
        intake_reverse,
        values_reversed,
        step_reverse,
        state_reverse,
        later_reverse,
        decay_reverse,
        saved_reverse,
        readout_grad_reverse,
        sum_grad_reverse,
    )
    values_grad = (
        values_grad_forward
        + jnp.flip(values_grad_reverse, 1)
        + skip[None, None, :, None] * core_grad.astype(jnp.float32)
    )
    step_total_forward = step_grad_forward - rate[None, :, None] * log_grad_forward
    step_total_reverse = jnp.flip(step_grad_reverse - rate[None, :, None] * log_grad_reverse, 2)
    decay_log_grad = jnp.sum(log_grad_forward * log_forward, axis=(0, 2)) + jnp.sum(
        log_grad_reverse * log_reverse, axis=(0, 2)
    )
    step_total = jnp.stack(
        [
            jnp.transpose(step_total_forward, (0, 2, 1)),
            jnp.transpose(step_total_reverse, (0, 2, 1)),
        ],
        axis=3,
    )
    raw_grad = step_total * jax.nn.sigmoid(step_raw + bias_here)
    step_bias_grad = jnp.transpose(jnp.sum(raw_grad, axis=(0, 1)))
    state_grads = jnp.concatenate(
        [
            intake_grad_forward,
            readout_grad_forward,
            jnp.flip(intake_grad_reverse, 1),
            jnp.flip(readout_grad_reverse, 1),
        ],
        axis=2,
    )
    active_grad = jnp.concatenate(
        [values_grad.reshape(sequences, block_size, value_width), state_grads], axis=2
    )
    pre_grad = active_grad * active_sigma * (1.0 + pre_active * (1.0 - active_sigma))
    following = from_behind(pre_grad[:, :edge], "seq", -1)
    grad_extended = jnp.concatenate([pre_grad, following], axis=1)
    conv_input_grad = jnp.zeros((sequences, block_size, channels), jnp.float32)
    tap_grads = []
    for lag in range(reach):
        conv_input_grad = (
            conv_input_grad
            + taps[:, lag]
            * grad_extended[:, lag : lag + block_size]
            * lag_masks[:, lag : lag + block_size, lag, None]
        )
        tap_grads.append(
            jnp.sum(
                pre_grad
                * extended[:, edge - lag : edge - lag + block_size]
                * lag_masks[:, :block_size, lag, None],
                axis=(0, 1),
            )
        )
    tap_grads.append(jnp.sum(pre_grad, axis=(0, 1)))
    taps_grad = jnp.stack(tap_grads, axis=1)
    value_conv_grad = jnp.transpose(
        taps_grad[:value_width].reshape(heads_here, HEADDIM, reach + 1), (1, 0, 2)
    )
    state_conv_grad = taps_grad[value_width:]
    proj_grad = jnp.concatenate(
        [
            gate_grad,
            conv_input_grad[..., :value_width].reshape(sequences, block_size, heads_here, HEADDIM),
            raw_grad,
        ],
        axis=3,
    ).astype(jnp.bfloat16)
    state_proj_grad = conv_input_grad[..., value_width:].astype(jnp.bfloat16)
    normed_part = jnp.einsum(
        "mthk,dhk->mtd", proj_grad, in_weights, preferred_element_type=jnp.float32
    )
    normed_part = normed_part + jnp.einsum(
        "mtn,dn->mtd", state_proj_grad, state_weights, preferred_element_type=jnp.float32
    )
    normed_grad = lax.psum(normed_part, "head")
    in_weight_grad = jnp.einsum(
        "mtd,mthk->dhk", normed, proj_grad, preferred_element_type=jnp.float32
    )
    state_weight_grad = jnp.einsum(
        "mtd,mtn->dn", normed, state_proj_grad, preferred_element_type=jnp.float32
    )
    norm_gain_grad = jnp.sum(normed_grad * unit, axis=(0, 1))
    unit_grad = normed_grad * norm_wide
    input_gradient = out_cotangent + in_scale * (
        unit_grad - unit * jnp.mean(unit_grad * unit, axis=2, keepdims=True)
    )
    in_weight_out, out_weight_out, value_conv_out, norm_gain_out, gate_gain_out = (
        lax.psum_scatter(in_weight_grad, "seq", scatter_dimension=0, tiled=True),
        lax.psum_scatter(out_weight_grad, "seq", scatter_dimension=0, tiled=True),
        lax.psum_scatter(value_conv_grad, "seq", scatter_dimension=0, tiled=True),
        lax.psum_scatter(norm_gain_grad, "seq", scatter_dimension=0, tiled=True),
        lax.psum_scatter(gate_gain_grad, "seq", scatter_dimension=0, tiled=True),
    )
    state_weight_out, state_conv_out = (
        lax.psum_scatter(state_weight_grad, ("seq", "head"), scatter_dimension=0, tiled=True),
        lax.psum_scatter(state_conv_grad, ("seq", "head"), scatter_dimension=0, tiled=True),
    )
    step_bias_out, decay_log_out, skip_out = lax.psum(
        (step_bias_grad, decay_log_grad, skip_grad), "seq"
    )
    return (
        output,
        input_gradient,
        in_weight_out,
        state_weight_out,
        state_conv_out,
        out_weight_out,
        value_conv_out,
        norm_gain_out,
        gate_gain_out,
        step_bias_out,
        decay_log_out,
        skip_out,
    )


LANES = 128
WIDE, LOW = jnp.float32, jnp.bfloat16
FAR = -1e30


def dot(left, right):
    return jnp.dot(left, right, preferred_element_type=WIDE)


def dot_nt(left, right):
    return lax.dot_general(left, right, (((1,), (1,)), ((), ())), preferred_element_type=WIDE)


def exact_dot(left, right):
    return jnp.dot(left, right, precision=lax.Precision.HIGHEST, preferred_element_type=WIDE)


def halves(value):
    high = value.astype(LOW)
    return jnp.concatenate([high, (value - high.astype(WIDE)).astype(LOW)], axis=1)


def iota(shape, axis):
    return lax.broadcasted_iota(jnp.int32, shape, axis)


def head_columns(heads):
    row = jnp.arange(2 * LANES)[:, None] % LANES
    head = jnp.arange(heads * HEADDIM)[None, :] // HEADDIM
    spread_both = [(row == 2 * head + d).astype(LOW) for d in range(2)]
    gather_both = [jnp.concatenate([s[:LANES].T, s[:LANES].T], axis=0) for s in spread_both]
    return spread_both, gather_both


def steps_of(raw, bias):
    shifted = raw + bias
    small = jnp.exp(-jnp.abs(shifted))
    exponent = jnp.exp(jnp.minimum(shifted, 0.0))
    step = jnp.where(
        shifted < -15.0, exponent, jnp.maximum(shifted, 0.0) + jnp.log1p(small)
    )
    sigma = exponent / (1.0 + small)
    ratio = jnp.where(shifted < -15.0, 1.0, sigma / step)
    return step, sigma, ratio


def odd_lanes(shape):
    return iota(shape, 1) % 2 == 1


def running_sums(value, flip):
    size = value.shape[0]
    row, col = iota((size, size), 0), iota((size, size), 1)
    before = exact_dot((row >= col).astype(WIDE), value)
    after = exact_dot((row <= col).astype(WIDE), value)
    odd = odd_lanes(value.shape)
    return jnp.where(odd, before, after) if flip else jnp.where(odd, after, before)


def start_masks(starts, block, blocks, shape):
    size = shape[0]
    start = starts[block]
    following = starts[jnp.minimum(block + 1, blocks - 1)]
    none = start >= size
    ended = jnp.logical_or(block == blocks - 1, following == 0)
    row, odd = iota(shape, 0), odd_lanes(shape)
    after = row >= start
    tail_forward = jnp.logical_or(after, none)
    tail_reverse = jnp.logical_or(jnp.logical_not(after), jnp.logical_or(none, start == 0))
    head_forward = jnp.logical_not(after)
    head_reverse = jnp.logical_and(jnp.logical_or(after, none), jnp.logical_not(ended))
    tail = jnp.where(odd, tail_reverse.astype(WIDE), tail_forward.astype(WIDE))
    head = jnp.where(odd, head_reverse.astype(WIDE), head_forward.astype(WIDE))
    whole_reverse = jnp.logical_and(jnp.logical_or(none, start == 0), jnp.logical_not(ended))
    whole = jnp.where(
        odd[:8],
        jnp.where(whole_reverse, 1.0, 0.0),
        jnp.where(none, 1.0, 0.0),
    )
    return tail, head, whole


def chain_last(cum):
    return jnp.where(odd_lanes((1, cum.shape[1])), cum[:1], cum[-1:])


def table_bias(starts, block, size):
    row, col = iota((size, size), 0), iota((size, size), 1)
    start = starts[block]
    same = (row >= start) == (col >= start)
    return jnp.where(jnp.logical_and(same, row != col), 0.0, FAR)


def lane_half(size, second):
    return ((iota((size, LANES), 1) >= HEADDIM) == second).astype(WIDE).astype(LOW)


def block_diagonal(pair):
    size = pair.shape[0]
    return jnp.concatenate([pair * lane_half(size, False), pair * lane_half(size, True)], axis=0)


def silu_slope(value, sigma):
    return sigma * (1.0 + value * (1.0 - sigma))


def below(value):
    return jnp.concatenate([jnp.zeros_like(value), value], axis=0)


def above(value):
    return jnp.concatenate([value, jnp.zeros_like(value)], axis=0)


def rows_sum(value):
    total = value[:8]
    for at in range(8, value.shape[0], 8):
        total = total + value[at : at + 8]
    return total


def parity(starts, block):
    return block % 2 == starts[starts.shape[0] - 1]


def skip_lanes(small, spread):
    parts = dot(small[:, small.shape[1] - LANES :].astype(LOW), spread[:LANES])
    return parts[6:7] + parts[7:8] + parts[8:9]


def step_rows(small, heads):
    part = small[:, small.shape[1] - LANES :]
    bias = part[0:1] + part[1:2] + part[2:3]
    rate = jnp.exp(part[3:4] + part[4:5] + part[5:6])
    return bias, jnp.where(iota((1, LANES), 1) < 2 * heads, rate, 0.0)


def own_rows(starts, chip, index, rows):
    core = starts[starts.shape[0] - 1]
    seq = 2 * chip + (core if index == 0 else 1 - core)
    return pl.ds(pl.multiple_of(seq * rows, 32), rows)


def forward_kernel(
    starts, mine, other, pay, spread_f, spread_r,
    normed_o, conv_o, pre_o, act_o, out_f_o, inner_r_o, cum_o, raw_o, state_f_o, local_r_o,
    decay_f_o, decay_r_o, weights_o, small_o,
    tail_s, state_s,
):
    block, blocks = pl.program_id(0), pl.num_programs(0)
    size = mine.shape[0]
    inner = out_f_o.shape[1]
    channels = inner + 4 * STATE
    reach = 4

    @pl.when(block == 0)
    def _():
        tail_s[...] = jnp.zeros_like(tail_s)
        state_s[...] = jnp.zeros_like(state_s)
        chips, _, both, _ = pay.shape
        rows = both - 16
        total = jnp.zeros(small_o.shape, WIDE)
        for chip in range(chips):
            for index in range(2):
                weights_o[own_rows(starts, chip, index, rows), :] = pay[chip, index, :rows, :]
                total = total + pay[chip, index, rows:, :].astype(WIDE)
        small_o[...] = total

    small = small_o[...]
    bias_row, rate_row = step_rows(small, inner // HEADDIM)
    norm_row = jnp.concatenate([small[5:6, inner:channels], small[6:7, inner:channels], small[7:8, inner:channels]], axis=1)
    taps = small[:8, :channels]
    wide = jnp.where(parity(starts, block), mine[...], other[...]).astype(WIDE)
    scale = lax.rsqrt(jnp.mean(wide * wide, axis=1, keepdims=True) + 1e-05)
    normed = (wide * scale * norm_row).astype(LOW)
    normed_o[...] = normed
    projected = dot(normed, weights_o[...])
    raw = projected[:, channels:]
    raw_o[...] = raw
    start = starts[block]
    previous = starts[jnp.maximum(block - 1, 0)]
    row = iota((size, LANES), 0)
    number = (row >= start).astype(jnp.int32)
    masks = []
    for lag in range(1, reach):
        source = row - lag
        inside = (source >= start).astype(jnp.int32)
        outside = jnp.where(
            jnp.logical_and(previous < size, source + size < previous), -1, 0
        )
        masks.append(
            (number == jnp.where(source >= 0, inside, outside)).astype(WIDE)
        )
    for at in range(0, channels, LANES):
        lanes = slice(at, at + LANES)
        low = projected[:, lanes].astype(LOW)
        conv_o[:, lanes] = low
        here = low.astype(WIDE)
        extended = jnp.concatenate([tail_s[:, lanes], here], axis=0)
        tail_s[:, lanes] = here[size - 8 :]
        pre = taps[4:5, lanes] + taps[0:1, lanes] * here
        for lag in range(1, reach):
            shifted = pltpu.roll(extended, lag, 0)[8:]
            pre = pre + taps[lag : lag + 1, lanes] * shifted * masks[lag - 1]
        pre_o[:, lanes] = pre
        act_o[:, lanes] = (pre * jax.nn.sigmoid(pre)).astype(LOW)

    step, _, _ = steps_of(raw, bias_row)
    cum = running_sums(-step * rate_row, False)
    cum_o[...] = cum
    late = cum - jnp.log(step)
    late_rows = late.T
    tail_mask, head_mask, whole = start_masks(starts, block, blocks, cum.shape)
    tail = halves(jnp.exp(chain_last(cum) - late) * tail_mask)
    head = halves(jnp.exp(cum) * head_mask)
    decay = halves(jnp.exp(jnp.broadcast_to(chain_last(cum), (8, LANES))) * whole)
    decay_f, decay_r = dot(decay, spread_f[...]), dot(decay, spread_r[...])
    decay_f_o[...] = decay_f
    decay_r_o[...] = decay_r

    values = act_o[:, :inner]
    values_wide = values.astype(WIDE)
    state_act = act_o[:, inner:]
    turned = state_act.astype(WIDE).T.astype(LOW)
    forward_act, reverse_act = state_act[:, : 2 * STATE], state_act[:, 2 * STATE :]
    row, col = iota((size, size), 0), iota((size, size), 1)
    lower = row > col
    lower_low = lower.astype(WIDE).astype(LOW)
    upper_low = (row < col).astype(WIDE).astype(LOW)
    scores = jnp.where(
        lower,
        dot(forward_act, below(turned[:STATE])),
        dot(reverse_act, below(turned[2 * STATE : 3 * STATE])),
    )
    bias = table_bias(starts, block, size)
    for pair in range(inner // LANES):
        lanes = slice(pair * LANES, (pair + 1) * LANES)
        lefts, rights = [], []
        for head_at in (2 * pair, 2 * pair + 1):
            c = 2 * head_at
            gap = jnp.where(
                lower,
                cum[:, c : c + 1] - late_rows[c : c + 1],
                cum[:, c + 1 : c + 2] - late_rows[c + 1 : c + 2],
            )
            mix = (scores * jnp.exp(gap + bias)).astype(LOW)
            lefts.append(mix * lower_low)
            rights.append(mix * upper_low)
        both = jnp.concatenate(
            [jnp.concatenate(lefts, axis=1), jnp.concatenate(rights, axis=1)], axis=0
        )
        result = dot(both, block_diagonal(act_o[:, lanes]))
        out_f_o[:, lanes] = result[:size]
        inner_r_o[:, lanes] = result[size:]

    state = state_s[...]
    state_f_o[...] = state
    carried = dot(forward_act, below(state.astype(LOW)))
    out_f_o[...] += dot(head, spread_f[...]) * carried
    local_f = dot(turned[:STATE], (dot(tail, spread_f[...]) * values_wide).astype(LOW))
    state_s[...] = decay_f[:1] * state + local_f
    local_r_o[...] = dot(
        turned[2 * STATE : 3 * STATE], (dot(tail, spread_r[...]) * values_wide).astype(LOW)
    )


def output_kernel(
    starts, normed, act, out_f, inner_r, cum, local_r, decay_r, mine, other, pay, small, spread_r,
    out_r_o, state_r_o, gate_o, unscaled_o, unscaled_grad_o, sums_o, keep_o, send_o, gate_w,
    state_s, out_w,
):
    step, blocks = pl.program_id(0), pl.num_programs(0)
    block = blocks - 1 - step
    inner = out_f.shape[1]

    @pl.when(step == 0)
    def _():
        state_s[...] = jnp.zeros_like(state_s)
        chips, slots, rows, cols = pay.shape
        groups, half = slots // 2, cols // 2
        for chip in range(chips):
            for slot in range(slots):
                at = slice((2 * chip + slot // groups) * rows, (2 * chip + slot // groups + 1) * rows)
                lanes = slice((slot % groups) * half, (slot % groups + 1) * half)
                gate_w[at, lanes] = pay[chip, slot, :, :half]
                out_w[at, lanes] = pay[chip, slot, :, half:]

    _, head_mask, _ = start_masks(starts, block, blocks, cum.shape)
    head = halves(jnp.exp(cum[...]) * head_mask)
    state = state_s[...]
    state_r_o[...] = state
    reverse_act = act[:, inner + 2 * STATE :]
    carried = dot(reverse_act, below(state.astype(LOW)))
    out_r = inner_r[...] + dot(head, spread_r[...]) * carried
    out_r_o[...] = out_r
    state_s[...] = decay_r[:1] * state + local_r[...]
    skip_row, gain_row = skip_lanes(small[...], spread_r), small[5:6, :inner]
    core = out_f[...] + out_r + skip_row * act[:, :inner].astype(WIDE)
    gate = dot(normed[...], gate_w[...])
    gate_o[...] = gate
    gated = core * gate * jax.nn.sigmoid(gate)
    unscaled = (gated * gain_row).astype(LOW)
    unscaled_o[...] = unscaled
    own = parity(starts, block)
    unscaled_grad = dot(jnp.where(own, mine[...], other[...]), out_w[...])
    unscaled_grad_o[...] = unscaled_grad
    squares = jnp.sum(gated * gated, axis=1, keepdims=True)
    products = jnp.sum(unscaled_grad * unscaled.astype(WIDE), axis=1, keepdims=True)
    size = out_r.shape[0]
    lane = iota((size, LANES), 1)
    sums_o[...] = jnp.where(lane == 0, squares, products).T[:8]
    pre_out = dot_nt(unscaled, out_w[...]).astype(LOW)

    @pl.when(own)
    def _():
        keep_o[...] = pre_out

    @pl.when(jnp.logical_not(own))
    def _():
        send_o[...] = pre_out


def gate_back_kernel(
    starts, own_sums, other_sums, mine, other, out_f, out_r, act, gate, unscaled_grad, cum, decay_r,
    small, spread_f, spread_r, gather_f, gather_r,
    total_o, core_grad_o, gate_grad_o, row_sums_o, back_f_o, later_r_o, gain_grad_o, skip_grad_o,
    later_s,
):
    block, blocks = pl.program_id(0), pl.num_programs(0)
    inner = out_f.shape[1]
    inner_width = HEADS * HEADDIM

    @pl.when(block == 0)
    def _():
        later_s[...] = jnp.zeros_like(later_s)
        gain_grad_o[...] = jnp.zeros_like(gain_grad_o)
        skip_grad_o[...] = jnp.zeros_like(skip_grad_o)

    size = out_f.shape[0]
    sums = own_sums[...] + other_sums[...]
    sums = jnp.concatenate([sums, jnp.zeros((size - 8, size), WIDE)], axis=0).T
    skip_row, gain_row = skip_lanes(small[...], spread_f), small[5:6, :inner]
    scale = lax.rsqrt(sums[:, 0:1] / inner_width + 1e-05)
    square_grad = sums[:, 1:2] * scale * scale * scale / inner_width
    cotangent = jnp.where(parity(starts, block), mine[...], other[...])
    total_o[...] = (scale * cotangent.astype(WIDE)).astype(LOW)
    values = act[:, :inner].astype(WIDE)
    core = out_f[...] + out_r[...] + skip_row * values
    gate_value = gate[...]
    sigma = jax.nn.sigmoid(gate_value)
    slope = gate_value * sigma
    gated = core * slope
    unscaled = scale * unscaled_grad[...]
    gain_grad_o[...] += rows_sum(unscaled * gated)
    gated_grad = unscaled * gain_row - gated * square_grad
    core_grad = (gated_grad * slope).astype(LOW)
    core_grad_o[...] = core_grad
    gate_grad_o[...] = (gated_grad * core * silu_slope(gate_value, sigma)).astype(LOW)
    grad_wide = core_grad.astype(WIDE)
    skip_grad_o[...] += rows_sum(grad_wide * values)
    row_sums_o[...] = dot(halves(grad_wide * out_f[...]), gather_f[...]) + dot(
        halves(grad_wide * out_r[...]), gather_r[...]
    )
    _, head_mask, _ = start_masks(starts, block, blocks, cum.shape)
    head = halves(jnp.exp(cum[...]) * head_mask)
    turned = act[:, inner:].astype(WIDE).T.astype(LOW)
    back_f_o[...] = dot(
        turned[STATE : 2 * STATE], (dot(head, spread_f[...]) * grad_wide).astype(LOW)
    )
    back_r = dot(turned[3 * STATE :], (dot(head, spread_r[...]) * grad_wide).astype(LOW))
    later = later_s[...]
    later_r_o[...] = later
    later_s[...] = decay_r[:1] * later + back_r


def chain_back_kernel(
    starts, core_grad, gate_grad, act, conv, pre, cum, raw, row_sums, state_f, state_f_next,
    state_r, state_r_last, back_f, later_r, decay_f, gate_w, weights, small, spread_f, spread_r,
    gather_f, gather_r,
    proj_o, keep_o, send_o, taps_grad_o, scalar_o,
    later_s, next_s, values_f_s, values_r_s, active_s,
):
    step_at, blocks = pl.program_id(0), pl.num_programs(0)
    block = blocks - 1 - step_at
    size, inner = core_grad.shape
    channels = inner + 4 * STATE
    reach = 4

    @pl.when(step_at == 0)
    def _():
        later_s[...] = jnp.zeros_like(later_s)
        next_s[...] = jnp.zeros_like(next_s)
        taps_grad_o[...] = jnp.zeros_like(taps_grad_o)
        scalar_o[...] = jnp.zeros_like(scalar_o)

    small_here = small[...]
    bias_row, rate_row = step_rows(small_here, inner // HEADDIM)
    skip_row, taps = skip_lanes(small_here, spread_f), small_here[:8, :channels]
    cum_here = cum[...]
    step, sigma, ratio = steps_of(raw[...], bias_row)
    late = cum_here - jnp.log(step)
    cum_rows = cum_here.T
    tail_mask, head_mask, _ = start_masks(starts, block, blocks, cum_here.shape)
    tail = halves(jnp.exp(chain_last(cum_here) - late) * tail_mask)
    head = halves(jnp.exp(cum_here) * head_mask)
    state_act = act[:, inner:]
    turned = state_act.astype(WIDE).T.astype(LOW)
    forward_act, reverse_act = state_act[:, : 2 * STATE], state_act[:, 2 * STATE :]
    row, col = iota((size, size), 0), iota((size, size), 1)
    ahead = col > row
    ahead_low = ahead.astype(WIDE).astype(LOW)
    behind_low = (col < row).astype(WIDE).astype(LOW)
    scores = jnp.where(
        ahead,
        dot(forward_act, above(turned[STATE : 2 * STATE])),
        dot(reverse_act, above(turned[3 * STATE :])),
    )
    bias = table_bias(starts, block, size)
    scores_grad = jnp.zeros((size, size), WIDE)
    for pair in range(inner // LANES):
        lanes = slice(pair * LANES, (pair + 1) * LANES)
        grad_blocks = block_diagonal(core_grad[:, lanes])
        mix_grad = dot_nt(act[:, lanes], grad_blocks)
        lefts, rights = [], []
        for at in range(2):
            c = 2 * (2 * pair + at)
            gap = jnp.where(
                ahead,
                cum_rows[c : c + 1] - late[:, c : c + 1],
                cum_rows[c + 1 : c + 2] - late[:, c + 1 : c + 2],
            )
            table = jnp.exp(gap + bias)
            mix = (scores * table).astype(LOW)
            lefts.append(mix * ahead_low)
            rights.append(mix * behind_low)
            scores_grad = scores_grad + mix_grad[:, at * size : (at + 1) * size] * table
        both = jnp.concatenate(
            [jnp.concatenate(lefts, axis=1), jnp.concatenate(rights, axis=1)], axis=0
        )
        result = dot(both, grad_blocks)
        values_f_s[:, lanes] = result[:size]
        values_r_s[:, lanes] = result[size:]

    grad_wide = core_grad[...].astype(WIDE)
    values = act[:, :inner].astype(WIDE)
    later_f, later_r_here = later_s[...], later_r[...]
    later_f_low, later_r_low = later_f.astype(LOW), later_r_here.astype(LOW)
    tail_f, tail_r = dot(tail, spread_f[...]), dot(tail, spread_r[...])
    values_f = values_f_s[...] + tail_f * dot(forward_act, above(later_f_low))
    values_r = values_r_s[...] + tail_r * dot(reverse_act, above(later_r_low))
    col_sums = dot(halves(values * values_f), gather_f[...]) + dot(
        halves(values * values_r), gather_r[...]
    )
    end_f = rows_sum(later_f * state_f_next[...])
    end_r = rows_sum(later_r_here * state_r_last[...])
    end_f = jnp.sum(dot(halves(end_f), gather_f[...]), axis=0, keepdims=True)
    end_r = jnp.sum(dot(halves(end_r), gather_r[...]), axis=0, keepdims=True)
    row = iota(cum_here.shape, 0)
    cum_grad = row_sums[...] - col_sums
    cum_grad = cum_grad + jnp.where(row == size - 1, end_f, 0.0) + jnp.where(row == 0, end_r, 0.0)
    log_grad = running_sums(cum_grad, True)
    raw_grad = col_sums * ratio - rate_row * log_grad * sigma
    scalar_o[0:8] += rows_sum(raw_grad)
    scalar_o[8:16] += rows_sum(log_grad * (-step * rate_row))

    mid = scores_grad.T
    pieces = []
    for act_pair, spread_head, state, later_low, forward_side in (
        (forward_act, spread_f, state_f, later_f_low, True),
        (reverse_act, spread_r, state_r, later_r_low, False),
    ):
        tail_here = tail_f if forward_side else tail_r
        scaled = (tail_here * values).astype(LOW)
        carried_grad = (dot(head, spread_head[...]) * grad_wide).astype(LOW)
        own = ahead_low if forward_side else behind_low
        mirrored = behind_low if forward_side else ahead_low
        sides = jnp.concatenate(
            [scores_grad.astype(LOW) * own, mid.astype(LOW) * mirrored], axis=1
        )
        swapped = pltpu.roll(act_pair.astype(WIDE), STATE, 1).astype(LOW)
        pieces.append(
            dot_nt(scaled, above(later_low))
            + dot_nt(carried_grad, below(state[...].astype(LOW)))
            + dot(sides, block_diagonal(swapped))
        )
    active_s[:, :inner] = values_f + values_r + skip_row * grad_wide
    active_s[:, inner : inner + LANES] = pieces[0]
    active_s[:, inner + LANES :] = pieces[1]
    decay = decay_f[...]
    later_s[...] = decay[:1] * later_f + back_f[...]

    start = starts[block]
    following = starts[jnp.minimum(block + 1, blocks - 1)]
    row = iota((size, LANES), 0)
    number = (row >= start).astype(jnp.int32)
    masks = []
    for lag in range(1, reach):
        source = row + lag
        inside = (source >= start).astype(jnp.int32)
        outside = jnp.where(start < size, 1, 0) + (source - size >= following).astype(jnp.int32)
        masks.append((number == jnp.where(source < size, inside, outside)).astype(WIDE))
    for at in range(0, channels, LANES):
        lanes = slice(at, at + LANES)
        pre_here = pre[:, lanes]
        grad = active_s[:, lanes] * silu_slope(pre_here, jax.nn.sigmoid(pre_here))
        extended = jnp.concatenate([grad, next_s[:, lanes]], axis=0)
        next_s[:, lanes] = grad[:8]
        source = conv[:, lanes].astype(WIDE)
        result = taps[0:1, lanes] * grad
        taps_grad_o[0:8, lanes] += rows_sum(grad * source)
        taps_grad_o[32:40, lanes] += rows_sum(grad)
        for lag in range(1, reach):
            shifted = pltpu.roll(extended, size + 8 - lag, 0)[:size] * masks[lag - 1]
            result = result + taps[lag : lag + 1, lanes] * shifted
            taps_grad_o[8 * lag : 8 * lag + 8, lanes] += rows_sum(shifted * source)
        proj_o[:, lanes] = result.astype(LOW)
    proj_o[:, channels:] = raw_grad.astype(LOW)
    normed = dot_nt(gate_grad[...], gate_w[...]) + dot_nt(proj_o[...], weights[...])
    own = parity(starts, block)

    @pl.when(own)
    def _():
        keep_o[...] = normed

    @pl.when(jnp.logical_not(own))
    def _():
        send_o[...] = normed.astype(LOW)


def by_block(kernel, blocks, reverse, ins, outs, scratch, name, work):
    def at(i):
        return blocks - 1 - i if reverse else i

    def spec(shape, kind):
        if kind == "scalar":
            return pl.BlockSpec(memory_space=pltpu.SMEM)
        if kind == "whole":
            return pl.BlockSpec(shape, lambda i: (0,) * len(shape))
        if kind == "rows":
            return pl.BlockSpec((shape[0] // blocks,) + shape[1:], lambda i: (at(i), 0))
        if kind == "half":
            return pl.BlockSpec((None,) + shape[1:], lambda i: (at(i) // 2, 0, 0))
        if kind == "lanes":
            return pl.BlockSpec((shape[0], shape[1] // blocks), lambda i: (0, at(i)))
        if kind == "next":
            return pl.BlockSpec(
                (shape[0] // blocks,) + shape[1:],
                lambda i: (jnp.minimum(at(i) + 1, blocks - 1), 0),
            )
        if kind == "last":
            return pl.BlockSpec(
                (shape[0] // blocks,) + shape[1:], lambda i: (jnp.maximum(at(i) - 1, 0), 0)
            )
        raise ValueError(kind)

    return pl.pallas_call(
        kernel,
        grid=(blocks,),
        in_specs=[spec(value.shape, kind) for value, kind in ins],
        out_specs=[spec(value.shape, kind) for value, kind in outs],
        out_shape=[value for value, _ in outs],
        scratch_shapes=[pltpu.VMEM(shape, dtype) for shape, dtype in scratch],
        compiler_params=pltpu.CompilerParams(
            dimension_semantics=("arbitrary",), vmem_limit_bytes=56 * 1024 * 1024
        ),
        cost_estimate=pl.CostEstimate(
            flops=work,
            transcendentals=0,
            bytes_accessed=sum(v.size * v.dtype.itemsize for v, _ in ins + outs),
        ),
        name=name,
    )(*[value for value, _ in ins])


def swap_core(value):
    return lax.ppermute(value, "core", [(0, 1), (1, 0)])


def spread_to(value, axis):
    count = lax.axis_size(axis)
    return lax.all_to_all(jnp.broadcast_to(value[None], (count,) + value.shape), axis, 0, 0)


def pass_on(values, axis):
    count = lax.axis_size(axis)
    return [
        lax.ppermute(values[0], axis, [(i, i + 1) for i in range(count - 1)]),
        lax.ppermute(values[1], axis, [(i + 1, i) for i in range(count - 1)]),
    ]


def line_order(passed, axis):
    count, mine = lax.axis_size(axis), lax.axis_index(axis)
    value = passed[0][0]
    result = jnp.zeros((count,) + value.shape, value.dtype)
    result = lax.dynamic_update_index_in_dim(result, value, mine, 0)
    for k in range(1, len(passed)):
        for piece, at in zip(passed[k], (mine - k, mine + k)):
            here = jnp.logical_and(at >= 0, at < count)
            result = lax.dynamic_update_index_in_dim(
                result, jnp.where(here, piece, value), jnp.where(here, at, mine), 0
            )
    return result


def line_end(result, passed, axis):
    at = lax.axis_size(axis) - 1 - lax.axis_index(axis)
    there = lax.dynamic_index_in_dim(result, at, 0, keepdims=False)
    there = there + (passed[0] + passed[1]).astype(there.dtype)
    return lax.dynamic_update_index_in_dim(result, there, at, 0)


def after(value, *others):
    return lax.optimization_barrier((value,) + others)[0]


def three_parts(value):
    high = lax.reduce_precision(value, 8, 7)
    middle = lax.reduce_precision(value - high, 8, 7)
    return jnp.stack([high, middle, lax.reduce_precision(value - high - middle, 8, 7)])


def placed(value, width, at):
    shape = value.shape[:-1] + (width,)
    return lax.dynamic_update_slice_in_dim(jnp.zeros(shape, value.dtype), value, at, value.ndim - 1)


def chip_plan(
    tokens,
    starts,
    in_weight,
    state_weight,
    state_conv,
    out_weight,
    value_conv,
    norm_gain,
    gate_gain,
    step_bias,
    decay_log,
    skip,
    out_cotangent,
):
    low, wide = LOW, WIDE
    sequences, block_size, width = tokens.shape
    chips, planes = lax.axis_size("chip"), lax.axis_size("head")
    chip, core, plane = lax.axis_index("chip"), lax.axis_index("core"), lax.axis_index("head")
    blocks = starts.shape[1]
    length = blocks * block_size
    rows, group = in_weight.shape[:2]
    groups = planes // 2
    heads_here = group * groups
    inner_here, group_inner = heads_here * HEADDIM, group * HEADDIM
    part, reach = value_conv.shape[0], state_conv.shape[1] - 1
    state_part = state_conv.shape[0]
    channels_state = state_weight.shape[1]
    channels = inner_here + channels_state
    seq = 2 * chip + core
    first = core == 0

    def own_plane(value):
        return lax.dynamic_slice_in_dim(value, plane * chips, chips, 0)

    tokens_plane = own_plane(tokens)
    tokens_plane, in_weight, out_weight = lax.optimization_barrier(
        (tokens_plane, in_weight, out_weight)
    )
    tokens_mine = lax.all_to_all(tokens_plane, "chip", 0, 0)
    tokens_other = swap_core(tokens_mine)

    step_at = (plane % groups) * 2 * group
    pair_weights = placed(in_weight[:, :, 2 * HEADDIM :].reshape(rows, 2 * group), LANES, step_at)
    tap_lanes = placed(value_conv.transpose(2, 1, 0), HEADDIM, part * seq).reshape(reach + 1, -1)
    gain_lanes = placed(gate_gain.transpose(1, 0), HEADDIM, part * seq).reshape(1, -1)
    extra_value = jnp.concatenate([tap_lanes, gain_lanes], axis=0)
    scalars = jnp.stack(
        [step_bias.T.reshape(-1), jnp.repeat(decay_log, 2), jnp.repeat(skip, 2)]
    )
    scalars = jnp.swapaxes(three_parts(jnp.where(seq == 0, scalars, 0.0)), 0, 1)
    extra_step = placed(scalars.reshape(9, 2 * group).astype(low), LANES, step_at)
    slab = jnp.concatenate(
        [
            jnp.concatenate(
                [in_weight[:, :, HEADDIM : 2 * HEADDIM].reshape(rows, group_inner), pair_weights],
                axis=1,
            ),
            jnp.concatenate(
                [
                    jnp.pad(extra_value, ((0, 16 - extra_value.shape[0]), (0, 0))),
                    jnp.pad(extra_step, ((0, 16 - extra_step.shape[0]), (0, 0))),
                ],
                axis=1,
            ),
        ],
        axis=0,
    )
    extra_state = jnp.concatenate(
        [
            placed(state_conv.T, channels_state, state_part * seq),
            placed(norm_gain, width, rows * seq).reshape(-1, channels_state),
        ],
        axis=0,
    )
    state_slab = jnp.concatenate(
        [state_weight, jnp.pad(extra_state, ((0, 16 - extra_state.shape[0]), (0, 0)))], axis=0
    )
    shifted = [slab] + [
        lax.ppermute(slab, "head", [(i, (i + k) % planes) for i in range(planes)])
        for k in range(1, planes)
    ]
    shifted = jnp.stack(shifted)

    def for_core(which):
        picked = [
            lax.dynamic_index_in_dim(shifted, (plane - which * groups - i) % planes, 0, False)
            for i in range(groups)
        ]
        steps = picked[0][:, group_inner:]
        for i in range(1, groups):
            steps = steps + picked[i][:, group_inner:]
        return jnp.concatenate(
            [picked[i][:, :group_inner] for i in range(groups)] + [state_slab, steps], axis=1
        )

    pay = spread_to(jnp.stack([for_core(core), swap_core(for_core(1 - core))]), "chip")

    late_slab = jnp.concatenate(
        [
            in_weight[:, :, :HEADDIM].reshape(rows, group_inner),
            out_weight.reshape(rows, group_inner),
        ],
        axis=1,
    )
    moves = [
        ((2 * p + k) * planes + z, (2 * p + z // groups) * planes + groups * k + z % groups)
        for p in range(chips)
        for k in range(2)
        for z in range(planes)
    ]
    late_slab = lax.ppermute(late_slab, ("chip", "core", "head"), moves)
    pay_late = lax.all_gather(late_slab, ("chip", "head")).reshape(chips, planes, rows, -1)
    cotangent_low = own_plane(out_cotangent).astype(low)
    cotangent_low, pay = lax.optimization_barrier((cotangent_low, pay))
    cotangent_mine = lax.all_to_all(cotangent_low, "chip", 0, 0)
    starts_row = lax.dynamic_index_in_dim(starts, plane * chips + chip, 0, keepdims=False)
    starts_row = jnp.concatenate([starts_row, core[None].astype(starts_row.dtype)])
    (spread_f, spread_r), (gather_f, gather_r) = head_columns(heads_here)

    def shape(rows_, cols, dtype):
        return jax.ShapeDtypeStruct((rows_, cols), dtype)

    half_low = jax.ShapeDtypeStruct((chips, block_size, width), low)
    half_wide = jax.ShapeDtypeStruct((chips, block_size, width), wide)
    states = blocks * STATE
    lane_cols = channels + LANES
    (
        normed, conv_input, pre_active, act, out_f, inner_r, cum, step_raw, state_f, local_r,
        decay_f, decay_r, weights, small,
    ) = by_block(
        forward_kernel, blocks, False,
        [
            (starts_row, "scalar"), (tokens_mine, "half"), (tokens_other, "half"), (pay, "whole"),
            (spread_f, "whole"), (spread_r, "whole"),
        ],
        [
            (shape(length, width, low), "rows"), (shape(length, channels, low), "rows"),
            (shape(length, channels, wide), "rows"), (shape(length, channels, low), "rows"),
            (shape(length, inner_here, wide), "rows"), (shape(length, inner_here, wide), "rows"),
            (shape(length, LANES, wide), "rows"), (shape(length, LANES, wide), "rows"),
            (shape(states, inner_here, wide), "rows"), (shape(states, inner_here, wide), "rows"),
            (shape(8 * blocks, inner_here, wide), "rows"), (shape(8 * blocks, inner_here, wide), "rows"),
            (shape(width, lane_cols, low), "whole"), (shape(16, lane_cols, wide), "whole"),
        ],
        [((8, channels), wide), ((STATE, inner_here), wide)],
        "forward", 20_000_000_000,
    )
    cotangent_mine, normed = lax.optimization_barrier((cotangent_mine, normed))
    cotangent_other = swap_core(cotangent_mine)
    (
        out_r, state_r, gate, unscaled, unscaled_grad, own_sums, keep, send, gate_w,
    ) = by_block(
        output_kernel, blocks, True,
        [
            (starts_row, "scalar"), (normed, "rows"), (act, "rows"), (out_f, "rows"), (inner_r, "rows"),
            (cum, "rows"), (local_r, "rows"), (decay_r, "rows"), (cotangent_mine, "half"),
            (cotangent_other, "half"), (pay_late, "whole"), (small, "whole"), (spread_r, "whole"),
        ],
        [
            (shape(length, inner_here, wide), "rows"), (shape(states, inner_here, wide), "rows"),
            (shape(length, inner_here, wide), "rows"), (shape(length, inner_here, low), "rows"),
            (shape(length, inner_here, wide), "rows"), (shape(8, length, wide), "lanes"),
            (half_low, "half"), (half_low, "half"), (shape(width, inner_here, low), "whole"),
        ],
        [((STATE, inner_here), wide), ((width, inner_here), low)],
        "outputs", 12_000_000_000,
    )
    other_sums = swap_core(own_sums)

    squares = (own_sums[0] + other_sums[0]).reshape(chips, 2, block_size)
    squares = lax.dynamic_index_in_dim(squares, core, 1, keepdims=False)
    gate_scale = lax.rsqrt(squares / (HEADS * HEADDIM) + 1e-05)
    out_delta = gate_scale[..., None] * (keep.astype(wide) + swap_core(send).astype(wide))
    out_delta, gate = lax.optimization_barrier((out_delta.astype(low), gate))
    out_moved = lax.all_to_all(out_delta, "chip", 0, 0)

    (total_grad, core_grad, gate_grad, row_sums, back_f, later_r, gain_grad, skip_grad) = by_block(
        gate_back_kernel, blocks, False,
        [
            (starts_row, "scalar"), (own_sums, "lanes"), (other_sums, "lanes"), (cotangent_mine, "half"),
            (cotangent_other, "half"), (out_f, "rows"), (out_r, "rows"),
            (act, "rows"), (gate, "rows"), (unscaled_grad, "rows"), (cum, "rows"), (decay_r, "rows"),
            (small, "whole"), (spread_f, "whole"), (spread_r, "whole"),
            (gather_f, "whole"), (gather_r, "whole"),
        ],
        [
            (shape(length, width, low), "rows"), (shape(length, inner_here, low), "rows"),
            (shape(length, inner_here, low), "rows"), (shape(length, LANES, wide), "rows"),
            (shape(states, inner_here, wide), "rows"), (shape(states, inner_here, wide), "rows"),
            (shape(8, inner_here, wide), "whole"), (shape(8, inner_here, wide), "whole"),
        ],
        [((STATE, inner_here), wide)],
        "gate_back", 12_000_000_000,
    )

    def weight_grad(left, right):
        result = lax.dot_general(left, right, (((0,), (0,)), ((), ())), preferred_element_type=wide)
        return result.astype(low)

    gate_grad, total_grad, out_moved = lax.optimization_barrier((gate_grad, total_grad, out_moved))
    out_delta = lax.all_gather(out_moved, "head").reshape(sequences, block_size, width)
    early_grad = jnp.concatenate(
        [weight_grad(normed, gate_grad), weight_grad(total_grad, unscaled)], axis=1
    ).reshape(chips, 2, rows, -1)
    early_grad, core_grad = lax.optimization_barrier((early_grad, core_grad))
    early_moved = lax.all_to_all(early_grad, "chip", 0, 0)
    rest_grad, keep, send, taps_grad, scalar_part = by_block(
        chain_back_kernel, blocks, True,
        [
            (starts_row, "scalar"), (core_grad, "rows"), (gate_grad, "rows"), (act, "rows"),
            (conv_input, "rows"), (pre_active, "rows"), (cum, "rows"), (step_raw, "rows"),
            (row_sums, "rows"), (state_f, "rows"), (state_f, "next"), (state_r, "rows"),
            (state_r, "last"), (back_f, "rows"), (later_r, "rows"), (decay_f, "rows"),
            (gate_w, "whole"), (weights, "whole"), (small, "whole"), (spread_f, "whole"),
            (spread_r, "whole"), (gather_f, "whole"), (gather_r, "whole"),
        ],
        [
            (shape(length, lane_cols, low), "rows"), (half_wide, "half"), (half_low, "half"),
            (shape(40, channels, wide), "whole"), (shape(16, LANES, wide), "whole"),
        ],
        [
            ((STATE, inner_here), wide), ((8, channels), wide), ((block_size, inner_here), wide),
            ((block_size, inner_here), wide), ((block_size, channels), wide),
        ],
        "chain_back", 35_000_000_000,
    )

    norm_row = small[5 : 5 + width // channels_state, inner_here:channels].reshape(width)
    tokens_wide = tokens_mine.astype(wide)
    in_scale = lax.rsqrt(jnp.mean(tokens_wide * tokens_wide, axis=2, keepdims=True) + 1e-05)
    unit = tokens_wide * in_scale
    normed_grad = keep + swap_core(send).astype(wide)
    unit_grad = normed_grad * norm_row
    delta = in_scale * (unit_grad - unit * jnp.mean(unit_grad * unit, axis=2, keepdims=True))
    (
        delta, early_moved, out_delta, normed_late, rest_grad, taps_grad, scalar_part, normed_grad,
    ) = lax.optimization_barrier(
        (
            delta.astype(low), early_moved, out_delta, normed, rest_grad, taps_grad, scalar_part,
            normed_grad,
        )
    )
    delta = lax.all_to_all(delta, "chip", 0, 0)
    norm_grad = jnp.sum(normed_grad * unit, axis=(0, 1))

    taps_grad = jnp.sum(taps_grad.reshape(reach + 1, 8, channels), axis=1)
    scalar_part = jnp.sum(scalar_part.reshape(2, 8, LANES), axis=1)
    skip_part = jnp.sum(skip_grad.reshape(8, heads_here, HEADDIM), axis=(0, 2))
    skip_part = jnp.pad(jnp.repeat(skip_part, 2)[None], ((0, 0), (0, LANES - 2 * heads_here)))
    lanes_value = jnp.concatenate(
        [taps_grad[:, :inner_here], jnp.sum(gain_grad, axis=0, keepdims=True)], axis=0
    )
    lanes_state = jnp.concatenate(
        [taps_grad[:, inner_here:], norm_grad.reshape(-1, channels_state)], axis=0
    )
    lanes_step = jnp.concatenate([scalar_part, skip_part], axis=0)
    extra = jnp.concatenate(
        [
            jnp.pad(lanes_value, ((0, 16 - lanes_value.shape[0]), (0, 0))),
            jnp.pad(lanes_state, ((0, 16 - lanes_state.shape[0]), (0, 0))),
            jnp.pad(lanes_step, ((0, 16 - lanes_step.shape[0]), (0, 0))),
        ],
        axis=1,
    ).astype(low)
    late_grad = weight_grad(normed_late, rest_grad).reshape(chips, 2, rows, lane_cols)
    late_grad = jnp.concatenate(
        [late_grad, jnp.broadcast_to(extra, (chips, 2) + extra.shape)], axis=2
    )
    late_grad, delta = lax.optimization_barrier((late_grad, delta))
    late_moved = lax.all_to_all(late_grad, "chip", 0, 0)
    near = pass_on([delta, delta], "head")
    *near, late_moved = lax.optimization_barrier((*near, late_moved))
    far = pass_on(near, "head")
    output = tokens.astype(wide) + out_delta.astype(wide)

    def between_cores(moved):
        total = jnp.sum(moved.astype(wide), axis=0).astype(low)
        mine = lax.dynamic_index_in_dim(total, core, 0, keepdims=False)
        got = swap_core(lax.dynamic_index_in_dim(total, 1 - core, 0, keepdims=False))
        return [jnp.where(first, mine, got), jnp.where(first, got, mine)]

    def group_lanes(value, at, i):
        return value[:, at + i * group_inner : at + (i + 1) * group_inner]

    early = between_cores(early_moved)
    late = between_cores(late_moved)
    state_sum = late[0][:, inner_here:channels].astype(wide) + late[1][:, inner_here:channels].astype(wide)
    state_sum = state_sum.astype(low)
    own_state = rows // planes
    state_pieces = [
        jnp.concatenate(
            [
                state_sum[i * own_state : (i + 1) * own_state],
                jnp.zeros((rows - own_state, channels_state), low),
                state_sum[rows:],
            ],
            axis=0,
        )
        for i in range(planes)
    ]
    payload = jnp.stack(
        [
            jnp.concatenate(
                [
                    group_lanes(late[which], 0, i),
                    late[which][:, channels:],
                    state_pieces[which * groups + i],
                    jnp.pad(
                        jnp.concatenate(
                            [
                                group_lanes(early[which], 0, i),
                                group_lanes(early[which], inner_here, i),
                            ],
                            axis=1,
                        ),
                        ((0, 16), (0, 0)),
                    ),
                ],
                axis=1,
            )
            for which in range(2)
            for i in range(groups)
        ]
    )
    total = jnp.sum(lax.all_to_all(payload, "head", 0, 0).astype(wide), axis=0)
    *far, total, output = lax.optimization_barrier((*far, total, output))
    farthest = pass_on(far, "head")
    received = line_order([[delta] * 2, near, far], "head")
    input_gradient = out_cotangent + received.reshape(sequences, block_size, width).astype(wide)
    input_gradient = input_gradient.reshape((planes, chips, block_size, width))
    input_gradient = line_end(input_gradient, farthest, "head")
    input_gradient = input_gradient.reshape(sequences, block_size, width)
    early_at = group_inner + LANES + channels_state
    late, early = total[:, :early_at], total[:rows, early_at:]
    step_lanes = lax.dynamic_slice_in_dim(
        late[:, group_inner : group_inner + LANES], step_at, 2 * group, 1
    )
    in_weight_out = jnp.concatenate(
        [
            early[:, :group_inner].reshape(rows, group, HEADDIM),
            late[:rows, :group_inner].reshape(rows, group, HEADDIM),
            step_lanes[:rows].reshape(rows, group, 2),
        ],
        axis=2,
    )
    out_weight_out = early[:, group_inner:].reshape(rows, group, HEADDIM)
    lanes = late[rows:, :group_inner].reshape(16, group, HEADDIM)
    lanes = lax.dynamic_slice_in_dim(lanes, part * seq, part, 2)
    value_conv_out = lanes[: reach + 1].transpose(2, 1, 0)
    gate_gain_out = lanes[reach + 1].transpose(1, 0)
    state_out = late[:, group_inner + LANES :]
    conv_at = state_part * seq + (state_part // planes) * plane
    state_conv_out = lax.dynamic_slice_in_dim(
        state_out[rows : rows + reach + 1], conv_at, state_part // planes, 1
    ).T
    norm_sum = state_out[rows + reach + 1 :][: width // channels_state].reshape(width)
    norm_gain_out = lax.dynamic_slice_in_dim(norm_sum, rows * seq, rows, 0)
    return (
        output,
        input_gradient,
        in_weight_out,
        state_out[:own_state],
        state_conv_out,
        out_weight_out,
        value_conv_out,
        norm_gain_out,
        gate_gain_out,
        step_lanes[rows].reshape(group, 2).T,
        jnp.sum(step_lanes[rows + 1].reshape(group, 2), axis=1),
        step_lanes[rows + 2].reshape(group, 2)[:, 0],
    )


def solution(mesh):
    devices_seq, planes = mesh.devices.shape
    seq, plan = "seq", split_plan
    if devices_seq % 2 == 0 and planes % 2 == 0 and devices_seq // 2 * planes == CHIP_SEQUENCES:
        shape = (devices_seq // 2, 2, planes)
        mesh = Mesh(mesh.devices.reshape(shape), ("chip", "core", "head"))
        seq, plan = ("chip", "core"), chip_plan
    both = seq + ("head",) if isinstance(seq, tuple) else (seq, "head")
    return jax.shard_map(
        plan,
        mesh=mesh,
        in_specs=(
            P(None, seq, None),
            P(),
            P(seq, "head", None),
            P(seq, None),
            P(seq, None),
            P(seq, "head", None),
            P(seq, "head", None),
            P(seq),
            P(seq, "head"),
            P(None, "head"),
            P("head"),
            P("head"),
            P(None, seq, None),
        ),
        out_specs=(
            P(None, seq, None),
            P(None, seq, None),
            P(seq, "head", None),
            P(both, None),
            P(both, None),
            P(seq, "head", None),
            P(seq, "head", None),
            P(seq),
            P(seq, "head"),
            P(None, "head"),
            P("head"),
            P("head"),
        ),
        check_vma=False,
    )
```

```python
import jax
import jax.numpy as jnp
from jax import lax
from jax.experimental import pallas as pl
from jax.experimental.pallas import tpu as pltpu
from jax.sharding import Mesh, PartitionSpec as P

HEADS = 24
HEADDIM = 64
STATE = 64
CHIP_SEQUENCES = 16


def from_behind(value, axis, by):
    devices = lax.axis_size(axis)
    pairs = [(i, i + by) for i in range(devices) if 0 <= i + by < devices]
    return lax.ppermute(value, axis, pairs)


def entering(value, axis, join, neutral, backward):
    count, mine = (lax.axis_size(axis), lax.axis_index(axis))
    pieces = jax.tree.map(lambda part: lax.all_gather(part, axis), value)
    if backward:
        pieces = jax.tree.map(lambda part: part[::-1], pieces)
        mine = count - 1 - mine
    running = jax.tree.map(
        lambda part, zero: jnp.full_like(part, 0) + jnp.asarray(zero, part.dtype), value, neutral
    )

    def step(position, running):
        longer = join(running, jax.tree.map(lambda part: part[position], pieces))
        return jax.tree.map(lambda new, old: jnp.where(position < mine, new, old), longer, running)

    return lax.fori_loop(0, count - 1, step, running)


def affine(earlier, later):
    return (earlier[0] * later[0], later[0][..., None, None] * earlier[1] + later[1])


def document_numbers(starts, first_position, count, block_size):
    blocks = starts.shape[1]
    begins = jnp.arange(blocks, dtype=jnp.int32)[None, :] * block_size + starts
    valid = starts < block_size
    places = first_position + jnp.arange(count, dtype=jnp.int32)
    hits = (begins[:, None, :] <= places[None, :, None]) & valid[:, None, :]
    return jnp.sum(hits.astype(jnp.int32), axis=2)


def running_sum(value):
    length, shift = value.shape[-1], 1
    while shift < length:
        pad = [(0, 0)] * (value.ndim - 1) + [(shift, 0)]
        value = value + jnp.pad(value[..., : length - shift], pad)
        shift *= 2
    return value


def chain_forward(readout, intake, values, log_decay, step_size, flags):
    block_size = readout.shape[1]
    segment = running_sum(flags)
    decay_sum = running_sum(log_decay)
    scores = jnp.einsum("mtn,mjn->mtj", readout, intake, preferred_element_type=jnp.float32)
    order = jnp.arange(block_size)
    mask = ((order[:, None] > order[None, :])[None] & (segment[:, :, None] == segment[:, None, :]))[
        :, None
    ]
    gap = jnp.where(mask, decay_sum[:, :, :, None] - decay_sum[:, :, None, :], 0.0)
    decay_table = jnp.where(mask, jnp.exp(gap), 0.0)
    mixing = (scores[:, None] * decay_table * step_size[:, :, None, :]).astype(jnp.bfloat16)
    inner = jnp.einsum("mhtj,mjhp->mthp", mixing, values, preferred_element_type=jnp.float32)
    tail_factor = (
        jnp.exp(decay_sum[:, :, -1:] - decay_sum) * (segment == segment[:, -1:])[:, None, :]
    )
    scaled_intake = (
        (tail_factor * step_size)[..., None] * intake[:, None].astype(jnp.float32)
    ).astype(jnp.bfloat16)
    local_state = jnp.einsum(
        "mhjn,mjhp->mhnp", scaled_intake, values, preferred_element_type=jnp.float32
    )
    block_decay = jnp.exp(decay_sum[:, :, -1]) * (segment[:, -1] == 0)[:, None]
    head_scale = jnp.exp(decay_sum) * (segment == 0)[:, None, :]
    saved = (scores, decay_table, mixing, tail_factor, scaled_intake, head_scale)
    return (inner, local_state, block_decay, saved)


def chain_finish(inner, readout, state_in, head_scale):
    state_low = state_in.astype(jnp.bfloat16)
    carried = jnp.einsum("mtn,mhnp->mthp", readout, state_low, preferred_element_type=jnp.float32)
    return (inner + jnp.swapaxes(head_scale, 1, 2)[..., None] * carried, carried, state_low)


def chain_back_state(grad_out, readout, carried, state_low, head_scale):
    grad_wide = grad_out.astype(jnp.float32)
    carried_grad = (jnp.swapaxes(head_scale, 1, 2)[..., None] * grad_wide).astype(jnp.bfloat16)
    state_in_grad = jnp.einsum(
        "mtn,mthp->mhnp", readout, carried_grad, preferred_element_type=jnp.float32
    )
    readout_grad = jnp.einsum(
        "mthp,mhnp->mtn", carried_grad, state_low, preferred_element_type=jnp.float32
    )
    sum_grad = jnp.swapaxes(jnp.sum(grad_wide * carried, axis=3), 1, 2) * head_scale
    return (state_in_grad, readout_grad, sum_grad)


def chain_back_rest(
    grad_out,
    readout,
    intake,
    values,
    step_size,
    state_in,
    later,
    block_decay,
    saved,
    readout_grad,
    sum_grad,
):
    scores, decay_table, mixing, tail_factor, scaled_intake, head_scale = saved
    later_low = later.astype(jnp.bfloat16)
    scaled_grad = jnp.einsum(
        "mjhp,mhnp->mhjn", values, later_low, preferred_element_type=jnp.float32
    )
    values_grad = jnp.einsum(
        "mhjn,mhnp->mjhp", scaled_intake, later_low, preferred_element_type=jnp.float32
    )
    tail_grad = jnp.einsum("mhjn,mjn->mhj", scaled_grad, intake.astype(jnp.float32))
    intake_grad = jnp.einsum("mhjn,mhj->mjn", scaled_grad, tail_factor * step_size)
    step_grad = tail_grad * tail_factor
    tail_term = tail_grad * tail_factor * step_size
    decay_grad = jnp.sum(later * state_in, axis=(2, 3)) * block_decay
    sum_grad = (sum_grad - tail_term).at[:, :, -1].add(jnp.sum(tail_term, axis=2) + decay_grad)
    mixing_grad = jnp.einsum(
        "mthp,mjhp->mhtj", grad_out, values, preferred_element_type=jnp.float32
    )
    values_grad = values_grad + jnp.einsum(
        "mhtj,mthp->mjhp", mixing, grad_out, preferred_element_type=jnp.float32
    )
    through = mixing_grad * decay_table
    scores_grad = jnp.sum(through * step_size[:, :, None, :], axis=1).astype(jnp.bfloat16)
    readout_grad = readout_grad + jnp.einsum(
        "mtj,mjn->mtn", scores_grad, intake, preferred_element_type=jnp.float32
    )
    intake_grad = intake_grad + jnp.einsum(
        "mtj,mtn->mjn", scores_grad, readout, preferred_element_type=jnp.float32
    )
    kernel = through * scores[:, None]
    step_grad = step_grad + jnp.sum(kernel, axis=2)
    weighted = kernel * step_size[:, :, None, :]
    sum_grad = sum_grad + jnp.sum(weighted, axis=3) - jnp.sum(weighted, axis=2)
    log_grad = jnp.flip(running_sum(jnp.flip(sum_grad, 2)), 2)
    return (values_grad, readout_grad, intake_grad, step_grad, log_grad)


def split_plan(
    tokens,
    starts,
    in_weight,
    state_weight,
    state_conv,
    out_weight,
    value_conv,
    norm_gain,
    gate_gain,
    step_bias,
    decay_log,
    skip,
    out_cotangent,
):
    sequences, block_size, width = tokens.shape
    place = lax.axis_index("seq")
    devices_seq = lax.axis_size("seq")
    in_weights, state_weights, state_taps, out_weights, value_taps, norm_whole, gate_whole = (
        lax.all_gather(in_weight, "seq", axis=0, tiled=True),
        lax.all_gather(state_weight, "seq", axis=0, tiled=True),
        lax.all_gather(state_conv, "seq", axis=0, tiled=True),
        lax.all_gather(out_weight, "seq", axis=0, tiled=True),
        lax.all_gather(value_conv, "seq", axis=0, tiled=True),
        lax.all_gather(norm_gain, "seq", axis=0, tiled=True),
        lax.all_gather(gate_gain, "seq", axis=0, tiled=True),
    )
    heads_here = in_weight.shape[1]
    value_width = heads_here * HEADDIM
    reach = state_conv.shape[1] - 1
    edge = reach - 1
    numbers = document_numbers(starts, place * block_size - edge, block_size + 2 * edge, block_size)
    lag_masks = jnp.stack(
        [
            numbers[:, edge:] == numbers[:, edge - lag : block_size + 2 * edge - lag]
            for lag in range(reach)
        ],
        axis=2,
    ).astype(jnp.float32)
    first = (
        numbers[:, edge : edge + block_size] != numbers[:, edge - 1 : edge + block_size - 1]
    ).astype(jnp.int32)
    positions = place * block_size + jnp.arange(block_size, dtype=jnp.int32)
    ending = (positions == devices_seq * block_size - 1)[None, :]
    last = (
        (numbers[:, edge + 1 : edge + block_size + 1] != numbers[:, edge : edge + block_size])
        | ending
    ).astype(jnp.int32)
    tokens_wide = tokens.astype(jnp.float32)
    in_scale = lax.rsqrt(jnp.mean(tokens_wide * tokens_wide, axis=2, keepdims=True) + 1e-05)
    unit = tokens_wide * in_scale
    norm_wide = norm_whole.astype(jnp.float32)
    normed = (unit * norm_wide).astype(jnp.bfloat16)
    projected = jnp.einsum("mtd,dhk->mthk", normed, in_weights, preferred_element_type=jnp.float32)
    state_proj = jnp.einsum(
        "mtd,dn->mtn", normed, state_weights, preferred_element_type=jnp.float32
    )
    gate = projected[..., :HEADDIM]
    step_raw = projected[..., 2 * HEADDIM :]
    conv_input = jnp.concatenate(
        [
            projected[..., HEADDIM : 2 * HEADDIM].reshape(sequences, block_size, value_width),
            state_proj,
        ],
        axis=2,
    ).astype(jnp.bfloat16)
    channels = conv_input.shape[2]
    halo_rows = from_behind(conv_input[:, block_size - edge :], "seq", 1)
    extended = jnp.concatenate([halo_rows, conv_input], axis=1)
    taps = jnp.concatenate(
        [jnp.transpose(value_taps, (1, 0, 2)).reshape(value_width, reach + 1), state_taps], axis=0
    ).astype(jnp.float32)
    pre_active = jnp.broadcast_to(taps[:, reach], (sequences, block_size, channels))
    for lag in range(reach):
        pre_active = (
            pre_active
            + taps[:, lag]
            * extended[:, edge - lag : edge - lag + block_size]
            * lag_masks[:, :block_size, lag, None]
        )
    active_sigma = jax.nn.sigmoid(pre_active)
    activated = (pre_active * active_sigma).astype(jnp.bfloat16)
    values = activated[..., :value_width].reshape(sequences, block_size, heads_here, HEADDIM)
    intake_forward = activated[..., value_width : value_width + STATE]
    readout_forward = activated[..., value_width + STATE : value_width + 2 * STATE]
    intake_reverse = jnp.flip(activated[..., value_width + 2 * STATE : value_width + 3 * STATE], 1)
    readout_reverse = jnp.flip(activated[..., value_width + 3 * STATE :], 1)
    values_reversed = jnp.flip(values, 1)
    rate = jnp.exp(decay_log)
    bias_here = jnp.transpose(step_bias)[None, None]
    step_all = jax.nn.softplus(step_raw + bias_here)
    step_forward = jnp.transpose(step_all[..., 0], (0, 2, 1))
    step_reverse = jnp.flip(jnp.transpose(step_all[..., 1], (0, 2, 1)), 2)
    log_forward = -step_forward * rate[None, :, None]
    log_reverse = -step_reverse * rate[None, :, None]
    inner_forward, local_forward, decay_forward, saved_forward = chain_forward(
        readout_forward, intake_forward, values, log_forward, step_forward, first
    )
    inner_reverse, local_reverse, decay_reverse, saved_reverse = chain_forward(
        readout_reverse,
        intake_reverse,
        values_reversed,
        log_reverse,
        step_reverse,
        jnp.flip(last, 1),
    )
    identity = (jnp.ones_like(decay_forward), jnp.zeros_like(local_forward))
    state_forward = entering((decay_forward, local_forward), "seq", affine, identity, False)[1]
    state_reverse = entering((decay_reverse, local_reverse), "seq", affine, identity, True)[1]
    out_forward, carried_forward, state_low_forward = chain_finish(
        inner_forward, readout_forward, state_forward, saved_forward[5]
    )
    out_reverse, carried_reverse, state_low_reverse = chain_finish(
        inner_reverse, readout_reverse, state_reverse, saved_reverse[5]
    )
    core = (
        out_forward
        + jnp.flip(out_reverse, 1)
        + skip[None, None, :, None] * values.astype(jnp.float32)
    )
    gate_sigma = jax.nn.sigmoid(gate)
    gated = core * gate * gate_sigma
    gate_gains = jnp.transpose(gate_whole).astype(jnp.float32)
    unscaled = (gated * gate_gains).astype(jnp.bfloat16)
    squares = jnp.sum(gated * gated, axis=(2, 3))
    partial_value = jnp.einsum(
        "mthp,dhp->mtd", unscaled, out_weights, preferred_element_type=jnp.float32
    )
    pre_out, square_sum = lax.psum((partial_value, squares), "head")
    inner_width = HEADS * HEADDIM
    gate_scale = lax.rsqrt(square_sum / inner_width + 1e-05)
    output = tokens_wide + gate_scale[..., None] * pre_out
    total_grad = (gate_scale[..., None] * out_cotangent).astype(jnp.bfloat16)
    unscaled_grad = jnp.einsum(
        "mtd,dhp->mthp", total_grad, out_weights, preferred_element_type=jnp.float32
    )
    out_weight_grad = jnp.einsum(
        "mtd,mthp->dhp", total_grad, unscaled, preferred_element_type=jnp.float32
    )
    scale_grad = jnp.sum(out_cotangent * pre_out, axis=2)
    square_grad = -0.5 * scale_grad * gate_scale**3 / inner_width
    gated_grad = unscaled_grad * gate_gains + 2.0 * gated * square_grad[..., None, None]
    gate_gain_grad = jnp.transpose(jnp.sum(unscaled_grad * gated, axis=(0, 1)))
    core_grad = (gated_grad * gate * gate_sigma).astype(jnp.bfloat16)
    gate_grad = gated_grad * core * gate_sigma * (1.0 + gate * (1.0 - gate_sigma))
    skip_grad = jnp.sum(core_grad.astype(jnp.float32) * values.astype(jnp.float32), axis=(0, 1, 3))
    core_reversed = jnp.flip(core_grad, 1)
    state_grad_forward, readout_grad_forward, sum_grad_forward = chain_back_state(
        core_grad, readout_forward, carried_forward, state_low_forward, saved_forward[5]
    )
    state_grad_reverse, readout_grad_reverse, sum_grad_reverse = chain_back_state(
        core_reversed, readout_reverse, carried_reverse, state_low_reverse, saved_reverse[5]
    )
    later_forward = entering((decay_forward, state_grad_forward), "seq", affine, identity, True)[1]
    later_reverse = entering((decay_reverse, state_grad_reverse), "seq", affine, identity, False)[1]
    (
        values_grad_forward,
        readout_grad_forward,
        intake_grad_forward,
        step_grad_forward,
        log_grad_forward,
    ) = chain_back_rest(
        core_grad,
        readout_forward,
        intake_forward,
        values,
        step_forward,
        state_forward,
        later_forward,
        decay_forward,
        saved_forward,
        readout_grad_forward,
        sum_grad_forward,
    )
    (
        values_grad_reverse,
        readout_grad_reverse,
        intake_grad_reverse,
        step_grad_reverse,
        log_grad_reverse,
    ) = chain_back_rest(
        core_reversed,
        readout_reverse,
        intake_reverse,
        values_reversed,
        step_reverse,
        state_reverse,
        later_reverse,
        decay_reverse,
        saved_reverse,
        readout_grad_reverse,
        sum_grad_reverse,
    )
    values_grad = (
        values_grad_forward
        + jnp.flip(values_grad_reverse, 1)
        + skip[None, None, :, None] * core_grad.astype(jnp.float32)
    )
    step_total_forward = step_grad_forward - rate[None, :, None] * log_grad_forward
    step_total_reverse = jnp.flip(step_grad_reverse - rate[None, :, None] * log_grad_reverse, 2)
    decay_log_grad = jnp.sum(log_grad_forward * log_forward, axis=(0, 2)) + jnp.sum(
        log_grad_reverse * log_reverse, axis=(0, 2)
    )
    step_total = jnp.stack(
        [
            jnp.transpose(step_total_forward, (0, 2, 1)),
            jnp.transpose(step_total_reverse, (0, 2, 1)),
        ],
        axis=3,
    )
    raw_grad = step_total * jax.nn.sigmoid(step_raw + bias_here)
    step_bias_grad = jnp.transpose(jnp.sum(raw_grad, axis=(0, 1)))
    state_grads = jnp.concatenate(
        [
            intake_grad_forward,
            readout_grad_forward,
            jnp.flip(intake_grad_reverse, 1),
            jnp.flip(readout_grad_reverse, 1),
        ],
        axis=2,
    )
    active_grad = jnp.concatenate(
        [values_grad.reshape(sequences, block_size, value_width), state_grads], axis=2
    )
    pre_grad = active_grad * active_sigma * (1.0 + pre_active * (1.0 - active_sigma))
    following = from_behind(pre_grad[:, :edge], "seq", -1)
    grad_extended = jnp.concatenate([pre_grad, following], axis=1)
    conv_input_grad = jnp.zeros((sequences, block_size, channels), jnp.float32)
    tap_grads = []
    for lag in range(reach):
        conv_input_grad = (
            conv_input_grad
            + taps[:, lag]
            * grad_extended[:, lag : lag + block_size]
            * lag_masks[:, lag : lag + block_size, lag, None]
        )
        tap_grads.append(
            jnp.sum(
                pre_grad
                * extended[:, edge - lag : edge - lag + block_size]
                * lag_masks[:, :block_size, lag, None],
                axis=(0, 1),
            )
        )
    tap_grads.append(jnp.sum(pre_grad, axis=(0, 1)))
    taps_grad = jnp.stack(tap_grads, axis=1)
    value_conv_grad = jnp.transpose(
        taps_grad[:value_width].reshape(heads_here, HEADDIM, reach + 1), (1, 0, 2)
    )
    state_conv_grad = taps_grad[value_width:]
    proj_grad = jnp.concatenate(
        [
            gate_grad,
            conv_input_grad[..., :value_width].reshape(sequences, block_size, heads_here, HEADDIM),
            raw_grad,
        ],
        axis=3,
    ).astype(jnp.bfloat16)
    state_proj_grad = conv_input_grad[..., value_width:].astype(jnp.bfloat16)
    normed_part = jnp.einsum(
        "mthk,dhk->mtd", proj_grad, in_weights, preferred_element_type=jnp.float32
    )
    normed_part = normed_part + jnp.einsum(
        "mtn,dn->mtd", state_proj_grad, state_weights, preferred_element_type=jnp.float32
    )
    normed_grad = lax.psum(normed_part, "head")
    in_weight_grad = jnp.einsum(
        "mtd,mthk->dhk", normed, proj_grad, preferred_element_type=jnp.float32
    )
    state_weight_grad = jnp.einsum(
        "mtd,mtn->dn", normed, state_proj_grad, preferred_element_type=jnp.float32
    )
    norm_gain_grad = jnp.sum(normed_grad * unit, axis=(0, 1))
    unit_grad = normed_grad * norm_wide
    input_gradient = out_cotangent + in_scale * (
        unit_grad - unit * jnp.mean(unit_grad * unit, axis=2, keepdims=True)
    )
    in_weight_out, out_weight_out, value_conv_out, norm_gain_out, gate_gain_out = (
        lax.psum_scatter(in_weight_grad, "seq", scatter_dimension=0, tiled=True),
        lax.psum_scatter(out_weight_grad, "seq", scatter_dimension=0, tiled=True),
        lax.psum_scatter(value_conv_grad, "seq", scatter_dimension=0, tiled=True),
        lax.psum_scatter(norm_gain_grad, "seq", scatter_dimension=0, tiled=True),
        lax.psum_scatter(gate_gain_grad, "seq", scatter_dimension=0, tiled=True),
    )
    state_weight_out, state_conv_out = (
        lax.psum_scatter(state_weight_grad, ("seq", "head"), scatter_dimension=0, tiled=True),
        lax.psum_scatter(state_conv_grad, ("seq", "head"), scatter_dimension=0, tiled=True),
    )
    step_bias_out, decay_log_out, skip_out = lax.psum(
        (step_bias_grad, decay_log_grad, skip_grad), "seq"
    )
    return (
        output,
        input_gradient,
        in_weight_out,
        state_weight_out,
        state_conv_out,
        out_weight_out,
        value_conv_out,
        norm_gain_out,
        gate_gain_out,
        step_bias_out,
        decay_log_out,
        skip_out,
    )


LANES = 128
WIDE, LOW = jnp.float32, jnp.bfloat16
FAR = -1e30


def dot(left, right):
    return jnp.dot(left, right, preferred_element_type=WIDE)


def dot_nt(left, right):
    return lax.dot_general(left, right, (((1,), (1,)), ((), ())), preferred_element_type=WIDE)


def halves(value):
    high = value.astype(LOW)
    return jnp.concatenate([high, (value - high.astype(WIDE)).astype(LOW)], axis=1)


def iota(shape, axis):
    return lax.broadcasted_iota(jnp.int32, shape, axis)


def head_columns(heads):
    row = jnp.arange(2 * LANES)[:, None] % LANES
    head = jnp.arange(heads * HEADDIM)[None, :] // HEADDIM
    spread_both = [(row == 2 * head + d).astype(LOW) for d in range(2)]
    gather_both = [jnp.concatenate([s[:LANES].T, s[:LANES].T], axis=0) for s in spread_both]
    return spread_both, gather_both


def steps_of(raw, bias):
    shifted = raw + bias
    small = jnp.exp(-jnp.abs(shifted))
    exponent = jnp.exp(jnp.minimum(shifted, 0.0))
    step = jnp.where(
        shifted < -15.0, exponent, jnp.maximum(shifted, 0.0) + jnp.log1p(small)
    )
    sigma = exponent / (1.0 + small)
    ratio = jnp.where(shifted < -15.0, 1.0, sigma / step)
    return step, sigma, ratio


def odd_lanes(shape):
    return iota(shape, 1) % 2 == 1


def running_sums(value, flip):
    size = value.shape[0]
    row, col = iota((2 * size, size), 0), iota((2 * size, size), 1)
    keep = jnp.logical_or(
        jnp.logical_and(row < size, row >= col), jnp.logical_and(row >= size, row - size <= col)
    )
    keep = keep.astype(WIDE).astype(LOW)
    high = value.astype(LOW)
    rest = value - high.astype(WIDE)
    middle = rest.astype(LOW)
    last = (rest - middle.astype(WIDE)).astype(LOW)
    sums = dot(keep, high) + dot(keep, middle) + dot(keep, last)
    odd = odd_lanes(value.shape)
    if flip:
        return jnp.where(odd, sums[:size], sums[size:])
    return jnp.where(odd, sums[size:], sums[:size])


def start_masks(starts, block, blocks, shape):
    size = shape[0]
    start = starts[block]
    following = starts[jnp.minimum(block + 1, blocks - 1)]
    none = start >= size
    ended = jnp.logical_or(block == blocks - 1, following == 0)
    row, odd = iota(shape, 0), odd_lanes(shape)
    after = row >= start
    tail_forward = jnp.logical_or(after, none)
    tail_reverse = jnp.logical_or(jnp.logical_not(after), jnp.logical_or(none, start == 0))
    head_forward = jnp.logical_not(after)
    head_reverse = jnp.logical_and(jnp.logical_or(after, none), jnp.logical_not(ended))
    tail = jnp.where(odd, tail_reverse.astype(WIDE), tail_forward.astype(WIDE))
    head = jnp.where(odd, head_reverse.astype(WIDE), head_forward.astype(WIDE))
    whole_reverse = jnp.logical_and(jnp.logical_or(none, start == 0), jnp.logical_not(ended))
    whole = jnp.where(
        odd[:8],
        jnp.where(whole_reverse, 1.0, 0.0),
        jnp.where(none, 1.0, 0.0),
    )
    return tail, head, whole


def chain_last(cum):
    return jnp.where(odd_lanes((1, cum.shape[1])), cum[:1], cum[-1:])


def table_bias(starts, block, size):
    row, col = iota((size, size), 0), iota((size, size), 1)
    start = starts[block]
    same = (row >= start) == (col >= start)
    return jnp.where(jnp.logical_and(same, row != col), 0.0, FAR)


def lane_half(size, second):
    return ((iota((size, LANES), 1) >= HEADDIM) == second).astype(WIDE).astype(LOW)


def block_diagonal(pair):
    size = pair.shape[0]
    return jnp.concatenate([pair * lane_half(size, False), pair * lane_half(size, True)], axis=0)


def silu_slope(value, sigma):
    return sigma * (1.0 + value * (1.0 - sigma))


def below(value):
    return jnp.concatenate([jnp.zeros_like(value), value], axis=0)


def above(value):
    return jnp.concatenate([value, jnp.zeros_like(value)], axis=0)


def rows_sum(value):
    total = value[:8]
    for at in range(8, value.shape[0], 8):
        total = total + value[at : at + 8]
    return total


def in_order(starts, mine, other):
    first = starts[starts.shape[0] - 1] == 0
    return jnp.concatenate(
        [jnp.where(first, mine[...], other[...]), jnp.where(first, other[...], mine[...])], axis=0
    )


def keep_own(starts, value, keep, send):
    first = starts[starts.shape[0] - 1] == 0
    size = value.shape[0] // 2
    keep[...] = jnp.where(first, value[:size], value[size:]).astype(keep.dtype)
    send[...] = jnp.where(first, value[size:], value[:size]).astype(send.dtype)


def document_of(starts, pair, blocks, size, place):
    far = 4 * size
    first, second = starts[2 * pair], starts[2 * pair + 1]
    before = starts[jnp.maximum(2 * pair - 1, 0)]
    behind = starts[jnp.minimum(2 * pair + 2, blocks - 1)]
    first = jnp.where(first < size, first, far)
    second = jnp.where(second < size, second + size, far)
    behind = jnp.where(behind < size, behind + 2 * size, far)
    before = jnp.where(before < size, before - size, -far)
    number = (place >= first).astype(jnp.int32) + (place >= second).astype(jnp.int32)
    return number + (place >= behind).astype(jnp.int32) + (place >= before).astype(jnp.int32)


def skip_lanes(small, spread):
    parts = dot(small[:, small.shape[1] - LANES :].astype(LOW), spread[:LANES])
    return parts[6:7] + parts[7:8] + parts[8:9]


def step_rows(small, heads):
    part = small[:, small.shape[1] - LANES :]
    bias = part[0:1] + part[1:2] + part[2:3]
    rate = jnp.exp(part[3:4] + part[4:5] + part[5:6])
    return bias, jnp.where(iota((1, LANES), 1) < 2 * heads, rate, 0.0)


def shard_rows(starts, side, index, rows):
    chip, core = starts[starts.shape[0] - 2], starts[starts.shape[0] - 1]
    seq = 2 * jnp.bitwise_xor(chip, side) + (core if index == 0 else 1 - core)
    return pl.ds(pl.multiple_of(seq * rows, 32), rows)


def forward_kernel(
    starts, mine, other, pay, pay_x, pay_y, pay_far, pay_far_other, spread_f, spread_r,
    normed_o, conv_o, pre_o, act_o, out_f_o, inner_r_o, cum_o, raw_o, state_f_o, local_r_o,
    decay_f_o, decay_r_o, weights_o, small_o,
    tail_s, state_s,
):
    pair, pairs = pl.program_id(0), pl.num_programs(0)
    blocks = 2 * pairs
    size = mine.shape[0]
    inner = out_f_o.shape[1]
    channels = inner + 4 * STATE
    reach = 4

    @pl.when(pair == 0)
    def _():
        tail_s[...] = jnp.zeros_like(tail_s)
        state_s[...] = jnp.zeros_like(state_s)
        rows = pay.shape[1] - 16
        shards = [pay.at[0], pay.at[1], pay_x.at[0], pay_x.at[1], pay_y.at[0], pay_y.at[1]]
        shards = shards + [pay_far, pay_far_other]
        total = jnp.zeros(small_o.shape, WIDE)
        for i, shard in enumerate(shards):
            weights_o[shard_rows(starts, i // 2, i % 2, rows), :] = shard[:rows, :]
            total = total + shard[rows:, :].astype(WIDE)
        small_o[...] = total

    small = small_o[...]
    bias_row, rate_row = step_rows(small, inner // HEADDIM)
    norm_row = jnp.concatenate([small[i : i + 1, inner:channels] for i in (5, 6, 7)], axis=1)
    taps = small[:8, :channels]
    wide = in_order(starts, mine, other).astype(WIDE)
    scale = lax.rsqrt(jnp.mean(wide * wide, axis=1, keepdims=True) + 1e-05)
    normed = (wide * scale * norm_row).astype(LOW)
    normed_o[...] = normed
    raw = dot(normed, weights_o[:, channels:])
    raw_o[...] = raw
    row = iota((2 * size, LANES), 0)
    number = document_of(starts, pair, blocks, size, row)
    masks = [
        (number == document_of(starts, pair, blocks, size, row - lag)).astype(WIDE)
        for lag in range(1, reach)
    ]
    for chunk in range(0, channels, 2 * LANES):
        both = dot(normed, weights_o[:, chunk : chunk + 2 * LANES]).astype(LOW)
        conv_o[:, chunk : chunk + 2 * LANES] = both
        for at in (0, LANES):
            lanes = slice(chunk + at, chunk + at + LANES)
            here = both[:, at : at + LANES].astype(WIDE)
            extended = jnp.concatenate([tail_s[:, lanes], here], axis=0)
            tail_s[:, lanes] = here[2 * size - 8 :]
            pre = taps[4:5, lanes] + taps[0:1, lanes] * here
            for lag in range(1, reach):
                shifted = pltpu.roll(extended, lag, 0)[8:]
                pre = pre + taps[lag : lag + 1, lanes] * shifted * masks[lag - 1]
            pre_o[:, lanes] = pre
            act_o[:, lanes] = (pre * jax.nn.sigmoid(pre)).astype(LOW)

    step, _, _ = steps_of(raw, bias_row)
    log_decay = -step * rate_row
    log_step = jnp.log(step)
    row, col = iota((size, size), 0), iota((size, size), 1)
    lower = row > col
    lower_low = lower.astype(WIDE).astype(LOW)
    upper_low = (row < col).astype(WIDE).astype(LOW)
    for sub in range(2):
        block = 2 * pair + sub
        rows = slice(sub * size, (sub + 1) * size)
        cum = running_sums(log_decay[rows], False)
        cum_o[rows] = cum
        late = cum - log_step[rows]
        late_rows = late.T
        tail_mask, head_mask, whole = start_masks(starts, block, blocks, cum.shape)
        tail = halves(jnp.exp(chain_last(cum) - late) * tail_mask)
        head = halves(jnp.exp(cum) * head_mask)
        decay = halves(jnp.exp(jnp.broadcast_to(chain_last(cum), (8, LANES))) * whole)
        decay_f = dot(decay, spread_f[...])
        decay_f_o[8 * sub : 8 * sub + 8] = decay_f
        decay_r_o[8 * sub : 8 * sub + 8] = dot(decay, spread_r[...])

        state_act = act_o[rows, inner:]
        turned = state_act.astype(WIDE).T.astype(LOW)
        forward_act, reverse_act = state_act[:, : 2 * STATE], state_act[:, 2 * STATE :]
        scores = jnp.where(
            lower,
            dot(forward_act, below(turned[:STATE])),
            dot(reverse_act, below(turned[2 * STATE : 3 * STATE])),
        )
        bias = table_bias(starts, block, size)
        for heads in range(inner // LANES):
            lanes = slice(heads * LANES, (heads + 1) * LANES)
            lefts, rights = [], []
            for head_at in (2 * heads, 2 * heads + 1):
                c = 2 * head_at
                gap = jnp.where(
                    lower,
                    cum[:, c : c + 1] - late_rows[c : c + 1],
                    cum[:, c + 1 : c + 2] - late_rows[c + 1 : c + 2],
                )
                mix = (scores * jnp.exp(gap + bias)).astype(LOW)
                lefts.append(mix * lower_low)
                rights.append(mix * upper_low)
            both = jnp.concatenate(
                [jnp.concatenate(lefts, axis=1), jnp.concatenate(rights, axis=1)], axis=0
            )
            result = dot(both, block_diagonal(act_o[rows, lanes]))
            out_f_o[rows, lanes] = result[:size]
            inner_r_o[rows, lanes] = result[size:]

        values_wide = act_o[rows, :inner].astype(WIDE)
        states = slice(sub * STATE, (sub + 1) * STATE)
        state = state_s[...]
        state_f_o[states] = state
        carried = dot(forward_act, below(state.astype(LOW)))
        out_f_o[rows] += dot(head, spread_f[...]) * carried
        local_f = dot(turned[:STATE], (dot(tail, spread_f[...]) * values_wide).astype(LOW))
        state_s[...] = decay_f[:1] * state + local_f
        local_r_o[states] = dot(
            turned[2 * STATE : 3 * STATE], (dot(tail, spread_r[...]) * values_wide).astype(LOW)
        )


def output_kernel(
    starts, normed, act, out_f, inner_r, cum, local_r, decay_r, mine, other, pay, small, spread_r,
    out_r_o, state_r_o, gate_o, unscaled_o, unscaled_grad_o, sums_o, keep_o, send_o, gate_w,
    state_s, out_w,
):
    step, pairs = pl.program_id(0), pl.num_programs(0)
    pair, blocks = pairs - 1 - step, 2 * pairs
    size, inner = mine.shape[0], out_f.shape[1]

    @pl.when(step == 0)
    def _():
        state_s[...] = jnp.zeros_like(state_s)
        seqs, planes, rows, cols = pay.shape
        groups, half = planes // 2, cols // 2
        core = starts[starts.shape[0] - 1]
        for seq in range(seqs):
            for group in range(groups):
                part = pay[seq, core * groups + group]
                at, lanes = slice(seq * rows, (seq + 1) * rows), slice(group * half, (group + 1) * half)
                gate_w[at, lanes] = part[:, :half]
                out_w[at, lanes] = part[:, half:]

    gate = dot(normed[...], gate_w[...])
    gate_o[...] = gate
    unscaled_grad = dot(in_order(starts, mine, other), out_w[...])
    unscaled_grad_o[...] = unscaled_grad
    for sub in (1, 0):
        rows, states = slice(sub * size, (sub + 1) * size), slice(sub * STATE, (sub + 1) * STATE)
        _, head_mask, _ = start_masks(starts, 2 * pair + sub, blocks, (size, LANES))
        head = halves(jnp.exp(cum[rows]) * head_mask)
        state = state_s[...]
        state_r_o[states] = state
        reverse_act = act[rows, inner + 2 * STATE :]
        carried = dot(reverse_act, below(state.astype(LOW)))
        out_r_o[rows] = inner_r[rows] + dot(head, spread_r[...]) * carried
        state_s[...] = decay_r[8 * sub : 8 * sub + 1] * state + local_r[states]
    skip_row, gain_row = skip_lanes(small[...], spread_r), small[5:6, :inner]
    core = out_f[...] + out_r_o[...] + skip_row * act[:, :inner].astype(WIDE)
    gated = core * gate * jax.nn.sigmoid(gate)
    unscaled = (gated * gain_row).astype(LOW)
    unscaled_o[...] = unscaled
    squares = jnp.sum(gated * gated, axis=1, keepdims=True)
    products = jnp.sum(unscaled_grad * unscaled.astype(WIDE), axis=1, keepdims=True)
    both = jnp.where(iota((2 * size, LANES), 1) == 0, squares, products)
    for sub in range(2):
        rows = slice(sub * size, (sub + 1) * size)
        sums_o[:, rows] = both[rows].T[:8]
    keep_own(starts, dot_nt(unscaled, out_w[...]), keep_o, send_o)


def gate_back_kernel(
    starts, own_sums, other_sums, mine, other, out_f, out_r, act, gate, unscaled_grad, cum, decay_r,
    small, spread_f, spread_r, gather_f, gather_r,
    total_o, core_grad_o, gate_grad_o, row_sums_o, back_f_o, later_r_o, gain_grad_o, skip_grad_o,
    later_s,
):
    pair, pairs = pl.program_id(0), pl.num_programs(0)
    blocks = 2 * pairs
    size, inner = mine.shape[0], out_f.shape[1]
    inner_width = HEADS * HEADDIM

    @pl.when(pair == 0)
    def _():
        later_s[...] = jnp.zeros_like(later_s)
        gain_grad_o[...] = jnp.zeros_like(gain_grad_o)
        skip_grad_o[...] = jnp.zeros_like(skip_grad_o)

    sums = own_sums[...] + other_sums[...]
    empty = jnp.zeros((size - 8, size), WIDE)
    sums = jnp.concatenate(
        [
            jnp.concatenate([sums[:, at : at + size], empty], axis=0).T
            for at in (0, size)
        ],
        axis=0,
    )
    skip_row, gain_row = skip_lanes(small[...], spread_f), small[5:6, :inner]
    scale = lax.rsqrt(sums[:, 0:1] / inner_width + 1e-05)
    square_grad = sums[:, 1:2] * scale * scale * scale / inner_width
    total_o[...] = (scale * in_order(starts, mine, other).astype(WIDE)).astype(LOW)
    values = act[:, :inner].astype(WIDE)
    core = out_f[...] + out_r[...] + skip_row * values
    gate_value = gate[...]
    sigma = jax.nn.sigmoid(gate_value)
    slope = gate_value * sigma
    gated = core * slope
    unscaled = scale * unscaled_grad[...]
    gain_grad_o[...] += rows_sum(unscaled * gated)
    gated_grad = unscaled * gain_row - gated * square_grad
    core_grad = (gated_grad * slope).astype(LOW)
    core_grad_o[...] = core_grad
    gate_grad_o[...] = (gated_grad * core * silu_slope(gate_value, sigma)).astype(LOW)
    grad_wide = core_grad.astype(WIDE)
    skip_grad_o[...] += rows_sum(grad_wide * values)
    row_sums_o[...] = dot(halves(grad_wide * out_f[...]), gather_f[...]) + dot(
        halves(grad_wide * out_r[...]), gather_r[...]
    )
    for sub in range(2):
        rows, states = slice(sub * size, (sub + 1) * size), slice(sub * STATE, (sub + 1) * STATE)
        _, head_mask, _ = start_masks(starts, 2 * pair + sub, blocks, (size, LANES))
        head = halves(jnp.exp(cum[rows]) * head_mask)
        turned = act[rows, inner:].astype(WIDE).T.astype(LOW)
        grad_here = core_grad_o[rows].astype(WIDE)
        back_f_o[states] = dot(
            turned[STATE : 2 * STATE], (dot(head, spread_f[...]) * grad_here).astype(LOW)
        )
        back_r = dot(turned[3 * STATE :], (dot(head, spread_r[...]) * grad_here).astype(LOW))
        later = later_s[...]
        later_r_o[states] = later
        later_s[...] = decay_r[8 * sub : 8 * sub + 1] * later + back_r


def chain_back_kernel(
    starts, core_grad, gate_grad, act, conv, pre, cum, raw, row_sums, state_f, state_f_next,
    state_r, state_r_last, back_f, later_r, decay_f, gate_w, weights, small, spread_f, spread_r,
    gather_f, gather_r,
    proj_o, keep_o, send_o, taps_grad_o, scalar_o,
    later_s, next_s, values_f_s, values_r_s, active_s, raw_grad_s,
):
    step_at, pairs = pl.program_id(0), pl.num_programs(0)
    pair, blocks = pairs - 1 - step_at, 2 * pairs
    size, inner = core_grad.shape[0] // 2, core_grad.shape[1]
    channels = inner + 4 * STATE
    reach = 4

    @pl.when(step_at == 0)
    def _():
        later_s[...] = jnp.zeros_like(later_s)
        next_s[...] = jnp.zeros_like(next_s)
        taps_grad_o[...] = jnp.zeros_like(taps_grad_o)
        scalar_o[...] = jnp.zeros_like(scalar_o)

    small_here = small[...]
    bias_row, rate_row = step_rows(small_here, inner // HEADDIM)
    skip_row, taps = skip_lanes(small_here, spread_f), small_here[:8, :channels]
    step_all, sigma_all, ratio_all = steps_of(raw[...], bias_row)
    log_step = jnp.log(step_all)
    row, col = iota((size, size), 0), iota((size, size), 1)
    ahead = col > row
    ahead_low = ahead.astype(WIDE).astype(LOW)
    behind_low = (col < row).astype(WIDE).astype(LOW)
    for sub in (1, 0):
        block = 2 * pair + sub
        rows, states = slice(sub * size, (sub + 1) * size), slice(sub * STATE, (sub + 1) * STATE)
        step, sigma, ratio = step_all[rows], sigma_all[rows], ratio_all[rows]
        cum_here = cum[rows]
        late = cum_here - log_step[rows]
        cum_rows = cum_here.T
        tail_mask, head_mask, _ = start_masks(starts, block, blocks, cum_here.shape)
        tail = halves(jnp.exp(chain_last(cum_here) - late) * tail_mask)
        head = halves(jnp.exp(cum_here) * head_mask)
        state_act = act[rows, inner:]
        turned = state_act.astype(WIDE).T.astype(LOW)
        forward_act, reverse_act = state_act[:, : 2 * STATE], state_act[:, 2 * STATE :]
        scores = jnp.where(
            ahead,
            dot(forward_act, above(turned[STATE : 2 * STATE])),
            dot(reverse_act, above(turned[3 * STATE :])),
        )
        bias = table_bias(starts, block, size)
        scores_grad = jnp.zeros((size, size), WIDE)
        for heads in range(inner // LANES):
            lanes = slice(heads * LANES, (heads + 1) * LANES)
            grad_blocks = block_diagonal(core_grad[rows, lanes])
            mix_grad = dot_nt(act[rows, lanes], grad_blocks)
            lefts, rights = [], []
            for at in range(2):
                c = 2 * (2 * heads + at)
                gap = jnp.where(
                    ahead,
                    cum_rows[c : c + 1] - late[:, c : c + 1],
                    cum_rows[c + 1 : c + 2] - late[:, c + 1 : c + 2],
                )
                table = jnp.exp(gap + bias)
                mix = (scores * table).astype(LOW)
                lefts.append(mix * ahead_low)
                rights.append(mix * behind_low)
                scores_grad = scores_grad + mix_grad[:, at * size : (at + 1) * size] * table
            both = jnp.concatenate(
                [jnp.concatenate(lefts, axis=1), jnp.concatenate(rights, axis=1)], axis=0
            )
            result = dot(both, grad_blocks)
            values_f_s[rows, lanes] = result[:size]
            values_r_s[rows, lanes] = result[size:]

        grad_wide = core_grad[rows].astype(WIDE)
        values = act[rows, :inner].astype(WIDE)
        later_f, later_r_here = later_s[...], later_r[states]
        later_f_low, later_r_low = later_f.astype(LOW), later_r_here.astype(LOW)
        tail_f, tail_r = dot(tail, spread_f[...]), dot(tail, spread_r[...])
        values_f = values_f_s[rows] + tail_f * dot(forward_act, above(later_f_low))
        values_r = values_r_s[rows] + tail_r * dot(reverse_act, above(later_r_low))
        col_sums = dot(halves(values * values_f), gather_f[...]) + dot(
            halves(values * values_r), gather_r[...]
        )
        after_f = state_f_next[...] if sub else state_f[STATE:]
        after_r = state_r[:STATE] if sub else state_r_last[...]
        end_f = dot(halves(rows_sum(later_f * after_f)), gather_f[...])
        end_r = dot(halves(rows_sum(later_r_here * after_r)), gather_r[...])
        end_f = jnp.sum(end_f, axis=0, keepdims=True)
        end_r = jnp.sum(end_r, axis=0, keepdims=True)
        at_row = iota(cum_here.shape, 0)
        cum_grad = row_sums[rows] - col_sums
        cum_grad = cum_grad + jnp.where(at_row == size - 1, end_f, 0.0)
        cum_grad = cum_grad + jnp.where(at_row == 0, end_r, 0.0)
        log_grad = running_sums(cum_grad, True)
        raw_grad = col_sums * ratio - rate_row * log_grad * sigma
        raw_grad_s[rows] = raw_grad
        scalar_o[0:8] += rows_sum(raw_grad)
        scalar_o[8:16] += rows_sum(log_grad * (-step * rate_row))

        mid = scores_grad.T
        pieces = []
        for act_pair, spread_head, state, later_low, forward_side in (
            (forward_act, spread_f, state_f, later_f_low, True),
            (reverse_act, spread_r, state_r, later_r_low, False),
        ):
            tail_here = tail_f if forward_side else tail_r
            scaled = (tail_here * values).astype(LOW)
            carried_grad = (dot(head, spread_head[...]) * grad_wide).astype(LOW)
            own = ahead_low if forward_side else behind_low
            mirrored = behind_low if forward_side else ahead_low
            sides = jnp.concatenate(
                [scores_grad.astype(LOW) * own, mid.astype(LOW) * mirrored], axis=1
            )
            swapped = pltpu.roll(act_pair.astype(WIDE), STATE, 1).astype(LOW)
            pieces.append(
                dot_nt(scaled, above(later_low))
                + dot_nt(carried_grad, below(state[states].astype(LOW)))
                + dot(sides, block_diagonal(swapped))
            )
        active_s[rows, :inner] = values_f + values_r + skip_row * grad_wide
        active_s[rows, inner : inner + LANES] = pieces[0]
        active_s[rows, inner + LANES :] = pieces[1]
        later_s[...] = decay_f[8 * sub : 8 * sub + 1] * later_f + back_f[states]

    row = iota((2 * size, LANES), 0)
    number = document_of(starts, pair, blocks, size, row)
    masks = [
        (number == document_of(starts, pair, blocks, size, row + lag)).astype(WIDE)
        for lag in range(1, reach)
    ]
    for at in range(0, channels, LANES):
        lanes = slice(at, at + LANES)
        pre_here = pre[:, lanes]
        grad = active_s[:, lanes] * silu_slope(pre_here, jax.nn.sigmoid(pre_here))
        extended = jnp.concatenate([grad, next_s[:, lanes]], axis=0)
        next_s[:, lanes] = grad[:8]
        source = conv[:, lanes].astype(WIDE)
        result = taps[0:1, lanes] * grad
        taps_grad_o[0:8, lanes] += rows_sum(grad * source)
        taps_grad_o[32:40, lanes] += rows_sum(grad)
        for lag in range(1, reach):
            shifted = pltpu.roll(extended, 2 * size + 8 - lag, 0)[: 2 * size] * masks[lag - 1]
            result = result + taps[lag : lag + 1, lanes] * shifted
            taps_grad_o[8 * lag : 8 * lag + 8, lanes] += rows_sum(shifted * source)
        proj_o[:, lanes] = result.astype(LOW)
    proj_o[:, channels:] = raw_grad_s[...].astype(LOW)
    normed = dot_nt(gate_grad[...], gate_w[...]) + dot_nt(proj_o[...], weights[...])
    keep_own(starts, normed, keep_o, send_o)


def by_pair(kernel, blocks, reverse, ins, outs, scratch, name, work):
    steps = blocks // 2

    def at(i):
        return steps - 1 - i if reverse else i

    def spec(shape, kind):
        part = (shape[0] // steps,) + shape[1:]
        single = (shape[0] // blocks,) + shape[1:]
        if kind == "scalar":
            return pl.BlockSpec(memory_space=pltpu.SMEM)
        if kind == "rows":
            return pl.BlockSpec(part, lambda i: (at(i), 0))
        if kind == "half":
            return pl.BlockSpec((None,) + shape[1:], lambda i: (at(i), 0, 0))
        if kind == "lanes":
            return pl.BlockSpec((shape[0], shape[1] // steps), lambda i: (0, at(i)))
        if kind == "next":
            return pl.BlockSpec(single, lambda i: (jnp.minimum(2 * at(i) + 2, blocks - 1), 0))
        if kind == "last":
            return pl.BlockSpec(single, lambda i: (jnp.maximum(2 * at(i) - 1, 0), 0))
        return pl.BlockSpec(shape, lambda i: (0,) * len(shape))

    return pl.pallas_call(
        kernel,
        grid=(steps,),
        in_specs=[spec(value.shape, kind) for value, kind in ins],
        out_specs=[spec(value.shape, kind) for value, kind in outs],
        out_shape=[value for value, _ in outs],
        scratch_shapes=[pltpu.VMEM(shape, dtype) for shape, dtype in scratch],
        compiler_params=pltpu.CompilerParams(
            dimension_semantics=("arbitrary",), vmem_limit_bytes=60 * 1024 * 1024
        ),
        cost_estimate=pl.CostEstimate(
            flops=work,
            transcendentals=0,
            bytes_accessed=sum(v.size * v.dtype.itemsize for v, _ in ins + outs),
        ),
        name=name,
    )(*[value for value, _ in ins])


def swap_core(value):
    return lax.ppermute(value, "core", [(0, 1), (1, 0)])


def swap_chip(value, side):
    return lax.ppermute(value, "chip", [(i, i ^ side) for i in range(4)])


def spread_to(value, axis):
    count = lax.axis_size(axis)
    return lax.all_to_all(jnp.broadcast_to(value[None], (count,) + value.shape), axis, 0, 0)


def shifted_sum(pieces, axis):
    count, mine = lax.axis_size(axis), lax.axis_index(axis)
    total = lax.dynamic_index_in_dim(pieces, mine, 0, keepdims=False).astype(WIDE)
    for k in range(1, count):
        piece = lax.dynamic_index_in_dim(pieces, (mine + k) % count, 0, keepdims=False)
        moved = lax.ppermute(piece, axis, [(i, (i + k) % count) for i in range(count)])
        total = total + moved.astype(WIDE)
    return total


def after(value, *others):
    return lax.optimization_barrier((value,) + others)[0]


def three_parts(value):
    high = lax.reduce_precision(value, 8, 7)
    middle = lax.reduce_precision(value - high, 8, 7)
    return jnp.stack([high, middle, lax.reduce_precision(value - high - middle, 8, 7)])


def placed(value, width, at):
    shape = value.shape[:-1] + (width,)
    return lax.dynamic_update_slice_in_dim(jnp.zeros(shape, value.dtype), value, at, value.ndim - 1)


def chip_plan(
    tokens,
    starts,
    in_weight,
    state_weight,
    state_conv,
    out_weight,
    value_conv,
    norm_gain,
    gate_gain,
    step_bias,
    decay_log,
    skip,
    out_cotangent,
):
    low, wide = LOW, WIDE
    sequences, block_size, width = tokens.shape
    chips, planes = lax.axis_size("chip"), lax.axis_size("head")
    chip, core, plane = lax.axis_index("chip"), lax.axis_index("core"), lax.axis_index("head")
    blocks = starts.shape[1]
    length = blocks * block_size
    rows, group = in_weight.shape[:2]
    groups = planes // 2
    heads_here = group * groups
    inner_here, group_inner = heads_here * HEADDIM, group * HEADDIM
    part, reach = value_conv.shape[0], state_conv.shape[1] - 1
    state_part = state_conv.shape[0]
    channels_state = state_weight.shape[1]
    channels = inner_here + channels_state
    seq = 2 * chip + core
    first = core == 0

    def own_plane(value):
        return lax.dynamic_slice_in_dim(value, plane * chips, chips, 0)

    tokens_plane = own_plane(tokens)
    tokens_plane, in_weight, out_weight = lax.optimization_barrier(
        (tokens_plane, in_weight, out_weight)
    )
    tokens_mine = lax.all_to_all(tokens_plane, "chip", 0, 0)

    step_at = (plane % groups) * 2 * group
    pair_weights = placed(in_weight[:, :, 2 * HEADDIM :].reshape(rows, 2 * group), LANES, step_at)
    tap_lanes = placed(value_conv.transpose(2, 1, 0), HEADDIM, part * seq).reshape(reach + 1, -1)
    gain_lanes = placed(gate_gain.transpose(1, 0), HEADDIM, part * seq).reshape(1, -1)
    extra_value = jnp.concatenate([tap_lanes, gain_lanes], axis=0)
    scalars = jnp.stack(
        [step_bias.T.reshape(-1), jnp.repeat(decay_log, 2), jnp.repeat(skip, 2)]
    )
    scalars = jnp.swapaxes(three_parts(jnp.where(seq == 0, scalars, 0.0)), 0, 1)
    extra_step = placed(scalars.reshape(9, 2 * group).astype(low), LANES, step_at)
    slab = jnp.concatenate(
        [
            jnp.concatenate(
                [in_weight[:, :, HEADDIM : 2 * HEADDIM].reshape(rows, group_inner), pair_weights],
                axis=1,
            ),
            jnp.concatenate(
                [
                    jnp.pad(extra_value, ((0, 16 - extra_value.shape[0]), (0, 0))),
                    jnp.pad(extra_step, ((0, 16 - extra_step.shape[0]), (0, 0))),
                ],
                axis=1,
            ),
        ],
        axis=0,
    )
    extra_state = jnp.concatenate(
        [
            placed(state_conv.T, channels_state, state_part * seq),
            placed(norm_gain, width, rows * seq).reshape(-1, channels_state),
        ],
        axis=0,
    )
    state_slab = jnp.concatenate(
        [state_weight, jnp.pad(extra_state, ((0, 16 - extra_state.shape[0]), (0, 0)))], axis=0
    )
    shifted = [slab] + [
        lax.ppermute(slab, "head", [(i, (i + k) % planes) for i in range(planes)])
        for k in range(1, planes)
    ]
    shifted = jnp.stack(shifted)

    def for_core(which):
        picked = [
            lax.dynamic_index_in_dim(shifted, (plane - which * groups - i) % planes, 0, False)
            for i in range(groups)
        ]
        steps = picked[0][:, group_inner:]
        for i in range(1, groups):
            steps = steps + picked[i][:, group_inner:]
        return jnp.concatenate(
            [picked[i][:, :group_inner] for i in range(groups)] + [state_slab, steps], axis=1
        )

    pay = jnp.stack([for_core(core), swap_core(for_core(1 - core))])
    pay, tokens_mine = lax.optimization_barrier((pay, tokens_mine))
    tokens_other = swap_core(tokens_mine)
    pay_x, pay_y = swap_chip(pay, 1), swap_chip(pay, 2)
    pays = (pay, pay_x, pay_y, swap_chip(pay_x[0], 2), swap_chip(pay_y[1], 1))

    late_slab = jnp.concatenate(
        [
            in_weight[:, :, :HEADDIM].reshape(rows, group_inner),
            out_weight.reshape(rows, group_inner),
        ],
        axis=1,
    )
    pay_late = lax.all_gather(late_slab, ("chip", "core", "head")).reshape(2 * chips, planes, rows, -1)
    cotangent_low = own_plane(out_cotangent).astype(low)
    cotangent_low, *pays = lax.optimization_barrier((cotangent_low, *pays))
    cotangent_mine = lax.all_to_all(cotangent_low, "chip", 0, 0)
    starts_row = lax.dynamic_index_in_dim(starts, plane * chips + chip, 0, keepdims=False)
    starts_row = jnp.concatenate([starts_row, jnp.stack([chip, core]).astype(starts_row.dtype)])
    (spread_f, spread_r), (gather_f, gather_r) = head_columns(heads_here)

    def shape(rows_, cols, dtype):
        return jax.ShapeDtypeStruct((rows_, cols), dtype)

    half_low = jax.ShapeDtypeStruct((chips, block_size, width), low)
    half_wide = jax.ShapeDtypeStruct((chips, block_size, width), wide)
    states = blocks * STATE
    lane_cols = channels + LANES
    (
        normed, conv_input, pre_active, act, out_f, inner_r, cum, step_raw, state_f, local_r,
        decay_f, decay_r, weights, small,
    ) = by_pair(
        forward_kernel, blocks, False,
        [
            (starts_row, "scalar"), (tokens_mine, "half"), (tokens_other, "half"),
            *((value, "whole") for value in pays),
            (spread_f, "whole"), (spread_r, "whole"),
        ],
        [
            (shape(length, width, low), "rows"), (shape(length, channels, low), "rows"),
            (shape(length, channels, wide), "rows"), (shape(length, channels, low), "rows"),
            (shape(length, inner_here, wide), "rows"), (shape(length, inner_here, wide), "rows"),
            (shape(length, LANES, wide), "rows"), (shape(length, LANES, wide), "rows"),
            (shape(states, inner_here, wide), "rows"), (shape(states, inner_here, wide), "rows"),
            (shape(8 * blocks, inner_here, wide), "rows"), (shape(8 * blocks, inner_here, wide), "rows"),
            (shape(width, lane_cols, low), "whole"), (shape(16, lane_cols, wide), "whole"),
        ],
        [((8, channels), wide), ((STATE, inner_here), wide)],
        "forward", 20_000_000_000,
    )
    cotangent_mine, normed = lax.optimization_barrier((cotangent_mine, normed))
    cotangent_other = swap_core(cotangent_mine)
    (
        out_r, state_r, gate, unscaled, unscaled_grad, own_sums, keep, send, gate_w,
    ) = by_pair(
        output_kernel, blocks, True,
        [
            (starts_row, "scalar"), (normed, "rows"), (act, "rows"), (out_f, "rows"), (inner_r, "rows"),
            (cum, "rows"), (local_r, "rows"), (decay_r, "rows"), (cotangent_mine, "half"),
            (cotangent_other, "half"), (pay_late, "whole"), (small, "whole"), (spread_r, "whole"),
        ],
        [
            (shape(length, inner_here, wide), "rows"), (shape(states, inner_here, wide), "rows"),
            (shape(length, inner_here, wide), "rows"), (shape(length, inner_here, low), "rows"),
            (shape(length, inner_here, wide), "rows"), (shape(8, length, wide), "lanes"),
            (half_low, "half"), (half_low, "half"), (shape(width, inner_here, low), "whole"),
        ],
        [((STATE, inner_here), wide), ((width, inner_here), low)],
        "outputs", 12_000_000_000,
    )
    other_sums = swap_core(own_sums)

    squares = (own_sums[0] + other_sums[0]).reshape(chips, 2, block_size)
    squares = lax.dynamic_index_in_dim(squares, core, 1, keepdims=False)
    gate_scale = lax.rsqrt(squares / (HEADS * HEADDIM) + 1e-05)
    out_delta = gate_scale[..., None] * (keep.astype(wide) + swap_core(send).astype(wide))
    out_delta, gate = lax.optimization_barrier((out_delta.astype(low), gate))
    out_moved = lax.all_to_all(out_delta, "chip", 0, 0)

    (total_grad, core_grad, gate_grad, row_sums, back_f, later_r, gain_grad, skip_grad) = by_pair(
        gate_back_kernel, blocks, False,
        [
            (starts_row, "scalar"), (own_sums, "lanes"), (other_sums, "lanes"), (cotangent_mine, "half"),
            (cotangent_other, "half"), (out_f, "rows"), (out_r, "rows"),
            (act, "rows"), (gate, "rows"), (unscaled_grad, "rows"), (cum, "rows"), (decay_r, "rows"),
            (small, "whole"), (spread_f, "whole"), (spread_r, "whole"),
            (gather_f, "whole"), (gather_r, "whole"),
        ],
        [
            (shape(length, width, low), "rows"), (shape(length, inner_here, low), "rows"),
            (shape(length, inner_here, low), "rows"), (shape(length, LANES, wide), "rows"),
            (shape(states, inner_here, wide), "rows"), (shape(states, inner_here, wide), "rows"),
            (shape(8, inner_here, wide), "whole"), (shape(8, inner_here, wide), "whole"),
        ],
        [((STATE, inner_here), wide)],
        "gate_back", 12_000_000_000,
    )

    def weight_grad(left, right):
        result = lax.dot_general(left, right, (((0,), (0,)), ((), ())), preferred_element_type=wide)
        return result.astype(low)

    gate_grad, total_grad, out_moved = lax.optimization_barrier((gate_grad, total_grad, out_moved))
    out_delta = lax.all_gather(out_moved, "head").reshape(sequences, block_size, width)
    early_grad = jnp.concatenate(
        [weight_grad(normed, gate_grad), weight_grad(total_grad, unscaled)], axis=1
    ).reshape(chips, 2, rows, -1)
    early_grad, core_grad = lax.optimization_barrier((early_grad, core_grad))
    early_moved = lax.all_to_all(early_grad, "chip", 0, 0)
    rest_grad, keep, send, taps_grad, scalar_part = by_pair(
        chain_back_kernel, blocks, True,
        [
            (starts_row, "scalar"), (core_grad, "rows"), (gate_grad, "rows"), (act, "rows"),
            (conv_input, "rows"), (pre_active, "rows"), (cum, "rows"), (step_raw, "rows"),
            (row_sums, "rows"), (state_f, "rows"), (state_f, "next"), (state_r, "rows"),
            (state_r, "last"), (back_f, "rows"), (later_r, "rows"), (decay_f, "rows"),
            (gate_w, "whole"), (weights, "whole"), (small, "whole"), (spread_f, "whole"),
            (spread_r, "whole"), (gather_f, "whole"), (gather_r, "whole"),
        ],
        [
            (shape(length, lane_cols, low), "rows"), (half_wide, "half"), (half_low, "half"),
            (shape(40, channels, wide), "whole"), (shape(16, LANES, wide), "whole"),
        ],
        [
            ((STATE, inner_here), wide), ((8, channels), wide), ((2 * block_size, inner_here), wide),
            ((2 * block_size, inner_here), wide), ((2 * block_size, channels), wide),
            ((2 * block_size, LANES), wide),
        ],
        "chain_back", 10_000_000_000,
    )

    norm_row = small[5 : 5 + width // channels_state, inner_here:channels].reshape(width)
    tokens_wide = tokens_mine.astype(wide)
    in_scale = lax.rsqrt(jnp.mean(tokens_wide * tokens_wide, axis=2, keepdims=True) + 1e-05)
    unit = tokens_wide * in_scale
    normed_grad = keep + swap_core(send).astype(wide)
    unit_grad = normed_grad * norm_row
    delta = in_scale * (unit_grad - unit * jnp.mean(unit_grad * unit, axis=2, keepdims=True))
    (
        delta, early_moved, normed_late, rest_grad, taps_grad, scalar_part, normed_grad,
    ) = lax.optimization_barrier(
        (
            delta.astype(low), early_moved, normed, rest_grad, taps_grad, scalar_part, normed_grad,
        )
    )
    delta = lax.all_to_all(delta, "chip", 0, 0)
    gathered = lax.all_gather(delta, "head").reshape(sequences, block_size, width)
    def between_cores(moved):
        total = jnp.sum(moved.astype(wide), axis=0).astype(low)
        mine = lax.dynamic_index_in_dim(total, core, 0, keepdims=False)
        got = swap_core(lax.dynamic_index_in_dim(total, 1 - core, 0, keepdims=False))
        return [jnp.where(first, mine, got), jnp.where(first, got, mine)]

    def over_planes(pieces):
        return jnp.sum(lax.all_to_all(jnp.stack(pieces), "head", 0, 0).astype(wide), axis=0)

    def group_lanes(value, at, i):
        return value[:, at + i * group_inner : at + (i + 1) * group_inner]

    early_moved, out_delta = lax.optimization_barrier((early_moved, out_delta))
    early = between_cores(early_moved)
    early = jnp.stack(
        [
            jnp.concatenate([group_lanes(v, 0, i), group_lanes(v, inner_here, i)], axis=1)
            for v in early
            for i in range(groups)
        ]
    )
    early, normed_late, rest_grad = lax.optimization_barrier((early, normed_late, rest_grad))
    early = shifted_sum(early, "head")
    norm_grad = jnp.sum(normed_grad * unit, axis=(0, 1))

    taps_grad = jnp.sum(taps_grad.reshape(reach + 1, 8, channels), axis=1)
    scalar_part = jnp.sum(scalar_part.reshape(2, 8, LANES), axis=1)
    skip_part = jnp.sum(skip_grad.reshape(8, heads_here, HEADDIM), axis=(0, 2))
    skip_part = jnp.pad(jnp.repeat(skip_part, 2)[None], ((0, 0), (0, LANES - 2 * heads_here)))
    lanes_value = jnp.concatenate(
        [taps_grad[:, :inner_here], jnp.sum(gain_grad, axis=0, keepdims=True)], axis=0
    )
    lanes_state = jnp.concatenate(
        [taps_grad[:, inner_here:], norm_grad.reshape(-1, channels_state)], axis=0
    )
    lanes_step = jnp.concatenate([scalar_part, skip_part], axis=0)
    extra = jnp.concatenate(
        [
            jnp.pad(lanes_value, ((0, 16 - lanes_value.shape[0]), (0, 0))),
            jnp.pad(lanes_state, ((0, 16 - lanes_state.shape[0]), (0, 0))),
            jnp.pad(lanes_step, ((0, 16 - lanes_step.shape[0]), (0, 0))),
        ],
        axis=1,
    ).astype(low)
    late_grad = weight_grad(normed_late, rest_grad).reshape(chips, 2, rows, lane_cols)
    late_grad = jnp.concatenate(
        [late_grad, jnp.broadcast_to(extra, (chips, 2) + extra.shape)], axis=2
    )
    late_grad, delta, early = lax.optimization_barrier((late_grad, delta, early))
    late_moved = lax.all_to_all(late_grad, "chip", 0, 0)
    output = tokens.astype(wide) + out_delta.astype(wide)

    late = between_cores(late_moved)
    state_sum = late[0][:, inner_here:channels].astype(wide) + late[1][:, inner_here:channels].astype(wide)
    state_sum = state_sum.astype(low)
    own_state = rows // planes
    state_pieces = [
        jnp.concatenate(
            [
                state_sum[i * own_state : (i + 1) * own_state],
                jnp.zeros((rows - own_state, channels_state), low),
                state_sum[rows:],
            ],
            axis=0,
        )
        for i in range(planes)
    ]
    late = over_planes(
        [
            jnp.concatenate(
                [group_lanes(late[which], 0, i), late[which][:, channels:], state_pieces[which * groups + i]],
                axis=1,
            )
            for which in range(2)
            for i in range(groups)
        ]
    )
    step_lanes = lax.dynamic_slice_in_dim(
        late[:, group_inner : group_inner + LANES], step_at, 2 * group, 1
    )
    in_weight_out = jnp.concatenate(
        [
            early[:, :group_inner].reshape(rows, group, HEADDIM),
            late[:rows, :group_inner].reshape(rows, group, HEADDIM),
            step_lanes[:rows].reshape(rows, group, 2),
        ],
        axis=2,
    )
    out_weight_out = early[:, group_inner:].reshape(rows, group, HEADDIM)
    lanes = late[rows:, :group_inner].reshape(16, group, HEADDIM)
    lanes = lax.dynamic_slice_in_dim(lanes, part * seq, part, 2)
    value_conv_out = lanes[: reach + 1].transpose(2, 1, 0)
    gate_gain_out = lanes[reach + 1].transpose(1, 0)
    state_out = late[:, group_inner + LANES :]
    conv_at = state_part * seq + (state_part // planes) * plane
    state_conv_out = lax.dynamic_slice_in_dim(
        state_out[rows : rows + reach + 1], conv_at, state_part // planes, 1
    ).T
    norm_sum = state_out[rows + reach + 1 :][: width // channels_state].reshape(width)
    norm_gain_out = lax.dynamic_slice_in_dim(norm_sum, rows * seq, rows, 0)
    small_outs = (
        in_weight_out,
        state_out[:own_state],
        state_conv_out,
        out_weight_out,
        value_conv_out,
        norm_gain_out,
        gate_gain_out,
        step_lanes[rows].reshape(group, 2).T,
        jnp.sum(step_lanes[rows + 1].reshape(group, 2), axis=1),
        step_lanes[rows + 2].reshape(group, 2)[:, 0],
    )
    gathered, output, *small_outs = lax.optimization_barrier((gathered, output) + small_outs)
    return (output, out_cotangent + gathered.astype(wide), *small_outs)


def solution(mesh):
    devices_seq, planes = mesh.devices.shape
    seq, plan = "seq", split_plan
    if devices_seq % 2 == 0 and planes % 2 == 0 and devices_seq // 2 * planes == CHIP_SEQUENCES:
        shape = (devices_seq // 2, 2, planes)
        mesh = Mesh(mesh.devices.reshape(shape), ("chip", "core", "head"))
        seq, plan = ("chip", "core"), chip_plan
    both = seq + ("head",) if isinstance(seq, tuple) else (seq, "head")
    return jax.shard_map(
        plan,
        mesh=mesh,
        in_specs=(
            P(None, seq, None),
            P(),
            P(seq, "head", None),
            P(seq, None),
            P(seq, None),
            P(seq, "head", None),
            P(seq, "head", None),
            P(seq),
            P(seq, "head"),
            P(None, "head"),
            P("head"),
            P("head"),
            P(None, seq, None),
        ),
        out_specs=(
            P(None, seq, None),
            P(None, seq, None),
            P(seq, "head", None),
            P(both, None),
            P(both, None),
            P(seq, "head", None),
            P(seq, "head", None),
            P(seq),
            P(seq, "head"),
            P(None, "head"),
            P("head"),
            P("head"),
        ),
        check_vma=False,
    )
```

```python
import jax
import jax.numpy as jnp
from jax import lax
from jax.experimental import pallas as pl
from jax.experimental.pallas import tpu as pltpu
from jax.sharding import Mesh, PartitionSpec as P

HEADS = 24
HEADDIM = 64
STATE = 64
CHIP_SEQUENCES = 16


def from_behind(value, axis, by):
    devices = lax.axis_size(axis)
    pairs = [(i, i + by) for i in range(devices) if 0 <= i + by < devices]
    return lax.ppermute(value, axis, pairs)


def entering(value, axis, join, neutral, backward):
    count, mine = (lax.axis_size(axis), lax.axis_index(axis))
    pieces = jax.tree.map(lambda part: lax.all_gather(part, axis), value)
    if backward:
        pieces = jax.tree.map(lambda part: part[::-1], pieces)
        mine = count - 1 - mine
    running = jax.tree.map(
        lambda part, zero: jnp.full_like(part, 0) + jnp.asarray(zero, part.dtype), value, neutral
    )

    def step(position, running):
        longer = join(running, jax.tree.map(lambda part: part[position], pieces))
        return jax.tree.map(lambda new, old: jnp.where(position < mine, new, old), longer, running)

    return lax.fori_loop(0, count - 1, step, running)


def affine(earlier, later):
    return (earlier[0] * later[0], later[0][..., None, None] * earlier[1] + later[1])


def document_numbers(starts, first_position, count, block_size):
    blocks = starts.shape[1]
    begins = jnp.arange(blocks, dtype=jnp.int32)[None, :] * block_size + starts
    valid = starts < block_size
    places = first_position + jnp.arange(count, dtype=jnp.int32)
    hits = (begins[:, None, :] <= places[None, :, None]) & valid[:, None, :]
    return jnp.sum(hits.astype(jnp.int32), axis=2)


def running_sum(value):
    length, shift = value.shape[-1], 1
    while shift < length:
        pad = [(0, 0)] * (value.ndim - 1) + [(shift, 0)]
        value = value + jnp.pad(value[..., : length - shift], pad)
        shift *= 2
    return value


def chain_forward(readout, intake, values, log_decay, step_size, flags):
    block_size = readout.shape[1]
    segment = running_sum(flags)
    decay_sum = running_sum(log_decay)
    scores = jnp.einsum("mtn,mjn->mtj", readout, intake, preferred_element_type=jnp.float32)
    order = jnp.arange(block_size)
    mask = ((order[:, None] > order[None, :])[None] & (segment[:, :, None] == segment[:, None, :]))[
        :, None
    ]
    gap = jnp.where(mask, decay_sum[:, :, :, None] - decay_sum[:, :, None, :], 0.0)
    decay_table = jnp.where(mask, jnp.exp(gap), 0.0)
    mixing = (scores[:, None] * decay_table * step_size[:, :, None, :]).astype(jnp.bfloat16)
    inner = jnp.einsum("mhtj,mjhp->mthp", mixing, values, preferred_element_type=jnp.float32)
    tail_factor = (
        jnp.exp(decay_sum[:, :, -1:] - decay_sum) * (segment == segment[:, -1:])[:, None, :]
    )
    scaled_intake = (
        (tail_factor * step_size)[..., None] * intake[:, None].astype(jnp.float32)
    ).astype(jnp.bfloat16)
    local_state = jnp.einsum(
        "mhjn,mjhp->mhnp", scaled_intake, values, preferred_element_type=jnp.float32
    )
    block_decay = jnp.exp(decay_sum[:, :, -1]) * (segment[:, -1] == 0)[:, None]
    head_scale = jnp.exp(decay_sum) * (segment == 0)[:, None, :]
    saved = (scores, decay_table, mixing, tail_factor, scaled_intake, head_scale)
    return (inner, local_state, block_decay, saved)


def chain_finish(inner, readout, state_in, head_scale):
    state_low = state_in.astype(jnp.bfloat16)
    carried = jnp.einsum("mtn,mhnp->mthp", readout, state_low, preferred_element_type=jnp.float32)
    return (inner + jnp.swapaxes(head_scale, 1, 2)[..., None] * carried, carried, state_low)


def chain_back_state(grad_out, readout, carried, state_low, head_scale):
    grad_wide = grad_out.astype(jnp.float32)
    carried_grad = (jnp.swapaxes(head_scale, 1, 2)[..., None] * grad_wide).astype(jnp.bfloat16)
    state_in_grad = jnp.einsum(
        "mtn,mthp->mhnp", readout, carried_grad, preferred_element_type=jnp.float32
    )
    readout_grad = jnp.einsum(
        "mthp,mhnp->mtn", carried_grad, state_low, preferred_element_type=jnp.float32
    )
    sum_grad = jnp.swapaxes(jnp.sum(grad_wide * carried, axis=3), 1, 2) * head_scale
    return (state_in_grad, readout_grad, sum_grad)


def chain_back_rest(
    grad_out,
    readout,
    intake,
    values,
    step_size,
    state_in,
    later,
    block_decay,
    saved,
    readout_grad,
    sum_grad,
):
    scores, decay_table, mixing, tail_factor, scaled_intake, head_scale = saved
    later_low = later.astype(jnp.bfloat16)
    scaled_grad = jnp.einsum(
        "mjhp,mhnp->mhjn", values, later_low, preferred_element_type=jnp.float32
    )
    values_grad = jnp.einsum(
        "mhjn,mhnp->mjhp", scaled_intake, later_low, preferred_element_type=jnp.float32
    )
    tail_grad = jnp.einsum("mhjn,mjn->mhj", scaled_grad, intake.astype(jnp.float32))
    intake_grad = jnp.einsum("mhjn,mhj->mjn", scaled_grad, tail_factor * step_size)
    step_grad = tail_grad * tail_factor
    tail_term = tail_grad * tail_factor * step_size
    decay_grad = jnp.sum(later * state_in, axis=(2, 3)) * block_decay
    sum_grad = (sum_grad - tail_term).at[:, :, -1].add(jnp.sum(tail_term, axis=2) + decay_grad)
    mixing_grad = jnp.einsum(
        "mthp,mjhp->mhtj", grad_out, values, preferred_element_type=jnp.float32
    )
    values_grad = values_grad + jnp.einsum(
        "mhtj,mthp->mjhp", mixing, grad_out, preferred_element_type=jnp.float32
    )
    through = mixing_grad * decay_table
    scores_grad = jnp.sum(through * step_size[:, :, None, :], axis=1).astype(jnp.bfloat16)
    readout_grad = readout_grad + jnp.einsum(
        "mtj,mjn->mtn", scores_grad, intake, preferred_element_type=jnp.float32
    )
    intake_grad = intake_grad + jnp.einsum(
        "mtj,mtn->mjn", scores_grad, readout, preferred_element_type=jnp.float32
    )
    kernel = through * scores[:, None]
    step_grad = step_grad + jnp.sum(kernel, axis=2)
    weighted = kernel * step_size[:, :, None, :]
    sum_grad = sum_grad + jnp.sum(weighted, axis=3) - jnp.sum(weighted, axis=2)
    log_grad = jnp.flip(running_sum(jnp.flip(sum_grad, 2)), 2)
    return (values_grad, readout_grad, intake_grad, step_grad, log_grad)


def split_plan(
    tokens,
    starts,
    in_weight,
    state_weight,
    state_conv,
    out_weight,
    value_conv,
    norm_gain,
    gate_gain,
    step_bias,
    decay_log,
    skip,
    out_cotangent,
):
    sequences, block_size, width = tokens.shape
    place = lax.axis_index("seq")
    devices_seq = lax.axis_size("seq")
    in_weights, state_weights, state_taps, out_weights, value_taps, norm_whole, gate_whole = (
        lax.all_gather(in_weight, "seq", axis=0, tiled=True),
        lax.all_gather(state_weight, "seq", axis=0, tiled=True),
        lax.all_gather(state_conv, "seq", axis=0, tiled=True),
        lax.all_gather(out_weight, "seq", axis=0, tiled=True),
        lax.all_gather(value_conv, "seq", axis=0, tiled=True),
        lax.all_gather(norm_gain, "seq", axis=0, tiled=True),
        lax.all_gather(gate_gain, "seq", axis=0, tiled=True),
    )
    heads_here = in_weight.shape[1]
    value_width = heads_here * HEADDIM
    reach = state_conv.shape[1] - 1
    edge = reach - 1
    numbers = document_numbers(starts, place * block_size - edge, block_size + 2 * edge, block_size)
    lag_masks = jnp.stack(
        [
            numbers[:, edge:] == numbers[:, edge - lag : block_size + 2 * edge - lag]
            for lag in range(reach)
        ],
        axis=2,
    ).astype(jnp.float32)
    first = (
        numbers[:, edge : edge + block_size] != numbers[:, edge - 1 : edge + block_size - 1]
    ).astype(jnp.int32)
    positions = place * block_size + jnp.arange(block_size, dtype=jnp.int32)
    ending = (positions == devices_seq * block_size - 1)[None, :]
    last = (
        (numbers[:, edge + 1 : edge + block_size + 1] != numbers[:, edge : edge + block_size])
        | ending
    ).astype(jnp.int32)
    tokens_wide = tokens.astype(jnp.float32)
    in_scale = lax.rsqrt(jnp.mean(tokens_wide * tokens_wide, axis=2, keepdims=True) + 1e-05)
    unit = tokens_wide * in_scale
    norm_wide = norm_whole.astype(jnp.float32)
    normed = (unit * norm_wide).astype(jnp.bfloat16)
    projected = jnp.einsum("mtd,dhk->mthk", normed, in_weights, preferred_element_type=jnp.float32)
    state_proj = jnp.einsum(
        "mtd,dn->mtn", normed, state_weights, preferred_element_type=jnp.float32
    )
    gate = projected[..., :HEADDIM]
    step_raw = projected[..., 2 * HEADDIM :]
    conv_input = jnp.concatenate(
        [
            projected[..., HEADDIM : 2 * HEADDIM].reshape(sequences, block_size, value_width),
            state_proj,
        ],
        axis=2,
    ).astype(jnp.bfloat16)
    channels = conv_input.shape[2]
    halo_rows = from_behind(conv_input[:, block_size - edge :], "seq", 1)
    extended = jnp.concatenate([halo_rows, conv_input], axis=1)
    taps = jnp.concatenate(
        [jnp.transpose(value_taps, (1, 0, 2)).reshape(value_width, reach + 1), state_taps], axis=0
    ).astype(jnp.float32)
    pre_active = jnp.broadcast_to(taps[:, reach], (sequences, block_size, channels))
    for lag in range(reach):
        pre_active = (
            pre_active
            + taps[:, lag]
            * extended[:, edge - lag : edge - lag + block_size]
            * lag_masks[:, :block_size, lag, None]
        )
    active_sigma = jax.nn.sigmoid(pre_active)
    activated = (pre_active * active_sigma).astype(jnp.bfloat16)
    values = activated[..., :value_width].reshape(sequences, block_size, heads_here, HEADDIM)
    intake_forward = activated[..., value_width : value_width + STATE]
    readout_forward = activated[..., value_width + STATE : value_width + 2 * STATE]
    intake_reverse = jnp.flip(activated[..., value_width + 2 * STATE : value_width + 3 * STATE], 1)
    readout_reverse = jnp.flip(activated[..., value_width + 3 * STATE :], 1)
    values_reversed = jnp.flip(values, 1)
    rate = jnp.exp(decay_log)
    bias_here = jnp.transpose(step_bias)[None, None]
    step_all = jax.nn.softplus(step_raw + bias_here)
    step_forward = jnp.transpose(step_all[..., 0], (0, 2, 1))
    step_reverse = jnp.flip(jnp.transpose(step_all[..., 1], (0, 2, 1)), 2)
    log_forward = -step_forward * rate[None, :, None]
    log_reverse = -step_reverse * rate[None, :, None]
    inner_forward, local_forward, decay_forward, saved_forward = chain_forward(
        readout_forward, intake_forward, values, log_forward, step_forward, first
    )
    inner_reverse, local_reverse, decay_reverse, saved_reverse = chain_forward(
        readout_reverse,
        intake_reverse,
        values_reversed,
        log_reverse,
        step_reverse,
        jnp.flip(last, 1),
    )
    identity = (jnp.ones_like(decay_forward), jnp.zeros_like(local_forward))
    state_forward = entering((decay_forward, local_forward), "seq", affine, identity, False)[1]
    state_reverse = entering((decay_reverse, local_reverse), "seq", affine, identity, True)[1]
    out_forward, carried_forward, state_low_forward = chain_finish(
        inner_forward, readout_forward, state_forward, saved_forward[5]
    )
    out_reverse, carried_reverse, state_low_reverse = chain_finish(
        inner_reverse, readout_reverse, state_reverse, saved_reverse[5]
    )
    core = (
        out_forward
        + jnp.flip(out_reverse, 1)
        + skip[None, None, :, None] * values.astype(jnp.float32)
    )
    gate_sigma = jax.nn.sigmoid(gate)
    gated = core * gate * gate_sigma
    gate_gains = jnp.transpose(gate_whole).astype(jnp.float32)
    unscaled = (gated * gate_gains).astype(jnp.bfloat16)
    squares = jnp.sum(gated * gated, axis=(2, 3))
    partial_value = jnp.einsum(
        "mthp,dhp->mtd", unscaled, out_weights, preferred_element_type=jnp.float32
    )
    pre_out, square_sum = lax.psum((partial_value, squares), "head")
    inner_width = HEADS * HEADDIM
    gate_scale = lax.rsqrt(square_sum / inner_width + 1e-05)
    output = tokens_wide + gate_scale[..., None] * pre_out
    total_grad = (gate_scale[..., None] * out_cotangent).astype(jnp.bfloat16)
    unscaled_grad = jnp.einsum(
        "mtd,dhp->mthp", total_grad, out_weights, preferred_element_type=jnp.float32
    )
    out_weight_grad = jnp.einsum(
        "mtd,mthp->dhp", total_grad, unscaled, preferred_element_type=jnp.float32
    )
    scale_grad = jnp.sum(out_cotangent * pre_out, axis=2)
    square_grad = -0.5 * scale_grad * gate_scale**3 / inner_width
    gated_grad = unscaled_grad * gate_gains + 2.0 * gated * square_grad[..., None, None]
    gate_gain_grad = jnp.transpose(jnp.sum(unscaled_grad * gated, axis=(0, 1)))
    core_grad = (gated_grad * gate * gate_sigma).astype(jnp.bfloat16)
    gate_grad = gated_grad * core * gate_sigma * (1.0 + gate * (1.0 - gate_sigma))
    skip_grad = jnp.sum(core_grad.astype(jnp.float32) * values.astype(jnp.float32), axis=(0, 1, 3))
    core_reversed = jnp.flip(core_grad, 1)
    state_grad_forward, readout_grad_forward, sum_grad_forward = chain_back_state(
        core_grad, readout_forward, carried_forward, state_low_forward, saved_forward[5]
    )
    state_grad_reverse, readout_grad_reverse, sum_grad_reverse = chain_back_state(
        core_reversed, readout_reverse, carried_reverse, state_low_reverse, saved_reverse[5]
    )
    later_forward = entering((decay_forward, state_grad_forward), "seq", affine, identity, True)[1]
    later_reverse = entering((decay_reverse, state_grad_reverse), "seq", affine, identity, False)[1]
    (
        values_grad_forward,
        readout_grad_forward,
        intake_grad_forward,
        step_grad_forward,
        log_grad_forward,
    ) = chain_back_rest(
        core_grad,
        readout_forward,
        intake_forward,
        values,
        step_forward,
        state_forward,
        later_forward,
        decay_forward,
        saved_forward,
        readout_grad_forward,
        sum_grad_forward,
    )
    (
        values_grad_reverse,
        readout_grad_reverse,
        intake_grad_reverse,
        step_grad_reverse,
        log_grad_reverse,
    ) = chain_back_rest(
        core_reversed,
        readout_reverse,
        intake_reverse,
        values_reversed,
        step_reverse,
        state_reverse,
        later_reverse,
        decay_reverse,
        saved_reverse,
        readout_grad_reverse,
        sum_grad_reverse,
    )
    values_grad = (
        values_grad_forward
        + jnp.flip(values_grad_reverse, 1)
        + skip[None, None, :, None] * core_grad.astype(jnp.float32)
    )
    step_total_forward = step_grad_forward - rate[None, :, None] * log_grad_forward
    step_total_reverse = jnp.flip(step_grad_reverse - rate[None, :, None] * log_grad_reverse, 2)
    decay_log_grad = jnp.sum(log_grad_forward * log_forward, axis=(0, 2)) + jnp.sum(
        log_grad_reverse * log_reverse, axis=(0, 2)
    )
    step_total = jnp.stack(
        [
            jnp.transpose(step_total_forward, (0, 2, 1)),
            jnp.transpose(step_total_reverse, (0, 2, 1)),
        ],
        axis=3,
    )
    raw_grad = step_total * jax.nn.sigmoid(step_raw + bias_here)
    step_bias_grad = jnp.transpose(jnp.sum(raw_grad, axis=(0, 1)))
    state_grads = jnp.concatenate(
        [
            intake_grad_forward,
            readout_grad_forward,
            jnp.flip(intake_grad_reverse, 1),
            jnp.flip(readout_grad_reverse, 1),
        ],
        axis=2,
    )
    active_grad = jnp.concatenate(
        [values_grad.reshape(sequences, block_size, value_width), state_grads], axis=2
    )
    pre_grad = active_grad * active_sigma * (1.0 + pre_active * (1.0 - active_sigma))
    following = from_behind(pre_grad[:, :edge], "seq", -1)
    grad_extended = jnp.concatenate([pre_grad, following], axis=1)
    conv_input_grad = jnp.zeros((sequences, block_size, channels), jnp.float32)
    tap_grads = []
    for lag in range(reach):
        conv_input_grad = (
            conv_input_grad
            + taps[:, lag]
            * grad_extended[:, lag : lag + block_size]
            * lag_masks[:, lag : lag + block_size, lag, None]
        )
        tap_grads.append(
            jnp.sum(
                pre_grad
                * extended[:, edge - lag : edge - lag + block_size]
                * lag_masks[:, :block_size, lag, None],
                axis=(0, 1),
            )
        )
    tap_grads.append(jnp.sum(pre_grad, axis=(0, 1)))
    taps_grad = jnp.stack(tap_grads, axis=1)
    value_conv_grad = jnp.transpose(
        taps_grad[:value_width].reshape(heads_here, HEADDIM, reach + 1), (1, 0, 2)
    )
    state_conv_grad = taps_grad[value_width:]
    proj_grad = jnp.concatenate(
        [
            gate_grad,
            conv_input_grad[..., :value_width].reshape(sequences, block_size, heads_here, HEADDIM),
            raw_grad,
        ],
        axis=3,
    ).astype(jnp.bfloat16)
    state_proj_grad = conv_input_grad[..., value_width:].astype(jnp.bfloat16)
    normed_part = jnp.einsum(
        "mthk,dhk->mtd", proj_grad, in_weights, preferred_element_type=jnp.float32
    )
    normed_part = normed_part + jnp.einsum(
        "mtn,dn->mtd", state_proj_grad, state_weights, preferred_element_type=jnp.float32
    )
    normed_grad = lax.psum(normed_part, "head")
    in_weight_grad = jnp.einsum(
        "mtd,mthk->dhk", normed, proj_grad, preferred_element_type=jnp.float32
    )
    state_weight_grad = jnp.einsum(
        "mtd,mtn->dn", normed, state_proj_grad, preferred_element_type=jnp.float32
    )
    norm_gain_grad = jnp.sum(normed_grad * unit, axis=(0, 1))
    unit_grad = normed_grad * norm_wide
    input_gradient = out_cotangent + in_scale * (
        unit_grad - unit * jnp.mean(unit_grad * unit, axis=2, keepdims=True)
    )
    in_weight_out, out_weight_out, value_conv_out, norm_gain_out, gate_gain_out = (
        lax.psum_scatter(in_weight_grad, "seq", scatter_dimension=0, tiled=True),
        lax.psum_scatter(out_weight_grad, "seq", scatter_dimension=0, tiled=True),
        lax.psum_scatter(value_conv_grad, "seq", scatter_dimension=0, tiled=True),
        lax.psum_scatter(norm_gain_grad, "seq", scatter_dimension=0, tiled=True),
        lax.psum_scatter(gate_gain_grad, "seq", scatter_dimension=0, tiled=True),
    )
    state_weight_out, state_conv_out = (
        lax.psum_scatter(state_weight_grad, ("seq", "head"), scatter_dimension=0, tiled=True),
        lax.psum_scatter(state_conv_grad, ("seq", "head"), scatter_dimension=0, tiled=True),
    )
    step_bias_out, decay_log_out, skip_out = lax.psum(
        (step_bias_grad, decay_log_grad, skip_grad), "seq"
    )
    return (
        output,
        input_gradient,
        in_weight_out,
        state_weight_out,
        state_conv_out,
        out_weight_out,
        value_conv_out,
        norm_gain_out,
        gate_gain_out,
        step_bias_out,
        decay_log_out,
        skip_out,
    )


LANES = 128
WIDE, LOW = jnp.float32, jnp.bfloat16
FAR = -1e30


def dot(left, right):
    return jnp.dot(left, right, preferred_element_type=WIDE)


def dot_nt(left, right):
    return lax.dot_general(left, right, (((1,), (1,)), ((), ())), preferred_element_type=WIDE)


def halves(value):
    high = value.astype(LOW)
    return jnp.concatenate([high, (value - high.astype(WIDE)).astype(LOW)], axis=1)


def iota(shape, axis):
    return lax.broadcasted_iota(jnp.int32, shape, axis)


def head_columns(heads):
    row = jnp.arange(2 * LANES)[:, None] % LANES
    head = jnp.arange(heads * HEADDIM)[None, :] // HEADDIM
    spread_both = [(row == 2 * head + d).astype(LOW) for d in range(2)]
    gather_both = [jnp.concatenate([s[:LANES].T, s[:LANES].T], axis=0) for s in spread_both]
    return spread_both, gather_both


def steps_of(raw, bias):
    shifted = raw + bias
    small = jnp.exp(-jnp.abs(shifted))
    exponent = jnp.exp(jnp.minimum(shifted, 0.0))
    step = jnp.where(
        shifted < -15.0, exponent, jnp.maximum(shifted, 0.0) + jnp.log1p(small)
    )
    sigma = exponent / (1.0 + small)
    ratio = jnp.where(shifted < -15.0, 1.0, sigma / step)
    return step, sigma, ratio


def odd_lanes(shape):
    return iota(shape, 1) % 2 == 1


def running_sums(value, flip):
    size = value.shape[0]
    row, col = iota((2 * size, size), 0), iota((2 * size, size), 1)
    keep = jnp.logical_or(
        jnp.logical_and(row < size, row >= col), jnp.logical_and(row >= size, row - size <= col)
    )
    keep = keep.astype(WIDE).astype(LOW)
    high = value.astype(LOW)
    rest = value - high.astype(WIDE)
    middle = rest.astype(LOW)
    last = (rest - middle.astype(WIDE)).astype(LOW)
    sums = dot(keep, high) + dot(keep, middle) + dot(keep, last)
    odd = odd_lanes(value.shape)
    if flip:
        return jnp.where(odd, sums[:size], sums[size:])
    return jnp.where(odd, sums[size:], sums[:size])


def start_masks(starts, block, blocks, shape):
    size = shape[0]
    start = starts[block]
    following = starts[jnp.minimum(block + 1, blocks - 1)]
    none = start >= size
    ended = jnp.logical_or(block == blocks - 1, following == 0)
    row, odd = iota(shape, 0), odd_lanes(shape)
    after = row >= start
    tail_forward = jnp.logical_or(after, none)
    tail_reverse = jnp.logical_or(jnp.logical_not(after), jnp.logical_or(none, start == 0))
    head_forward = jnp.logical_not(after)
    head_reverse = jnp.logical_and(jnp.logical_or(after, none), jnp.logical_not(ended))
    tail = jnp.where(odd, tail_reverse.astype(WIDE), tail_forward.astype(WIDE))
    head = jnp.where(odd, head_reverse.astype(WIDE), head_forward.astype(WIDE))
    whole_reverse = jnp.logical_and(jnp.logical_or(none, start == 0), jnp.logical_not(ended))
    whole = jnp.where(
        odd[:8],
        jnp.where(whole_reverse, 1.0, 0.0),
        jnp.where(none, 1.0, 0.0),
    )
    return tail, head, whole


def chain_last(cum):
    return jnp.where(odd_lanes((1, cum.shape[1])), cum[:1], cum[-1:])


def table_bias(starts, block, size):
    row, col = iota((size, size), 0), iota((size, size), 1)
    start = starts[block]
    same = (row >= start) == (col >= start)
    return jnp.where(jnp.logical_and(same, row != col), 0.0, FAR)


def lane_half(size, second):
    return ((iota((size, LANES), 1) >= HEADDIM) == second).astype(WIDE).astype(LOW)


def block_diagonal(pair):
    size = pair.shape[0]
    return jnp.concatenate([pair * lane_half(size, False), pair * lane_half(size, True)], axis=0)


def silu_slope(value, sigma):
    return sigma * (1.0 + value * (1.0 - sigma))


def below(value):
    return jnp.concatenate([jnp.zeros_like(value), value], axis=0)


def above(value):
    return jnp.concatenate([value, jnp.zeros_like(value)], axis=0)


def rows_sum(value):
    total = value[:8]
    for at in range(8, value.shape[0], 8):
        total = total + value[at : at + 8]
    return total


def in_order(starts, mine, other):
    first = starts[starts.shape[0] - 1] == 0
    return jnp.concatenate(
        [jnp.where(first, mine[...], other[...]), jnp.where(first, other[...], mine[...])], axis=0
    )


def keep_own(starts, value, keep, send):
    first = starts[starts.shape[0] - 1] == 0
    size = value.shape[0] // 2
    keep[...] = jnp.where(first, value[:size], value[size:]).astype(keep.dtype)
    send[...] = jnp.where(first, value[size:], value[:size]).astype(send.dtype)


def document_of(starts, pair, blocks, size, place):
    far = 4 * size
    first, second = starts[2 * pair], starts[2 * pair + 1]
    before = starts[jnp.maximum(2 * pair - 1, 0)]
    behind = starts[jnp.minimum(2 * pair + 2, blocks - 1)]
    first = jnp.where(first < size, first, far)
    second = jnp.where(second < size, second + size, far)
    behind = jnp.where(behind < size, behind + 2 * size, far)
    before = jnp.where(before < size, before - size, -far)
    number = (place >= first).astype(jnp.int32) + (place >= second).astype(jnp.int32)
    return number + (place >= behind).astype(jnp.int32) + (place >= before).astype(jnp.int32)


def skip_lanes(small, spread):
    parts = dot(small[:, small.shape[1] - LANES :].astype(LOW), spread[:LANES])
    return parts[6:7] + parts[7:8] + parts[8:9]


def step_rows(small, heads):
    part = small[:, small.shape[1] - LANES :]
    bias = part[0:1] + part[1:2] + part[2:3]
    rate = jnp.exp(part[3:4] + part[4:5] + part[5:6])
    return bias, jnp.where(iota((1, LANES), 1) < 2 * heads, rate, 0.0)


def shard_rows(starts, side, index, rows):
    chip, core = starts[starts.shape[0] - 2], starts[starts.shape[0] - 1]
    seq = 2 * jnp.bitwise_xor(chip, side) + (core if index == 0 else 1 - core)
    return pl.ds(pl.multiple_of(seq * rows, 32), rows)


def forward_kernel(
    starts, mine, other, pay, pay_x, pay_y, pay_far, pay_far_other, spread_f, spread_r,
    normed_o, conv_o, pre_o, act_o, out_f_o, cum_o, raw_o, state_f_o, decay_f_o, decay_r_o,
    weights_o, small_o, core_o, state_r_o,
    tail_s, state_s, sum_s, head_s, read_s, local_s, decay_s,
):
    step_at = pl.program_id(0)
    pairs = pl.num_programs(0) // 2
    blocks = 2 * pairs
    size = mine.shape[0]
    inner = out_f_o.shape[1]
    channels = inner + 4 * STATE
    reach = 4

    @pl.when(step_at == 0)
    def _():
        tail_s[...] = jnp.zeros_like(tail_s)
        state_s[...] = jnp.zeros_like(state_s)
        rows = pay.shape[1] - 16
        shards = [pay.at[0], pay.at[1], pay_x.at[0], pay_x.at[1], pay_y.at[0], pay_y.at[1]]
        shards = shards + [pay_far, pay_far_other]
        total = jnp.zeros(small_o.shape, WIDE)
        for i, shard in enumerate(shards):
            weights_o[shard_rows(starts, i // 2, i % 2, rows), :] = shard[:rows, :]
            total = total + shard[rows:, :].astype(WIDE)
        small_o[...] = total

    @pl.when(step_at < pairs)
    def _():
        pair = step_at
        small = small_o[...]
        bias_row, rate_row = step_rows(small, inner // HEADDIM)
        skip_row = skip_lanes(small, spread_f)
        norm_row = jnp.concatenate([small[i : i + 1, inner:channels] for i in (5, 6, 7)], axis=1)
        taps = small[:8, :channels]
        wide = in_order(starts, mine, other).astype(WIDE)
        scale = lax.rsqrt(jnp.mean(wide * wide, axis=1, keepdims=True) + 1e-05)
        normed = (wide * scale * norm_row).astype(LOW)
        normed_o[...] = normed
        raw = dot(normed, weights_o[:, channels:])
        raw_o[...] = raw

        step, _, _ = steps_of(raw, bias_row)
        log_decay = -step * rate_row
        subs = [slice(0, size), slice(size, 2 * size)]
        cums = [running_sums(log_decay[rows], False) for rows in subs]
        cum = jnp.concatenate(cums, axis=0)
        cum_o[...] = cum
        late = cum - jnp.log(step)
        masks = [start_masks(starts, 2 * pair + sub, blocks, (size, LANES)) for sub in range(2)]
        last = [jnp.broadcast_to(chain_last(value), (size, LANES)) for value in cums]
        tail = jnp.exp(jnp.concatenate(last, axis=0) - late)
        tail = halves(tail * jnp.concatenate([mask[0] for mask in masks], axis=0))
        head = halves(jnp.exp(cum) * jnp.concatenate([mask[1] for mask in masks], axis=0))
        decay = [jnp.exp(value[:8]) * mask[2] for value, mask in zip(last, masks)]
        decay = halves(jnp.concatenate(decay, axis=0))
        decay_f, decay_r = dot(decay, spread_f[...]), dot(decay, spread_r[...])
        decay_f_o[...], decay_r_o[...] = decay_f, decay_r

        row = iota((2 * size, LANES), 0)
        number = document_of(starts, pair, blocks, size, row)
        lag_masks = [
            (number == document_of(starts, pair, blocks, size, row - lag)).astype(WIDE)
            for lag in range(1, reach)
        ]
        for chunk in range(0, channels, 2 * LANES):
            both = dot(normed, weights_o[:, chunk : chunk + 2 * LANES]).astype(LOW)
            conv_o[:, chunk : chunk + 2 * LANES] = both
            for at in (0, LANES):
                lanes = slice(chunk + at, chunk + at + LANES)
                here = both[:, at : at + LANES].astype(WIDE)
                extended = jnp.concatenate([tail_s[:, lanes], here], axis=0)
                tail_s[:, lanes] = here[2 * size - 8 :]
                pre = taps[4:5, lanes] + taps[0:1, lanes] * here
                for lag in range(1, reach):
                    shifted = pltpu.roll(extended, lag, 0)[8:]
                    pre = pre + taps[lag : lag + 1, lanes] * shifted * lag_masks[lag - 1]
                pre_o[:, lanes] = pre
                act_o[:, lanes] = (pre * jax.nn.sigmoid(pre)).astype(LOW)

        values_wide = act_o[:, :inner].astype(WIDE)
        scaled_f = (dot(tail, spread_f[...]) * values_wide).astype(LOW)
        scaled_r = (dot(tail, spread_r[...]) * values_wide).astype(LOW)
        head_f = dot(head, spread_f[...])
        here = pl.ds(pl.multiple_of(pair * 2 * size, 2 * size), 2 * size)
        head_s[here] = head
        read_s[here] = act_o[:, inner + 2 * STATE :]
        row, col = iota((size, size), 0), iota((size, size), 1)
        lower = row > col
        lower_low = lower.astype(WIDE).astype(LOW)
        upper_low = (row < col).astype(WIDE).astype(LOW)
        for sub, rows in enumerate(subs):
            block = 2 * pair + sub
            late_rows = late[rows].T
            state_act = act_o[rows, inner:]
            turned = state_act.astype(WIDE).T.astype(LOW)
            forward_act, reverse_act = state_act[:, : 2 * STATE], state_act[:, 2 * STATE :]
            scores = jnp.where(
                lower,
                dot(forward_act, below(turned[:STATE])),
                dot(reverse_act, below(turned[2 * STATE : 3 * STATE])),
            )
            bias = table_bias(starts, block, size)
            state = state_s[...]
            states = slice(sub * STATE, (sub + 1) * STATE)
            state_f_o[states] = state
            carried = dot(forward_act, below(state.astype(LOW))) * head_f[rows]
            local_f = dot(turned[:STATE], scaled_f[rows])
            state_s[...] = decay_f[8 * sub : 8 * sub + 1] * state + local_f
            local_r = dot(turned[2 * STATE : 3 * STATE], scaled_r[rows])
            local_s[pl.ds(pl.multiple_of(block * STATE, STATE), STATE)] = local_r
            decay_s[pl.ds(pl.multiple_of(block * 8, 8), 8)] = decay_r[8 * sub : 8 * sub + 8]
            base = skip_row * values_wide[rows]
            at = pl.ds(pl.multiple_of(block * size, size), size)
            for heads in range(inner // LANES):
                lanes = slice(heads * LANES, (heads + 1) * LANES)
                lefts, rights = [], []
                for head_at in (2 * heads, 2 * heads + 1):
                    c = 2 * head_at
                    gap = jnp.where(
                        lower,
                        cums[sub][:, c : c + 1] - late_rows[c : c + 1],
                        cums[sub][:, c + 1 : c + 2] - late_rows[c + 1 : c + 2],
                    )
                    mix = (scores * jnp.exp(gap + bias)).astype(LOW)
                    lefts.append(mix * lower_low)
                    rights.append(mix * upper_low)
                both = jnp.concatenate(
                    [jnp.concatenate(lefts, axis=1), jnp.concatenate(rights, axis=1)], axis=0
                )
                result = dot(both, block_diagonal(act_o[rows, lanes]))
                out_f = result[:size] + carried[:, lanes]
                out_f_o[rows, lanes] = out_f
                sum_s[at, lanes] = out_f + result[size:] + base[:, lanes]

    @pl.when(step_at == pairs)
    def _():
        state_s[...] = jnp.zeros_like(state_s)

    @pl.when(step_at >= pairs)
    def _():
        pair = 2 * pairs - 1 - step_at
        here = pl.ds(pl.multiple_of(pair * 2 * size, 2 * size), 2 * size)
        head_r = dot(head_s[here], spread_r[...])
        for sub in (1, 0):
            block, rows = 2 * pair + sub, slice(sub * size, (sub + 1) * size)
            at = pl.ds(pl.multiple_of(block * size, size), size)
            state = state_s[...]
            state_r_o[sub * STATE : (sub + 1) * STATE] = state
            carried = dot(read_s[at], below(state.astype(LOW)))
            core_o[rows] = sum_s[at] + head_r[rows] * carried
            local_r = local_s[pl.ds(pl.multiple_of(block * STATE, STATE), STATE)]
            decay_r = decay_s[pl.ds(pl.multiple_of(block * 8, 8), 8)]
            state_s[...] = decay_r[:1] * state + local_r


def output_kernel(
    starts, normed, core, mine, other, pay, small,
    gate_o, unscaled_o, unscaled_grad_o, sums_o, keep_o, send_o, gate_w,
    out_w,
):
    size, inner = mine.shape[0], core.shape[1]

    @pl.when(pl.program_id(0) == 0)
    def _():
        seqs, planes, rows, cols = pay.shape
        groups, half = planes // 2, cols // 2
        core_at = starts[starts.shape[0] - 1]
        for seq in range(seqs):
            for group in range(groups):
                part = pay[seq, core_at * groups + group]
                at, lanes = slice(seq * rows, (seq + 1) * rows), slice(group * half, (group + 1) * half)
                gate_w[at, lanes] = part[:, :half]
                out_w[at, lanes] = part[:, half:]

    gate = dot(normed[...], gate_w[...])
    gate_o[...] = gate.astype(gate_o.dtype)
    unscaled_grad = dot(in_order(starts, mine, other), out_w[...])
    unscaled_grad_o[...] = unscaled_grad.astype(unscaled_grad_o.dtype)
    gated = core[...] * gate * jax.nn.sigmoid(gate)
    unscaled = (gated * small[5:6, :inner]).astype(LOW)
    unscaled_o[...] = unscaled
    squares = jnp.sum(gated * gated, axis=1, keepdims=True)
    products = jnp.sum(unscaled_grad * unscaled.astype(WIDE), axis=1, keepdims=True)
    both = jnp.where(iota((2 * size, LANES), 1) == 0, squares, products)
    for sub in range(2):
        rows = slice(sub * size, (sub + 1) * size)
        sums_o[:, rows] = both[rows].T[:8]
    keep_own(starts, dot_nt(unscaled, out_w[...]), keep_o, send_o)


def gate_back_kernel(
    starts, own_sums, other_sums, mine, other, out_f, core, act, gate, unscaled_grad, cum, decay_r,
    small, spread_f, spread_r, gather_f, gather_r,
    total_o, core_grad_o, gate_grad_o, row_sums_o, back_f_o, later_r_o, gain_grad_o, skip_grad_o,
    later_s,
):
    pair, pairs = pl.program_id(0), pl.num_programs(0)
    blocks = 2 * pairs
    size, inner = mine.shape[0], out_f.shape[1]
    inner_width = HEADS * HEADDIM

    @pl.when(pair == 0)
    def _():
        later_s[...] = jnp.zeros_like(later_s)
        gain_grad_o[...] = jnp.zeros_like(gain_grad_o)
        skip_grad_o[...] = jnp.zeros_like(skip_grad_o)

    sums = own_sums[...] + other_sums[...]
    empty = jnp.zeros((size - 8, size), WIDE)
    sums = jnp.concatenate(
        [
            jnp.concatenate([sums[:, at : at + size], empty], axis=0).T
            for at in (0, size)
        ],
        axis=0,
    )
    skip_row, gain_row = skip_lanes(small[...], spread_f), small[5:6, :inner]
    scale = lax.rsqrt(sums[:, 0:1] / inner_width + 1e-05)
    square_grad = sums[:, 1:2] * scale * scale * scale / inner_width
    total_o[...] = (scale * in_order(starts, mine, other).astype(WIDE)).astype(LOW)
    values = act[:, :inner].astype(WIDE)
    core_here = core[...]
    gate_value = gate[...].astype(WIDE)
    sigma = jax.nn.sigmoid(gate_value)
    slope = gate_value * sigma
    gated = core_here * slope
    unscaled = scale * unscaled_grad[...].astype(WIDE)
    gain_grad_o[...] += rows_sum(unscaled * gated)
    gated_grad = unscaled * gain_row - gated * square_grad
    core_grad = (gated_grad * slope).astype(LOW)
    core_grad_o[...] = core_grad
    gate_grad_o[...] = (gated_grad * core_here * silu_slope(gate_value, sigma)).astype(LOW)
    grad_wide = core_grad.astype(WIDE)
    skip_grad_o[...] += rows_sum(grad_wide * values)
    out_f_here = out_f[...]
    out_r_here = core_here - out_f_here - skip_row * values
    row_sums_o[...] = dot(halves(grad_wide * out_f_here), gather_f[...]) + dot(
        halves(grad_wide * out_r_here), gather_r[...]
    )
    for sub in range(2):
        rows, states = slice(sub * size, (sub + 1) * size), slice(sub * STATE, (sub + 1) * STATE)
        _, head_mask, _ = start_masks(starts, 2 * pair + sub, blocks, (size, LANES))
        head = halves(jnp.exp(cum[rows]) * head_mask)
        turned = act[rows, inner:].astype(WIDE).T.astype(LOW)
        grad_here = core_grad_o[rows].astype(WIDE)
        back_f_o[states] = dot(
            turned[STATE : 2 * STATE], (dot(head, spread_f[...]) * grad_here).astype(LOW)
        )
        back_r = dot(turned[3 * STATE :], (dot(head, spread_r[...]) * grad_here).astype(LOW))
        later = later_s[...]
        later_r_o[states] = later
        later_s[...] = decay_r[8 * sub : 8 * sub + 1] * later + back_r


def chain_back_kernel(
    starts, core_grad, gate_grad, act, conv, pre, cum, raw, row_sums, state_f, state_f_next,
    state_r, state_r_last, back_f, later_r, decay_f, gate_w, weights, small, spread_f, spread_r,
    gather_f, gather_r,
    proj_o, keep_o, send_o, taps_grad_o, scalar_o,
    later_s, next_s, values_f_s, values_r_s, active_s, raw_grad_s,
):
    step_at, pairs = pl.program_id(0), pl.num_programs(0)
    pair, blocks = pairs - 1 - step_at, 2 * pairs
    size, inner = core_grad.shape[0] // 2, core_grad.shape[1]
    channels = inner + 4 * STATE
    reach = 4

    @pl.when(step_at == 0)
    def _():
        later_s[...] = jnp.zeros_like(later_s)
        next_s[...] = jnp.zeros_like(next_s)
        taps_grad_o[...] = jnp.zeros_like(taps_grad_o)
        scalar_o[...] = jnp.zeros_like(scalar_o)

    small_here = small[...]
    bias_row, rate_row = step_rows(small_here, inner // HEADDIM)
    skip_row, taps = skip_lanes(small_here, spread_f), small_here[:8, :channels]
    step_all, sigma_all, ratio_all = steps_of(raw[...], bias_row)
    log_step = jnp.log(step_all)
    row, col = iota((size, size), 0), iota((size, size), 1)
    ahead = col > row
    ahead_low = ahead.astype(WIDE).astype(LOW)
    behind_low = (col < row).astype(WIDE).astype(LOW)
    for sub in (1, 0):
        block = 2 * pair + sub
        rows, states = slice(sub * size, (sub + 1) * size), slice(sub * STATE, (sub + 1) * STATE)
        step, sigma, ratio = step_all[rows], sigma_all[rows], ratio_all[rows]
        cum_here = cum[rows]
        late = cum_here - log_step[rows]
        cum_rows = cum_here.T
        tail_mask, head_mask, _ = start_masks(starts, block, blocks, cum_here.shape)
        tail = halves(jnp.exp(chain_last(cum_here) - late) * tail_mask)
        head = halves(jnp.exp(cum_here) * head_mask)
        state_act = act[rows, inner:]
        turned = state_act.astype(WIDE).T.astype(LOW)
        forward_act, reverse_act = state_act[:, : 2 * STATE], state_act[:, 2 * STATE :]
        scores = jnp.where(
            ahead,
            dot(forward_act, above(turned[STATE : 2 * STATE])),
            dot(reverse_act, above(turned[3 * STATE :])),
        )
        bias = table_bias(starts, block, size)
        scores_grad = jnp.zeros((size, size), WIDE)
        for heads in range(inner // LANES):
            lanes = slice(heads * LANES, (heads + 1) * LANES)
            grad_blocks = block_diagonal(core_grad[rows, lanes])
            mix_grad = dot_nt(act[rows, lanes], grad_blocks)
            lefts, rights = [], []
            for at in range(2):
                c = 2 * (2 * heads + at)
                gap = jnp.where(
                    ahead,
                    cum_rows[c : c + 1] - late[:, c : c + 1],
                    cum_rows[c + 1 : c + 2] - late[:, c + 1 : c + 2],
                )
                table = jnp.exp(gap + bias)
                mix = (scores * table).astype(LOW)
                lefts.append(mix * ahead_low)
                rights.append(mix * behind_low)
                scores_grad = scores_grad + mix_grad[:, at * size : (at + 1) * size] * table
            both = jnp.concatenate(
                [jnp.concatenate(lefts, axis=1), jnp.concatenate(rights, axis=1)], axis=0
            )
            result = dot(both, grad_blocks)
            values_f_s[rows, lanes] = result[:size]
            values_r_s[rows, lanes] = result[size:]

        grad_wide = core_grad[rows].astype(WIDE)
        values = act[rows, :inner].astype(WIDE)
        later_f, later_r_here = later_s[...], later_r[states]
        later_f_low, later_r_low = later_f.astype(LOW), later_r_here.astype(LOW)
        tail_f, tail_r = dot(tail, spread_f[...]), dot(tail, spread_r[...])
        values_f = values_f_s[rows] + tail_f * dot(forward_act, above(later_f_low))
        values_r = values_r_s[rows] + tail_r * dot(reverse_act, above(later_r_low))
        col_sums = dot(halves(values * values_f), gather_f[...]) + dot(
            halves(values * values_r), gather_r[...]
        )
        after_f = state_f_next[...] if sub else state_f[STATE:]
        after_r = state_r[:STATE] if sub else state_r_last[...]
        end_f = dot(halves(rows_sum(later_f * after_f)), gather_f[...])
        end_r = dot(halves(rows_sum(later_r_here * after_r)), gather_r[...])
        end_f = jnp.sum(end_f, axis=0, keepdims=True)
        end_r = jnp.sum(end_r, axis=0, keepdims=True)
        at_row = iota(cum_here.shape, 0)
        cum_grad = row_sums[rows] - col_sums
        cum_grad = cum_grad + jnp.where(at_row == size - 1, end_f, 0.0)
        cum_grad = cum_grad + jnp.where(at_row == 0, end_r, 0.0)
        log_grad = running_sums(cum_grad, True)
        raw_grad = col_sums * ratio - rate_row * log_grad * sigma
        raw_grad_s[rows] = raw_grad
        scalar_o[0:8] += rows_sum(raw_grad)
        scalar_o[8:16] += rows_sum(log_grad * (-step * rate_row))

        mid = scores_grad.T
        pieces = []
        for act_pair, spread_head, state, later_low, forward_side in (
            (forward_act, spread_f, state_f, later_f_low, True),
            (reverse_act, spread_r, state_r, later_r_low, False),
        ):
            tail_here = tail_f if forward_side else tail_r
            scaled = (tail_here * values).astype(LOW)
            carried_grad = (dot(head, spread_head[...]) * grad_wide).astype(LOW)
            own = ahead_low if forward_side else behind_low
            mirrored = behind_low if forward_side else ahead_low
            sides = jnp.concatenate(
                [scores_grad.astype(LOW) * own, mid.astype(LOW) * mirrored], axis=1
            )
            swapped = pltpu.roll(act_pair.astype(WIDE), STATE, 1).astype(LOW)
            pieces.append(
                dot_nt(scaled, above(later_low))
                + dot_nt(carried_grad, below(state[states].astype(LOW)))
                + dot(sides, block_diagonal(swapped))
            )
        active_s[rows, :inner] = values_f + values_r + skip_row * grad_wide
        active_s[rows, inner : inner + LANES] = pieces[0]
        active_s[rows, inner + LANES :] = pieces[1]
        later_s[...] = decay_f[8 * sub : 8 * sub + 1] * later_f + back_f[states]

    row = iota((2 * size, LANES), 0)
    number = document_of(starts, pair, blocks, size, row)
    masks = [
        (number == document_of(starts, pair, blocks, size, row + lag)).astype(WIDE)
        for lag in range(1, reach)
    ]
    for at in range(0, channels, LANES):
        lanes = slice(at, at + LANES)
        pre_here = pre[:, lanes]
        grad = active_s[:, lanes] * silu_slope(pre_here, jax.nn.sigmoid(pre_here))
        extended = jnp.concatenate([grad, next_s[:, lanes]], axis=0)
        next_s[:, lanes] = grad[:8]
        source = conv[:, lanes].astype(WIDE)
        result = taps[0:1, lanes] * grad
        taps_grad_o[0:8, lanes] += rows_sum(grad * source)
        taps_grad_o[32:40, lanes] += rows_sum(grad)
        for lag in range(1, reach):
            shifted = pltpu.roll(extended, 2 * size + 8 - lag, 0)[: 2 * size] * masks[lag - 1]
            result = result + taps[lag : lag + 1, lanes] * shifted
            taps_grad_o[8 * lag : 8 * lag + 8, lanes] += rows_sum(shifted * source)
        proj_o[:, lanes] = result.astype(LOW)
    proj_o[:, channels:] = raw_grad_s[...].astype(LOW)
    normed = dot_nt(gate_grad[...], gate_w[...]) + dot_nt(proj_o[...], weights[...])
    keep_own(starts, normed, keep_o, send_o)


def by_pair(kernel, blocks, order, ins, outs, scratch, name, work):
    steps = blocks // 2

    def at(i):
        if order == "both":
            return jnp.minimum(i, steps - 1)
        return steps - 1 - i if order == "down" else i

    def spec(shape, kind):
        part = (shape[0] // steps,) + shape[1:]
        single = (shape[0] // blocks,) + shape[1:]
        if kind == "scalar":
            return pl.BlockSpec(memory_space=pltpu.SMEM)
        if kind == "rows":
            return pl.BlockSpec(part, lambda i: (at(i), 0))
        if kind == "back":
            return pl.BlockSpec(part, lambda i: (steps - 1 - jnp.maximum(i - steps, 0), 0))
        if kind == "half":
            return pl.BlockSpec((None,) + shape[1:], lambda i: (at(i), 0, 0))
        if kind == "lanes":
            return pl.BlockSpec((shape[0], shape[1] // steps), lambda i: (0, at(i)))
        if kind == "next":
            return pl.BlockSpec(single, lambda i: (jnp.minimum(2 * at(i) + 2, blocks - 1), 0))
        if kind == "last":
            return pl.BlockSpec(single, lambda i: (jnp.maximum(2 * at(i) - 1, 0), 0))
        return pl.BlockSpec(shape, lambda i: (0,) * len(shape))

    return pl.pallas_call(
        kernel,
        grid=(2 * steps if order == "both" else steps,),
        in_specs=[spec(value.shape, kind) for value, kind in ins],
        out_specs=[spec(value.shape, kind) for value, kind in outs],
        out_shape=[value for value, _ in outs],
        scratch_shapes=[pltpu.VMEM(shape, dtype) for shape, dtype in scratch],
        compiler_params=pltpu.CompilerParams(
            dimension_semantics=("arbitrary",), vmem_limit_bytes=60 * 1024 * 1024
        ),
        cost_estimate=pl.CostEstimate(
            flops=work,
            transcendentals=0,
            bytes_accessed=sum(v.size * v.dtype.itemsize for v, _ in ins + outs),
        ),
        name=name,
    )(*[value for value, _ in ins])


def swap_core(value):
    return lax.ppermute(value, "core", [(0, 1), (1, 0)])


def swap_chip(value, side):
    return lax.ppermute(value, "chip", [(i, i ^ side) for i in range(4)])


def spread_to(value, axis):
    count = lax.axis_size(axis)
    return lax.all_to_all(jnp.broadcast_to(value[None], (count,) + value.shape), axis, 0, 0)


def shifted_sum(pieces, axis):
    count, mine = lax.axis_size(axis), lax.axis_index(axis)
    total = lax.dynamic_index_in_dim(pieces, mine, 0, keepdims=False).astype(WIDE)
    for k in range(1, count):
        piece = lax.dynamic_index_in_dim(pieces, (mine + k) % count, 0, keepdims=False)
        moved = lax.ppermute(piece, axis, [(i, (i + k) % count) for i in range(count)])
        total = total + moved.astype(WIDE)
    return total


def after(value, *others):
    return lax.optimization_barrier((value,) + others)[0]


def three_parts(value):
    high = lax.reduce_precision(value, 8, 7)
    middle = lax.reduce_precision(value - high, 8, 7)
    return jnp.stack([high, middle, lax.reduce_precision(value - high - middle, 8, 7)])


def placed(value, width, at):
    shape = value.shape[:-1] + (width,)
    return lax.dynamic_update_slice_in_dim(jnp.zeros(shape, value.dtype), value, at, value.ndim - 1)


def chip_plan(
    tokens,
    starts,
    in_weight,
    state_weight,
    state_conv,
    out_weight,
    value_conv,
    norm_gain,
    gate_gain,
    step_bias,
    decay_log,
    skip,
    out_cotangent,
):
    low, wide = LOW, WIDE
    sequences, block_size, width = tokens.shape
    chips, planes = lax.axis_size("chip"), lax.axis_size("head")
    chip, core, plane = lax.axis_index("chip"), lax.axis_index("core"), lax.axis_index("head")
    blocks = starts.shape[1]
    length = blocks * block_size
    rows, group = in_weight.shape[:2]
    groups = planes // 2
    heads_here = group * groups
    inner_here, group_inner = heads_here * HEADDIM, group * HEADDIM
    part, reach = value_conv.shape[0], state_conv.shape[1] - 1
    state_part = state_conv.shape[0]
    channels_state = state_weight.shape[1]
    channels = inner_here + channels_state
    seq = 2 * chip + core
    first = core == 0

    def own_plane(value):
        return lax.dynamic_slice_in_dim(value, plane * chips, chips, 0)

    tokens_plane = own_plane(tokens)
    tokens_plane, in_weight, out_weight = lax.optimization_barrier(
        (tokens_plane, in_weight, out_weight)
    )
    tokens_mine = lax.all_to_all(tokens_plane, "chip", 0, 0)

    step_at = (plane % groups) * 2 * group
    pair_weights = placed(in_weight[:, :, 2 * HEADDIM :].reshape(rows, 2 * group), LANES, step_at)
    tap_lanes = placed(value_conv.transpose(2, 1, 0), HEADDIM, part * seq).reshape(reach + 1, -1)
    gain_lanes = placed(gate_gain.transpose(1, 0), HEADDIM, part * seq).reshape(1, -1)
    extra_value = jnp.concatenate([tap_lanes, gain_lanes], axis=0)
    scalars = jnp.stack(
        [step_bias.T.reshape(-1), jnp.repeat(decay_log, 2), jnp.repeat(skip, 2)]
    )
    scalars = jnp.swapaxes(three_parts(jnp.where(seq == 0, scalars, 0.0)), 0, 1)
    extra_step = placed(scalars.reshape(9, 2 * group).astype(low), LANES, step_at)
    slab = jnp.concatenate(
        [
            jnp.concatenate(
                [in_weight[:, :, HEADDIM : 2 * HEADDIM].reshape(rows, group_inner), pair_weights],
                axis=1,
            ),
            jnp.concatenate(
                [
                    jnp.pad(extra_value, ((0, 16 - extra_value.shape[0]), (0, 0))),
                    jnp.pad(extra_step, ((0, 16 - extra_step.shape[0]), (0, 0))),
                ],
                axis=1,
            ),
        ],
        axis=0,
    )
    extra_state = jnp.concatenate(
        [
            placed(state_conv.T, channels_state, state_part * seq),
            placed(norm_gain, width, rows * seq).reshape(-1, channels_state),
        ],
        axis=0,
    )
    state_slab = jnp.concatenate(
        [state_weight, jnp.pad(extra_state, ((0, 16 - extra_state.shape[0]), (0, 0)))], axis=0
    )
    shifted = [slab] + [
        lax.ppermute(slab, "head", [(i, (i + k) % planes) for i in range(planes)])
        for k in range(1, planes)
    ]
    shifted = jnp.stack(shifted)

    def for_core(which):
        picked = [
            lax.dynamic_index_in_dim(shifted, (plane - which * groups - i) % planes, 0, False)
            for i in range(groups)
        ]
        steps = picked[0][:, group_inner:]
        for i in range(1, groups):
            steps = steps + picked[i][:, group_inner:]
        return jnp.concatenate(
            [picked[i][:, :group_inner] for i in range(groups)] + [state_slab, steps], axis=1
        )

    pay = jnp.stack([for_core(core), swap_core(for_core(1 - core))])
    pay, tokens_mine = lax.optimization_barrier((pay, tokens_mine))
    tokens_other = swap_core(tokens_mine)
    pay_x, pay_y = swap_chip(pay, 1), swap_chip(pay, 2)
    pays = (pay, pay_x, pay_y, swap_chip(pay_x[0], 2), swap_chip(pay_y[1], 1))

    late_slab = jnp.concatenate(
        [
            in_weight[:, :, :HEADDIM].reshape(rows, group_inner),
            out_weight.reshape(rows, group_inner),
        ],
        axis=1,
    )
    pay_late = lax.all_gather(late_slab, ("chip", "core", "head")).reshape(2 * chips, planes, rows, -1)
    cotangent_low = own_plane(out_cotangent).astype(low)
    cotangent_low, *pays = lax.optimization_barrier((cotangent_low, *pays))
    cotangent_mine = lax.all_to_all(cotangent_low, "chip", 0, 0)
    starts_row = lax.dynamic_index_in_dim(starts, plane * chips + chip, 0, keepdims=False)
    starts_row = jnp.concatenate([starts_row, jnp.stack([chip, core]).astype(starts_row.dtype)])
    (spread_f, spread_r), (gather_f, gather_r) = head_columns(heads_here)

    def shape(rows_, cols, dtype):
        return jax.ShapeDtypeStruct((rows_, cols), dtype)

    half_low = jax.ShapeDtypeStruct((chips, block_size, width), low)
    half_wide = jax.ShapeDtypeStruct((chips, block_size, width), wide)
    states = blocks * STATE
    lane_cols = channels + LANES
    (
        normed, conv_input, pre_active, act, out_f, cum, step_raw, state_f, decay_f, decay_r, weights,
        small, core_out, state_r,
    ) = by_pair(
        forward_kernel, blocks, "both",
        [
            (starts_row, "scalar"), (tokens_mine, "half"), (tokens_other, "half"),
            *((value, "whole") for value in pays),
            (spread_f, "whole"), (spread_r, "whole"),
        ],
        [
            (shape(length, width, low), "rows"), (shape(length, channels, low), "rows"),
            (shape(length, channels, wide), "rows"), (shape(length, channels, low), "rows"),
            (shape(length, inner_here, wide), "rows"),
            (shape(length, LANES, wide), "rows"), (shape(length, LANES, wide), "rows"),
            (shape(states, inner_here, wide), "rows"),
            (shape(8 * blocks, inner_here, wide), "rows"), (shape(8 * blocks, inner_here, wide), "rows"),
            (shape(width, lane_cols, low), "whole"), (shape(16, lane_cols, wide), "whole"),
            (shape(length, inner_here, wide), "back"), (shape(states, inner_here, wide), "back"),
        ],
        [
            ((8, channels), wide), ((STATE, inner_here), wide), ((length, inner_here), wide),
            ((length, 2 * LANES), low), ((length, 2 * STATE), low), ((states, inner_here), wide),
            ((8 * blocks, inner_here), wide),
        ],
        "forward", 20_000_000_000,
    )
    cotangent_mine, normed = lax.optimization_barrier((cotangent_mine, normed))
    cotangent_other = swap_core(cotangent_mine)
    gate, unscaled, unscaled_grad, own_sums, keep, send, gate_w = by_pair(
        output_kernel, blocks, "up",
        [
            (starts_row, "scalar"), (normed, "rows"), (core_out, "rows"), (cotangent_mine, "half"),
            (cotangent_other, "half"), (pay_late, "whole"), (small, "whole"),
        ],
        [
            (shape(length, inner_here, wide), "rows"), (shape(length, inner_here, low), "rows"),
            (shape(length, inner_here, wide), "rows"), (shape(8, length, wide), "lanes"),
            (half_low, "half"), (half_low, "half"), (shape(width, inner_here, low), "whole"),
        ],
        [((width, inner_here), low)],
        "outputs", 12_000_000_000,
    )
    other_sums = swap_core(own_sums)

    squares = (own_sums[0] + other_sums[0]).reshape(chips, 2, block_size)
    squares = lax.dynamic_index_in_dim(squares, core, 1, keepdims=False)
    gate_scale = lax.rsqrt(squares / (HEADS * HEADDIM) + 1e-05)
    out_delta = gate_scale[..., None] * (keep.astype(wide) + swap_core(send).astype(wide))
    out_delta, gate = lax.optimization_barrier((out_delta.astype(low), gate))
    out_moved = lax.all_to_all(out_delta, "chip", 0, 0)

    (total_grad, core_grad, gate_grad, row_sums, back_f, later_r, gain_grad, skip_grad) = by_pair(
        gate_back_kernel, blocks, "up",
        [
            (starts_row, "scalar"), (own_sums, "lanes"), (other_sums, "lanes"), (cotangent_mine, "half"),
            (cotangent_other, "half"), (out_f, "rows"), (core_out, "rows"),
            (act, "rows"), (gate, "rows"), (unscaled_grad, "rows"), (cum, "rows"), (decay_r, "rows"),
            (small, "whole"), (spread_f, "whole"), (spread_r, "whole"),
            (gather_f, "whole"), (gather_r, "whole"),
        ],
        [
            (shape(length, width, low), "rows"), (shape(length, inner_here, low), "rows"),
            (shape(length, inner_here, low), "rows"), (shape(length, LANES, wide), "rows"),
            (shape(states, inner_here, wide), "rows"), (shape(states, inner_here, wide), "rows"),
            (shape(8, inner_here, wide), "whole"), (shape(8, inner_here, wide), "whole"),
        ],
        [((STATE, inner_here), wide)],
        "gate_back", 12_000_000_000,
    )

    def weight_grad(left, right):
        result = lax.dot_general(left, right, (((0,), (0,)), ((), ())), preferred_element_type=wide)
        return result.astype(low)

    gate_grad, total_grad, out_moved = lax.optimization_barrier((gate_grad, total_grad, out_moved))
    out_delta = lax.all_gather(out_moved, "head").reshape(sequences, block_size, width)
    early_grad = jnp.concatenate(
        [weight_grad(normed, gate_grad), weight_grad(total_grad, unscaled)], axis=1
    ).reshape(chips, 2, rows, -1)
    early_grad, core_grad = lax.optimization_barrier((early_grad, core_grad))
    early_moved = lax.all_to_all(early_grad, "chip", 0, 0)
    rest_grad, keep, send, taps_grad, scalar_part = by_pair(
        chain_back_kernel, blocks, "down",
        [
            (starts_row, "scalar"), (core_grad, "rows"), (gate_grad, "rows"), (act, "rows"),
            (conv_input, "rows"), (pre_active, "rows"), (cum, "rows"), (step_raw, "rows"),
            (row_sums, "rows"), (state_f, "rows"), (state_f, "next"), (state_r, "rows"),
            (state_r, "last"), (back_f, "rows"), (later_r, "rows"), (decay_f, "rows"),
            (gate_w, "whole"), (weights, "whole"), (small, "whole"), (spread_f, "whole"),
            (spread_r, "whole"), (gather_f, "whole"), (gather_r, "whole"),
        ],
        [
            (shape(length, lane_cols, low), "rows"), (half_wide, "half"), (half_low, "half"),
            (shape(40, channels, wide), "whole"), (shape(16, LANES, wide), "whole"),
        ],
        [
            ((STATE, inner_here), wide), ((8, channels), wide), ((2 * block_size, inner_here), wide),
            ((2 * block_size, inner_here), wide), ((2 * block_size, channels), wide),
            ((2 * block_size, LANES), wide),
        ],
        "chain_back", 10_000_000_000,
    )

    norm_row = small[5 : 5 + width // channels_state, inner_here:channels].reshape(width)
    tokens_wide = tokens_mine.astype(wide)
    in_scale = lax.rsqrt(jnp.mean(tokens_wide * tokens_wide, axis=2, keepdims=True) + 1e-05)
    unit = tokens_wide * in_scale
    normed_grad = keep + swap_core(send).astype(wide)
    unit_grad = normed_grad * norm_row
    delta = in_scale * (unit_grad - unit * jnp.mean(unit_grad * unit, axis=2, keepdims=True))
    (
        delta, early_moved, normed_late, rest_grad, taps_grad, scalar_part, normed_grad,
    ) = lax.optimization_barrier(
        (
            delta.astype(low), early_moved, normed, rest_grad, taps_grad, scalar_part, normed_grad,
        )
    )
    delta = lax.all_to_all(delta, "chip", 0, 0)
    gathered = lax.all_gather(delta, "head").reshape(sequences, block_size, width)
    def between_cores(moved):
        total = jnp.sum(moved.astype(wide), axis=0).astype(low)
        mine = lax.dynamic_index_in_dim(total, core, 0, keepdims=False)
        got = swap_core(lax.dynamic_index_in_dim(total, 1 - core, 0, keepdims=False))
        return [jnp.where(first, mine, got), jnp.where(first, got, mine)]

    def group_lanes(value, at, i):
        return value[:, at + i * group_inner : at + (i + 1) * group_inner]

    early_moved, out_delta = lax.optimization_barrier((early_moved, out_delta))
    early = between_cores(early_moved)
    early = jnp.stack(
        [
            jnp.concatenate([group_lanes(v, 0, i), group_lanes(v, inner_here, i)], axis=1)
            for v in early
            for i in range(groups)
        ]
    )
    early, normed_late, rest_grad = lax.optimization_barrier((early, normed_late, rest_grad))
    early = shifted_sum(early, "head")
    norm_grad = jnp.sum(normed_grad * unit, axis=(0, 1))

    taps_grad = jnp.sum(taps_grad.reshape(reach + 1, 8, channels), axis=1)
    scalar_part = jnp.sum(scalar_part.reshape(2, 8, LANES), axis=1)
    skip_part = jnp.sum(skip_grad.reshape(8, heads_here, HEADDIM), axis=(0, 2))
    skip_part = jnp.pad(jnp.repeat(skip_part, 2)[None], ((0, 0), (0, LANES - 2 * heads_here)))
    lanes_value = jnp.concatenate(
        [taps_grad[:, :inner_here], jnp.sum(gain_grad, axis=0, keepdims=True)], axis=0
    )
    lanes_state = jnp.concatenate(
        [taps_grad[:, inner_here:], norm_grad.reshape(-1, channels_state)], axis=0
    )
    lanes_step = jnp.concatenate([scalar_part, skip_part], axis=0)
    extra = jnp.concatenate(
        [
            jnp.pad(lanes_value, ((0, 16 - lanes_value.shape[0]), (0, 0))),
            jnp.pad(lanes_state, ((0, 16 - lanes_state.shape[0]), (0, 0))),
            jnp.pad(lanes_step, ((0, 16 - lanes_step.shape[0]), (0, 0))),
        ],
        axis=1,
    ).astype(low)
    extra, early = lax.optimization_barrier((extra, early))
    small_sum = extra.astype(wide)
    for side in range(1, chips):
        small_sum = small_sum + swap_chip(extra, side).astype(wide)
    small_low = small_sum.astype(low)
    for k in range(1, planes):
        moved = lax.ppermute(small_low, "head", [(i, (i + k) % planes) for i in range(planes)])
        small_sum = small_sum + moved.astype(wide)
    small_other = swap_core(small_sum)
    of_heads = jnp.where(plane // groups == core, small_sum, small_other)
    step_lanes = lax.dynamic_slice_in_dim(of_heads[:3, channels:], step_at, 2 * group, 1)
    lanes = lax.dynamic_slice_in_dim(
        of_heads[:, :inner_here], (plane % groups) * group_inner, group_inner, 1
    ).reshape(16, group, HEADDIM)
    lanes = lax.dynamic_slice_in_dim(lanes, part * seq, part, 2)
    value_conv_out = lanes[: reach + 1].transpose(2, 1, 0)
    gate_gain_out = lanes[reach + 1].transpose(1, 0)
    state_lanes = small_sum[:, inner_here:channels] + small_other[:, inner_here:channels]
    conv_at = state_part * seq + (state_part // planes) * plane
    state_conv_out = lax.dynamic_slice_in_dim(
        state_lanes[: reach + 1], conv_at, state_part // planes, 1
    ).T
    norm_sum = state_lanes[reach + 1 :][: width // channels_state].reshape(width)
    norm_gain_out = lax.dynamic_slice_in_dim(norm_sum, rows * seq, rows, 0)
    step_bias_out = step_lanes[0].reshape(group, 2).T
    decay_log_out = jnp.sum(step_lanes[1].reshape(group, 2), axis=1)
    skip_out = step_lanes[2].reshape(group, 2)[:, 0]

    late_grad = weight_grad(normed_late, rest_grad).reshape(chips, 2, rows, lane_cols)
    late_grad, delta, early = lax.optimization_barrier((late_grad, delta, early))
    late_moved = lax.all_to_all(late_grad, "chip", 0, 0)
    output = tokens.astype(wide) + out_delta.astype(wide)

    late = between_cores(late_moved)
    state_sum = late[0][:, inner_here:channels].astype(wide) + late[1][:, inner_here:channels].astype(wide)
    state_sum = state_sum.astype(low).reshape(planes, -1, group_inner + LANES)
    state_rows = state_sum.shape[1]
    late = jnp.stack(
        [
            jnp.concatenate(
                [
                    jnp.concatenate([group_lanes(late[which], 0, i), late[which][:, channels:]], axis=1),
                    jnp.pad(state_sum[which * groups + i], ((0, -state_rows % 16), (0, 0))),
                ],
                axis=0,
            )
            for which in range(2)
            for i in range(groups)
        ]
    )
    late, gathered = lax.optimization_barrier((late, gathered))
    input_gradient = out_cotangent + gathered.astype(wide)
    late = jnp.sum(lax.all_to_all(late, "head", 0, 0).astype(wide), axis=0)
    late_steps = lax.dynamic_slice_in_dim(late[:rows, group_inner:], step_at, 2 * group, 1)
    in_weight_out = jnp.concatenate(
        [
            early[:, :group_inner].reshape(rows, group, HEADDIM),
            late[:rows, :group_inner].reshape(rows, group, HEADDIM),
            late_steps.reshape(rows, group, 2),
        ],
        axis=2,
    )
    out_weight_out = early[:, group_inner:].reshape(rows, group, HEADDIM)
    state_weight_out = late[rows : rows + state_rows].reshape(-1, channels_state)
    return (
        output,
        input_gradient,
        in_weight_out,
        state_weight_out,
        state_conv_out,
        out_weight_out,
        value_conv_out,
        norm_gain_out,
        gate_gain_out,
        step_bias_out,
        decay_log_out,
        skip_out,
    )


def solution(mesh):
    devices_seq, planes = mesh.devices.shape
    seq, plan = "seq", split_plan
    if devices_seq % 2 == 0 and planes % 2 == 0 and devices_seq // 2 * planes == CHIP_SEQUENCES:
        shape = (devices_seq // 2, 2, planes)
        mesh = Mesh(mesh.devices.reshape(shape), ("chip", "core", "head"))
        seq, plan = ("chip", "core"), chip_plan
    both = seq + ("head",) if isinstance(seq, tuple) else (seq, "head")
    return jax.shard_map(
        plan,
        mesh=mesh,
        in_specs=(
            P(None, seq, None),
            P(),
            P(seq, "head", None),
            P(seq, None),
            P(seq, None),
            P(seq, "head", None),
            P(seq, "head", None),
            P(seq),
            P(seq, "head"),
            P(None, "head"),
            P("head"),
            P("head"),
            P(None, seq, None),
        ),
        out_specs=(
            P(None, seq, None),
            P(None, seq, None),
            P(seq, "head", None),
            P(both, None),
            P(both, None),
            P(seq, "head", None),
            P(seq, "head", None),
            P(seq),
            P(seq, "head"),
            P(None, "head"),
            P("head"),
            P("head"),
        ),
        check_vma=False,
    )
```

```python
import jax
import jax.numpy as jnp
from jax import lax
from jax.experimental import pallas as pl
from jax.experimental.pallas import tpu as pltpu
from jax.sharding import Mesh, PartitionSpec as P

HEADS = 24
HEADDIM = 64
STATE = 64
CHIP_SEQUENCES = 16


def from_behind(value, axis, by):
    devices = lax.axis_size(axis)
    pairs = [(i, i + by) for i in range(devices) if 0 <= i + by < devices]
    return lax.ppermute(value, axis, pairs)


def entering(value, axis, join, neutral, backward):
    count, mine = (lax.axis_size(axis), lax.axis_index(axis))
    pieces = jax.tree.map(lambda part: lax.all_gather(part, axis), value)
    if backward:
        pieces = jax.tree.map(lambda part: part[::-1], pieces)
        mine = count - 1 - mine
    running = jax.tree.map(
        lambda part, zero: jnp.full_like(part, 0) + jnp.asarray(zero, part.dtype), value, neutral
    )

    def step(position, running):
        longer = join(running, jax.tree.map(lambda part: part[position], pieces))
        return jax.tree.map(lambda new, old: jnp.where(position < mine, new, old), longer, running)

    return lax.fori_loop(0, count - 1, step, running)


def affine(earlier, later):
    return (earlier[0] * later[0], later[0][..., None, None] * earlier[1] + later[1])


def document_numbers(starts, first_position, count, block_size):
    blocks = starts.shape[1]
    begins = jnp.arange(blocks, dtype=jnp.int32)[None, :] * block_size + starts
    valid = starts < block_size
    places = first_position + jnp.arange(count, dtype=jnp.int32)
    hits = (begins[:, None, :] <= places[None, :, None]) & valid[:, None, :]
    return jnp.sum(hits.astype(jnp.int32), axis=2)


def running_sum(value):
    length, shift = value.shape[-1], 1
    while shift < length:
        pad = [(0, 0)] * (value.ndim - 1) + [(shift, 0)]
        value = value + jnp.pad(value[..., : length - shift], pad)
        shift *= 2
    return value


def chain_forward(readout, intake, values, log_decay, step_size, flags):
    block_size = readout.shape[1]
    segment = running_sum(flags)
    decay_sum = running_sum(log_decay)
    scores = jnp.einsum("mtn,mjn->mtj", readout, intake, preferred_element_type=jnp.float32)
    order = jnp.arange(block_size)
    mask = ((order[:, None] > order[None, :])[None] & (segment[:, :, None] == segment[:, None, :]))[
        :, None
    ]
    gap = jnp.where(mask, decay_sum[:, :, :, None] - decay_sum[:, :, None, :], 0.0)
    decay_table = jnp.where(mask, jnp.exp(gap), 0.0)
    mixing = (scores[:, None] * decay_table * step_size[:, :, None, :]).astype(jnp.bfloat16)
    inner = jnp.einsum("mhtj,mjhp->mthp", mixing, values, preferred_element_type=jnp.float32)
    tail_factor = (
        jnp.exp(decay_sum[:, :, -1:] - decay_sum) * (segment == segment[:, -1:])[:, None, :]
    )
    scaled_intake = (
        (tail_factor * step_size)[..., None] * intake[:, None].astype(jnp.float32)
    ).astype(jnp.bfloat16)
    local_state = jnp.einsum(
        "mhjn,mjhp->mhnp", scaled_intake, values, preferred_element_type=jnp.float32
    )
    block_decay = jnp.exp(decay_sum[:, :, -1]) * (segment[:, -1] == 0)[:, None]
    head_scale = jnp.exp(decay_sum) * (segment == 0)[:, None, :]
    saved = (scores, decay_table, mixing, tail_factor, scaled_intake, head_scale)
    return (inner, local_state, block_decay, saved)


def chain_finish(inner, readout, state_in, head_scale):
    state_low = state_in.astype(jnp.bfloat16)
    carried = jnp.einsum("mtn,mhnp->mthp", readout, state_low, preferred_element_type=jnp.float32)
    return (inner + jnp.swapaxes(head_scale, 1, 2)[..., None] * carried, carried, state_low)


def chain_back_state(grad_out, readout, carried, state_low, head_scale):
    grad_wide = grad_out.astype(jnp.float32)
    carried_grad = (jnp.swapaxes(head_scale, 1, 2)[..., None] * grad_wide).astype(jnp.bfloat16)
    state_in_grad = jnp.einsum(
        "mtn,mthp->mhnp", readout, carried_grad, preferred_element_type=jnp.float32
    )
    readout_grad = jnp.einsum(
        "mthp,mhnp->mtn", carried_grad, state_low, preferred_element_type=jnp.float32
    )
    sum_grad = jnp.swapaxes(jnp.sum(grad_wide * carried, axis=3), 1, 2) * head_scale
    return (state_in_grad, readout_grad, sum_grad)


def chain_back_rest(
    grad_out,
    readout,
    intake,
    values,
    step_size,
    state_in,
    later,
    block_decay,
    saved,
    readout_grad,
    sum_grad,
):
    scores, decay_table, mixing, tail_factor, scaled_intake, head_scale = saved
    later_low = later.astype(jnp.bfloat16)
    scaled_grad = jnp.einsum(
        "mjhp,mhnp->mhjn", values, later_low, preferred_element_type=jnp.float32
    )
    values_grad = jnp.einsum(
        "mhjn,mhnp->mjhp", scaled_intake, later_low, preferred_element_type=jnp.float32
    )
    tail_grad = jnp.einsum("mhjn,mjn->mhj", scaled_grad, intake.astype(jnp.float32))
    intake_grad = jnp.einsum("mhjn,mhj->mjn", scaled_grad, tail_factor * step_size)
    step_grad = tail_grad * tail_factor
    tail_term = tail_grad * tail_factor * step_size
    decay_grad = jnp.sum(later * state_in, axis=(2, 3)) * block_decay
    sum_grad = (sum_grad - tail_term).at[:, :, -1].add(jnp.sum(tail_term, axis=2) + decay_grad)
    mixing_grad = jnp.einsum(
        "mthp,mjhp->mhtj", grad_out, values, preferred_element_type=jnp.float32
    )
    values_grad = values_grad + jnp.einsum(
        "mhtj,mthp->mjhp", mixing, grad_out, preferred_element_type=jnp.float32
    )
    through = mixing_grad * decay_table
    scores_grad = jnp.sum(through * step_size[:, :, None, :], axis=1).astype(jnp.bfloat16)
    readout_grad = readout_grad + jnp.einsum(
        "mtj,mjn->mtn", scores_grad, intake, preferred_element_type=jnp.float32
    )
    intake_grad = intake_grad + jnp.einsum(
        "mtj,mtn->mjn", scores_grad, readout, preferred_element_type=jnp.float32
    )
    kernel = through * scores[:, None]
    step_grad = step_grad + jnp.sum(kernel, axis=2)
    weighted = kernel * step_size[:, :, None, :]
    sum_grad = sum_grad + jnp.sum(weighted, axis=3) - jnp.sum(weighted, axis=2)
    log_grad = jnp.flip(running_sum(jnp.flip(sum_grad, 2)), 2)
    return (values_grad, readout_grad, intake_grad, step_grad, log_grad)


def split_plan(
    tokens,
    starts,
    in_weight,
    state_weight,
    state_conv,
    out_weight,
    value_conv,
    norm_gain,
    gate_gain,
    step_bias,
    decay_log,
    skip,
    out_cotangent,
):
    sequences, block_size, width = tokens.shape
    place = lax.axis_index("seq")
    devices_seq = lax.axis_size("seq")
    in_weights, state_weights, state_taps, out_weights, value_taps, norm_whole, gate_whole = (
        lax.all_gather(in_weight, "seq", axis=0, tiled=True),
        lax.all_gather(state_weight, "seq", axis=0, tiled=True),
        lax.all_gather(state_conv, "seq", axis=0, tiled=True),
        lax.all_gather(out_weight, "seq", axis=0, tiled=True),
        lax.all_gather(value_conv, "seq", axis=0, tiled=True),
        lax.all_gather(norm_gain, "seq", axis=0, tiled=True),
        lax.all_gather(gate_gain, "seq", axis=0, tiled=True),
    )
    heads_here = in_weight.shape[1]
    value_width = heads_here * HEADDIM
    reach = state_conv.shape[1] - 1
    edge = reach - 1
    numbers = document_numbers(starts, place * block_size - edge, block_size + 2 * edge, block_size)
    lag_masks = jnp.stack(
        [
            numbers[:, edge:] == numbers[:, edge - lag : block_size + 2 * edge - lag]
            for lag in range(reach)
        ],
        axis=2,
    ).astype(jnp.float32)
    first = (
        numbers[:, edge : edge + block_size] != numbers[:, edge - 1 : edge + block_size - 1]
    ).astype(jnp.int32)
    positions = place * block_size + jnp.arange(block_size, dtype=jnp.int32)
    ending = (positions == devices_seq * block_size - 1)[None, :]
    last = (
        (numbers[:, edge + 1 : edge + block_size + 1] != numbers[:, edge : edge + block_size])
        | ending
    ).astype(jnp.int32)
    tokens_wide = tokens.astype(jnp.float32)
    in_scale = lax.rsqrt(jnp.mean(tokens_wide * tokens_wide, axis=2, keepdims=True) + 1e-05)
    unit = tokens_wide * in_scale
    norm_wide = norm_whole.astype(jnp.float32)
    normed = (unit * norm_wide).astype(jnp.bfloat16)
    projected = jnp.einsum("mtd,dhk->mthk", normed, in_weights, preferred_element_type=jnp.float32)
    state_proj = jnp.einsum(
        "mtd,dn->mtn", normed, state_weights, preferred_element_type=jnp.float32
    )
    gate = projected[..., :HEADDIM]
    step_raw = projected[..., 2 * HEADDIM :]
    conv_input = jnp.concatenate(
        [
            projected[..., HEADDIM : 2 * HEADDIM].reshape(sequences, block_size, value_width),
            state_proj,
        ],
        axis=2,
    ).astype(jnp.bfloat16)
    channels = conv_input.shape[2]
    halo_rows = from_behind(conv_input[:, block_size - edge :], "seq", 1)
    extended = jnp.concatenate([halo_rows, conv_input], axis=1)
    taps = jnp.concatenate(
        [jnp.transpose(value_taps, (1, 0, 2)).reshape(value_width, reach + 1), state_taps], axis=0
    ).astype(jnp.float32)
    pre_active = jnp.broadcast_to(taps[:, reach], (sequences, block_size, channels))
    for lag in range(reach):
        pre_active = (
            pre_active
            + taps[:, lag]
            * extended[:, edge - lag : edge - lag + block_size]
            * lag_masks[:, :block_size, lag, None]
        )
    active_sigma = jax.nn.sigmoid(pre_active)
    activated = (pre_active * active_sigma).astype(jnp.bfloat16)
    values = activated[..., :value_width].reshape(sequences, block_size, heads_here, HEADDIM)
    intake_forward = activated[..., value_width : value_width + STATE]
    readout_forward = activated[..., value_width + STATE : value_width + 2 * STATE]
    intake_reverse = jnp.flip(activated[..., value_width + 2 * STATE : value_width + 3 * STATE], 1)
    readout_reverse = jnp.flip(activated[..., value_width + 3 * STATE :], 1)
    values_reversed = jnp.flip(values, 1)
    rate = jnp.exp(decay_log)
    bias_here = jnp.transpose(step_bias)[None, None]
    step_all = jax.nn.softplus(step_raw + bias_here)
    step_forward = jnp.transpose(step_all[..., 0], (0, 2, 1))
    step_reverse = jnp.flip(jnp.transpose(step_all[..., 1], (0, 2, 1)), 2)
    log_forward = -step_forward * rate[None, :, None]
    log_reverse = -step_reverse * rate[None, :, None]
    inner_forward, local_forward, decay_forward, saved_forward = chain_forward(
        readout_forward, intake_forward, values, log_forward, step_forward, first
    )
    inner_reverse, local_reverse, decay_reverse, saved_reverse = chain_forward(
        readout_reverse,
        intake_reverse,
        values_reversed,
        log_reverse,
        step_reverse,
        jnp.flip(last, 1),
    )
    identity = (jnp.ones_like(decay_forward), jnp.zeros_like(local_forward))
    state_forward = entering((decay_forward, local_forward), "seq", affine, identity, False)[1]
    state_reverse = entering((decay_reverse, local_reverse), "seq", affine, identity, True)[1]
    out_forward, carried_forward, state_low_forward = chain_finish(
        inner_forward, readout_forward, state_forward, saved_forward[5]
    )
    out_reverse, carried_reverse, state_low_reverse = chain_finish(
        inner_reverse, readout_reverse, state_reverse, saved_reverse[5]
    )
    core = (
        out_forward
        + jnp.flip(out_reverse, 1)
        + skip[None, None, :, None] * values.astype(jnp.float32)
    )
    gate_sigma = jax.nn.sigmoid(gate)
    gated = core * gate * gate_sigma
    gate_gains = jnp.transpose(gate_whole).astype(jnp.float32)
    unscaled = (gated * gate_gains).astype(jnp.bfloat16)
    squares = jnp.sum(gated * gated, axis=(2, 3))
    partial_value = jnp.einsum(
        "mthp,dhp->mtd", unscaled, out_weights, preferred_element_type=jnp.float32
    )
    pre_out, square_sum = lax.psum((partial_value, squares), "head")
    inner_width = HEADS * HEADDIM
    gate_scale = lax.rsqrt(square_sum / inner_width + 1e-05)
    output = tokens_wide + gate_scale[..., None] * pre_out
    total_grad = (gate_scale[..., None] * out_cotangent).astype(jnp.bfloat16)
    unscaled_grad = jnp.einsum(
        "mtd,dhp->mthp", total_grad, out_weights, preferred_element_type=jnp.float32
    )
    out_weight_grad = jnp.einsum(
        "mtd,mthp->dhp", total_grad, unscaled, preferred_element_type=jnp.float32
    )
    scale_grad = jnp.sum(out_cotangent * pre_out, axis=2)
    square_grad = -0.5 * scale_grad * gate_scale**3 / inner_width
    gated_grad = unscaled_grad * gate_gains + 2.0 * gated * square_grad[..., None, None]
    gate_gain_grad = jnp.transpose(jnp.sum(unscaled_grad * gated, axis=(0, 1)))
    core_grad = (gated_grad * gate * gate_sigma).astype(jnp.bfloat16)
    gate_grad = gated_grad * core * gate_sigma * (1.0 + gate * (1.0 - gate_sigma))
    skip_grad = jnp.sum(core_grad.astype(jnp.float32) * values.astype(jnp.float32), axis=(0, 1, 3))
    core_reversed = jnp.flip(core_grad, 1)
    state_grad_forward, readout_grad_forward, sum_grad_forward = chain_back_state(
        core_grad, readout_forward, carried_forward, state_low_forward, saved_forward[5]
    )
    state_grad_reverse, readout_grad_reverse, sum_grad_reverse = chain_back_state(
        core_reversed, readout_reverse, carried_reverse, state_low_reverse, saved_reverse[5]
    )
    later_forward = entering((decay_forward, state_grad_forward), "seq", affine, identity, True)[1]
    later_reverse = entering((decay_reverse, state_grad_reverse), "seq", affine, identity, False)[1]
    (
        values_grad_forward,
        readout_grad_forward,
        intake_grad_forward,
        step_grad_forward,
        log_grad_forward,
    ) = chain_back_rest(
        core_grad,
        readout_forward,
        intake_forward,
        values,
        step_forward,
        state_forward,
        later_forward,
        decay_forward,
        saved_forward,
        readout_grad_forward,
        sum_grad_forward,
    )
    (
        values_grad_reverse,
        readout_grad_reverse,
        intake_grad_reverse,
        step_grad_reverse,
        log_grad_reverse,
    ) = chain_back_rest(
        core_reversed,
        readout_reverse,
        intake_reverse,
        values_reversed,
        step_reverse,
        state_reverse,
        later_reverse,
        decay_reverse,
        saved_reverse,
        readout_grad_reverse,
        sum_grad_reverse,
    )
    values_grad = (
        values_grad_forward
        + jnp.flip(values_grad_reverse, 1)
        + skip[None, None, :, None] * core_grad.astype(jnp.float32)
    )
    step_total_forward = step_grad_forward - rate[None, :, None] * log_grad_forward
    step_total_reverse = jnp.flip(step_grad_reverse - rate[None, :, None] * log_grad_reverse, 2)
    decay_log_grad = jnp.sum(log_grad_forward * log_forward, axis=(0, 2)) + jnp.sum(
        log_grad_reverse * log_reverse, axis=(0, 2)
    )
    step_total = jnp.stack(
        [
            jnp.transpose(step_total_forward, (0, 2, 1)),
            jnp.transpose(step_total_reverse, (0, 2, 1)),
        ],
        axis=3,
    )
    raw_grad = step_total * jax.nn.sigmoid(step_raw + bias_here)
    step_bias_grad = jnp.transpose(jnp.sum(raw_grad, axis=(0, 1)))
    state_grads = jnp.concatenate(
        [
            intake_grad_forward,
            readout_grad_forward,
            jnp.flip(intake_grad_reverse, 1),
            jnp.flip(readout_grad_reverse, 1),
        ],
        axis=2,
    )
    active_grad = jnp.concatenate(
        [values_grad.reshape(sequences, block_size, value_width), state_grads], axis=2
    )
    pre_grad = active_grad * active_sigma * (1.0 + pre_active * (1.0 - active_sigma))
    following = from_behind(pre_grad[:, :edge], "seq", -1)
    grad_extended = jnp.concatenate([pre_grad, following], axis=1)
    conv_input_grad = jnp.zeros((sequences, block_size, channels), jnp.float32)
    tap_grads = []
    for lag in range(reach):
        conv_input_grad = (
            conv_input_grad
            + taps[:, lag]
            * grad_extended[:, lag : lag + block_size]
            * lag_masks[:, lag : lag + block_size, lag, None]
        )
        tap_grads.append(
            jnp.sum(
                pre_grad
                * extended[:, edge - lag : edge - lag + block_size]
                * lag_masks[:, :block_size, lag, None],
                axis=(0, 1),
            )
        )
    tap_grads.append(jnp.sum(pre_grad, axis=(0, 1)))
    taps_grad = jnp.stack(tap_grads, axis=1)
    value_conv_grad = jnp.transpose(
        taps_grad[:value_width].reshape(heads_here, HEADDIM, reach + 1), (1, 0, 2)
    )
    state_conv_grad = taps_grad[value_width:]
    proj_grad = jnp.concatenate(
        [
            gate_grad,
            conv_input_grad[..., :value_width].reshape(sequences, block_size, heads_here, HEADDIM),
            raw_grad,
        ],
        axis=3,
    ).astype(jnp.bfloat16)
    state_proj_grad = conv_input_grad[..., value_width:].astype(jnp.bfloat16)
    normed_part = jnp.einsum(
        "mthk,dhk->mtd", proj_grad, in_weights, preferred_element_type=jnp.float32
    )
    normed_part = normed_part + jnp.einsum(
        "mtn,dn->mtd", state_proj_grad, state_weights, preferred_element_type=jnp.float32
    )
    normed_grad = lax.psum(normed_part, "head")
    in_weight_grad = jnp.einsum(
        "mtd,mthk->dhk", normed, proj_grad, preferred_element_type=jnp.float32
    )
    state_weight_grad = jnp.einsum(
        "mtd,mtn->dn", normed, state_proj_grad, preferred_element_type=jnp.float32
    )
    norm_gain_grad = jnp.sum(normed_grad * unit, axis=(0, 1))
    unit_grad = normed_grad * norm_wide
    input_gradient = out_cotangent + in_scale * (
        unit_grad - unit * jnp.mean(unit_grad * unit, axis=2, keepdims=True)
    )
    in_weight_out, out_weight_out, value_conv_out, norm_gain_out, gate_gain_out = (
        lax.psum_scatter(in_weight_grad, "seq", scatter_dimension=0, tiled=True),
        lax.psum_scatter(out_weight_grad, "seq", scatter_dimension=0, tiled=True),
        lax.psum_scatter(value_conv_grad, "seq", scatter_dimension=0, tiled=True),
        lax.psum_scatter(norm_gain_grad, "seq", scatter_dimension=0, tiled=True),
        lax.psum_scatter(gate_gain_grad, "seq", scatter_dimension=0, tiled=True),
    )
    state_weight_out, state_conv_out = (
        lax.psum_scatter(state_weight_grad, ("seq", "head"), scatter_dimension=0, tiled=True),
        lax.psum_scatter(state_conv_grad, ("seq", "head"), scatter_dimension=0, tiled=True),
    )
    step_bias_out, decay_log_out, skip_out = lax.psum(
        (step_bias_grad, decay_log_grad, skip_grad), "seq"
    )
    return (
        output,
        input_gradient,
        in_weight_out,
        state_weight_out,
        state_conv_out,
        out_weight_out,
        value_conv_out,
        norm_gain_out,
        gate_gain_out,
        step_bias_out,
        decay_log_out,
        skip_out,
    )


LANES = 128
WIDE, LOW = jnp.float32, jnp.bfloat16
FAR = -1e30


def dot(left, right):
    return jnp.dot(left, right, preferred_element_type=WIDE)


def dot_nt(left, right):
    return lax.dot_general(left, right, (((1,), (1,)), ((), ())), preferred_element_type=WIDE)


def halves(value):
    high = value.astype(LOW)
    return jnp.concatenate([high, (value - high.astype(WIDE)).astype(LOW)], axis=1)


def iota(shape, axis):
    return lax.broadcasted_iota(jnp.int32, shape, axis)


def head_columns(heads):
    row = jnp.arange(2 * LANES)[:, None] % LANES
    head = jnp.arange(heads * HEADDIM)[None, :] // HEADDIM
    spread_both = [(row == 2 * head + d).astype(LOW) for d in range(2)]
    gather_both = [jnp.concatenate([s[:LANES].T, s[:LANES].T], axis=0) for s in spread_both]
    return spread_both, gather_both


def steps_of(raw, bias):
    shifted = raw + bias
    small = jnp.exp(-jnp.abs(shifted))
    exponent = jnp.exp(jnp.minimum(shifted, 0.0))
    step = jnp.where(
        shifted < -15.0, exponent, jnp.maximum(shifted, 0.0) + jnp.log1p(small)
    )
    sigma = exponent / (1.0 + small)
    ratio = jnp.where(shifted < -15.0, 1.0, sigma / step)
    return step, sigma, ratio


def odd_lanes(shape):
    return iota(shape, 1) % 2 == 1


def running_sums(value, flip):
    size = value.shape[0]
    row, col = iota((2 * size, size), 0), iota((2 * size, size), 1)
    keep = jnp.logical_or(
        jnp.logical_and(row < size, row >= col), jnp.logical_and(row >= size, row - size <= col)
    )
    keep = keep.astype(WIDE).astype(LOW)
    high = value.astype(LOW)
    rest = value - high.astype(WIDE)
    middle = rest.astype(LOW)
    last = (rest - middle.astype(WIDE)).astype(LOW)
    sums = dot(keep, high) + dot(keep, middle) + dot(keep, last)
    odd = odd_lanes(value.shape)
    if flip:
        return jnp.where(odd, sums[:size], sums[size:])
    return jnp.where(odd, sums[size:], sums[:size])


def start_masks(starts, block, blocks, shape):
    size = shape[0]
    start = starts[block]
    following = starts[jnp.minimum(block + 1, blocks - 1)]
    none = start >= size
    ended = jnp.logical_or(block == blocks - 1, following == 0)
    row, odd = iota(shape, 0), odd_lanes(shape)
    after = row >= start
    tail_forward = jnp.logical_or(after, none)
    tail_reverse = jnp.logical_or(jnp.logical_not(after), jnp.logical_or(none, start == 0))
    head_forward = jnp.logical_not(after)
    head_reverse = jnp.logical_and(jnp.logical_or(after, none), jnp.logical_not(ended))
    tail = jnp.where(odd, tail_reverse.astype(WIDE), tail_forward.astype(WIDE))
    head = jnp.where(odd, head_reverse.astype(WIDE), head_forward.astype(WIDE))
    whole_reverse = jnp.logical_and(jnp.logical_or(none, start == 0), jnp.logical_not(ended))
    whole = jnp.where(
        odd[:8],
        jnp.where(whole_reverse, 1.0, 0.0),
        jnp.where(none, 1.0, 0.0),
    )
    return tail, head, whole


def chain_last(cum):
    return jnp.where(odd_lanes((1, cum.shape[1])), cum[:1], cum[-1:])


def table_bias(starts, block, size):
    row, col = iota((size, size), 0), iota((size, size), 1)
    start = starts[block]
    same = (row >= start) == (col >= start)
    return jnp.where(jnp.logical_and(same, row != col), 0.0, FAR)


def lane_half(size, second):
    return ((iota((size, LANES), 1) >= HEADDIM) == second).astype(WIDE).astype(LOW)


def block_diagonal(pair):
    size = pair.shape[0]
    return jnp.concatenate([pair * lane_half(size, False), pair * lane_half(size, True)], axis=0)


def silu_slope(value, sigma):
    return sigma * (1.0 + value * (1.0 - sigma))


def below(value):
    return jnp.concatenate([jnp.zeros_like(value), value], axis=0)


def above(value):
    return jnp.concatenate([value, jnp.zeros_like(value)], axis=0)


def rows_sum(value):
    total = value[:8]
    for at in range(8, value.shape[0], 8):
        total = total + value[at : at + 8]
    return total


def in_order(starts, mine, other):
    first = starts[starts.shape[0] - 1] == 0
    return jnp.concatenate(
        [jnp.where(first, mine[...], other[...]), jnp.where(first, other[...], mine[...])], axis=0
    )


def keep_own(starts, value, keep, send):
    first = starts[starts.shape[0] - 1] == 0
    size = value.shape[0] // 2
    keep[...] = jnp.where(first, value[:size], value[size:]).astype(keep.dtype)
    send[...] = jnp.where(first, value[size:], value[:size]).astype(send.dtype)


def document_of(starts, pair, blocks, size, place):
    far = 4 * size
    first, second = starts[2 * pair], starts[2 * pair + 1]
    before = starts[jnp.maximum(2 * pair - 1, 0)]
    behind = starts[jnp.minimum(2 * pair + 2, blocks - 1)]
    first = jnp.where(first < size, first, far)
    second = jnp.where(second < size, second + size, far)
    behind = jnp.where(behind < size, behind + 2 * size, far)
    before = jnp.where(before < size, before - size, -far)
    number = (place >= first).astype(jnp.int32) + (place >= second).astype(jnp.int32)
    return number + (place >= behind).astype(jnp.int32) + (place >= before).astype(jnp.int32)


def skip_lanes(small, spread):
    parts = dot(small[:, small.shape[1] - LANES :].astype(LOW), spread[:LANES])
    return parts[6:7] + parts[7:8] + parts[8:9]


def step_rows(small, heads):
    part = small[:, small.shape[1] - LANES :]
    bias = part[0:1] + part[1:2] + part[2:3]
    rate = jnp.exp(part[3:4] + part[4:5] + part[5:6])
    return bias, jnp.where(iota((1, LANES), 1) < 2 * heads, rate, 0.0)


def shard_rows(starts, side, index, rows):
    chip, core = starts[starts.shape[0] - 2], starts[starts.shape[0] - 1]
    seq = 2 * jnp.bitwise_xor(chip, side) + (core if index == 0 else 1 - core)
    return pl.ds(pl.multiple_of(seq * rows, 32), rows)


def forward_kernel(
    starts, mine, other, pay, pay_x, pay_y, pay_far, pay_far_other, spread_f, spread_r,
    normed_o, conv_o, pre_o, act_o, out_f_o, cum_o, raw_o, state_f_o, decay_f_o, decay_r_o,
    weights_o, small_o, core_o, state_r_o,
    tail_s, state_s, sum_s, head_s, read_s, local_s, decay_s,
):
    step_at = pl.program_id(0)
    pairs = pl.num_programs(0) // 2
    blocks = 2 * pairs
    size = mine.shape[0]
    inner = out_f_o.shape[1]
    channels = inner + 4 * STATE
    reach = 4

    @pl.when(step_at == 0)
    def _():
        tail_s[...] = jnp.zeros_like(tail_s)
        state_s[...] = jnp.zeros_like(state_s)
        rows = pay.shape[1] - 16
        shards = [pay.at[0], pay.at[1], pay_x.at[0], pay_x.at[1], pay_y.at[0], pay_y.at[1]]
        shards = shards + [pay_far, pay_far_other]
        total = jnp.zeros(small_o.shape, WIDE)
        for i, shard in enumerate(shards):
            weights_o[shard_rows(starts, i // 2, i % 2, rows), :] = shard[:rows, :]
            total = total + shard[rows:, :].astype(WIDE)
        small_o[...] = total

    @pl.when(step_at < pairs)
    def _():
        pair = step_at
        small = small_o[...]
        bias_row, rate_row = step_rows(small, inner // HEADDIM)
        skip_row = skip_lanes(small, spread_f)
        norm_row = jnp.concatenate([small[i : i + 1, inner:channels] for i in (5, 6, 7)], axis=1)
        taps = small[:8, :channels]
        wide = in_order(starts, mine, other).astype(WIDE)
        scale = lax.rsqrt(jnp.mean(wide * wide, axis=1, keepdims=True) + 1e-05)
        normed = (wide * scale * norm_row).astype(LOW)
        normed_o[...] = normed
        raw = dot(normed, weights_o[:, channels:])
        raw_o[...] = raw

        step, _, _ = steps_of(raw, bias_row)
        log_decay = -step * rate_row
        subs = [slice(0, size), slice(size, 2 * size)]
        cums = [running_sums(log_decay[rows], False) for rows in subs]
        cum = jnp.concatenate(cums, axis=0)
        cum_o[...] = cum
        late = cum - jnp.log(step)
        masks = [start_masks(starts, 2 * pair + sub, blocks, (size, LANES)) for sub in range(2)]
        last = [jnp.broadcast_to(chain_last(value), (size, LANES)) for value in cums]
        tail = jnp.exp(jnp.concatenate(last, axis=0) - late)
        tail = halves(tail * jnp.concatenate([mask[0] for mask in masks], axis=0))
        head = halves(jnp.exp(cum) * jnp.concatenate([mask[1] for mask in masks], axis=0))
        decay = [jnp.exp(value[:8]) * mask[2] for value, mask in zip(last, masks)]
        decay = halves(jnp.concatenate(decay, axis=0))
        decay_f, decay_r = dot(decay, spread_f[...]), dot(decay, spread_r[...])
        decay_f_o[...], decay_r_o[...] = decay_f, decay_r

        row = iota((2 * size, LANES), 0)
        number = document_of(starts, pair, blocks, size, row)
        lag_masks = [
            (number == document_of(starts, pair, blocks, size, row - lag)).astype(WIDE)
            for lag in range(1, reach)
        ]
        for chunk in range(0, channels, 2 * LANES):
            both = dot(normed, weights_o[:, chunk : chunk + 2 * LANES]).astype(LOW)
            conv_o[:, chunk : chunk + 2 * LANES] = both
            for at in (0, LANES):
                lanes = slice(chunk + at, chunk + at + LANES)
                here = both[:, at : at + LANES].astype(WIDE)
                extended = jnp.concatenate([tail_s[:, lanes], here], axis=0)
                tail_s[:, lanes] = here[2 * size - 8 :]
                pre = taps[4:5, lanes] + taps[0:1, lanes] * here
                for lag in range(1, reach):
                    shifted = pltpu.roll(extended, lag, 0)[8:]
                    pre = pre + taps[lag : lag + 1, lanes] * shifted * lag_masks[lag - 1]
                pre_o[:, lanes] = pre
                act_o[:, lanes] = (pre * jax.nn.sigmoid(pre)).astype(LOW)

        values_wide = act_o[:, :inner].astype(WIDE)
        scaled_f = (dot(tail, spread_f[...]) * values_wide).astype(LOW)
        scaled_r = (dot(tail, spread_r[...]) * values_wide).astype(LOW)
        head_f = dot(head, spread_f[...])
        here = pl.ds(pl.multiple_of(pair * 2 * size, 2 * size), 2 * size)
        head_s[here] = head
        read_s[here] = act_o[:, inner + 2 * STATE :]
        row, col = iota((size, size), 0), iota((size, size), 1)
        lower = row > col
        lower_low = lower.astype(WIDE).astype(LOW)
        upper_low = (row < col).astype(WIDE).astype(LOW)
        for sub, rows in enumerate(subs):
            block = 2 * pair + sub
            late_rows = late[rows].T
            state_act = act_o[rows, inner:]
            turned = state_act.astype(WIDE).T.astype(LOW)
            forward_act, reverse_act = state_act[:, : 2 * STATE], state_act[:, 2 * STATE :]
            scores = jnp.where(
                lower,
                dot(forward_act, below(turned[:STATE])),
                dot(reverse_act, below(turned[2 * STATE : 3 * STATE])),
            )
            bias = table_bias(starts, block, size)
            state = state_s[...]
            states = slice(sub * STATE, (sub + 1) * STATE)
            state_f_o[states] = state
            carried = dot(forward_act, below(state.astype(LOW))) * head_f[rows]
            local_f = dot(turned[:STATE], scaled_f[rows])
            state_s[...] = decay_f[8 * sub : 8 * sub + 1] * state + local_f
            local_r = dot(turned[2 * STATE : 3 * STATE], scaled_r[rows])
            local_s[pl.ds(pl.multiple_of(block * STATE, STATE), STATE)] = local_r
            decay_s[pl.ds(pl.multiple_of(block * 8, 8), 8)] = decay_r[8 * sub : 8 * sub + 8]
            base = skip_row * values_wide[rows]
            at = pl.ds(pl.multiple_of(block * size, size), size)
            for heads in range(inner // LANES):
                lanes = slice(heads * LANES, (heads + 1) * LANES)
                lefts, rights = [], []
                for head_at in (2 * heads, 2 * heads + 1):
                    c = 2 * head_at
                    gap = jnp.where(
                        lower,
                        cums[sub][:, c : c + 1] - late_rows[c : c + 1],
                        cums[sub][:, c + 1 : c + 2] - late_rows[c + 1 : c + 2],
                    )
                    mix = (scores * jnp.exp(gap + bias)).astype(LOW)
                    lefts.append(mix * lower_low)
                    rights.append(mix * upper_low)
                both = jnp.concatenate(
                    [jnp.concatenate(lefts, axis=1), jnp.concatenate(rights, axis=1)], axis=0
                )
                result = dot(both, block_diagonal(act_o[rows, lanes]))
                out_f = result[:size] + carried[:, lanes]
                out_f_o[rows, lanes] = out_f
                sum_s[at, lanes] = out_f + result[size:] + base[:, lanes]

    @pl.when(step_at == pairs)
    def _():
        state_s[...] = jnp.zeros_like(state_s)

    @pl.when(step_at >= pairs)
    def _():
        pair = 2 * pairs - 1 - step_at
        here = pl.ds(pl.multiple_of(pair * 2 * size, 2 * size), 2 * size)
        head_r = dot(head_s[here], spread_r[...])
        for sub in (1, 0):
            block, rows = 2 * pair + sub, slice(sub * size, (sub + 1) * size)
            at = pl.ds(pl.multiple_of(block * size, size), size)
            state = state_s[...]
            state_r_o[sub * STATE : (sub + 1) * STATE] = state
            carried = dot(read_s[at], below(state.astype(LOW)))
            core_o[rows] = sum_s[at] + head_r[rows] * carried
            local_r = local_s[pl.ds(pl.multiple_of(block * STATE, STATE), STATE)]
            decay_r = decay_s[pl.ds(pl.multiple_of(block * 8, 8), 8)]
            state_s[...] = decay_r[:1] * state + local_r


def output_kernel(
    starts, normed, core, mine, other, pay, small,
    gate_o, unscaled_o, unscaled_grad_o, sums_o, keep_o, send_o, gate_w,
    out_w,
):
    size, inner = mine.shape[0], core.shape[1]

    @pl.when(pl.program_id(0) == 0)
    def _():
        seqs, planes, rows, cols = pay.shape
        groups, half = planes // 2, cols // 2
        core_at = starts[starts.shape[0] - 1]
        for seq in range(seqs):
            for group in range(groups):
                part = pay[seq, core_at * groups + group]
                at, lanes = slice(seq * rows, (seq + 1) * rows), slice(group * half, (group + 1) * half)
                gate_w[at, lanes] = part[:, :half]
                out_w[at, lanes] = part[:, half:]

    gate = dot(normed[...], gate_w[...])
    gate_o[...] = gate.astype(gate_o.dtype)
    unscaled_grad = dot(in_order(starts, mine, other), out_w[...])
    unscaled_grad_o[...] = unscaled_grad.astype(unscaled_grad_o.dtype)
    gated = core[...] * gate * jax.nn.sigmoid(gate)
    unscaled = (gated * small[5:6, :inner]).astype(LOW)
    unscaled_o[...] = unscaled
    squares = jnp.sum(gated * gated, axis=1, keepdims=True)
    products = jnp.sum(unscaled_grad * unscaled.astype(WIDE), axis=1, keepdims=True)
    both = jnp.where(iota((2 * size, LANES), 1) == 0, squares, products)
    for sub in range(2):
        rows = slice(sub * size, (sub + 1) * size)
        sums_o[:, rows] = both[rows].T[:8]
    keep_own(starts, dot_nt(unscaled, out_w[...]), keep_o, send_o)


def gate_back_kernel(
    starts, own_sums, other_sums, mine, other, out_f, core, act, gate, unscaled_grad, cum, decay_r,
    small, spread_f, spread_r, gather_f, gather_r,
    total_o, core_grad_o, gate_grad_o, row_sums_o, back_f_o, later_r_o, gain_grad_o, skip_grad_o,
    later_s,
):
    pair, pairs = pl.program_id(0), pl.num_programs(0)
    blocks = 2 * pairs
    size, inner = mine.shape[0], out_f.shape[1]
    inner_width = HEADS * HEADDIM

    @pl.when(pair == 0)
    def _():
        later_s[...] = jnp.zeros_like(later_s)
        gain_grad_o[...] = jnp.zeros_like(gain_grad_o)
        skip_grad_o[...] = jnp.zeros_like(skip_grad_o)

    sums = own_sums[...] + other_sums[...]
    empty = jnp.zeros((size - 8, size), WIDE)
    sums = jnp.concatenate(
        [
            jnp.concatenate([sums[:, at : at + size], empty], axis=0).T
            for at in (0, size)
        ],
        axis=0,
    )
    skip_row, gain_row = skip_lanes(small[...], spread_f), small[5:6, :inner]
    scale = lax.rsqrt(sums[:, 0:1] / inner_width + 1e-05)
    square_grad = sums[:, 1:2] * scale * scale * scale / inner_width
    total_o[...] = (scale * in_order(starts, mine, other).astype(WIDE)).astype(LOW)
    values = act[:, :inner].astype(WIDE)
    core_here = core[...]
    gate_value = gate[...].astype(WIDE)
    sigma = jax.nn.sigmoid(gate_value)
    slope = gate_value * sigma
    gated = core_here * slope
    unscaled = scale * unscaled_grad[...].astype(WIDE)
    gain_grad_o[...] += rows_sum(unscaled * gated)
    gated_grad = unscaled * gain_row - gated * square_grad
    core_grad = (gated_grad * slope).astype(LOW)
    core_grad_o[...] = core_grad
    gate_grad_o[...] = (gated_grad * core_here * silu_slope(gate_value, sigma)).astype(LOW)
    grad_wide = core_grad.astype(WIDE)
    skip_grad_o[...] += rows_sum(grad_wide * values)
    out_f_here = out_f[...]
    out_r_here = core_here - out_f_here - skip_row * values
    row_sums_o[...] = dot(halves(grad_wide * out_f_here), gather_f[...]) + dot(
        halves(grad_wide * out_r_here), gather_r[...]
    )
    for sub in range(2):
        rows, states = slice(sub * size, (sub + 1) * size), slice(sub * STATE, (sub + 1) * STATE)
        _, head_mask, _ = start_masks(starts, 2 * pair + sub, blocks, (size, LANES))
        head = halves(jnp.exp(cum[rows]) * head_mask)
        turned = act[rows, inner:].astype(WIDE).T.astype(LOW)
        grad_here = core_grad_o[rows].astype(WIDE)
        back_f_o[states] = dot(
            turned[STATE : 2 * STATE], (dot(head, spread_f[...]) * grad_here).astype(LOW)
        )
        back_r = dot(turned[3 * STATE :], (dot(head, spread_r[...]) * grad_here).astype(LOW))
        later = later_s[...]
        later_r_o[states] = later
        later_s[...] = decay_r[8 * sub : 8 * sub + 1] * later + back_r


def chain_back_kernel(
    starts, core_grad, gate_grad, act, conv, pre, cum, raw, row_sums, state_f, state_f_next,
    state_r, state_r_last, back_f, later_r, decay_f, gate_w, weights, small, spread_f, spread_r,
    gather_f, gather_r,
    proj_o, keep_o, send_o, taps_grad_o, scalar_o,
    later_s, next_s, values_f_s, values_r_s, active_s, raw_grad_s,
):
    step_at, pairs = pl.program_id(0), pl.num_programs(0)
    pair, blocks = pairs - 1 - step_at, 2 * pairs
    size, inner = core_grad.shape[0] // 2, core_grad.shape[1]
    channels = inner + 4 * STATE
    reach = 4

    @pl.when(step_at == 0)
    def _():
        later_s[...] = jnp.zeros_like(later_s)
        next_s[...] = jnp.zeros_like(next_s)
        taps_grad_o[...] = jnp.zeros_like(taps_grad_o)
        scalar_o[...] = jnp.zeros_like(scalar_o)

    small_here = small[...]
    bias_row, rate_row = step_rows(small_here, inner // HEADDIM)
    skip_row, taps = skip_lanes(small_here, spread_f), small_here[:8, :channels]
    step_all, sigma_all, ratio_all = steps_of(raw[...], bias_row)
    log_step = jnp.log(step_all)
    row, col = iota((size, size), 0), iota((size, size), 1)
    ahead = col > row
    ahead_low = ahead.astype(WIDE).astype(LOW)
    behind_low = (col < row).astype(WIDE).astype(LOW)
    for sub in (1, 0):
        block = 2 * pair + sub
        rows, states = slice(sub * size, (sub + 1) * size), slice(sub * STATE, (sub + 1) * STATE)
        step, sigma, ratio = step_all[rows], sigma_all[rows], ratio_all[rows]
        cum_here = cum[rows]
        late = cum_here - log_step[rows]
        cum_rows = cum_here.T
        tail_mask, head_mask, _ = start_masks(starts, block, blocks, cum_here.shape)
        tail = halves(jnp.exp(chain_last(cum_here) - late) * tail_mask)
        head = halves(jnp.exp(cum_here) * head_mask)
        state_act = act[rows, inner:]
        turned = state_act.astype(WIDE).T.astype(LOW)
        forward_act, reverse_act = state_act[:, : 2 * STATE], state_act[:, 2 * STATE :]
        scores = jnp.where(
            ahead,
            dot(forward_act, above(turned[STATE : 2 * STATE])),
            dot(reverse_act, above(turned[3 * STATE :])),
        )
        bias = table_bias(starts, block, size)
        scores_grad = jnp.zeros((size, size), WIDE)
        for heads in range(inner // LANES):
            lanes = slice(heads * LANES, (heads + 1) * LANES)
            grad_blocks = block_diagonal(core_grad[rows, lanes])
            mix_grad = dot_nt(act[rows, lanes], grad_blocks)
            lefts, rights = [], []
            for at in range(2):
                c = 2 * (2 * heads + at)
                gap = jnp.where(
                    ahead,
                    cum_rows[c : c + 1] - late[:, c : c + 1],
                    cum_rows[c + 1 : c + 2] - late[:, c + 1 : c + 2],
                )
                table = jnp.exp(gap + bias)
                mix = (scores * table).astype(LOW)
                lefts.append(mix * ahead_low)
                rights.append(mix * behind_low)
                scores_grad = scores_grad + mix_grad[:, at * size : (at + 1) * size] * table
            both = jnp.concatenate(
                [jnp.concatenate(lefts, axis=1), jnp.concatenate(rights, axis=1)], axis=0
            )
            result = dot(both, grad_blocks)
            values_f_s[rows, lanes] = result[:size]
            values_r_s[rows, lanes] = result[size:]

        grad_wide = core_grad[rows].astype(WIDE)
        values = act[rows, :inner].astype(WIDE)
        later_f, later_r_here = later_s[...], later_r[states]
        later_f_low, later_r_low = later_f.astype(LOW), later_r_here.astype(LOW)
        tail_f, tail_r = dot(tail, spread_f[...]), dot(tail, spread_r[...])
        values_f = values_f_s[rows] + tail_f * dot(forward_act, above(later_f_low))
        values_r = values_r_s[rows] + tail_r * dot(reverse_act, above(later_r_low))
        col_sums = dot(halves(values * values_f), gather_f[...]) + dot(
            halves(values * values_r), gather_r[...]
        )
        after_f = state_f_next[...] if sub else state_f[STATE:]
        after_r = state_r[:STATE] if sub else state_r_last[...]
        end_f = dot(halves(rows_sum(later_f * after_f)), gather_f[...])
        end_r = dot(halves(rows_sum(later_r_here * after_r)), gather_r[...])
        end_f = jnp.sum(end_f, axis=0, keepdims=True)
        end_r = jnp.sum(end_r, axis=0, keepdims=True)
        at_row = iota(cum_here.shape, 0)
        cum_grad = row_sums[rows] - col_sums
        cum_grad = cum_grad + jnp.where(at_row == size - 1, end_f, 0.0)
        cum_grad = cum_grad + jnp.where(at_row == 0, end_r, 0.0)
        log_grad = running_sums(cum_grad, True)
        raw_grad = col_sums * ratio - rate_row * log_grad * sigma
        raw_grad_s[rows] = raw_grad
        scalar_o[0:8] += rows_sum(raw_grad)
        scalar_o[8:16] += rows_sum(log_grad * (-step * rate_row))

        mid = scores_grad.T
        pieces = []
        for act_pair, spread_head, state, later_low, forward_side in (
            (forward_act, spread_f, state_f, later_f_low, True),
            (reverse_act, spread_r, state_r, later_r_low, False),
        ):
            tail_here = tail_f if forward_side else tail_r
            scaled = (tail_here * values).astype(LOW)
            carried_grad = (dot(head, spread_head[...]) * grad_wide).astype(LOW)
            own = ahead_low if forward_side else behind_low
            mirrored = behind_low if forward_side else ahead_low
            sides = jnp.concatenate(
                [scores_grad.astype(LOW) * own, mid.astype(LOW) * mirrored], axis=1
            )
            swapped = pltpu.roll(act_pair.astype(WIDE), STATE, 1).astype(LOW)
            pieces.append(
                dot_nt(scaled, above(later_low))
                + dot_nt(carried_grad, below(state[states].astype(LOW)))
                + dot(sides, block_diagonal(swapped))
            )
        active_s[rows, :inner] = values_f + values_r + skip_row * grad_wide
        active_s[rows, inner : inner + LANES] = pieces[0]
        active_s[rows, inner + LANES :] = pieces[1]
        later_s[...] = decay_f[8 * sub : 8 * sub + 1] * later_f + back_f[states]

    row = iota((2 * size, LANES), 0)
    number = document_of(starts, pair, blocks, size, row)
    masks = [
        (number == document_of(starts, pair, blocks, size, row + lag)).astype(WIDE)
        for lag in range(1, reach)
    ]
    for at in range(0, channels, LANES):
        lanes = slice(at, at + LANES)
        pre_here = pre[:, lanes]
        grad = active_s[:, lanes] * silu_slope(pre_here, jax.nn.sigmoid(pre_here))
        extended = jnp.concatenate([grad, next_s[:, lanes]], axis=0)
        next_s[:, lanes] = grad[:8]
        source = conv[:, lanes].astype(WIDE)
        result = taps[0:1, lanes] * grad
        taps_grad_o[0:8, lanes] += rows_sum(grad * source)
        taps_grad_o[32:40, lanes] += rows_sum(grad)
        for lag in range(1, reach):
            shifted = pltpu.roll(extended, 2 * size + 8 - lag, 0)[: 2 * size] * masks[lag - 1]
            result = result + taps[lag : lag + 1, lanes] * shifted
            taps_grad_o[8 * lag : 8 * lag + 8, lanes] += rows_sum(shifted * source)
        proj_o[:, lanes] = result.astype(LOW)
    proj_o[:, channels:] = raw_grad_s[...].astype(LOW)
    normed = dot_nt(gate_grad[...], gate_w[...]) + dot_nt(proj_o[...], weights[...])
    keep_own(starts, normed, keep_o, send_o)


def by_pair(kernel, blocks, order, ins, outs, scratch, name, work):
    steps = blocks // 2

    def at(i):
        if order == "both":
            return jnp.minimum(i, steps - 1)
        return steps - 1 - i if order == "down" else i

    def spec(shape, kind):
        part = (shape[0] // steps,) + shape[1:]
        single = (shape[0] // blocks,) + shape[1:]
        if kind == "scalar":
            return pl.BlockSpec(memory_space=pltpu.SMEM)
        if kind == "rows":
            return pl.BlockSpec(part, lambda i: (at(i), 0))
        if kind == "back":
            return pl.BlockSpec(part, lambda i: (steps - 1 - jnp.maximum(i - steps, 0), 0))
        if kind == "half":
            return pl.BlockSpec((None,) + shape[1:], lambda i: (at(i), 0, 0))
        if kind == "lanes":
            return pl.BlockSpec((shape[0], shape[1] // steps), lambda i: (0, at(i)))
        if kind == "next":
            return pl.BlockSpec(single, lambda i: (jnp.minimum(2 * at(i) + 2, blocks - 1), 0))
        if kind == "last":
            return pl.BlockSpec(single, lambda i: (jnp.maximum(2 * at(i) - 1, 0), 0))
        return pl.BlockSpec(shape, lambda i: (0,) * len(shape))

    return pl.pallas_call(
        kernel,
        grid=(2 * steps if order == "both" else steps,),
        in_specs=[spec(value.shape, kind) for value, kind in ins],
        out_specs=[spec(value.shape, kind) for value, kind in outs],
        out_shape=[value for value, _ in outs],
        scratch_shapes=[pltpu.VMEM(shape, dtype) for shape, dtype in scratch],
        compiler_params=pltpu.CompilerParams(
            dimension_semantics=("arbitrary",), vmem_limit_bytes=60 * 1024 * 1024
        ),
        cost_estimate=pl.CostEstimate(
            flops=work,
            transcendentals=0,
            bytes_accessed=sum(v.size * v.dtype.itemsize for v, _ in ins + outs),
        ),
        name=name,
    )(*[value for value, _ in ins])


def swap_core(value):
    return lax.ppermute(value, "core", [(0, 1), (1, 0)])


def swap_chip(value, side):
    return lax.ppermute(value, "chip", [(i, i ^ side) for i in range(4)])


def spread_to(value, axis):
    count = lax.axis_size(axis)
    return lax.all_to_all(jnp.broadcast_to(value[None], (count,) + value.shape), axis, 0, 0)


def shifted_sum(pieces, axis):
    count, mine = lax.axis_size(axis), lax.axis_index(axis)
    total = lax.dynamic_index_in_dim(pieces, mine, 0, keepdims=False).astype(WIDE)
    for k in range(1, count):
        piece = lax.dynamic_index_in_dim(pieces, (mine + k) % count, 0, keepdims=False)
        moved = lax.ppermute(piece, axis, [(i, (i + k) % count) for i in range(count)])
        total = total + moved.astype(WIDE)
    return total


def after(value, *others):
    return lax.optimization_barrier((value,) + others)[0]


def three_parts(value):
    high = lax.reduce_precision(value, 8, 7)
    middle = lax.reduce_precision(value - high, 8, 7)
    return jnp.stack([high, middle, lax.reduce_precision(value - high - middle, 8, 7)])


def placed(value, width, at):
    shape = value.shape[:-1] + (width,)
    return lax.dynamic_update_slice_in_dim(jnp.zeros(shape, value.dtype), value, at, value.ndim - 1)


def chip_plan(
    tokens,
    starts,
    in_weight,
    state_weight,
    state_conv,
    out_weight,
    value_conv,
    norm_gain,
    gate_gain,
    step_bias,
    decay_log,
    skip,
    out_cotangent,
):
    low, wide = LOW, WIDE
    sequences, block_size, width = tokens.shape
    chips, planes = lax.axis_size("chip"), lax.axis_size("head")
    chip, core, plane = lax.axis_index("chip"), lax.axis_index("core"), lax.axis_index("head")
    blocks = starts.shape[1]
    length = blocks * block_size
    rows, group = in_weight.shape[:2]
    groups = planes // 2
    heads_here = group * groups
    inner_here, group_inner = heads_here * HEADDIM, group * HEADDIM
    part, reach = value_conv.shape[0], state_conv.shape[1] - 1
    state_part = state_conv.shape[0]
    channels_state = state_weight.shape[1]
    channels = inner_here + channels_state
    seq = 2 * chip + core
    first = core == 0

    def own_plane(value):
        return lax.dynamic_slice_in_dim(value, plane * chips, chips, 0)

    tokens_plane = own_plane(tokens)
    tokens_plane, in_weight, out_weight = lax.optimization_barrier(
        (tokens_plane, in_weight, out_weight)
    )
    tokens_mine = lax.all_to_all(tokens_plane, "chip", 0, 0)

    step_at = (plane % groups) * 2 * group
    pair_weights = placed(in_weight[:, :, 2 * HEADDIM :].reshape(rows, 2 * group), LANES, step_at)
    tap_lanes = placed(value_conv.transpose(2, 1, 0), HEADDIM, part * seq).reshape(reach + 1, -1)
    gain_lanes = placed(gate_gain.transpose(1, 0), HEADDIM, part * seq).reshape(1, -1)
    extra_value = jnp.concatenate([tap_lanes, gain_lanes], axis=0)
    scalars = jnp.stack(
        [step_bias.T.reshape(-1), jnp.repeat(decay_log, 2), jnp.repeat(skip, 2)]
    )
    scalars = jnp.swapaxes(three_parts(jnp.where(seq == 0, scalars, 0.0)), 0, 1)
    extra_step = placed(scalars.reshape(9, 2 * group).astype(low), LANES, step_at)
    slab = jnp.concatenate(
        [
            jnp.concatenate(
                [in_weight[:, :, HEADDIM : 2 * HEADDIM].reshape(rows, group_inner), pair_weights],
                axis=1,
            ),
            jnp.concatenate(
                [
                    jnp.pad(extra_value, ((0, 16 - extra_value.shape[0]), (0, 0))),
                    jnp.pad(extra_step, ((0, 16 - extra_step.shape[0]), (0, 0))),
                ],
                axis=1,
            ),
        ],
        axis=0,
    )
    extra_state = jnp.concatenate(
        [
            placed(state_conv.T, channels_state, state_part * seq),
            placed(norm_gain, width, rows * seq).reshape(-1, channels_state),
        ],
        axis=0,
    )
    state_slab = jnp.concatenate(
        [state_weight, jnp.pad(extra_state, ((0, 16 - extra_state.shape[0]), (0, 0)))], axis=0
    )
    shifted = [slab] + [
        lax.ppermute(slab, "head", [(i, (i + k) % planes) for i in range(planes)])
        for k in range(1, planes)
    ]
    shifted = jnp.stack(shifted)

    def for_core(which):
        picked = [
            lax.dynamic_index_in_dim(shifted, (plane - which * groups - i) % planes, 0, False)
            for i in range(groups)
        ]
        steps = picked[0][:, group_inner:]
        for i in range(1, groups):
            steps = steps + picked[i][:, group_inner:]
        return jnp.concatenate(
            [picked[i][:, :group_inner] for i in range(groups)] + [state_slab, steps], axis=1
        )

    pay = jnp.stack([for_core(core), swap_core(for_core(1 - core))])
    pay, tokens_mine = lax.optimization_barrier((pay, tokens_mine))
    tokens_other = swap_core(tokens_mine)
    pay_x, pay_y = swap_chip(pay, 1), swap_chip(pay, 2)
    pays = (pay, pay_x, pay_y, swap_chip(pay_x[0], 2), swap_chip(pay_y[1], 1))

    late_slab = jnp.concatenate(
        [
            in_weight[:, :, :HEADDIM].reshape(rows, group_inner),
            out_weight.reshape(rows, group_inner),
        ],
        axis=1,
    )
    pay_late = lax.all_gather(late_slab, ("chip", "core", "head")).reshape(2 * chips, planes, rows, -1)
    cotangent_low = own_plane(out_cotangent).astype(low)
    cotangent_low, *pays = lax.optimization_barrier((cotangent_low, *pays))
    cotangent_mine = lax.all_to_all(cotangent_low, "chip", 0, 0)
    starts_row = lax.dynamic_index_in_dim(starts, plane * chips + chip, 0, keepdims=False)
    starts_row = jnp.concatenate([starts_row, jnp.stack([chip, core]).astype(starts_row.dtype)])
    (spread_f, spread_r), (gather_f, gather_r) = head_columns(heads_here)

    def shape(rows_, cols, dtype):
        return jax.ShapeDtypeStruct((rows_, cols), dtype)

    half_low = jax.ShapeDtypeStruct((chips, block_size, width), low)
    half_wide = jax.ShapeDtypeStruct((chips, block_size, width), wide)
    states = blocks * STATE
    lane_cols = channels + LANES
    (
        normed, conv_input, pre_active, act, out_f, cum, step_raw, state_f, decay_f, decay_r, weights,
        small, core_out, state_r,
    ) = by_pair(
        forward_kernel, blocks, "both",
        [
            (starts_row, "scalar"), (tokens_mine, "half"), (tokens_other, "half"),
            *((value, "whole") for value in pays),
            (spread_f, "whole"), (spread_r, "whole"),
        ],
        [
            (shape(length, width, low), "rows"), (shape(length, channels, low), "rows"),
            (shape(length, channels, wide), "rows"), (shape(length, channels, low), "rows"),
            (shape(length, inner_here, wide), "rows"),
            (shape(length, LANES, wide), "rows"), (shape(length, LANES, wide), "rows"),
            (shape(states, inner_here, wide), "rows"),
            (shape(8 * blocks, inner_here, wide), "rows"), (shape(8 * blocks, inner_here, wide), "rows"),
            (shape(width, lane_cols, low), "whole"), (shape(16, lane_cols, wide), "whole"),
            (shape(length, inner_here, wide), "back"), (shape(states, inner_here, wide), "back"),
        ],
        [
            ((8, channels), wide), ((STATE, inner_here), wide), ((length, inner_here), wide),
            ((length, 2 * LANES), low), ((length, 2 * STATE), low), ((states, inner_here), wide),
            ((8 * blocks, inner_here), wide),
        ],
        "forward", 20_000_000_000,
    )
    cotangent_mine, normed = lax.optimization_barrier((cotangent_mine, normed))
    cotangent_other = swap_core(cotangent_mine)
    gate, unscaled, unscaled_grad, own_sums, keep, send, gate_w = by_pair(
        output_kernel, blocks, "up",
        [
            (starts_row, "scalar"), (normed, "rows"), (core_out, "rows"), (cotangent_mine, "half"),
            (cotangent_other, "half"), (pay_late, "whole"), (small, "whole"),
        ],
        [
            (shape(length, inner_here, wide), "rows"), (shape(length, inner_here, low), "rows"),
            (shape(length, inner_here, wide), "rows"), (shape(8, length, wide), "lanes"),
            (half_low, "half"), (half_low, "half"), (shape(width, inner_here, low), "whole"),
        ],
        [((width, inner_here), low)],
        "outputs", 12_000_000_000,
    )
    other_sums = swap_core(own_sums)

    squares = (own_sums[0] + other_sums[0]).reshape(chips, 2, block_size)
    squares = lax.dynamic_index_in_dim(squares, core, 1, keepdims=False)
    gate_scale = lax.rsqrt(squares / (HEADS * HEADDIM) + 1e-05)
    out_delta = gate_scale[..., None] * (keep.astype(wide) + swap_core(send).astype(wide))
    out_delta, gate = lax.optimization_barrier((out_delta.astype(low), gate))
    out_moved = lax.all_to_all(out_delta, "chip", 0, 0)

    (total_grad, core_grad, gate_grad, row_sums, back_f, later_r, gain_grad, skip_grad) = by_pair(
        gate_back_kernel, blocks, "up",
        [
            (starts_row, "scalar"), (own_sums, "lanes"), (other_sums, "lanes"), (cotangent_mine, "half"),
            (cotangent_other, "half"), (out_f, "rows"), (core_out, "rows"),
            (act, "rows"), (gate, "rows"), (unscaled_grad, "rows"), (cum, "rows"), (decay_r, "rows"),
            (small, "whole"), (spread_f, "whole"), (spread_r, "whole"),
            (gather_f, "whole"), (gather_r, "whole"),
        ],
        [
            (shape(length, width, low), "rows"), (shape(length, inner_here, low), "rows"),
            (shape(length, inner_here, low), "rows"), (shape(length, LANES, wide), "rows"),
            (shape(states, inner_here, wide), "rows"), (shape(states, inner_here, wide), "rows"),
            (shape(8, inner_here, wide), "whole"), (shape(8, inner_here, wide), "whole"),
        ],
        [((STATE, inner_here), wide)],
        "gate_back", 12_000_000_000,
    )

    def weight_grad(left, right):
        result = lax.dot_general(left, right, (((0,), (0,)), ((), ())), preferred_element_type=wide)
        return result.astype(low)

    gate_grad, total_grad, out_moved = lax.optimization_barrier((gate_grad, total_grad, out_moved))
    out_delta = lax.all_gather(out_moved, "head").reshape(sequences, block_size, width)
    early_grad = jnp.concatenate(
        [weight_grad(normed, gate_grad), weight_grad(total_grad, unscaled)], axis=1
    ).reshape(chips, 2, rows, -1)
    early_grad, core_grad = lax.optimization_barrier((early_grad, core_grad))
    early_moved = lax.all_to_all(early_grad, "chip", 0, 0)
    rest_grad, keep, send, taps_grad, scalar_part = by_pair(
        chain_back_kernel, blocks, "down",
        [
            (starts_row, "scalar"), (core_grad, "rows"), (gate_grad, "rows"), (act, "rows"),
            (conv_input, "rows"), (pre_active, "rows"), (cum, "rows"), (step_raw, "rows"),
            (row_sums, "rows"), (state_f, "rows"), (state_f, "next"), (state_r, "rows"),
            (state_r, "last"), (back_f, "rows"), (later_r, "rows"), (decay_f, "rows"),
            (gate_w, "whole"), (weights, "whole"), (small, "whole"), (spread_f, "whole"),
            (spread_r, "whole"), (gather_f, "whole"), (gather_r, "whole"),
        ],
        [
            (shape(length, lane_cols, low), "rows"), (half_wide, "half"), (half_low, "half"),
            (shape(40, channels, wide), "whole"), (shape(16, LANES, wide), "whole"),
        ],
        [
            ((STATE, inner_here), wide), ((8, channels), wide), ((2 * block_size, inner_here), wide),
            ((2 * block_size, inner_here), wide), ((2 * block_size, channels), wide),
            ((2 * block_size, LANES), wide),
        ],
        "chain_back", 1_000_000_000,
    )

    norm_row = small[5 : 5 + width // channels_state, inner_here:channels].reshape(width)
    tokens_wide = tokens_mine.astype(wide)
    in_scale = lax.rsqrt(jnp.mean(tokens_wide * tokens_wide, axis=2, keepdims=True) + 1e-05)
    unit = tokens_wide * in_scale
    normed_grad = keep + swap_core(send).astype(wide)
    unit_grad = normed_grad * norm_row
    delta = in_scale * (unit_grad - unit * jnp.mean(unit_grad * unit, axis=2, keepdims=True))
    (
        delta, early_moved, normed_late, rest_grad, taps_grad, scalar_part, normed_grad,
    ) = lax.optimization_barrier(
        (
            delta.astype(low), early_moved, normed, rest_grad, taps_grad, scalar_part, normed_grad,
        )
    )
    delta = lax.all_to_all(delta, "chip", 0, 0)
    gathered = lax.all_gather(delta, "head").reshape(sequences, block_size, width)
    def between_cores(moved):
        total = jnp.sum(moved.astype(wide), axis=0).astype(low)
        mine = lax.dynamic_index_in_dim(total, core, 0, keepdims=False)
        got = swap_core(lax.dynamic_index_in_dim(total, 1 - core, 0, keepdims=False))
        return [jnp.where(first, mine, got), jnp.where(first, got, mine)]

    def group_lanes(value, at, i):
        return value[:, at + i * group_inner : at + (i + 1) * group_inner]

    early = between_cores(early_moved)
    early = jnp.stack(
        [
            jnp.concatenate([group_lanes(v, 0, i), group_lanes(v, inner_here, i)], axis=1)
            for v in early
            for i in range(groups)
        ]
    )
    early, out_delta, normed_late, rest_grad = lax.optimization_barrier(
        (early, out_delta, normed_late, rest_grad)
    )
    early = shifted_sum(early, "head")
    norm_grad = jnp.sum(normed_grad * unit, axis=(0, 1))

    taps_grad = jnp.sum(taps_grad.reshape(reach + 1, 8, channels), axis=1)
    scalar_part = jnp.sum(scalar_part.reshape(2, 8, LANES), axis=1)
    skip_part = jnp.sum(skip_grad.reshape(8, heads_here, HEADDIM), axis=(0, 2))
    skip_part = jnp.pad(jnp.repeat(skip_part, 2)[None], ((0, 0), (0, LANES - 2 * heads_here)))
    lanes_value = jnp.concatenate(
        [taps_grad[:, :inner_here], jnp.sum(gain_grad, axis=0, keepdims=True)], axis=0
    )
    lanes_state = jnp.concatenate(
        [taps_grad[:, inner_here:], norm_grad.reshape(-1, channels_state)], axis=0
    )
    lanes_step = jnp.concatenate([scalar_part, skip_part], axis=0)
    extra = jnp.concatenate(
        [
            jnp.pad(lanes_value, ((0, 16 - lanes_value.shape[0]), (0, 0))),
            jnp.pad(lanes_state, ((0, 16 - lanes_state.shape[0]), (0, 0))),
            jnp.pad(lanes_step, ((0, 16 - lanes_step.shape[0]), (0, 0))),
        ],
        axis=1,
    ).astype(low)
    extra, early = lax.optimization_barrier((extra, early))
    small_sum = extra.astype(wide)
    for side in range(1, chips):
        small_sum = small_sum + swap_chip(extra, side).astype(wide)
    small_low = small_sum.astype(low)
    for k in range(1, planes):
        moved = lax.ppermute(small_low, "head", [(i, (i + k) % planes) for i in range(planes)])
        small_sum = small_sum + moved.astype(wide)
    small_other = swap_core(small_sum)
    of_heads = jnp.where(plane // groups == core, small_sum, small_other)
    step_lanes = lax.dynamic_slice_in_dim(of_heads[:3, channels:], step_at, 2 * group, 1)
    lanes = lax.dynamic_slice_in_dim(
        of_heads[:, :inner_here], (plane % groups) * group_inner, group_inner, 1
    ).reshape(16, group, HEADDIM)
    lanes = lax.dynamic_slice_in_dim(lanes, part * seq, part, 2)
    value_conv_out = lanes[: reach + 1].transpose(2, 1, 0)
    gate_gain_out = lanes[reach + 1].transpose(1, 0)
    state_lanes = small_sum[:, inner_here:channels] + small_other[:, inner_here:channels]
    conv_at = state_part * seq + (state_part // planes) * plane
    state_conv_out = lax.dynamic_slice_in_dim(
        state_lanes[: reach + 1], conv_at, state_part // planes, 1
    ).T
    norm_sum = state_lanes[reach + 1 :][: width // channels_state].reshape(width)
    norm_gain_out = lax.dynamic_slice_in_dim(norm_sum, rows * seq, rows, 0)
    step_bias_out = step_lanes[0].reshape(group, 2).T
    decay_log_out = jnp.sum(step_lanes[1].reshape(group, 2), axis=1)
    skip_out = step_lanes[2].reshape(group, 2)[:, 0]

    late_grad = weight_grad(normed_late, rest_grad).reshape(chips, 2, rows, lane_cols)
    late_grad, delta, early = lax.optimization_barrier((late_grad, delta, early))
    late_moved = lax.all_to_all(late_grad, "chip", 0, 0)
    output = tokens.astype(wide) + out_delta.astype(wide)

    late = between_cores(late_moved)
    state_sum = late[0][:, inner_here:channels].astype(wide) + late[1][:, inner_here:channels].astype(wide)
    state_sum = state_sum.astype(low).reshape(planes, -1, group_inner + LANES)
    state_rows = state_sum.shape[1]
    late = jnp.stack(
        [
            jnp.concatenate(
                [
                    jnp.concatenate([group_lanes(late[which], 0, i), late[which][:, channels:]], axis=1),
                    jnp.pad(state_sum[which * groups + i], ((0, -state_rows % 16), (0, 0))),
                ],
                axis=0,
            )
            for which in range(2)
            for i in range(groups)
        ]
    )
    late, gathered = lax.optimization_barrier((late, gathered))
    input_gradient = out_cotangent + gathered.astype(wide)
    late = shifted_sum(late, "head")
    late_steps = lax.dynamic_slice_in_dim(late[:rows, group_inner:], step_at, 2 * group, 1)
    in_weight_out = jnp.concatenate(
        [
            early[:, :group_inner].reshape(rows, group, HEADDIM),
            late[:rows, :group_inner].reshape(rows, group, HEADDIM),
            late_steps.reshape(rows, group, 2),
        ],
        axis=2,
    )
    out_weight_out = early[:, group_inner:].reshape(rows, group, HEADDIM)
    state_weight_out = late[rows : rows + state_rows].reshape(-1, channels_state)
    return (
        output,
        input_gradient,
        in_weight_out,
        state_weight_out,
        state_conv_out,
        out_weight_out,
        value_conv_out,
        norm_gain_out,
        gate_gain_out,
        step_bias_out,
        decay_log_out,
        skip_out,
    )


def solution(mesh):
    devices_seq, planes = mesh.devices.shape
    seq, plan = "seq", split_plan
    if devices_seq % 2 == 0 and planes % 2 == 0 and devices_seq // 2 * planes == CHIP_SEQUENCES:
        shape = (devices_seq // 2, 2, planes)
        mesh = Mesh(mesh.devices.reshape(shape), ("chip", "core", "head"))
        seq, plan = ("chip", "core"), chip_plan
    both = seq + ("head",) if isinstance(seq, tuple) else (seq, "head")
    return jax.shard_map(
        plan,
        mesh=mesh,
        in_specs=(
            P(None, seq, None),
            P(),
            P(seq, "head", None),
            P(seq, None),
            P(seq, None),
            P(seq, "head", None),
            P(seq, "head", None),
            P(seq),
            P(seq, "head"),
            P(None, "head"),
            P("head"),
            P("head"),
            P(None, seq, None),
        ),
        out_specs=(
            P(None, seq, None),
            P(None, seq, None),
            P(seq, "head", None),
            P(both, None),
            P(both, None),
            P(seq, "head", None),
            P(seq, "head", None),
            P(seq),
            P(seq, "head"),
            P(None, "head"),
            P("head"),
            P("head"),
        ),
        check_vma=False,
    )
```

```python
import jax
import jax.numpy as jnp
from jax import lax
from jax.experimental import pallas as pl
from jax.experimental.layout import Layout, with_layout_constraint
from jax.experimental.pallas import tpu as pltpu
from jax.sharding import Mesh, PartitionSpec as P

HEADS = 24
HEADDIM = 64
STATE = 64
CHIP_SEQUENCES = 16


def from_behind(value, axis, by):
    devices = lax.axis_size(axis)
    pairs = [(i, i + by) for i in range(devices) if 0 <= i + by < devices]
    return lax.ppermute(value, axis, pairs)


def entering(value, axis, join, neutral, backward):
    count, mine = (lax.axis_size(axis), lax.axis_index(axis))
    pieces = jax.tree.map(lambda part: lax.all_gather(part, axis), value)
    if backward:
        pieces = jax.tree.map(lambda part: part[::-1], pieces)
        mine = count - 1 - mine
    running = jax.tree.map(
        lambda part, zero: jnp.full_like(part, 0) + jnp.asarray(zero, part.dtype), value, neutral
    )

    def step(position, running):
        longer = join(running, jax.tree.map(lambda part: part[position], pieces))
        return jax.tree.map(lambda new, old: jnp.where(position < mine, new, old), longer, running)

    return lax.fori_loop(0, count - 1, step, running)


def affine(earlier, later):
    return (earlier[0] * later[0], later[0][..., None, None] * earlier[1] + later[1])


def document_numbers(starts, first_position, count, block_size):
    blocks = starts.shape[1]
    begins = jnp.arange(blocks, dtype=jnp.int32)[None, :] * block_size + starts
    valid = starts < block_size
    places = first_position + jnp.arange(count, dtype=jnp.int32)
    hits = (begins[:, None, :] <= places[None, :, None]) & valid[:, None, :]
    return jnp.sum(hits.astype(jnp.int32), axis=2)


def running_sum(value):
    length, shift = value.shape[-1], 1
    while shift < length:
        pad = [(0, 0)] * (value.ndim - 1) + [(shift, 0)]
        value = value + jnp.pad(value[..., : length - shift], pad)
        shift *= 2
    return value


def chain_forward(readout, intake, values, log_decay, step_size, flags):
    block_size = readout.shape[1]
    segment = running_sum(flags)
    decay_sum = running_sum(log_decay)
    scores = jnp.einsum("mtn,mjn->mtj", readout, intake, preferred_element_type=jnp.float32)
    order = jnp.arange(block_size)
    mask = ((order[:, None] > order[None, :])[None] & (segment[:, :, None] == segment[:, None, :]))[
        :, None
    ]
    gap = jnp.where(mask, decay_sum[:, :, :, None] - decay_sum[:, :, None, :], 0.0)
    decay_table = jnp.where(mask, jnp.exp(gap), 0.0)
    mixing = (scores[:, None] * decay_table * step_size[:, :, None, :]).astype(jnp.bfloat16)
    inner = jnp.einsum("mhtj,mjhp->mthp", mixing, values, preferred_element_type=jnp.float32)
    tail_factor = (
        jnp.exp(decay_sum[:, :, -1:] - decay_sum) * (segment == segment[:, -1:])[:, None, :]
    )
    scaled_intake = (
        (tail_factor * step_size)[..., None] * intake[:, None].astype(jnp.float32)
    ).astype(jnp.bfloat16)
    local_state = jnp.einsum(
        "mhjn,mjhp->mhnp", scaled_intake, values, preferred_element_type=jnp.float32
    )
    block_decay = jnp.exp(decay_sum[:, :, -1]) * (segment[:, -1] == 0)[:, None]
    head_scale = jnp.exp(decay_sum) * (segment == 0)[:, None, :]
    saved = (scores, decay_table, mixing, tail_factor, scaled_intake, head_scale)
    return (inner, local_state, block_decay, saved)


def chain_finish(inner, readout, state_in, head_scale):
    state_low = state_in.astype(jnp.bfloat16)
    carried = jnp.einsum("mtn,mhnp->mthp", readout, state_low, preferred_element_type=jnp.float32)
    return (inner + jnp.swapaxes(head_scale, 1, 2)[..., None] * carried, carried, state_low)


def chain_back_state(grad_out, readout, carried, state_low, head_scale):
    grad_wide = grad_out.astype(jnp.float32)
    carried_grad = (jnp.swapaxes(head_scale, 1, 2)[..., None] * grad_wide).astype(jnp.bfloat16)
    state_in_grad = jnp.einsum(
        "mtn,mthp->mhnp", readout, carried_grad, preferred_element_type=jnp.float32
    )
    readout_grad = jnp.einsum(
        "mthp,mhnp->mtn", carried_grad, state_low, preferred_element_type=jnp.float32
    )
    sum_grad = jnp.swapaxes(jnp.sum(grad_wide * carried, axis=3), 1, 2) * head_scale
    return (state_in_grad, readout_grad, sum_grad)


def chain_back_rest(
    grad_out,
    readout,
    intake,
    values,
    step_size,
    state_in,
    later,
    block_decay,
    saved,
    readout_grad,
    sum_grad,
):
    scores, decay_table, mixing, tail_factor, scaled_intake, head_scale = saved
    later_low = later.astype(jnp.bfloat16)
    scaled_grad = jnp.einsum(
        "mjhp,mhnp->mhjn", values, later_low, preferred_element_type=jnp.float32
    )
    values_grad = jnp.einsum(
        "mhjn,mhnp->mjhp", scaled_intake, later_low, preferred_element_type=jnp.float32
    )
    tail_grad = jnp.einsum("mhjn,mjn->mhj", scaled_grad, intake.astype(jnp.float32))
    intake_grad = jnp.einsum("mhjn,mhj->mjn", scaled_grad, tail_factor * step_size)
    step_grad = tail_grad * tail_factor
    tail_term = tail_grad * tail_factor * step_size
    decay_grad = jnp.sum(later * state_in, axis=(2, 3)) * block_decay
    sum_grad = (sum_grad - tail_term).at[:, :, -1].add(jnp.sum(tail_term, axis=2) + decay_grad)
    mixing_grad = jnp.einsum(
        "mthp,mjhp->mhtj", grad_out, values, preferred_element_type=jnp.float32
    )
    values_grad = values_grad + jnp.einsum(
        "mhtj,mthp->mjhp", mixing, grad_out, preferred_element_type=jnp.float32
    )
    through = mixing_grad * decay_table
    scores_grad = jnp.sum(through * step_size[:, :, None, :], axis=1).astype(jnp.bfloat16)
    readout_grad = readout_grad + jnp.einsum(
        "mtj,mjn->mtn", scores_grad, intake, preferred_element_type=jnp.float32
    )
    intake_grad = intake_grad + jnp.einsum(
        "mtj,mtn->mjn", scores_grad, readout, preferred_element_type=jnp.float32
    )
    kernel = through * scores[:, None]
    step_grad = step_grad + jnp.sum(kernel, axis=2)
    weighted = kernel * step_size[:, :, None, :]
    sum_grad = sum_grad + jnp.sum(weighted, axis=3) - jnp.sum(weighted, axis=2)
    log_grad = jnp.flip(running_sum(jnp.flip(sum_grad, 2)), 2)
    return (values_grad, readout_grad, intake_grad, step_grad, log_grad)


def split_plan(
    tokens,
    starts,
    in_weight,
    state_weight,
    state_conv,
    out_weight,
    value_conv,
    norm_gain,
    gate_gain,
    step_bias,
    decay_log,
    skip,
    out_cotangent,
):
    sequences, block_size, width = tokens.shape
    place = lax.axis_index("seq")
    devices_seq = lax.axis_size("seq")
    in_weights, state_weights, state_taps, out_weights, value_taps, norm_whole, gate_whole = (
        lax.all_gather(in_weight, "seq", axis=0, tiled=True),
        lax.all_gather(state_weight, "seq", axis=0, tiled=True),
        lax.all_gather(state_conv, "seq", axis=0, tiled=True),
        lax.all_gather(out_weight, "seq", axis=0, tiled=True),
        lax.all_gather(value_conv, "seq", axis=0, tiled=True),
        lax.all_gather(norm_gain, "seq", axis=0, tiled=True),
        lax.all_gather(gate_gain, "seq", axis=0, tiled=True),
    )
    heads_here = in_weight.shape[1]
    value_width = heads_here * HEADDIM
    reach = state_conv.shape[1] - 1
    edge = reach - 1
    numbers = document_numbers(starts, place * block_size - edge, block_size + 2 * edge, block_size)
    lag_masks = jnp.stack(
        [
            numbers[:, edge:] == numbers[:, edge - lag : block_size + 2 * edge - lag]
            for lag in range(reach)
        ],
        axis=2,
    ).astype(jnp.float32)
    first = (
        numbers[:, edge : edge + block_size] != numbers[:, edge - 1 : edge + block_size - 1]
    ).astype(jnp.int32)
    positions = place * block_size + jnp.arange(block_size, dtype=jnp.int32)
    ending = (positions == devices_seq * block_size - 1)[None, :]
    last = (
        (numbers[:, edge + 1 : edge + block_size + 1] != numbers[:, edge : edge + block_size])
        | ending
    ).astype(jnp.int32)
    tokens_wide = tokens.astype(jnp.float32)
    in_scale = lax.rsqrt(jnp.mean(tokens_wide * tokens_wide, axis=2, keepdims=True) + 1e-05)
    unit = tokens_wide * in_scale
    norm_wide = norm_whole.astype(jnp.float32)
    normed = (unit * norm_wide).astype(jnp.bfloat16)
    projected = jnp.einsum("mtd,dhk->mthk", normed, in_weights, preferred_element_type=jnp.float32)
    state_proj = jnp.einsum(
        "mtd,dn->mtn", normed, state_weights, preferred_element_type=jnp.float32
    )
    gate = projected[..., :HEADDIM]
    step_raw = projected[..., 2 * HEADDIM :]
    conv_input = jnp.concatenate(
        [
            projected[..., HEADDIM : 2 * HEADDIM].reshape(sequences, block_size, value_width),
            state_proj,
        ],
        axis=2,
    ).astype(jnp.bfloat16)
    channels = conv_input.shape[2]
    halo_rows = from_behind(conv_input[:, block_size - edge :], "seq", 1)
    extended = jnp.concatenate([halo_rows, conv_input], axis=1)
    taps = jnp.concatenate(
        [jnp.transpose(value_taps, (1, 0, 2)).reshape(value_width, reach + 1), state_taps], axis=0
    ).astype(jnp.float32)
    pre_active = jnp.broadcast_to(taps[:, reach], (sequences, block_size, channels))
    for lag in range(reach):
        pre_active = (
            pre_active
            + taps[:, lag]
            * extended[:, edge - lag : edge - lag + block_size]
            * lag_masks[:, :block_size, lag, None]
        )
    active_sigma = jax.nn.sigmoid(pre_active)
    activated = (pre_active * active_sigma).astype(jnp.bfloat16)
    values = activated[..., :value_width].reshape(sequences, block_size, heads_here, HEADDIM)
    intake_forward = activated[..., value_width : value_width + STATE]
    readout_forward = activated[..., value_width + STATE : value_width + 2 * STATE]
    intake_reverse = jnp.flip(activated[..., value_width + 2 * STATE : value_width + 3 * STATE], 1)
    readout_reverse = jnp.flip(activated[..., value_width + 3 * STATE :], 1)
    values_reversed = jnp.flip(values, 1)
    rate = jnp.exp(decay_log)
    bias_here = jnp.transpose(step_bias)[None, None]
    step_all = jax.nn.softplus(step_raw + bias_here)
    step_forward = jnp.transpose(step_all[..., 0], (0, 2, 1))
    step_reverse = jnp.flip(jnp.transpose(step_all[..., 1], (0, 2, 1)), 2)
    log_forward = -step_forward * rate[None, :, None]
    log_reverse = -step_reverse * rate[None, :, None]
    inner_forward, local_forward, decay_forward, saved_forward = chain_forward(
        readout_forward, intake_forward, values, log_forward, step_forward, first
    )
    inner_reverse, local_reverse, decay_reverse, saved_reverse = chain_forward(
        readout_reverse,
        intake_reverse,
        values_reversed,
        log_reverse,
        step_reverse,
        jnp.flip(last, 1),
    )
    identity = (jnp.ones_like(decay_forward), jnp.zeros_like(local_forward))
    state_forward = entering((decay_forward, local_forward), "seq", affine, identity, False)[1]
    state_reverse = entering((decay_reverse, local_reverse), "seq", affine, identity, True)[1]
    out_forward, carried_forward, state_low_forward = chain_finish(
        inner_forward, readout_forward, state_forward, saved_forward[5]
    )
    out_reverse, carried_reverse, state_low_reverse = chain_finish(
        inner_reverse, readout_reverse, state_reverse, saved_reverse[5]
    )
    core = (
        out_forward
        + jnp.flip(out_reverse, 1)
        + skip[None, None, :, None] * values.astype(jnp.float32)
    )
    gate_sigma = jax.nn.sigmoid(gate)
    gated = core * gate * gate_sigma
    gate_gains = jnp.transpose(gate_whole).astype(jnp.float32)
    unscaled = (gated * gate_gains).astype(jnp.bfloat16)
    squares = jnp.sum(gated * gated, axis=(2, 3))
    partial_value = jnp.einsum(
        "mthp,dhp->mtd", unscaled, out_weights, preferred_element_type=jnp.float32
    )
    pre_out, square_sum = lax.psum((partial_value, squares), "head")
    inner_width = HEADS * HEADDIM
    gate_scale = lax.rsqrt(square_sum / inner_width + 1e-05)
    output = tokens_wide + gate_scale[..., None] * pre_out
    total_grad = (gate_scale[..., None] * out_cotangent).astype(jnp.bfloat16)
    unscaled_grad = jnp.einsum(
        "mtd,dhp->mthp", total_grad, out_weights, preferred_element_type=jnp.float32
    )
    out_weight_grad = jnp.einsum(
        "mtd,mthp->dhp", total_grad, unscaled, preferred_element_type=jnp.float32
    )
    scale_grad = jnp.sum(out_cotangent * pre_out, axis=2)
    square_grad = -0.5 * scale_grad * gate_scale**3 / inner_width
    gated_grad = unscaled_grad * gate_gains + 2.0 * gated * square_grad[..., None, None]
    gate_gain_grad = jnp.transpose(jnp.sum(unscaled_grad * gated, axis=(0, 1)))
    core_grad = (gated_grad * gate * gate_sigma).astype(jnp.bfloat16)
    gate_grad = gated_grad * core * gate_sigma * (1.0 + gate * (1.0 - gate_sigma))
    skip_grad = jnp.sum(core_grad.astype(jnp.float32) * values.astype(jnp.float32), axis=(0, 1, 3))
    core_reversed = jnp.flip(core_grad, 1)
    state_grad_forward, readout_grad_forward, sum_grad_forward = chain_back_state(
        core_grad, readout_forward, carried_forward, state_low_forward, saved_forward[5]
    )
    state_grad_reverse, readout_grad_reverse, sum_grad_reverse = chain_back_state(
        core_reversed, readout_reverse, carried_reverse, state_low_reverse, saved_reverse[5]
    )
    later_forward = entering((decay_forward, state_grad_forward), "seq", affine, identity, True)[1]
    later_reverse = entering((decay_reverse, state_grad_reverse), "seq", affine, identity, False)[1]
    (
        values_grad_forward,
        readout_grad_forward,
        intake_grad_forward,
        step_grad_forward,
        log_grad_forward,
    ) = chain_back_rest(
        core_grad,
        readout_forward,
        intake_forward,
        values,
        step_forward,
        state_forward,
        later_forward,
        decay_forward,
        saved_forward,
        readout_grad_forward,
        sum_grad_forward,
    )
    (
        values_grad_reverse,
        readout_grad_reverse,
        intake_grad_reverse,
        step_grad_reverse,
        log_grad_reverse,
    ) = chain_back_rest(
        core_reversed,
        readout_reverse,
        intake_reverse,
        values_reversed,
        step_reverse,
        state_reverse,
        later_reverse,
        decay_reverse,
        saved_reverse,
        readout_grad_reverse,
        sum_grad_reverse,
    )
    values_grad = (
        values_grad_forward
        + jnp.flip(values_grad_reverse, 1)
        + skip[None, None, :, None] * core_grad.astype(jnp.float32)
    )
    step_total_forward = step_grad_forward - rate[None, :, None] * log_grad_forward
    step_total_reverse = jnp.flip(step_grad_reverse - rate[None, :, None] * log_grad_reverse, 2)
    decay_log_grad = jnp.sum(log_grad_forward * log_forward, axis=(0, 2)) + jnp.sum(
        log_grad_reverse * log_reverse, axis=(0, 2)
    )
    step_total = jnp.stack(
        [
            jnp.transpose(step_total_forward, (0, 2, 1)),
            jnp.transpose(step_total_reverse, (0, 2, 1)),
        ],
        axis=3,
    )
    raw_grad = step_total * jax.nn.sigmoid(step_raw + bias_here)
    step_bias_grad = jnp.transpose(jnp.sum(raw_grad, axis=(0, 1)))
    state_grads = jnp.concatenate(
        [
            intake_grad_forward,
            readout_grad_forward,
            jnp.flip(intake_grad_reverse, 1),
            jnp.flip(readout_grad_reverse, 1),
        ],
        axis=2,
    )
    active_grad = jnp.concatenate(
        [values_grad.reshape(sequences, block_size, value_width), state_grads], axis=2
    )
    pre_grad = active_grad * active_sigma * (1.0 + pre_active * (1.0 - active_sigma))
    following = from_behind(pre_grad[:, :edge], "seq", -1)
    grad_extended = jnp.concatenate([pre_grad, following], axis=1)
    conv_input_grad = jnp.zeros((sequences, block_size, channels), jnp.float32)
    tap_grads = []
    for lag in range(reach):
        conv_input_grad = (
            conv_input_grad
            + taps[:, lag]
            * grad_extended[:, lag : lag + block_size]
            * lag_masks[:, lag : lag + block_size, lag, None]
        )
        tap_grads.append(
            jnp.sum(
                pre_grad
                * extended[:, edge - lag : edge - lag + block_size]
                * lag_masks[:, :block_size, lag, None],
                axis=(0, 1),
            )
        )
    tap_grads.append(jnp.sum(pre_grad, axis=(0, 1)))
    taps_grad = jnp.stack(tap_grads, axis=1)
    value_conv_grad = jnp.transpose(
        taps_grad[:value_width].reshape(heads_here, HEADDIM, reach + 1), (1, 0, 2)
    )
    state_conv_grad = taps_grad[value_width:]
    proj_grad = jnp.concatenate(
        [
            gate_grad,
            conv_input_grad[..., :value_width].reshape(sequences, block_size, heads_here, HEADDIM),
            raw_grad,
        ],
        axis=3,
    ).astype(jnp.bfloat16)
    state_proj_grad = conv_input_grad[..., value_width:].astype(jnp.bfloat16)
    normed_part = jnp.einsum(
        "mthk,dhk->mtd", proj_grad, in_weights, preferred_element_type=jnp.float32
    )
    normed_part = normed_part + jnp.einsum(
        "mtn,dn->mtd", state_proj_grad, state_weights, preferred_element_type=jnp.float32
    )
    normed_grad = lax.psum(normed_part, "head")
    in_weight_grad = jnp.einsum(
        "mtd,mthk->dhk", normed, proj_grad, preferred_element_type=jnp.float32
    )
    state_weight_grad = jnp.einsum(
        "mtd,mtn->dn", normed, state_proj_grad, preferred_element_type=jnp.float32
    )
    norm_gain_grad = jnp.sum(normed_grad * unit, axis=(0, 1))
    unit_grad = normed_grad * norm_wide
    input_gradient = out_cotangent + in_scale * (
        unit_grad - unit * jnp.mean(unit_grad * unit, axis=2, keepdims=True)
    )
    in_weight_out, out_weight_out, value_conv_out, norm_gain_out, gate_gain_out = (
        lax.psum_scatter(in_weight_grad, "seq", scatter_dimension=0, tiled=True),
        lax.psum_scatter(out_weight_grad, "seq", scatter_dimension=0, tiled=True),
        lax.psum_scatter(value_conv_grad, "seq", scatter_dimension=0, tiled=True),
        lax.psum_scatter(norm_gain_grad, "seq", scatter_dimension=0, tiled=True),
        lax.psum_scatter(gate_gain_grad, "seq", scatter_dimension=0, tiled=True),
    )
    state_weight_out, state_conv_out = (
        lax.psum_scatter(state_weight_grad, ("seq", "head"), scatter_dimension=0, tiled=True),
        lax.psum_scatter(state_conv_grad, ("seq", "head"), scatter_dimension=0, tiled=True),
    )
    step_bias_out, decay_log_out, skip_out = lax.psum(
        (step_bias_grad, decay_log_grad, skip_grad), "seq"
    )
    return (
        output,
        input_gradient,
        in_weight_out,
        state_weight_out,
        state_conv_out,
        out_weight_out,
        value_conv_out,
        norm_gain_out,
        gate_gain_out,
        step_bias_out,
        decay_log_out,
        skip_out,
    )


LANES = 128
WIDE, LOW = jnp.float32, jnp.bfloat16
FAR = -1e30


def dot(left, right):
    return jnp.dot(left, right, preferred_element_type=WIDE)


def dot_nt(left, right):
    return lax.dot_general(left, right, (((1,), (1,)), ((), ())), preferred_element_type=WIDE)


def halves(value):
    high = value.astype(LOW)
    return jnp.concatenate([high, (value - high.astype(WIDE)).astype(LOW)], axis=1)


def iota(shape, axis):
    return lax.broadcasted_iota(jnp.int32, shape, axis)


def head_columns(heads):
    row = jnp.arange(2 * LANES)[:, None] % LANES
    head = jnp.arange(heads * HEADDIM)[None, :] // HEADDIM
    spread_both = [(row == 2 * head + d).astype(LOW) for d in range(2)]
    gather_both = [jnp.concatenate([s[:LANES].T, s[:LANES].T], axis=0) for s in spread_both]
    return spread_both, gather_both


def steps_of(raw, bias):
    shifted = raw + bias
    small = jnp.exp(-jnp.abs(shifted))
    exponent = jnp.exp(jnp.minimum(shifted, 0.0))
    step = jnp.where(
        shifted < -15.0, exponent, jnp.maximum(shifted, 0.0) + jnp.log1p(small)
    )
    sigma = exponent / (1.0 + small)
    ratio = jnp.where(shifted < -15.0, 1.0, sigma / step)
    return step, sigma, ratio


def odd_lanes(shape):
    return iota(shape, 1) % 2 == 1


def running_sums(value, flip):
    size = value.shape[0]
    row, col = iota((2 * size, size), 0), iota((2 * size, size), 1)
    keep = jnp.logical_or(
        jnp.logical_and(row < size, row >= col), jnp.logical_and(row >= size, row - size <= col)
    )
    keep = keep.astype(WIDE).astype(LOW)
    high = value.astype(LOW)
    rest = value - high.astype(WIDE)
    middle = rest.astype(LOW)
    last = (rest - middle.astype(WIDE)).astype(LOW)
    sums = dot(keep, high) + dot(keep, middle) + dot(keep, last)
    odd = odd_lanes(value.shape)
    if flip:
        return jnp.where(odd, sums[:size], sums[size:])
    return jnp.where(odd, sums[size:], sums[:size])


def start_masks(starts, block, blocks, shape):
    size = shape[0]
    start = starts[block]
    following = starts[jnp.minimum(block + 1, blocks - 1)]
    none = start >= size
    ended = jnp.logical_or(block == blocks - 1, following == 0)
    row, odd = iota(shape, 0), odd_lanes(shape)
    after = row >= start
    tail_forward = jnp.logical_or(after, none)
    tail_reverse = jnp.logical_or(jnp.logical_not(after), jnp.logical_or(none, start == 0))
    head_forward = jnp.logical_not(after)
    head_reverse = jnp.logical_and(jnp.logical_or(after, none), jnp.logical_not(ended))
    tail = jnp.where(odd, tail_reverse.astype(WIDE), tail_forward.astype(WIDE))
    head = jnp.where(odd, head_reverse.astype(WIDE), head_forward.astype(WIDE))
    whole_reverse = jnp.logical_and(jnp.logical_or(none, start == 0), jnp.logical_not(ended))
    whole = jnp.where(
        odd[:8],
        jnp.where(whole_reverse, 1.0, 0.0),
        jnp.where(none, 1.0, 0.0),
    )
    return tail, head, whole


def chain_last(cum):
    return jnp.where(odd_lanes((1, cum.shape[1])), cum[:1], cum[-1:])


def table_bias(starts, block, size):
    row, col = iota((size, size), 0), iota((size, size), 1)
    start = starts[block]
    same = (row >= start) == (col >= start)
    return jnp.where(jnp.logical_and(same, row != col), 0.0, FAR)


def lane_half(size, second):
    return ((iota((size, LANES), 1) >= HEADDIM) == second).astype(WIDE).astype(LOW)


def block_diagonal(pair):
    size = pair.shape[0]
    return jnp.concatenate([pair * lane_half(size, False), pair * lane_half(size, True)], axis=0)


def silu_slope(value, sigma):
    return sigma * (1.0 + value * (1.0 - sigma))


def below(value):
    return jnp.concatenate([jnp.zeros_like(value), value], axis=0)


def above(value):
    return jnp.concatenate([value, jnp.zeros_like(value)], axis=0)


def rows_sum(value):
    total = value[:8]
    for at in range(8, value.shape[0], 8):
        total = total + value[at : at + 8]
    return total


def in_order(starts, mine, other):
    first = starts[starts.shape[0] - 1] == 0
    return jnp.concatenate(
        [jnp.where(first, mine[...], other[...]), jnp.where(first, other[...], mine[...])], axis=0
    )


def keep_own(starts, value, keep, send):
    first = starts[starts.shape[0] - 1] == 0
    size = value.shape[0] // 2
    keep[...] = jnp.where(first, value[:size], value[size:]).astype(keep.dtype)
    send[...] = jnp.where(first, value[size:], value[:size]).astype(send.dtype)


def document_of(starts, pair, blocks, size, place):
    far = 4 * size
    first, second = starts[2 * pair], starts[2 * pair + 1]
    before = starts[jnp.maximum(2 * pair - 1, 0)]
    behind = starts[jnp.minimum(2 * pair + 2, blocks - 1)]
    first = jnp.where(first < size, first, far)
    second = jnp.where(second < size, second + size, far)
    behind = jnp.where(behind < size, behind + 2 * size, far)
    before = jnp.where(before < size, before - size, -far)
    number = (place >= first).astype(jnp.int32) + (place >= second).astype(jnp.int32)
    return number + (place >= behind).astype(jnp.int32) + (place >= before).astype(jnp.int32)


def skip_lanes(small, spread):
    parts = dot(small[:, small.shape[1] - LANES :].astype(LOW), spread[:LANES])
    return parts[6:7] + parts[7:8] + parts[8:9]


def step_rows(small, heads):
    part = small[:, small.shape[1] - LANES :]
    bias = part[0:1] + part[1:2] + part[2:3]
    rate = jnp.exp(part[3:4] + part[4:5] + part[5:6])
    return bias, jnp.where(iota((1, LANES), 1) < 2 * heads, rate, 0.0)


def shard_rows(starts, side, index, rows):
    chip, core = starts[starts.shape[0] - 2], starts[starts.shape[0] - 1]
    seq = 2 * jnp.bitwise_xor(chip, side) + (core if index == 0 else 1 - core)
    return pl.ds(pl.multiple_of(seq * rows, 32), rows)


def forward_kernel(
    starts, mine, other, pay, pay_x, pay_y, pay_far, pay_far_other, spread_f, spread_r,
    normed_o, conv_o, pre_o, act_o, out_f_o, cum_o, raw_o, state_f_o, decay_f_o, decay_r_o,
    weights_o, small_o, core_o, state_r_o,
    tail_s, state_s, sum_s, head_s, read_s, local_s, decay_s,
):
    step_at = pl.program_id(0)
    pairs = pl.num_programs(0) // 2
    blocks = 2 * pairs
    size = mine.shape[0]
    inner = out_f_o.shape[1]
    channels = inner + 4 * STATE
    reach = 4

    @pl.when(step_at == 0)
    def _():
        tail_s[...] = jnp.zeros_like(tail_s)
        state_s[...] = jnp.zeros_like(state_s)
        rows = pay.shape[1] - 16
        shards = [pay.at[0], pay.at[1], pay_x.at[0], pay_x.at[1], pay_y.at[0], pay_y.at[1]]
        shards = shards + [pay_far, pay_far_other]
        total = jnp.zeros(small_o.shape, WIDE)
        for i, shard in enumerate(shards):
            weights_o[shard_rows(starts, i // 2, i % 2, rows), :] = shard[:rows, :]
            total = total + shard[rows:, :].astype(WIDE)
        small_o[...] = total

    @pl.when(step_at < pairs)
    def _():
        pair = step_at
        small = small_o[...]
        bias_row, rate_row = step_rows(small, inner // HEADDIM)
        skip_row = skip_lanes(small, spread_f)
        norm_row = jnp.concatenate([small[i : i + 1, inner:channels] for i in (5, 6, 7)], axis=1)
        taps = small[:8, :channels]
        wide = in_order(starts, mine, other).astype(WIDE)
        scale = lax.rsqrt(jnp.mean(wide * wide, axis=1, keepdims=True) + 1e-05)
        normed = (wide * scale * norm_row).astype(LOW)
        normed_o[...] = normed
        raw = dot(normed, weights_o[:, channels:])
        raw_o[...] = raw

        step, _, _ = steps_of(raw, bias_row)
        log_decay = -step * rate_row
        subs = [slice(0, size), slice(size, 2 * size)]
        cums = [running_sums(log_decay[rows], False) for rows in subs]
        cum = jnp.concatenate(cums, axis=0)
        cum_o[...] = cum
        late = cum - jnp.log(step)
        masks = [start_masks(starts, 2 * pair + sub, blocks, (size, LANES)) for sub in range(2)]
        last = [jnp.broadcast_to(chain_last(value), (size, LANES)) for value in cums]
        tail = jnp.exp(jnp.concatenate(last, axis=0) - late)
        tail = halves(tail * jnp.concatenate([mask[0] for mask in masks], axis=0))
        head = halves(jnp.exp(cum) * jnp.concatenate([mask[1] for mask in masks], axis=0))
        decay = [jnp.exp(value[:8]) * mask[2] for value, mask in zip(last, masks)]
        decay = halves(jnp.concatenate(decay, axis=0))
        decay_f, decay_r = dot(decay, spread_f[...]), dot(decay, spread_r[...])
        decay_f_o[...], decay_r_o[...] = decay_f, decay_r

        row = iota((2 * size, LANES), 0)
        number = document_of(starts, pair, blocks, size, row)
        lag_masks = [
            (number == document_of(starts, pair, blocks, size, row - lag)).astype(WIDE)
            for lag in range(1, reach)
        ]
        for chunk in range(0, channels, 2 * LANES):
            both = dot(normed, weights_o[:, chunk : chunk + 2 * LANES]).astype(LOW)
            conv_o[:, chunk : chunk + 2 * LANES] = both
            for at in (0, LANES):
                lanes = slice(chunk + at, chunk + at + LANES)
                here = both[:, at : at + LANES].astype(WIDE)
                extended = jnp.concatenate([tail_s[:, lanes], here], axis=0)
                tail_s[:, lanes] = here[2 * size - 8 :]
                pre = taps[4:5, lanes] + taps[0:1, lanes] * here
                for lag in range(1, reach):
                    shifted = pltpu.roll(extended, lag, 0)[8:]
                    pre = pre + taps[lag : lag + 1, lanes] * shifted * lag_masks[lag - 1]
                pre_o[:, lanes] = pre
                act_o[:, lanes] = (pre * jax.nn.sigmoid(pre)).astype(LOW)

        values_wide = act_o[:, :inner].astype(WIDE)
        scaled_f = (dot(tail, spread_f[...]) * values_wide).astype(LOW)
        scaled_r = (dot(tail, spread_r[...]) * values_wide).astype(LOW)
        head_f = dot(head, spread_f[...])
        here = pl.ds(pl.multiple_of(pair * 2 * size, 2 * size), 2 * size)
        head_s[here] = head
        read_s[here] = act_o[:, inner + 2 * STATE :]
        row, col = iota((size, size), 0), iota((size, size), 1)
        lower = row > col
        lower_low = lower.astype(WIDE).astype(LOW)
        upper_low = (row < col).astype(WIDE).astype(LOW)
        for sub, rows in enumerate(subs):
            block = 2 * pair + sub
            late_rows = late[rows].T
            state_act = act_o[rows, inner:]
            turned = state_act.astype(WIDE).T.astype(LOW)
            forward_act, reverse_act = state_act[:, : 2 * STATE], state_act[:, 2 * STATE :]
            scores = jnp.where(
                lower,
                dot(forward_act, below(turned[:STATE])),
                dot(reverse_act, below(turned[2 * STATE : 3 * STATE])),
            )
            bias = table_bias(starts, block, size)
            state = state_s[...]
            states = slice(sub * STATE, (sub + 1) * STATE)
            state_f_o[states] = state
            carried = dot(forward_act, below(state.astype(LOW))) * head_f[rows]
            local_f = dot(turned[:STATE], scaled_f[rows])
            state_s[...] = decay_f[8 * sub : 8 * sub + 1] * state + local_f
            local_r = dot(turned[2 * STATE : 3 * STATE], scaled_r[rows])
            local_s[pl.ds(pl.multiple_of(block * STATE, STATE), STATE)] = local_r
            decay_s[pl.ds(pl.multiple_of(block * 8, 8), 8)] = decay_r[8 * sub : 8 * sub + 8]
            base = skip_row * values_wide[rows]
            at = pl.ds(pl.multiple_of(block * size, size), size)
            for heads in range(inner // LANES):
                lanes = slice(heads * LANES, (heads + 1) * LANES)
                lefts, rights = [], []
                for head_at in (2 * heads, 2 * heads + 1):
                    c = 2 * head_at
                    gap = jnp.where(
                        lower,
                        cums[sub][:, c : c + 1] - late_rows[c : c + 1],
                        cums[sub][:, c + 1 : c + 2] - late_rows[c + 1 : c + 2],
                    )
                    mix = (scores * jnp.exp(gap + bias)).astype(LOW)
                    lefts.append(mix * lower_low)
                    rights.append(mix * upper_low)
                both = jnp.concatenate(
                    [jnp.concatenate(lefts, axis=1), jnp.concatenate(rights, axis=1)], axis=0
                )
                result = dot(both, block_diagonal(act_o[rows, lanes]))
                out_f = result[:size] + carried[:, lanes]
                out_f_o[rows, lanes] = out_f
                sum_s[at, lanes] = out_f + result[size:] + base[:, lanes]

    @pl.when(step_at == pairs)
    def _():
        state_s[...] = jnp.zeros_like(state_s)

    @pl.when(step_at >= pairs)
    def _():
        pair = 2 * pairs - 1 - step_at
        here = pl.ds(pl.multiple_of(pair * 2 * size, 2 * size), 2 * size)
        head_r = dot(head_s[here], spread_r[...])
        for sub in (1, 0):
            block, rows = 2 * pair + sub, slice(sub * size, (sub + 1) * size)
            at = pl.ds(pl.multiple_of(block * size, size), size)
            state = state_s[...]
            state_r_o[sub * STATE : (sub + 1) * STATE] = state
            carried = dot(read_s[at], below(state.astype(LOW)))
            core_o[rows] = sum_s[at] + head_r[rows] * carried
            local_r = local_s[pl.ds(pl.multiple_of(block * STATE, STATE), STATE)]
            decay_r = decay_s[pl.ds(pl.multiple_of(block * 8, 8), 8)]
            state_s[...] = decay_r[:1] * state + local_r


def output_kernel(
    starts, normed, core, mine, other, pay, small,
    gate_o, unscaled_o, unscaled_grad_o, sums_o, keep_o, send_o, gate_w,
    out_w,
):
    size, inner = mine.shape[0], core.shape[1]

    @pl.when(pl.program_id(0) == 0)
    def _():
        seqs, planes, rows, cols = pay.shape
        groups, half = planes // 2, cols // 2
        core_at = starts[starts.shape[0] - 1]
        for seq in range(seqs):
            for group in range(groups):
                part = pay[seq, core_at * groups + group]
                at, lanes = slice(seq * rows, (seq + 1) * rows), slice(group * half, (group + 1) * half)
                gate_w[at, lanes] = part[:, :half]
                out_w[at, lanes] = part[:, half:]

    gate = dot(normed[...], gate_w[...])
    gate_o[...] = gate.astype(gate_o.dtype)
    unscaled_grad = dot(in_order(starts, mine, other), out_w[...])
    unscaled_grad_o[...] = unscaled_grad.astype(unscaled_grad_o.dtype)
    gated = core[...] * gate * jax.nn.sigmoid(gate)
    unscaled = (gated * small[5:6, :inner]).astype(LOW)
    unscaled_o[...] = unscaled
    squares = jnp.sum(gated * gated, axis=1, keepdims=True)
    products = jnp.sum(unscaled_grad * unscaled.astype(WIDE), axis=1, keepdims=True)
    both = jnp.where(iota((2 * size, LANES), 1) == 0, squares, products)
    for sub in range(2):
        rows = slice(sub * size, (sub + 1) * size)
        sums_o[:, rows] = both[rows].T[:8]
    keep_own(starts, dot_nt(unscaled, out_w[...]), keep_o, send_o)


def gate_back_kernel(
    starts, own_sums, other_sums, mine, other, out_f, core, act, gate, unscaled_grad, cum, decay_r,
    small, spread_f, spread_r, gather_f, gather_r,
    total_o, core_grad_o, gate_grad_o, row_sums_o, back_f_o, later_r_o, gain_grad_o, skip_grad_o,
    later_s,
):
    pair, pairs = pl.program_id(0), pl.num_programs(0)
    blocks = 2 * pairs
    size, inner = mine.shape[0], out_f.shape[1]
    inner_width = HEADS * HEADDIM

    @pl.when(pair == 0)
    def _():
        later_s[...] = jnp.zeros_like(later_s)
        gain_grad_o[...] = jnp.zeros_like(gain_grad_o)
        skip_grad_o[...] = jnp.zeros_like(skip_grad_o)

    sums = own_sums[...] + other_sums[...]
    empty = jnp.zeros((size - 8, size), WIDE)
    sums = jnp.concatenate(
        [
            jnp.concatenate([sums[:, at : at + size], empty], axis=0).T
            for at in (0, size)
        ],
        axis=0,
    )
    skip_row, gain_row = skip_lanes(small[...], spread_f), small[5:6, :inner]
    scale = lax.rsqrt(sums[:, 0:1] / inner_width + 1e-05)
    square_grad = sums[:, 1:2] * scale * scale * scale / inner_width
    total_o[...] = (scale * in_order(starts, mine, other).astype(WIDE)).astype(LOW)
    values = act[:, :inner].astype(WIDE)
    core_here = core[...]
    gate_value = gate[...].astype(WIDE)
    sigma = jax.nn.sigmoid(gate_value)
    slope = gate_value * sigma
    gated = core_here * slope
    unscaled = scale * unscaled_grad[...].astype(WIDE)
    gain_grad_o[...] += rows_sum(unscaled * gated)
    gated_grad = unscaled * gain_row - gated * square_grad
    core_grad = (gated_grad * slope).astype(LOW)
    core_grad_o[...] = core_grad
    gate_grad_o[...] = (gated_grad * core_here * silu_slope(gate_value, sigma)).astype(LOW)
    grad_wide = core_grad.astype(WIDE)
    skip_grad_o[...] += rows_sum(grad_wide * values)
    out_f_here = out_f[...]
    out_r_here = core_here - out_f_here - skip_row * values
    row_sums_o[...] = dot(halves(grad_wide * out_f_here), gather_f[...]) + dot(
        halves(grad_wide * out_r_here), gather_r[...]
    )
    for sub in range(2):
        rows, states = slice(sub * size, (sub + 1) * size), slice(sub * STATE, (sub + 1) * STATE)
        _, head_mask, _ = start_masks(starts, 2 * pair + sub, blocks, (size, LANES))
        head = halves(jnp.exp(cum[rows]) * head_mask)
        turned = act[rows, inner:].astype(WIDE).T.astype(LOW)
        grad_here = core_grad_o[rows].astype(WIDE)
        back_f_o[states] = dot(
            turned[STATE : 2 * STATE], (dot(head, spread_f[...]) * grad_here).astype(LOW)
        )
        back_r = dot(turned[3 * STATE :], (dot(head, spread_r[...]) * grad_here).astype(LOW))
        later = later_s[...]
        later_r_o[states] = later
        later_s[...] = decay_r[8 * sub : 8 * sub + 1] * later + back_r


def chain_back_kernel(
    starts, core_grad, gate_grad, act, conv, pre, cum, raw, row_sums, state_f, state_f_next,
    state_r, state_r_last, back_f, later_r, decay_f, gate_w, weights, small, spread_f, spread_r,
    gather_f, gather_r,
    proj_o, keep_o, send_o, taps_grad_o, scalar_o,
    later_s, next_s, values_f_s, values_r_s, active_s, raw_grad_s,
):
    step_at, pairs = pl.program_id(0), pl.num_programs(0)
    pair, blocks = pairs - 1 - step_at, 2 * pairs
    size, inner = core_grad.shape[0] // 2, core_grad.shape[1]
    channels = inner + 4 * STATE
    reach = 4

    @pl.when(step_at == 0)
    def _():
        later_s[...] = jnp.zeros_like(later_s)
        next_s[...] = jnp.zeros_like(next_s)
        taps_grad_o[...] = jnp.zeros_like(taps_grad_o)
        scalar_o[...] = jnp.zeros_like(scalar_o)

    small_here = small[...]
    bias_row, rate_row = step_rows(small_here, inner // HEADDIM)
    skip_row, taps = skip_lanes(small_here, spread_f), small_here[:8, :channels]
    step_all, sigma_all, ratio_all = steps_of(raw[...], bias_row)
    log_step = jnp.log(step_all)
    row, col = iota((size, size), 0), iota((size, size), 1)
    ahead = col > row
    ahead_low = ahead.astype(WIDE).astype(LOW)
    behind_low = (col < row).astype(WIDE).astype(LOW)
    for sub in (1, 0):
        block = 2 * pair + sub
        rows, states = slice(sub * size, (sub + 1) * size), slice(sub * STATE, (sub + 1) * STATE)
        step, sigma, ratio = step_all[rows], sigma_all[rows], ratio_all[rows]
        cum_here = cum[rows]
        late = cum_here - log_step[rows]
        cum_rows = cum_here.T
        tail_mask, head_mask, _ = start_masks(starts, block, blocks, cum_here.shape)
        tail = halves(jnp.exp(chain_last(cum_here) - late) * tail_mask)
        head = halves(jnp.exp(cum_here) * head_mask)
        state_act = act[rows, inner:]
        turned = state_act.astype(WIDE).T.astype(LOW)
        forward_act, reverse_act = state_act[:, : 2 * STATE], state_act[:, 2 * STATE :]
        scores = jnp.where(
            ahead,
            dot(forward_act, above(turned[STATE : 2 * STATE])),
            dot(reverse_act, above(turned[3 * STATE :])),
        )
        bias = table_bias(starts, block, size)
        scores_grad = jnp.zeros((size, size), WIDE)
        for heads in range(inner // LANES):
            lanes = slice(heads * LANES, (heads + 1) * LANES)
            grad_blocks = block_diagonal(core_grad[rows, lanes])
            mix_grad = dot_nt(act[rows, lanes], grad_blocks)
            lefts, rights = [], []
            for at in range(2):
                c = 2 * (2 * heads + at)
                gap = jnp.where(
                    ahead,
                    cum_rows[c : c + 1] - late[:, c : c + 1],
                    cum_rows[c + 1 : c + 2] - late[:, c + 1 : c + 2],
                )
                table = jnp.exp(gap + bias)
                mix = (scores * table).astype(LOW)
                lefts.append(mix * ahead_low)
                rights.append(mix * behind_low)
                scores_grad = scores_grad + mix_grad[:, at * size : (at + 1) * size] * table
            both = jnp.concatenate(
                [jnp.concatenate(lefts, axis=1), jnp.concatenate(rights, axis=1)], axis=0
            )
            result = dot(both, grad_blocks)
            values_f_s[rows, lanes] = result[:size]
            values_r_s[rows, lanes] = result[size:]

        grad_wide = core_grad[rows].astype(WIDE)
        values = act[rows, :inner].astype(WIDE)
        later_f, later_r_here = later_s[...], later_r[states]
        later_f_low, later_r_low = later_f.astype(LOW), later_r_here.astype(LOW)
        tail_f, tail_r = dot(tail, spread_f[...]), dot(tail, spread_r[...])
        values_f = values_f_s[rows] + tail_f * dot(forward_act, above(later_f_low))
        values_r = values_r_s[rows] + tail_r * dot(reverse_act, above(later_r_low))
        col_sums = dot(halves(values * values_f), gather_f[...]) + dot(
            halves(values * values_r), gather_r[...]
        )
        after_f = state_f_next[...] if sub else state_f[STATE:]
        after_r = state_r[:STATE] if sub else state_r_last[...]
        end_f = dot(halves(rows_sum(later_f * after_f)), gather_f[...])
        end_r = dot(halves(rows_sum(later_r_here * after_r)), gather_r[...])
        end_f = jnp.sum(end_f, axis=0, keepdims=True)
        end_r = jnp.sum(end_r, axis=0, keepdims=True)
        at_row = iota(cum_here.shape, 0)
        cum_grad = row_sums[rows] - col_sums
        cum_grad = cum_grad + jnp.where(at_row == size - 1, end_f, 0.0)
        cum_grad = cum_grad + jnp.where(at_row == 0, end_r, 0.0)
        log_grad = running_sums(cum_grad, True)
        raw_grad = col_sums * ratio - rate_row * log_grad * sigma
        raw_grad_s[rows] = raw_grad
        scalar_o[0:8] += rows_sum(raw_grad)
        scalar_o[8:16] += rows_sum(log_grad * (-step * rate_row))

        mid = scores_grad.T
        pieces = []
        for act_pair, spread_head, state, later_low, forward_side in (
            (forward_act, spread_f, state_f, later_f_low, True),
            (reverse_act, spread_r, state_r, later_r_low, False),
        ):
            tail_here = tail_f if forward_side else tail_r
            scaled = (tail_here * values).astype(LOW)
            carried_grad = (dot(head, spread_head[...]) * grad_wide).astype(LOW)
            own = ahead_low if forward_side else behind_low
            mirrored = behind_low if forward_side else ahead_low
            sides = jnp.concatenate(
                [scores_grad.astype(LOW) * own, mid.astype(LOW) * mirrored], axis=1
            )
            swapped = pltpu.roll(act_pair.astype(WIDE), STATE, 1).astype(LOW)
            pieces.append(
                dot_nt(scaled, above(later_low))
                + dot_nt(carried_grad, below(state[states].astype(LOW)))
                + dot(sides, block_diagonal(swapped))
            )
        active_s[rows, :inner] = values_f + values_r + skip_row * grad_wide
        active_s[rows, inner : inner + LANES] = pieces[0]
        active_s[rows, inner + LANES :] = pieces[1]
        later_s[...] = decay_f[8 * sub : 8 * sub + 1] * later_f + back_f[states]

    row = iota((2 * size, LANES), 0)
    number = document_of(starts, pair, blocks, size, row)
    masks = [
        (number == document_of(starts, pair, blocks, size, row + lag)).astype(WIDE)
        for lag in range(1, reach)
    ]
    for at in range(0, channels, LANES):
        lanes = slice(at, at + LANES)
        pre_here = pre[:, lanes]
        grad = active_s[:, lanes] * silu_slope(pre_here, jax.nn.sigmoid(pre_here))
        extended = jnp.concatenate([grad, next_s[:, lanes]], axis=0)
        next_s[:, lanes] = grad[:8]
        source = conv[:, lanes].astype(WIDE)
        result = taps[0:1, lanes] * grad
        taps_grad_o[0:8, lanes] += rows_sum(grad * source)
        taps_grad_o[32:40, lanes] += rows_sum(grad)
        for lag in range(1, reach):
            shifted = pltpu.roll(extended, 2 * size + 8 - lag, 0)[: 2 * size] * masks[lag - 1]
            result = result + taps[lag : lag + 1, lanes] * shifted
            taps_grad_o[8 * lag : 8 * lag + 8, lanes] += rows_sum(shifted * source)
        proj_o[:, lanes] = result.astype(LOW)
    proj_o[:, channels:] = raw_grad_s[...].astype(LOW)
    normed = dot_nt(gate_grad[...], gate_w[...]) + dot_nt(proj_o[...], weights[...])
    keep_own(starts, normed, keep_o, send_o)


def by_pair(kernel, blocks, order, ins, outs, scratch, name, work):
    steps = blocks // 2

    def at(i):
        if order == "both":
            return jnp.minimum(i, steps - 1)
        return steps - 1 - i if order == "down" else i

    def spec(shape, kind):
        part = (shape[0] // steps,) + shape[1:]
        single = (shape[0] // blocks,) + shape[1:]
        if kind == "scalar":
            return pl.BlockSpec(memory_space=pltpu.SMEM)
        if kind == "rows":
            return pl.BlockSpec(part, lambda i: (at(i), 0))
        if kind == "back":
            return pl.BlockSpec(part, lambda i: (steps - 1 - jnp.maximum(i - steps, 0), 0))
        if kind == "half":
            return pl.BlockSpec((None,) + shape[1:], lambda i: (at(i), 0, 0))
        if kind == "lanes":
            return pl.BlockSpec((shape[0], shape[1] // steps), lambda i: (0, at(i)))
        if kind == "next":
            return pl.BlockSpec(single, lambda i: (jnp.minimum(2 * at(i) + 2, blocks - 1), 0))
        if kind == "last":
            return pl.BlockSpec(single, lambda i: (jnp.maximum(2 * at(i) - 1, 0), 0))
        return pl.BlockSpec(shape, lambda i: (0,) * len(shape))

    return pl.pallas_call(
        kernel,
        grid=(2 * steps if order == "both" else steps,),
        in_specs=[spec(value.shape, kind) for value, kind in ins],
        out_specs=[spec(value.shape, kind) for value, kind in outs],
        out_shape=[value for value, _ in outs],
        scratch_shapes=[pltpu.VMEM(shape, dtype) for shape, dtype in scratch],
        compiler_params=pltpu.CompilerParams(
            dimension_semantics=("arbitrary",), vmem_limit_bytes=60 * 1024 * 1024
        ),
        cost_estimate=pl.CostEstimate(
            flops=work,
            transcendentals=0,
            bytes_accessed=sum(v.size * v.dtype.itemsize for v, _ in ins + outs),
        ),
        name=name,
    )(*[value for value, _ in ins])


def swap_core(value):
    return lax.ppermute(value, "core", [(0, 1), (1, 0)])


def swap_chip(value, side):
    return lax.ppermute(value, "chip", [(i, i ^ side) for i in range(4)])


def spread_to(value, axis):
    count = lax.axis_size(axis)
    return lax.all_to_all(jnp.broadcast_to(value[None], (count,) + value.shape), axis, 0, 0)


def shifted_sum(pieces, axis):
    count, mine = lax.axis_size(axis), lax.axis_index(axis)
    total = lax.dynamic_index_in_dim(pieces, mine, 0, keepdims=False).astype(WIDE)
    for k in range(1, count):
        piece = lax.dynamic_index_in_dim(pieces, (mine + k) % count, 0, keepdims=False)
        moved = lax.ppermute(piece, axis, [(i, (i + k) % count) for i in range(count)])
        total = total + moved.astype(WIDE)
    return total


def after(value, *others):
    return lax.optimization_barrier((value,) + others)[0]


def three_parts(value):
    high = lax.reduce_precision(value, 8, 7)
    middle = lax.reduce_precision(value - high, 8, 7)
    return jnp.stack([high, middle, lax.reduce_precision(value - high - middle, 8, 7)])


def placed(value, width, at):
    shape = value.shape[:-1] + (width,)
    return lax.dynamic_update_slice_in_dim(jnp.zeros(shape, value.dtype), value, at, value.ndim - 1)


def chip_plan(
    tokens,
    starts,
    in_weight,
    state_weight,
    state_conv,
    out_weight,
    value_conv,
    norm_gain,
    gate_gain,
    step_bias,
    decay_log,
    skip,
    out_cotangent,
):
    low, wide = LOW, WIDE
    sequences, block_size, width = tokens.shape
    chips, planes = lax.axis_size("chip"), lax.axis_size("head")
    chip, core, plane = lax.axis_index("chip"), lax.axis_index("core"), lax.axis_index("head")
    blocks = starts.shape[1]
    length = blocks * block_size
    rows, group = in_weight.shape[:2]
    groups = planes // 2
    heads_here = group * groups
    inner_here, group_inner = heads_here * HEADDIM, group * HEADDIM
    part, reach = value_conv.shape[0], state_conv.shape[1] - 1
    state_part = state_conv.shape[0]
    channels_state = state_weight.shape[1]
    channels = inner_here + channels_state
    seq = 2 * chip + core
    first = core == 0

    def own_plane(value):
        return lax.dynamic_slice_in_dim(value, plane * chips, chips, 0)

    tokens_plane = own_plane(tokens)
    tokens_plane, in_weight, out_weight = lax.optimization_barrier(
        (tokens_plane, in_weight, out_weight)
    )
    tokens_mine = lax.all_to_all(tokens_plane, "chip", 0, 0)

    step_at = (plane % groups) * 2 * group
    pair_weights = placed(in_weight[:, :, 2 * HEADDIM :].reshape(rows, 2 * group), LANES, step_at)
    tap_lanes = placed(value_conv.transpose(2, 1, 0), HEADDIM, part * seq).reshape(reach + 1, -1)
    gain_lanes = placed(gate_gain.transpose(1, 0), HEADDIM, part * seq).reshape(1, -1)
    extra_value = jnp.concatenate([tap_lanes, gain_lanes], axis=0)
    scalars = jnp.stack(
        [step_bias.T.reshape(-1), jnp.repeat(decay_log, 2), jnp.repeat(skip, 2)]
    )
    scalars = jnp.swapaxes(three_parts(jnp.where(seq == 0, scalars, 0.0)), 0, 1)
    extra_step = placed(scalars.reshape(9, 2 * group).astype(low), LANES, step_at)
    slab = jnp.concatenate(
        [
            jnp.concatenate(
                [in_weight[:, :, HEADDIM : 2 * HEADDIM].reshape(rows, group_inner), pair_weights],
                axis=1,
            ),
            jnp.concatenate(
                [
                    jnp.pad(extra_value, ((0, 16 - extra_value.shape[0]), (0, 0))),
                    jnp.pad(extra_step, ((0, 16 - extra_step.shape[0]), (0, 0))),
                ],
                axis=1,
            ),
        ],
        axis=0,
    )
    extra_state = jnp.concatenate(
        [
            placed(state_conv.T, channels_state, state_part * seq),
            placed(norm_gain, width, rows * seq).reshape(-1, channels_state),
        ],
        axis=0,
    )
    state_slab = jnp.concatenate(
        [state_weight, jnp.pad(extra_state, ((0, 16 - extra_state.shape[0]), (0, 0)))], axis=0
    )
    shifted = [slab] + [
        lax.ppermute(slab, "head", [(i, (i + k) % planes) for i in range(planes)])
        for k in range(1, planes)
    ]
    shifted = jnp.stack(shifted)

    def for_core(which):
        picked = [
            lax.dynamic_index_in_dim(shifted, (plane - which * groups - i) % planes, 0, False)
            for i in range(groups)
        ]
        steps = picked[0][:, group_inner:]
        for i in range(1, groups):
            steps = steps + picked[i][:, group_inner:]
        return jnp.concatenate(
            [picked[i][:, :group_inner] for i in range(groups)] + [state_slab, steps], axis=1
        )

    pay = jnp.stack([for_core(core), swap_core(for_core(1 - core))])
    pay, tokens_mine = lax.optimization_barrier((pay, tokens_mine))
    tokens_other = swap_core(tokens_mine)
    pay_x, pay_y = swap_chip(pay, 1), swap_chip(pay, 2)
    pays = (pay, pay_x, pay_y, swap_chip(pay_x[0], 2), swap_chip(pay_y[1], 1))

    late_slab = jnp.concatenate(
        [
            in_weight[:, :, :HEADDIM].reshape(rows, group_inner),
            out_weight.reshape(rows, group_inner),
        ],
        axis=1,
    )
    pay_late = lax.all_gather(late_slab, ("chip", "core", "head")).reshape(2 * chips, planes, rows, -1)
    cotangent_low = own_plane(out_cotangent).astype(low)
    cotangent_low, *pays = lax.optimization_barrier((cotangent_low, *pays))
    cotangent_mine = lax.all_to_all(cotangent_low, "chip", 0, 0)
    starts_row = lax.dynamic_index_in_dim(starts, plane * chips + chip, 0, keepdims=False)
    starts_row = jnp.concatenate([starts_row, jnp.stack([chip, core]).astype(starts_row.dtype)])
    (spread_f, spread_r), (gather_f, gather_r) = head_columns(heads_here)

    def shape(rows_, cols, dtype):
        return jax.ShapeDtypeStruct((rows_, cols), dtype)

    half_low = jax.ShapeDtypeStruct((chips, block_size, width), low)
    half_wide = jax.ShapeDtypeStruct((chips, block_size, width), wide)
    states = blocks * STATE
    lane_cols = channels + LANES
    (
        normed, conv_input, pre_active, act, out_f, cum, step_raw, state_f, decay_f, decay_r, weights,
        small, core_out, state_r,
    ) = by_pair(
        forward_kernel, blocks, "both",
        [
            (starts_row, "scalar"), (tokens_mine, "half"), (tokens_other, "half"),
            *((value, "whole") for value in pays),
            (spread_f, "whole"), (spread_r, "whole"),
        ],
        [
            (shape(length, width, low), "rows"), (shape(length, channels, low), "rows"),
            (shape(length, channels, wide), "rows"), (shape(length, channels, low), "rows"),
            (shape(length, inner_here, wide), "rows"),
            (shape(length, LANES, wide), "rows"), (shape(length, LANES, wide), "rows"),
            (shape(states, inner_here, wide), "rows"),
            (shape(8 * blocks, inner_here, wide), "rows"), (shape(8 * blocks, inner_here, wide), "rows"),
            (shape(width, lane_cols, low), "whole"), (shape(16, lane_cols, wide), "whole"),
            (shape(length, inner_here, wide), "back"), (shape(states, inner_here, wide), "back"),
        ],
        [
            ((8, channels), wide), ((STATE, inner_here), wide), ((length, inner_here), wide),
            ((length, 2 * LANES), low), ((length, 2 * STATE), low), ((states, inner_here), wide),
            ((8 * blocks, inner_here), wide),
        ],
        "forward", 20_000_000_000,
    )
    cotangent_mine, normed = lax.optimization_barrier((cotangent_mine, normed))
    cotangent_other = swap_core(cotangent_mine)
    gate, unscaled, unscaled_grad, own_sums, keep, send, gate_w = by_pair(
        output_kernel, blocks, "up",
        [
            (starts_row, "scalar"), (normed, "rows"), (core_out, "rows"), (cotangent_mine, "half"),
            (cotangent_other, "half"), (pay_late, "whole"), (small, "whole"),
        ],
        [
            (shape(length, inner_here, wide), "rows"), (shape(length, inner_here, low), "rows"),
            (shape(length, inner_here, wide), "rows"), (shape(8, length, wide), "lanes"),
            (half_low, "half"), (half_low, "half"), (shape(width, inner_here, low), "whole"),
        ],
        [((width, inner_here), low)],
        "outputs", 12_000_000_000,
    )
    other_sums = swap_core(own_sums)

    squares = (own_sums[0] + other_sums[0]).reshape(chips, 2, block_size)
    squares = lax.dynamic_index_in_dim(squares, core, 1, keepdims=False)
    gate_scale = lax.rsqrt(squares / (HEADS * HEADDIM) + 1e-05)
    out_delta = gate_scale[..., None] * (keep.astype(wide) + swap_core(send).astype(wide))
    out_delta, gate = lax.optimization_barrier((out_delta.astype(low), gate))
    out_moved = lax.all_to_all(out_delta, "chip", 0, 0)

    (total_grad, core_grad, gate_grad, row_sums, back_f, later_r, gain_grad, skip_grad) = by_pair(
        gate_back_kernel, blocks, "up",
        [
            (starts_row, "scalar"), (own_sums, "lanes"), (other_sums, "lanes"), (cotangent_mine, "half"),
            (cotangent_other, "half"), (out_f, "rows"), (core_out, "rows"),
            (act, "rows"), (gate, "rows"), (unscaled_grad, "rows"), (cum, "rows"), (decay_r, "rows"),
            (small, "whole"), (spread_f, "whole"), (spread_r, "whole"),
            (gather_f, "whole"), (gather_r, "whole"),
        ],
        [
            (shape(length, width, low), "rows"), (shape(length, inner_here, low), "rows"),
            (shape(length, inner_here, low), "rows"), (shape(length, LANES, wide), "rows"),
            (shape(states, inner_here, wide), "rows"), (shape(states, inner_here, wide), "rows"),
            (shape(8, inner_here, wide), "whole"), (shape(8, inner_here, wide), "whole"),
        ],
        [((STATE, inner_here), wide)],
        "gate_back", 12_000_000_000,
    )

    def weight_grad(left, right):
        result = lax.dot_general(left, right, (((0,), (0,)), ((), ())), preferred_element_type=wide)
        return result.astype(low)

    gate_grad, total_grad, out_moved = lax.optimization_barrier((gate_grad, total_grad, out_moved))
    out_delta = lax.all_gather(out_moved, "head").reshape(sequences, block_size, width)
    early_grad = jnp.concatenate(
        [
            with_layout_constraint(weight_grad(left, right), Layout((0, 1)))
            for left, right in ((normed, gate_grad), (total_grad, unscaled))
        ],
        axis=1,
    ).reshape(chips, 2, rows, -1)
    early_grad, core_grad = lax.optimization_barrier((early_grad, core_grad))
    early_moved = lax.all_to_all(early_grad, "chip", 0, 0)
    rest_grad, keep, send, taps_grad, scalar_part = by_pair(
        chain_back_kernel, blocks, "down",
        [
            (starts_row, "scalar"), (core_grad, "rows"), (gate_grad, "rows"), (act, "rows"),
            (conv_input, "rows"), (pre_active, "rows"), (cum, "rows"), (step_raw, "rows"),
            (row_sums, "rows"), (state_f, "rows"), (state_f, "next"), (state_r, "rows"),
            (state_r, "last"), (back_f, "rows"), (later_r, "rows"), (decay_f, "rows"),
            (gate_w, "whole"), (weights, "whole"), (small, "whole"), (spread_f, "whole"),
            (spread_r, "whole"), (gather_f, "whole"), (gather_r, "whole"),
        ],
        [
            (shape(length, lane_cols, low), "rows"), (half_wide, "half"), (half_low, "half"),
            (shape(40, channels, wide), "whole"), (shape(16, LANES, wide), "whole"),
        ],
        [
            ((STATE, inner_here), wide), ((8, channels), wide), ((2 * block_size, inner_here), wide),
            ((2 * block_size, inner_here), wide), ((2 * block_size, channels), wide),
            ((2 * block_size, LANES), wide),
        ],
        "chain_back", 1_000_000_000,
    )

    norm_row = small[5 : 5 + width // channels_state, inner_here:channels].reshape(width)
    tokens_wide = tokens_mine.astype(wide)
    in_scale = lax.rsqrt(jnp.mean(tokens_wide * tokens_wide, axis=2, keepdims=True) + 1e-05)
    unit = tokens_wide * in_scale
    normed_grad = keep + swap_core(send).astype(wide)
    unit_grad = normed_grad * norm_row
    delta = in_scale * (unit_grad - unit * jnp.mean(unit_grad * unit, axis=2, keepdims=True))
    (
        delta, early_moved, normed_late, rest_grad, taps_grad, scalar_part, normed_grad,
    ) = lax.optimization_barrier(
        (
            delta.astype(low), early_moved, normed, rest_grad, taps_grad, scalar_part, normed_grad,
        )
    )
    delta = lax.all_to_all(delta, "chip", 0, 0)
    gathered = lax.all_gather(delta, "head").reshape(sequences, block_size, width)
    def between_cores(moved):
        total = jnp.sum(moved.astype(wide), axis=0).astype(low)
        mine = lax.dynamic_index_in_dim(total, core, 0, keepdims=False)
        got = swap_core(lax.dynamic_index_in_dim(total, 1 - core, 0, keepdims=False))
        return [jnp.where(first, mine, got), jnp.where(first, got, mine)]

    def group_lanes(value, at, i):
        return value[:, at + i * group_inner : at + (i + 1) * group_inner]

    early = between_cores(early_moved)
    early = jnp.stack(
        [
            jnp.concatenate([group_lanes(v, 0, i), group_lanes(v, inner_here, i)], axis=1)
            for v in early
            for i in range(groups)
        ]
    )
    early, out_delta, normed_late, rest_grad = lax.optimization_barrier(
        (early, out_delta, normed_late, rest_grad)
    )
    early = shifted_sum(early, "head")
    norm_grad = jnp.sum(normed_grad * unit, axis=(0, 1))

    taps_grad = jnp.sum(taps_grad.reshape(reach + 1, 8, channels), axis=1)
    scalar_part = jnp.sum(scalar_part.reshape(2, 8, LANES), axis=1)
    skip_part = jnp.sum(skip_grad.reshape(8, heads_here, HEADDIM), axis=(0, 2))
    skip_part = jnp.pad(jnp.repeat(skip_part, 2)[None], ((0, 0), (0, LANES - 2 * heads_here)))
    lanes_value = jnp.concatenate(
        [taps_grad[:, :inner_here], jnp.sum(gain_grad, axis=0, keepdims=True)], axis=0
    )
    lanes_state = jnp.concatenate(
        [taps_grad[:, inner_here:], norm_grad.reshape(-1, channels_state)], axis=0
    )
    lanes_step = jnp.concatenate([scalar_part, skip_part], axis=0)
    extra = jnp.concatenate(
        [
            jnp.pad(lanes_value, ((0, 16 - lanes_value.shape[0]), (0, 0))),
            jnp.pad(lanes_state, ((0, 16 - lanes_state.shape[0]), (0, 0))),
            jnp.pad(lanes_step, ((0, 16 - lanes_step.shape[0]), (0, 0))),
        ],
        axis=1,
    ).astype(low)
    extra, early = lax.optimization_barrier((extra, early))
    small_sum = extra.astype(wide)
    for side in range(1, chips):
        small_sum = small_sum + swap_chip(extra, side).astype(wide)
    small_low = small_sum.astype(low)
    for k in range(1, planes):
        moved = lax.ppermute(small_low, "head", [(i, (i + k) % planes) for i in range(planes)])
        small_sum = small_sum + moved.astype(wide)
    small_other = swap_core(small_sum)
    of_heads = jnp.where(plane // groups == core, small_sum, small_other)
    step_lanes = lax.dynamic_slice_in_dim(of_heads[:3, channels:], step_at, 2 * group, 1)
    lanes = lax.dynamic_slice_in_dim(
        of_heads[:, :inner_here], (plane % groups) * group_inner, group_inner, 1
    ).reshape(16, group, HEADDIM)
    lanes = lax.dynamic_slice_in_dim(lanes, part * seq, part, 2)
    value_conv_out = lanes[: reach + 1].transpose(2, 1, 0)
    gate_gain_out = lanes[reach + 1].transpose(1, 0)
    state_lanes = small_sum[:, inner_here:channels] + small_other[:, inner_here:channels]
    conv_at = state_part * seq + (state_part // planes) * plane
    state_conv_out = lax.dynamic_slice_in_dim(
        state_lanes[: reach + 1], conv_at, state_part // planes, 1
    ).T
    norm_sum = state_lanes[reach + 1 :][: width // channels_state].reshape(width)
    norm_gain_out = lax.dynamic_slice_in_dim(norm_sum, rows * seq, rows, 0)
    step_bias_out = step_lanes[0].reshape(group, 2).T
    decay_log_out = jnp.sum(step_lanes[1].reshape(group, 2), axis=1)
    skip_out = step_lanes[2].reshape(group, 2)[:, 0]

    late_grad = weight_grad(normed_late, rest_grad).reshape(chips, 2, rows, lane_cols)
    late_grad, delta, early = lax.optimization_barrier((late_grad, delta, early))
    late_moved = lax.all_to_all(late_grad, "chip", 0, 0)
    output = tokens.astype(wide) + out_delta.astype(wide)

    late = between_cores(late_moved)
    state_sum = late[0][:, inner_here:channels].astype(wide) + late[1][:, inner_here:channels].astype(wide)
    state_sum = state_sum.astype(low).reshape(planes, -1, group_inner + LANES)
    state_rows = state_sum.shape[1]
    late = jnp.stack(
        [
            jnp.concatenate(
                [
                    jnp.concatenate([group_lanes(late[which], 0, i), late[which][:, channels:]], axis=1),
                    jnp.pad(state_sum[which * groups + i], ((0, -state_rows % 16), (0, 0))),
                ],
                axis=0,
            )
            for which in range(2)
            for i in range(groups)
        ]
    )
    late, gathered = lax.optimization_barrier((late, gathered))
    input_gradient = out_cotangent + gathered.astype(wide)
    late = shifted_sum(late, "head")
    late_steps = lax.dynamic_slice_in_dim(late[:rows, group_inner:], step_at, 2 * group, 1)
    in_weight_out = jnp.concatenate(
        [
            early[:, :group_inner].reshape(rows, group, HEADDIM),
            late[:rows, :group_inner].reshape(rows, group, HEADDIM),
            late_steps.reshape(rows, group, 2),
        ],
        axis=2,
    )
    out_weight_out = early[:, group_inner:].reshape(rows, group, HEADDIM)
    state_weight_out = late[rows : rows + state_rows].reshape(-1, channels_state)
    return (
        output,
        input_gradient,
        in_weight_out,
        state_weight_out,
        state_conv_out,
        out_weight_out,
        value_conv_out,
        norm_gain_out,
        gate_gain_out,
        step_bias_out,
        decay_log_out,
        skip_out,
    )


def solution(mesh):
    devices_seq, planes = mesh.devices.shape
    seq, plan = "seq", split_plan
    if devices_seq % 2 == 0 and planes % 2 == 0 and devices_seq // 2 * planes == CHIP_SEQUENCES:
        shape = (devices_seq // 2, 2, planes)
        mesh = Mesh(mesh.devices.reshape(shape), ("chip", "core", "head"))
        seq, plan = ("chip", "core"), chip_plan
    both = seq + ("head",) if isinstance(seq, tuple) else (seq, "head")
    return jax.shard_map(
        plan,
        mesh=mesh,
        in_specs=(
            P(None, seq, None),
            P(),
            P(seq, "head", None),
            P(seq, None),
            P(seq, None),
            P(seq, "head", None),
            P(seq, "head", None),
            P(seq),
            P(seq, "head"),
            P(None, "head"),
            P("head"),
            P("head"),
            P(None, seq, None),
        ),
        out_specs=(
            P(None, seq, None),
            P(None, seq, None),
            P(seq, "head", None),
            P(both, None),
            P(both, None),
            P(seq, "head", None),
            P(seq, "head", None),
            P(seq),
            P(seq, "head"),
            P(None, "head"),
            P("head"),
            P("head"),
        ),
        check_vma=False,
    )
```
